32 devices in a mesh: rep: 2 (over x), fsdp: 4 (over y, core), seq: 4 (over z).
Axes of the slice: x: 2, y: 2, z: 4, core: 2. Of those that a mesh axis runs over, the one named last changes fastest.
Arguments:
- tokens: bfloat16 [2, 16, 1024, 768], P(None, ('rep', 'fsdp'), 'seq'), may hold values from -6 to 6
- segments: int32 [2, 16, 1024], P(None, ('rep', 'fsdp')), may hold values from 0 to 1023, as said below
- positions: int32 [2, 16, 1024], P(None, ('rep', 'fsdp'), 'seq'), may hold values from 0 to 1023, as said below
- gain_attn: bfloat16 [768], P('fsdp'), may hold values from 0.5 to 1.5
- w_qkv: bfloat16 [768, 2304], P('fsdp'), may hold values from -0.21875 to 0.21875
- w_out: bfloat16 [768, 768], P('fsdp'), may hold values from -0.875 to 0.875
- gain_mlp: bfloat16 [768], P('fsdp'), may hold values from 0.5 to 1.5
- w_in: bfloat16 [768, 2304], P('fsdp'), may hold values from -0.21875 to 0.21875
- w_mlp_out: bfloat16 [1152, 768], P('fsdp'), may hold values from -0.375 to 0.375
- cotangent: bfloat16 [2, 16, 1024, 768], P(None, ('rep', 'fsdp'), 'seq'), may hold values from -6 to 6
Outputs:
- block_out: bfloat16 [2, 16, 1024, 768], P(None, ('rep', 'fsdp'), 'seq')
- input_grad: float32 [2, 16, 1024, 768], P(None, ('rep', 'fsdp'), 'seq')
- grad_gain_attn: float32 [768], P('fsdp')
- grad_qkv: float32 [768, 2304], P('fsdp')
- grad_out: float32 [768, 768], P('fsdp')
- grad_gain_mlp: float32 [768], P('fsdp')
- grad_in: float32 [768, 2304], P('fsdp')
- grad_mlp_out: float32 [1152, 768], P('fsdp')
The draws below stay inside these ranges and needn't reach their ends.
Inputs may be any that keep to these rules, and one draw needn't show every extreme that they name: `segments`: along each sequence segment numbers start at 0, never fall and rise by one where a new document begins; documents range from a single token to the whole sequence. `positions`: each token's position is 0 at the first token of its document (as given by segments) and rises by one along the document.
All inputs are finite; a program needn't handle non-finite values.
Results may differ from the reference program's by a relative error of at most 0.02.
Values may be sent and summed in bfloat16 or wider, within the bound.
A program may use at most 192 MiB of HBM per device.

```python
import math
import jax
import jax.numpy as jnp
from jax import lax

D = 768
HEADS = 12
HDIM = 64
FF = 1152
LEN = 1024
MICRO = 2
BATCH = 16


def doc_marks(key):
    base = jax.random.fold_in(key, 17)
    rate_key, flag_key = jax.random.split(base)
    picks = jax.random.randint(rate_key, (MICRO, BATCH, 1), 0, 4)
    table = jnp.array([max(LEN // 32, 2), max(LEN // 8, 2), max(LEN // 2, 2), 4 * LEN], jnp.int32)
    denom = table[picks]
    raw = jax.random.randint(flag_key, (MICRO, BATCH, LEN), 0, 1 << 20)
    index = jnp.arange(LEN, dtype=jnp.int32)
    flags = jnp.logical_or(raw % denom == 0, index == 0)
    micro_ids = jnp.arange(MICRO, dtype=jnp.int32)[:, None, None]
    batch_ids = jnp.arange(BATCH, dtype=jnp.int32)[None, :, None]
    every_one = jnp.logical_and(micro_ids == 0, batch_ids == 0)
    single_doc = jnp.logical_and(micro_ids == 0, batch_ids == 1)
    flags = jnp.logical_or(flags, every_one)
    flags = jnp.where(single_doc, index == 0, flags)
    segs = jnp.cumsum(flags.astype(jnp.int32), axis=2) - 1
    starts = lax.cummax(jnp.where(flags, index, 0), axis=2)
    return (segs.astype(jnp.int32), (index - starts).astype(jnp.int32))


def draw_segments(key, part):
    return doc_marks(key)[0]


def draw_positions(key, part):
    return doc_marks(key)[1]


def steps_of(own_key, dims, cuts, least, largest):
    def one(position, shards_of):
        draws = jax.random.uniform(jax.random.fold_in(jax.random.fold_in(own_key, 6), position), (shards_of,), jnp.float32, least / len(cuts), largest / len(cuts))
        return jnp.repeat(jnp.exp(draws), dims[position] // shards_of).reshape((-1,) + (1,) * (len(dims) - position - 1))

    level = one(*cuts[0])
    for cut in cuts[1:]:
        level = level * one(*cut)
    return level


def centred(own_key, extent, spread, bound, pieces=(), held_as=jnp.bfloat16):
    values = jax.random.normal(own_key, extent, jnp.float32) * spread
    if len(pieces) > 0:
        values = steps_of(own_key, extent, pieces, -0.22, 0.18) * values
    return jnp.clip(values, min=-bound, max=bound).astype(held_as)


def setup_inputs(seed: int = 0) -> dict:
    key_of = jax.random.split(jax.random.key(seed), 11)
    return {
        "tokens": centred(key_of[0], (MICRO, BATCH, LEN, D), 1.0, 6.0, ((1, 8), (2, 4))),
        "segments": draw_segments(jax.random.fold_in(key_of[10], 71), 0),
        "positions": draw_positions(jax.random.fold_in(key_of[10], 71), 0),
        "gain_attn": jnp.clip(1.0 + 0.1 * jax.random.normal(key_of[3], (D,), jnp.float32), 0.5, 1.5).astype(jnp.bfloat16),
        "w_qkv": centred(key_of[4], (D, 3 * D), D ** -0.5, 0.21875, ((0, 4),)),
        "w_out": centred(key_of[5], (D, D), (D // 16) ** -0.5, 0.875, ((0, 4),)),
        "gain_mlp": jnp.clip(1.0 + 0.1 * jax.random.normal(key_of[6], (D,), jnp.float32), 0.5, 1.5).astype(jnp.bfloat16),
        "w_in": centred(key_of[7], (D, 2 * FF), D ** -0.5, 0.21875, ((0, 4),)),
        "w_mlp_out": centred(key_of[8], (FF, D), (FF // 4) ** -0.5, 0.375, ((0, 4),)),
        "cotangent": centred(key_of[9], (MICRO, BATCH, LEN, D), 1.0, 6.0, ((1, 8), (2, 4))),
    }


@jax.custom_vjp
def low(v):
    return lax.optimization_barrier(v.astype(jnp.bfloat16)).astype(jnp.float32)

@jax.custom_vjp
def lowprecision_backward(v):
    return v

def low_keep(v):
    return (low(v), None)

def low_pass(kept, grad):
    return (grad,)

def back_keep(v):
    return (v, None)

def back_low(kept, grad):
    return (low(grad),)
low.defvjp(low_keep, low_pass)
lowprecision_backward.defvjp(back_keep, back_low)
eps = 1e-05
theta = 160000.0

def norm_apply(values, gain):
    mean = lax.optimization_barrier(jnp.mean(values, axis=-1, keepdims=True))
    centered = values - mean
    var = lax.optimization_barrier(jnp.mean(centered * centered, axis=-1, keepdims=True))
    return centered * lax.rsqrt(var + eps) * gain

def rotary_tables(pos):
    half = jnp.arange(0, HDIM, 2).astype(jnp.float32) / HDIM
    inverse = jnp.exp(-half * math.log(theta))
    angles = pos.astype(jnp.float32)[..., None] * inverse
    angles = jnp.concatenate([angles, angles], -1)
    return (jnp.cos(angles), jnp.sin(angles))

def rotate(values, cosine, sine):
    shaped = values.reshape(values.shape[:-1] + (HEADS, HDIM))
    first = shaped[..., :HDIM // 2]
    second_normalized = shaped[..., HDIM // 2:]
    turned = jnp.concatenate([-second_normalized, first], -1)
    out = shaped * cosine[..., None, :] + turned * sine[..., None, :]
    return out.reshape(values.shape)

def group_forward(gathered_input, segg, posg, gain_one, query_key_value_weight, output_projection_weight, gain_two, input_projection_weight, perceptron_weight):
    running_max = lax.Precision.HIGHEST
    normalized_input = low(norm_apply(gathered_input, gain_one))
    query_key_value = lowprecision_backward(jnp.einsum('hpr,rn->hpn', normalized_input, query_key_value_weight, precision=running_max))
    cosine, sine = rotary_tables(posg)
    query = low(rotate(query_key_value[..., :D], cosine, sine))
    key = low(rotate(query_key_value[..., D:2 * D], cosine, sine))
    value = low(query_key_value[..., 2 * D:])
    shape = gathered_input.shape[:2] + (HEADS, HDIM)
    query = query.reshape(shape)
    key = key.reshape(shape)
    value = value.reshape(shape)
    scores = lowprecision_backward(jnp.einsum('sqhd,skhd->shqk', query, key, precision=running_max) * HDIM ** (-0.5))
    same = segg[:, :, None] == segg[:, None, :]
    scores = jnp.where(same[:, None], scores, -1000000000.0)
    probs = low(jax.nn.softmax(scores, axis=-1))
    attention_mixed_output = jnp.einsum('shqk,skhd->sqhd', probs, value, precision=running_max).reshape(gathered_input.shape)
    attention_mixed_output = low(lowprecision_backward(attention_mixed_output))
    attention_residual_sum = gathered_input + lowprecision_backward(jnp.einsum('hpr,rn->hpn', attention_mixed_output, output_projection_weight, precision=running_max))
    second_normalized = low(norm_apply(attention_residual_sum, gain_two))
    hidden_activation = lowprecision_backward(jnp.einsum('hpr,rn->hpn', second_normalized, input_projection_weight, precision=running_max))
    middle_residual = low(jax.nn.gelu(hidden_activation[..., :FF], approximate=False) * hidden_activation[..., FF:])
    return attention_residual_sum + lowprecision_backward(jnp.einsum('gmi,ip->gmp', middle_residual, perceptron_weight, precision=running_max))

def reference(tokens, segments, positions, gain_attn, w_qkv, w_out, gain_mlp, w_in, w_mlp_out, cotangent):
    groups = MICRO * BATCH // 4
    inputs = tokens.astype(jnp.float32).reshape(groups, 4, LEN, D)
    segs = segments.reshape(groups, 4, LEN)
    places = positions.reshape(groups, 4, LEN)
    params = (gain_attn.astype(jnp.float32), w_qkv.astype(jnp.float32), w_out.astype(jnp.float32), gain_mlp.astype(jnp.float32), w_in.astype(jnp.float32), w_mlp_out.astype(jnp.float32))

    def whole(inputs, gain_one, query_key_value_weight, output_projection_weight, gain_two, input_projection_weight, perceptron_weight):

        def single(item):
            return group_forward(item[0], item[1], item[2], gain_one, query_key_value_weight, output_projection_weight, gain_two, input_projection_weight, perceptron_weight)
        return lax.map(jax.checkpoint(single), (inputs, segs, places))
    result, pullback = jax.vjp(whole, inputs, *params)
    grads = pullback(cotangent.astype(jnp.float32).reshape(groups, 4, LEN, D))
    block_out = result.reshape(MICRO, BATCH, LEN, D).astype(jnp.bfloat16)
    input_grad = grads[0].reshape(MICRO, BATCH, LEN, D)
    return (block_out, input_grad, grads[1], grads[2], grads[3], grads[4], grads[5], grads[6])
```

```python
import functools
import math

import jax
import jax.numpy as jnp
from jax import lax
from jax.experimental import pallas as pl
from jax.experimental.pallas import tpu as pltpu
from jax.sharding import PartitionSpec as P

D = 768
HEADS = 12
HDIM = 64
FF = 1152
EPS = 1e-05
THETA = 160000.0
MASKED = -1000000000.0
TILE = 256
PAIR = 2 * HDIM
HCHUNK = 384
f32 = jnp.float32
bf16 = jnp.bfloat16
VMEM_LIMIT = 56 * 2**20


def dot_nn(left, right):
    return lax.dot_general(left, right, (((1,), (0,)), ((), ())), preferred_element_type=f32)


def dot_nt(left, right):
    return lax.dot_general(left, right, (((1,), (1,)), ((), ())), preferred_element_type=f32)


def dot_tn(left, right):
    return lax.dot_general(left, right, (((0,), (0,)), ((), ())), preferred_element_type=f32)


def normalize(values):
    mean = jnp.mean(values, axis=-1, keepdims=True)
    centered = values - mean
    var = jnp.mean(centered * centered, axis=-1, keepdims=True)
    scale = lax.rsqrt(var + EPS)
    return centered * scale, scale


def norm_back(unit, scale, gain, grad):
    gain_terms = grad * unit
    inner = grad * gain
    first = jnp.mean(inner, axis=-1, keepdims=True)
    second = jnp.mean(inner * unit, axis=-1, keepdims=True)
    return scale * (inner - first - unit * second), gain_terms


def lane_halves(shape):
    lane = lax.broadcasted_iota(jnp.int32, shape, len(shape) - 1)
    return lane % HDIM < HDIM // 2


def rotate_pair(values, cosine, signed_sine):
    swapped = jnp.where(
        lane_halves(values.shape),
        pltpu.roll(values, PAIR - HDIM // 2, 1),
        pltpu.roll(values, HDIM // 2, 1),
    )
    return values * cosine + swapped * signed_sine


def first_kernel(x_ref, gain_ref, w_ref, cos_ref, sin_ref, a_ref, qkv_ref):
    unit, _ = normalize(x_ref[...].astype(f32))
    a = (unit * gain_ref[...]).astype(bf16)
    a_ref[...] = a
    cosine, sine = cos_ref[...], sin_ref[...]
    for column in range(0, 3 * D, TILE):
        part = dot_nn(a, w_ref[:, column : column + TILE])
        for half in range(0, TILE, PAIR):
            start = column + half
            piece = part[:, half : half + PAIR]
            if start < 2 * D:
                piece = rotate_pair(piece, cosine, sine)
            if start < D:
                piece = piece * HDIM**-0.5
            qkv_ref[:, start : start + PAIR] = piece.astype(bf16)


def attend_kernel(q_ref, k_ref, v_ref, rows_ref, cols_ref, o_ref, p_ref):
    k, v = k_ref[...], v_ref[...]
    lane = lax.broadcasted_iota(jnp.int32, (1, PAIR), 1)
    length = k.shape[0]
    for tile in range(0, length, TILE):
        q = q_ref[tile : tile + TILE, :]
        same = rows_ref[tile : tile + TILE, :] == cols_ref[...]
        out = None
        for head in range(2):
            mine = (lane < HDIM) if head == 0 else (lane >= HDIM)
            zero = jnp.zeros((), bf16)
            scores = dot_nt(jnp.where(mine, q, zero), k)
            scores = jnp.where(same, scores, MASKED)
            top = jnp.max(scores, axis=-1, keepdims=True)
            raised = jnp.exp(scores - top)
            total = jnp.sum(raised, axis=-1, keepdims=True)
            probs = (raised * (1.0 / total)).astype(bf16)
            p_ref[head, tile : tile + TILE, :] = probs
            part = dot_nn(probs, jnp.where(mine, v, zero))
            out = part if out is None else out + part
        o_ref[tile : tile + TILE, :] = out.astype(bf16)


def middle_kernel(
    o_ref, x_ref, gain_ref, w_out_ref, w_in_ref, w_mlp_ref,
    x1_ref, b_ref, m_ref, slope_ref, act_ref, y_ref,
):
    x1 = x_ref[...].astype(f32) + dot_nn(o_ref[...], w_out_ref[...])
    x1_ref[...] = x1
    unit, _ = normalize(x1)
    b = (unit * gain_ref[...]).astype(bf16)
    b_ref[...] = b
    y = x1
    for column in range(0, FF, HCHUNK):
        hin = dot_nn(b, w_in_ref[:, column : column + HCHUNK])
        gate = dot_nn(b, w_in_ref[:, FF + column : FF + column + HCHUNK])
        phi = 0.5 + 0.5 * lax.erf(hin * math.sqrt(0.5))
        act = hin * phi
        slope = phi + hin * (jnp.exp(hin * hin * -0.5) * (1.0 / math.sqrt(2.0 * math.pi)))
        m = (act * gate).astype(bf16)
        m_ref[:, column : column + HCHUNK] = m
        act_ref[:, column : column + HCHUNK] = act.astype(bf16)
        slope_ref[:, column : column + HCHUNK] = (slope * gate).astype(bf16)
        y = y + dot_nn(m, w_mlp_ref[column : column + HCHUNK, :])
    y_ref[...] = y.astype(bf16)


def middle_back_kernel(
    dy_ref, x1_ref, slope_ref, act_ref, gain_ref, w_out_ref, w_in_ref, w_mlp_ref,
    dh_ref, low_ref, dx1_ref, do_ref, dgain_ref,
):
    dy = dy_ref[...]
    db = None
    for column in range(0, FF, HCHUNK):
        dm = dot_nt(dy, w_mlp_ref[column : column + HCHUNK, :])
        first = (dm * slope_ref[:, column : column + HCHUNK].astype(f32)).astype(bf16)
        second = (dm * act_ref[:, column : column + HCHUNK].astype(f32)).astype(bf16)
        dh_ref[:, column : column + HCHUNK] = first
        dh_ref[:, FF + column : FF + column + HCHUNK] = second
        part = dot_nt(first, w_in_ref[:, column : column + HCHUNK]) + dot_nt(
            second, w_in_ref[:, FF + column : FF + column + HCHUNK]
        )
        db = part if db is None else db + part
    unit, scale = normalize(x1_ref[...])
    back, terms = norm_back(unit, scale, gain_ref[...], db)

    @pl.when(pl.program_id(0) == 0)
    def _():
        dgain_ref[...] = jnp.zeros_like(dgain_ref)

    dgain_ref[...] += jnp.sum(terms, axis=0, keepdims=True)
    dx1 = dy.astype(f32) + back
    dx1_ref[...] = dx1
    low = dx1.astype(bf16)
    low_ref[...] = low
    do_ref[...] = dot_nt(low, w_out_ref[...]).astype(bf16)


def attend_back_kernel(
    q_ref, k_ref, v_ref, o_ref, do_ref, p_ref, cos_ref, sin_ref,
    dq_ref, dk_ref, dv_ref, key_sum, value_sum,
):
    k, v = k_ref[...], v_ref[...]
    lane = lax.broadcasted_iota(jnp.int32, (1, PAIR), 1)
    length = k.shape[0]
    zero = jnp.zeros((), bf16)
    cosine, sine = cos_ref[...], sin_ref[...]
    for tile in range(0, length, TILE):
        rows = slice(tile, tile + TILE)
        q, do = q_ref[rows, :], do_ref[rows, :]
        inner = do.astype(f32) * o_ref[rows, :].astype(f32)
        dq = None
        for head in range(2):
            mine = (lane < HDIM) if head == 0 else (lane >= HDIM)
            do_head = jnp.where(mine, do, zero)
            delta = jnp.sum(jnp.where(mine, inner, 0.0), axis=-1, keepdims=True)
            probs = p_ref[head, rows, :]
            dp = dot_nt(do_head, v)
            ds = (probs.astype(f32) * (dp - delta)).astype(bf16)
            value_part = dot_tn(probs, do_head)
            key_part = dot_tn(ds, jnp.where(mine, q, zero))
            if tile == 0 and head == 0:
                value_sum[...] = value_part
                key_sum[...] = key_part
            else:
                value_sum[...] += value_part
                key_sum[...] += key_part
            part = dot_nn(ds, jnp.where(mine, k, zero))
            dq = part if dq is None else dq + part
        dq = rotate_pair(dq * HDIM**-0.5, cosine[rows], -sine[rows])
        dq_ref[rows, :] = dq.astype(bf16)
    dk_ref[...] = rotate_pair(key_sum[...], cosine, -sine).astype(bf16)
    dv_ref[...] = value_sum[...].astype(bf16)


def last_kernel(dq_ref, dk_ref, dv_ref, x_ref, dx1_ref, gain_ref, w_ref, dx_ref, dgain_ref):
    da = dot_nt(dq_ref[...], w_ref[:, :D])
    da = da + dot_nt(dk_ref[...], w_ref[:, D : 2 * D])
    da = da + dot_nt(dv_ref[...], w_ref[:, 2 * D :])
    unit, scale = normalize(x_ref[...].astype(f32))
    back, terms = norm_back(unit, scale, gain_ref[...], da)

    @pl.when(pl.program_id(0) == 0)
    def _():
        dgain_ref[...] = jnp.zeros_like(dgain_ref)

    dgain_ref[...] += jnp.sum(terms, axis=0, keepdims=True)
    dx_ref[...] = (dx1_ref[...] + back).astype(bf16)


def rows_spec(width):
    return pl.BlockSpec((TILE, width), lambda i: (i, 0))


def whole_spec(*shape):
    return pl.BlockSpec(shape, lambda i: (0,) * len(shape))


def pair_spec(length, offset=0):
    return pl.BlockSpec((length, PAIR), lambda i: (0, i + offset))


def struct(dtype, *shape):
    return jax.ShapeDtypeStruct(shape, dtype)


def call(kernel, grid, in_specs, out_specs, out_shape, flops, scratch=()):
    return pl.pallas_call(
        kernel,
        grid=(grid,),
        in_specs=in_specs,
        out_specs=out_specs,
        out_shape=out_shape,
        scratch_shapes=list(scratch),
        compiler_params=pltpu.CompilerParams(
            dimension_semantics=("arbitrary",), vmem_limit_bytes=VMEM_LIMIT
        ),
        cost_estimate=pl.CostEstimate(flops=flops, bytes_accessed=10 * 2**20, transcendentals=0),
    )


def exchange(array, axis, mask, size):
    return lax.ppermute(array, axis, [(i, i ^ mask) for i in range(size)])


def take(array, index):
    return lax.dynamic_index_in_dim(array, index, 0, keepdims=False)


def swap_blocks(blocks, me, size):
    received = [take(blocks, me)]
    for k in range(1, size):
        received.append(exchange(take(blocks, me ^ k), "seq", k, size))
    return received


def swap_back(slots, me, size):
    arrived = jnp.stack(
        [slots[0]] + [exchange(slots[k], "seq", k, size) for k in range(1, size)]
    )
    return jnp.stack([take(arrived, me ^ s) for s in range(size)])


def gather_weight(shard, me, size):
    parts = shard[None]
    bit = size // 2
    while bit:
        parts = jnp.concatenate([parts, exchange(parts, "fsdp", bit, size)], 0)
        bit //= 2
    order = [0]
    bit = size // 2
    while bit:
        order = order + [o ^ bit for o in order]
        bit //= 2
    back = [order.index(j) for j in range(size)]
    relative = [parts[back[j]] for j in range(size)]
    stacked = jnp.stack(relative)
    ordered = jnp.stack([take(stacked, me ^ j) for j in range(size)])
    return ordered.reshape((size * shard.shape[0],) + shard.shape[1:])


def add_low(left, right):
    return (left.astype(f32) + right.astype(f32)).astype(bf16)


def reduce_packed(packed, sizes):
    fsdp, rep, seq = sizes
    me = lax.axis_index("fsdp")
    array = jnp.stack([take(packed, me ^ j) for j in range(fsdp)])
    bit = 1
    while bit < fsdp:
        halves = array.reshape((array.shape[0] // 2, 2) + array.shape[1:])
        array = add_low(halves[:, 0], exchange(halves[:, 1], "fsdp", bit, fsdp))
        bit *= 2
    array = array[0]
    steps = []
    for axis, size in (("rep", rep), ("seq", seq)):
        bit = 1
        while bit < size:
            steps.append((axis, bit, size))
            bit *= 2
    for axis, bit, size in steps:
        mine = (lax.axis_index(axis) // bit) % 2
        halves = array.reshape(2, array.shape[0] // 2, array.shape[1])
        array = add_low(take(halves, mine), exchange(take(halves, 1 - mine), axis, bit, size))
    for axis, bit, size in reversed(steps):
        mine = (lax.axis_index(axis) // bit) % 2
        other = exchange(array, axis, bit, size)
        first = jnp.where(mine == 0, array, other)
        second = jnp.where(mine == 0, other, array)
        array = jnp.concatenate([first, second], 0)
    return array


def padded_rows(rows, align):
    return -(-rows // align) * align


def body(sizes, tokens, segments, positions, gain_attn, w_qkv, w_out, gain_mlp, w_in, w_mlp_out, cotangent):
    fsdp, rep, seq = sizes
    micro, batch, rows, _ = tokens.shape
    assert micro * batch == seq and rows % TILE == 0
    length = seq * rows
    me_seq, me_fsdp = lax.axis_index("seq"), lax.axis_index("fsdp")

    x_slots = swap_blocks(tokens.reshape(seq, rows, D), me_seq, seq)
    x = jnp.concatenate(x_slots, 0)

    marks = take(segments.reshape(seq, length), me_seq)
    place = jnp.arange(length, dtype=jnp.int32) - jnp.sum(
        (marks[None, :] < marks[:, None]).astype(jnp.int32), axis=1
    )
    slot_order = [me_seq ^ k for k in range(seq)]
    marks = jnp.concatenate([take(marks.reshape(seq, rows), s) for s in slot_order])
    place = jnp.concatenate([take(place.reshape(seq, rows), s) for s in slot_order])
    half = jnp.arange(0, HDIM, 2).astype(f32) / HDIM
    angles = place.astype(f32)[:, None] * jnp.exp(-half * math.log(THETA))
    cosine, sine = jnp.cos(angles), jnp.sin(angles)
    cosine = jnp.concatenate([cosine] * 4, -1)
    sine = jnp.concatenate([-sine, sine] * 2, -1)

    gather = lambda shard: gather_weight(shard, me_fsdp, fsdp)
    gains = gather(jnp.stack([gain_attn, gain_mlp], 1)).astype(f32)
    gain_one, gain_two = gains[:, 0][None], gains[:, 1][None]
    wq = gather(w_qkv)

    tiles, pairs = length // TILE, HEADS // 2
    a, qkv = call(
        first_kernel, tiles,
        [rows_spec(D), whole_spec(1, D), whole_spec(D, 3 * D), rows_spec(PAIR), rows_spec(PAIR)],
        [rows_spec(D), rows_spec(3 * D)],
        [struct(bf16, length, D), struct(bf16, length, 3 * D)],
        2 * length * D * 3 * D,
    )(x, gain_one, wq, cosine, sine)

    prob_spec = pl.BlockSpec((2, length, length), lambda i: (i, 0, 0))
    o, probs = call(
        attend_kernel, pairs,
        [pair_spec(length), pair_spec(length, pairs), pair_spec(length, 2 * pairs),
         whole_spec(length, 1), whole_spec(1, length)],
        [pair_spec(length), prob_spec],
        [struct(bf16, length, D), struct(bf16, HEADS, length, length)],
        16 * length * length * D,
    )(qkv, qkv, qkv, marks[:, None], marks[None, :])

    wo, wi, wm = gather(w_out), gather(w_in), gather(w_mlp_out)
    x1, b, m, slope, act, y = call(
        middle_kernel, tiles,
        [rows_spec(D), rows_spec(D), whole_spec(1, D), whole_spec(D, D), whole_spec(D, 2 * FF), whole_spec(FF, D)],
        [rows_spec(D), rows_spec(D), rows_spec(FF), rows_spec(FF), rows_spec(FF), rows_spec(D)],
        [struct(f32, length, D), struct(bf16, length, D), struct(bf16, length, FF),
         struct(bf16, length, FF), struct(bf16, length, FF), struct(bf16, length, D)],
        2 * length * (D * D + 3 * D * FF),
    )(o, x, gain_two, wo, wi, wm)
    block_out = swap_back([y[k * rows : (k + 1) * rows] for k in range(seq)], me_seq, seq)

    dy = jnp.concatenate(swap_blocks(cotangent.reshape(seq, rows, D), me_seq, seq), 0)
    dh, low, dx1, do, dgain_two = call(
        middle_back_kernel, tiles,
        [rows_spec(D), rows_spec(D), rows_spec(FF), rows_spec(FF), whole_spec(1, D),
         whole_spec(D, D), whole_spec(D, 2 * FF), whole_spec(FF, D)],
        [rows_spec(2 * FF), rows_spec(D), rows_spec(D), rows_spec(D), whole_spec(1, D)],
        [struct(bf16, length, 2 * FF), struct(bf16, length, D), struct(f32, length, D),
         struct(bf16, length, D), struct(f32, 1, D)],
        2 * length * (D * D + 3 * D * FF),
    )(dy, x1, slope, act, gain_two, wo, wi, wm)

    grad_mlp = dot_tn(m, dy).astype(bf16).reshape(fsdp, FF // fsdp, D)
    grad_in = dot_tn(b, dh).astype(bf16).reshape(fsdp, D // fsdp, 3, D).swapaxes(1, 2).reshape(fsdp, 3 * D // fsdp, D)
    grad_out = dot_tn(o, low).astype(bf16).reshape(fsdp, D // fsdp, D)
    parts = [grad_out, grad_mlp, grad_in]
    used = sum(part.shape[1] for part in parts)
    align = 8 * rep * seq
    spare = padded_rows(used, align) - used
    if spare:
        parts.append(jnp.zeros((fsdp, spare, D), bf16))
    reduced = reduce_packed(jnp.concatenate(parts, 1), sizes)

    dq, dk, dv = call(
        attend_back_kernel, pairs,
        [pair_spec(length), pair_spec(length, pairs), pair_spec(length, 2 * pairs),
         pair_spec(length), pair_spec(length), prob_spec, whole_spec(length, PAIR), whole_spec(length, PAIR)],
        [pair_spec(length)] * 3,
        [struct(bf16, length, D)] * 3,
        32 * length * length * D,
        [pltpu.VMEM((length, PAIR), f32)] * 2,
    )(qkv, qkv, qkv, o, do, probs, cosine, sine)

    dx, dgain_one = call(
        last_kernel, tiles,
        [rows_spec(D)] * 5 + [whole_spec(1, D), whole_spec(D, 3 * D)],
        [rows_spec(D), whole_spec(1, D)],
        [struct(bf16, length, D), struct(f32, 1, D)],
        2 * length * D * 3 * D,
    )(dq, dk, dv, x, dx1, gain_one, wq)
    input_grad = swap_back([dx[k * rows : (k + 1) * rows] for k in range(seq)], me_seq, seq)

    grad_qkv = dot_tn(a, jnp.concatenate([dq, dk, dv], 1)).astype(bf16).reshape(fsdp, D // fsdp, 3 * D)
    spare = padded_rows(D // fsdp, align) - D // fsdp
    if spare:
        grad_qkv = jnp.pad(grad_qkv, ((0, 0), (0, spare), (0, 0)))
    qkv_reduced = reduce_packed(grad_qkv, sizes)[: D // fsdp].astype(f32)

    dgains = jnp.concatenate([dgain_one, dgain_two], 0)
    for axis, size in (("fsdp", fsdp), ("rep", rep), ("seq", seq)):
        bit = 1
        while bit < size:
            dgains = dgains + exchange(dgains, axis, bit, size)
            bit *= 2
    dgains = lax.dynamic_slice_in_dim(dgains, me_fsdp * (D // fsdp), D // fsdp, 1)

    first = D // fsdp
    second = first + FF // fsdp
    third = second + 3 * D // fsdp
    full = reduced.astype(f32)
    return (
        block_out.reshape(tokens.shape),
        input_grad.astype(f32).reshape(tokens.shape),
        dgains[0],
        qkv_reduced,
        full[:first],
        dgains[1],
        full[second:third].reshape(3, D // fsdp, D).swapaxes(0, 1).reshape(D // fsdp, 3 * D),
        full[first:second],
    )


def solution(mesh):
    sizes = (mesh.shape["fsdp"], mesh.shape["rep"], mesh.shape["seq"])
    wide = P(None, ("rep", "fsdp"), "seq", None)
    placed = (
        wide, P(None, ("rep", "fsdp"), None), P(None, ("rep", "fsdp"), "seq"),
        P("fsdp"), P("fsdp", None), P("fsdp", None), P("fsdp"), P("fsdp", None), P("fsdp", None), wide,
    )
    return jax.shard_map(
        functools.partial(body, sizes),
        mesh=mesh,
        in_specs=placed,
        out_specs=(
            wide, wide, P("fsdp"), P("fsdp", None), P("fsdp", None), P("fsdp"), P("fsdp", None), P("fsdp", None),
        ),
        check_vma=False,
    )
```

```python
import functools
import math

import jax
import jax.numpy as jnp
from jax import lax
from jax.experimental import pallas as pl
from jax.experimental.pallas import tpu as pltpu
from jax.sharding import PartitionSpec as P

D = 768
HEADS = 12
HDIM = 64
FF = 1152
EPS = 1e-05
THETA = 160000.0
MASKED = -1000000000.0
TILE = 256
PAIR = 2 * HDIM
HCHUNK = 384
f32 = jnp.float32
bf16 = jnp.bfloat16
VMEM_LIMIT = 56 * 2**20


def dot_nn(left, right):
    return lax.dot_general(left, right, (((1,), (0,)), ((), ())), preferred_element_type=f32)


def dot_nt(left, right):
    return lax.dot_general(left, right, (((1,), (1,)), ((), ())), preferred_element_type=f32)


def dot_tn(left, right):
    return lax.dot_general(left, right, (((0,), (0,)), ((), ())), preferred_element_type=f32)


def normalize(values):
    mean = jnp.mean(values, axis=-1, keepdims=True)
    centered = values - mean
    var = jnp.mean(centered * centered, axis=-1, keepdims=True)
    scale = lax.rsqrt(var + EPS)
    return centered * scale, scale


def norm_back(unit, scale, gain, grad):
    gain_terms = grad * unit
    inner = grad * gain
    first = jnp.mean(inner, axis=-1, keepdims=True)
    second = jnp.mean(inner * unit, axis=-1, keepdims=True)
    return scale * (inner - first - unit * second), gain_terms


def lane_halves(shape):
    lane = lax.broadcasted_iota(jnp.int32, shape, len(shape) - 1)
    return lane % HDIM < HDIM // 2


def rotate_pair(values, cosine, signed_sine):
    swapped = jnp.where(
        lane_halves(values.shape),
        pltpu.roll(values, PAIR - HDIM // 2, 1),
        pltpu.roll(values, HDIM // 2, 1),
    )
    return values * cosine + swapped * signed_sine


def first_kernel(x_ref, gain_ref, w_ref, cos_ref, sin_ref, a_ref, qkv_ref):
    unit, _ = normalize(x_ref[...].astype(f32))
    a = (unit * gain_ref[...]).astype(bf16)
    a_ref[...] = a
    cosine, sine = cos_ref[...], sin_ref[...]
    for column in range(0, 3 * D, TILE):
        part = dot_nn(a, w_ref[:, column : column + TILE])
        for half in range(0, TILE, PAIR):
            start = column + half
            piece = part[:, half : half + PAIR]
            if start < 2 * D:
                piece = rotate_pair(piece, cosine, sine)
            if start < D:
                piece = piece * HDIM**-0.5
            qkv_ref[:, start : start + PAIR] = piece.astype(bf16)


def attend_kernel(
    sizes, q_ref, k_ref, v_ref, rows_ref, cols_ref, cot_ref, o_ref, p_ref, dy_ref, bounce, *sem_refs
):
    seq = sizes[2]
    step, last = pl.program_id(0), pl.num_programs(0) - 1
    sems = Sems(*sem_refs)
    me_seq = lax.axis_index("seq")
    into = sems.copy(cot_ref.at[me_seq], bounce)
    outof = sems.copy(bounce, dy_ref.at[0])
    blocks = [sems.remote(cot_ref.at[flip(me_seq, k)], dy_ref.at[k], "seq", k) for k in range(1, seq)]

    @pl.when(step == 0)
    def _():
        into.start()
        meet([("seq", k) for k in range(1, seq)])
        start_all(blocks)
        into.wait()
        outof.start()

    k, v = k_ref[...], v_ref[...]
    lane = lax.broadcasted_iota(jnp.int32, (1, PAIR), 1)
    length = k.shape[0]
    zero = jnp.zeros((), bf16)
    for tile in range(0, length, TILE):
        q = q_ref[tile : tile + TILE, :]
        same = rows_ref[tile : tile + TILE, :] == cols_ref[...]
        out = None
        for head in range(2):
            mine = (lane < HDIM) if head == 0 else (lane >= HDIM)
            scores = dot_nt(jnp.where(mine, q, zero), k)
            scores = jnp.where(same, scores, MASKED)
            top = jnp.max(scores, axis=-1, keepdims=True)
            raised = jnp.exp(scores - top)
            total = jnp.sum(raised, axis=-1, keepdims=True)
            probs = (raised * (1.0 / total)).astype(bf16)
            p_ref[head, tile : tile + TILE, :] = probs
            part = dot_nn(probs, jnp.where(mine, v, zero))
            out = part if out is None else out + part
        o_ref[tile : tile + TILE, :] = out.astype(bf16)

    @pl.when(step == last)
    def _():
        outof.wait()
        wait_all(blocks)


def middle_kernel(
    o_ref, x_ref, gain_ref, w_out_ref, w_in_ref, w_mlp_ref,
    x1_ref, b_ref, m_ref, slope_ref, act_ref, y_ref,
):
    x1 = x_ref[...].astype(f32) + dot_nn(o_ref[...], w_out_ref[...])
    x1_ref[...] = x1
    unit, _ = normalize(x1)
    b = (unit * gain_ref[...]).astype(bf16)
    b_ref[...] = b
    y = x1
    for column in range(0, FF, HCHUNK):
        hin = dot_nn(b, w_in_ref[:, column : column + HCHUNK])
        gate = dot_nn(b, w_in_ref[:, FF + column : FF + column + HCHUNK])
        phi = 0.5 + 0.5 * lax.erf(hin * math.sqrt(0.5))
        act = hin * phi
        slope = phi + hin * (jnp.exp(hin * hin * -0.5) * (1.0 / math.sqrt(2.0 * math.pi)))
        m = (act * gate).astype(bf16)
        m_ref[:, column : column + HCHUNK] = m
        act_ref[:, column : column + HCHUNK] = act.astype(bf16)
        slope_ref[:, column : column + HCHUNK] = (slope * gate).astype(bf16)
        y = y + dot_nn(m, w_mlp_ref[column : column + HCHUNK, :])
    y_ref[...] = y.astype(bf16)


def middle_back_kernel(
    dy_ref, x1_ref, slope_ref, act_ref, gain_ref, w_out_ref, w_in_ref, w_mlp_ref,
    dh_ref, low_ref, dx1_ref, do_ref, dgain_ref,
):
    dy = dy_ref[...]
    db = None
    for column in range(0, FF, HCHUNK):
        dm = dot_nt(dy, w_mlp_ref[column : column + HCHUNK, :])
        first = (dm * slope_ref[:, column : column + HCHUNK].astype(f32)).astype(bf16)
        second = (dm * act_ref[:, column : column + HCHUNK].astype(f32)).astype(bf16)
        dh_ref[:, column : column + HCHUNK] = first
        dh_ref[:, FF + column : FF + column + HCHUNK] = second
        part = dot_nt(first, w_in_ref[:, column : column + HCHUNK]) + dot_nt(
            second, w_in_ref[:, FF + column : FF + column + HCHUNK]
        )
        db = part if db is None else db + part
    unit, scale = normalize(x1_ref[...])
    back, terms = norm_back(unit, scale, gain_ref[...], db)

    @pl.when(pl.program_id(0) == 0)
    def _():
        dgain_ref[...] = jnp.zeros_like(dgain_ref)

    dgain_ref[...] += jnp.sum(terms, axis=0, keepdims=True)
    dx1 = dy.astype(f32) + back
    dx1_ref[...] = dx1
    low = dx1.astype(bf16)
    low_ref[...] = low
    do_ref[...] = dot_nt(low, w_out_ref[...]).astype(bf16)


def early_order(sizes, rep_first):
    fsdp, rep, _ = sizes
    core = [("fsdp", 1)]
    rest = [("fsdp", b) for b in bits_of(fsdp)[1:]]
    copies = [("rep", b) for b in bits_of(rep)]
    return core + (copies + rest if rep_first else rest + copies)


def late_order(sizes):
    return [("seq", b) for b in bits_of(sizes[2])]


def early_reducers(sizes, shapes):
    orders = [early_order(sizes, w == 2) for w in range(3)]
    early = len(orders[0])
    return [Reducer(shape, sizes, order + late_order(sizes)) for shape, order in zip(shapes, orders)], early


def attend_back_kernel(sizes, shapes, q_ref, k_ref, v_ref, o_ref, do_ref, p_ref, cos_ref, sin_ref, y_ref, *refs):
    count = len(shapes)
    reducers, early = early_reducers(sizes, shapes)
    refs = list(refs)
    pop = lambda n: [refs.pop(0) for _ in range(n)]
    grads = pop(count)
    dq_ref, dk_ref, dv_ref, home_ref = pop(4)
    sums_out = pop(count)
    key_sum, value_sum, bounce = pop(3)
    kept = pop(count)
    lands = [pop(len(r.scratch(0, early))) for r in reducers]
    sems = Sems(*refs)
    me = lax.axis_index("fsdp")
    step, last = pl.program_id(0), pl.num_programs(0) - 1
    into, outof, blocks = give_back(y_ref, home_ref, bounce, sems)
    loads, stores = [], []
    for w, reducer in enumerate(reducers):
        keep = reducer.steps[0]["keep"]
        for j in keep:
            loads.append(sems.copy(grads[w].at[flip(me, j)], kept[w].at[j // 2]))
        stores.append(sems.copy(kept[w].at[0], sums_out[w]))
        parts = lambda j, w=w: kept[w].at[j // 2] if j % 2 == 0 else grads[w].at[flip(me, j)]
        reducer.bind(parts, lands[w], sems, 0, early)

    @pl.when(step == 0)
    def _():
        into.start()
        start_all(loads)
        meet(
            [("seq", k) for k in range(1, sizes[2])]
            + [("fsdp", b) for b in bits_of(sizes[0])]
            + [("rep", b) for b in bits_of(sizes[1])]
        )
        for reducer in reducers:
            reducer.start(0)
        start_all(blocks)
        into.wait()
        outof.start()

    @pl.when(step == 1)
    def _():
        wait_all(loads)
        for reducer in reducers:
            reducer.finish(0)
            reducer.start(1)

    for w, reducer in enumerate(reducers):
        for s in range(1, early - 1):
            @pl.when(step == min(2 + w + s, 5))
            def _(reducer=reducer, s=s):
                reducer.finish(s)
                reducer.start(s + 1)

    k, v = k_ref[...], v_ref[...]
    lane = lax.broadcasted_iota(jnp.int32, (1, PAIR), 1)
    length = k.shape[0]
    zero = jnp.zeros((), bf16)
    cosine, sine = cos_ref[...], sin_ref[...]
    for tile in range(0, length, TILE):
        rows = slice(tile, tile + TILE)
        q, do = q_ref[rows, :], do_ref[rows, :]
        inner = do.astype(f32) * o_ref[rows, :].astype(f32)
        dq = None
        for head in range(2):
            mine = (lane < HDIM) if head == 0 else (lane >= HDIM)
            do_head = jnp.where(mine, do, zero)
            delta = jnp.sum(jnp.where(mine, inner, 0.0), axis=-1, keepdims=True)
            probs = p_ref[head, rows, :]
            dp = dot_nt(do_head, v)
            ds = (probs.astype(f32) * (dp - delta)).astype(bf16)
            value_part = dot_tn(probs, do_head)
            key_part = dot_tn(ds, jnp.where(mine, q, zero))
            if tile == 0 and head == 0:
                value_sum[...] = value_part
                key_sum[...] = key_part
            else:
                value_sum[...] += value_part
                key_sum[...] += key_part
            part = dot_nn(ds, jnp.where(mine, k, zero))
            dq = part if dq is None else dq + part
        dq = rotate_pair(dq * HDIM**-0.5, cosine[rows], -sine[rows])
        dq_ref[rows, :] = dq.astype(bf16)
    dk_ref[...] = rotate_pair(key_sum[...], cosine, -sine).astype(bf16)
    dv_ref[...] = value_sum[...].astype(bf16)

    @pl.when(step == last)
    def _():
        for w, reducer in enumerate(reducers):
            reducer.finish(early - 1)
            stores[w].start()
        wait_all(stores)
        outof.wait()
        wait_all(blocks)


def leave_kernel(sizes, shapes, late_shapes, dx_ref, gains_ref, *refs):
    count, more = len(shapes), len(late_shapes)
    fsdp, rep, seq = sizes
    reducers, early = early_reducers(sizes, shapes)
    whole = [Reducer(shape, sizes, early_order(sizes, w == 1) + late_order(sizes)) for w, shape in enumerate(late_shapes)]
    refs = list(refs)
    pop = lambda n: [refs.pop(0) for _ in range(n)]
    sums_in, grads = pop(count), pop(more)
    (home_ref,) = pop(1)
    sums_out, wholes_out = pop(count), pop(more)
    (gains_out,) = pop(1)
    (bounce,) = pop(1)
    held, kept, finals = pop(count), pop(more), pop(count + more)
    lands = [pop(len(r.scratch(early, len(r.steps)))) for r in reducers]
    whole_lands = [pop(len(r.scratch(0, len(r.steps)))) for r in whole]
    (gain_lands,) = pop(1)
    sems = Sems(*refs)
    me = lax.axis_index("fsdp")
    into, outof, blocks = give_back(dx_ref, home_ref, bounce, sems)
    loads = [sems.copy(sums_in[w], held[w]) for w in range(count)]
    stores = [sems.copy(finals[w], out) for w, out in enumerate(sums_out + wholes_out)]
    for w, reducer in enumerate(reducers):
        reducer.bind(lambda j, w=w: held[w], lands[w], sems, early, len(reducer.steps), finals[w])
    whole_loads = []
    for w, reducer in enumerate(whole):
        whole_loads.append([sems.copy(grads[w].at[flip(me, j)], kept[w].at[j // 2]) for j in reducer.steps[0]["keep"]])
        parts = lambda j, w=w: kept[w].at[j // 2] if j % 2 == 0 else grads[w].at[flip(me, j)]
        reducer.bind(parts, whole_lands[w], sems, 0, len(reducer.steps), finals[count + w])
    partners = [("seq", k) for k in range(1, seq)] + [("fsdp", b) for b in bits_of(fsdp)] + [("rep", b) for b in bits_of(rep)]
    hops = [("fsdp", b) for b in bits_of(fsdp)] + [("rep", b) for b in bits_of(rep)] + [("seq", b) for b in bits_of(seq)]
    gain_moves = [sems.remote(gains_out, gain_lands.at[i], axis, bit) for i, (axis, bit) in enumerate(hops)]
    into.start()
    start_all(loads)
    for group in whole_loads:
        start_all(group)
    gains_out[...] = gains_ref[...]
    meet(partners)
    for reducer in whole:
        reducer.start(0)
    gain_moves[0].start()
    start_all(blocks)
    wait_all(loads)
    for reducer in reducers:
        reducer.start(early)
    into.wait()
    outof.start()
    for group in whole_loads:
        wait_all(group)
    longest = max(len(r.steps) for r in whole)
    for s in range(longest):
        for reducer in whole:
            if s < len(reducer.steps):
                reducer.finish(s)
                if s + 1 < len(reducer.steps):
                    reducer.start(s + 1)
        for reducer in reducers:
            if s + early < len(reducer.steps):
                reducer.finish(s + early)
                if s + early + 1 < len(reducer.steps):
                    reducer.start(s + early + 1)
        if s < len(hops):
            gain_moves[s].wait()
            gains_out[...] += gain_lands[s]
            if s + 1 < len(hops):
                gain_moves[s + 1].start()
    start_all(stores)
    wait_all(stores)
    outof.wait()
    wait_all(blocks)


def last_kernel(dq_ref, dk_ref, dv_ref, x_ref, dx1_ref, gain_ref, w_ref, dx_ref, dgain_ref):
    da = dot_nt(dq_ref[...], w_ref[:, :D])
    da = da + dot_nt(dk_ref[...], w_ref[:, D : 2 * D])
    da = da + dot_nt(dv_ref[...], w_ref[:, 2 * D :])
    unit, scale = normalize(x_ref[...].astype(f32))
    back, terms = norm_back(unit, scale, gain_ref[...], da)

    @pl.when(pl.program_id(0) == 0)
    def _():
        dgain_ref[...] = jnp.zeros_like(dgain_ref)

    dgain_ref[...] += jnp.sum(terms, axis=0, keepdims=True)
    dx_ref[...] = (dx1_ref[...] + back).astype(bf16)


def rows_spec(width):
    return pl.BlockSpec((TILE, width), lambda i: (i, 0))


def whole_spec(*shape):
    return pl.BlockSpec(shape, lambda i: (0,) * len(shape))


def pair_spec(length, offset=0):
    return pl.BlockSpec((length, PAIR), lambda i: (0, i + offset))


def struct(dtype, *shape):
    return jax.ShapeDtypeStruct(shape, dtype)


def call(kernel, grid, in_specs, out_specs, out_shape, flops, scratch=(), collective=None):
    return pl.pallas_call(
        kernel,
        grid=(grid,),
        in_specs=in_specs,
        out_specs=out_specs,
        out_shape=out_shape,
        scratch_shapes=list(scratch),
        compiler_params=pltpu.CompilerParams(
            dimension_semantics=("arbitrary",), vmem_limit_bytes=VMEM_LIMIT,
            collective_id=collective, has_side_effects=collective is not None,
        ),
        cost_estimate=pl.CostEstimate(flops=flops, bytes_accessed=10 * 2**20, transcendentals=0),
    )


MESH = pl.DeviceIdType.MESH
ANY = pl.BlockSpec(memory_space=pl.ANY)


def take(array, index):
    return lax.dynamic_index_in_dim(array, index, 0, keepdims=False)


def flip(index, mask):
    bit = 1
    while bit <= mask:
        if mask & bit:
            index = index + bit - 2 * bit * ((index // bit) % 2)
        bit *= 2
    return index


def bits_of(size):
    return [1 << i for i in range(size.bit_length() - 1)]


def meet(partners):
    barrier = pltpu.get_barrier_semaphore()
    for axis, mask in partners:
        pl.semaphore_signal(
            barrier, inc=1, device_id={axis: flip(lax.axis_index(axis), mask)}, device_id_type=MESH
        )
    pl.semaphore_wait(barrier, len(partners))


class Sems:
    def __init__(self, send, recv, local):
        self.send, self.recv, self.local = send, recv, local
        self.remote_used = self.local_used = 0

    def remote(self, src, dst, axis, mask):
        i = self.remote_used
        self.remote_used += 1
        return pltpu.make_async_remote_copy(
            src_ref=src, dst_ref=dst, send_sem=self.send.at[i], recv_sem=self.recv.at[i],
            device_id={axis: flip(lax.axis_index(axis), mask)}, device_id_type=MESH,
        )

    def copy(self, src, dst):
        i = self.local_used
        self.local_used += 1
        return pltpu.make_async_copy(src, dst, self.local.at[i])


def sem_shapes(remote, local):
    dma = pltpu.SemaphoreType.DMA
    return [dma((remote,)), dma((remote,)), dma((max(local, 1),))]


def start_all(copies):
    for copy in copies:
        copy.start()


def wait_all(copies):
    for copy in copies:
        copy.wait()


def enter_kernel(sizes, count, *refs):
    fsdp, rep, seq = sizes
    tokens, shards = refs[0], refs[1 : 1 + count]
    x_out, fulls = refs[1 + count], refs[2 + count : 2 + 2 * count]
    bounce_x, bounces = refs[2 + 2 * count], refs[3 + 2 * count : 3 + 3 * count]
    sems = Sems(*refs[3 + 3 * count :])
    me, me_seq, me_rep = lax.axis_index("fsdp"), lax.axis_index("seq"), lax.axis_index("rep")
    into = [sems.copy(tokens.at[me_seq], bounce_x)] + [sems.copy(shards[w], bounces[w]) for w in range(count)]
    outof = [sems.copy(bounce_x, x_out.at[0])] + [sems.copy(bounces[w], fulls[w].at[me]) for w in range(count)]
    start_all(into)
    meet([("seq", k) for k in range(1, seq)] + [("fsdp", b) for b in bits_of(fsdp)] + [("rep", b) for b in bits_of(rep)])
    blocks = [sems.remote(tokens.at[flip(me_seq, k)], x_out.at[k], "seq", k) for k in range(1, seq)]
    start_all(blocks)

    def piece(ref, w, index):
        width = shards[w].shape[-1] // rep
        return ref.at[index, :, pl.ds(pl.multiple_of(me_rep * width, 128), width)]

    def first_piece(w):
        width = shards[w].shape[-1] // rep
        return shards[w].at[:, pl.ds(pl.multiple_of(me_rep * width, 128), width)]

    held = [0]
    pending = []
    for bit in reversed(bits_of(fsdp)[1:]):
        over = []
        for w in range(count):
            moved = []
            for h in held:
                src = first_piece(w) if h == 0 else piece(fulls[w], w, flip(me, h))
                moved.append(sems.remote(src, piece(fulls[w], w, flip(me, h)), "fsdp", bit))
            start_all(moved)
            over.append(moved)
        relays = []
        for w in range(count):
            for copy in over[w]:
                copy.wait_recv()
            moved = []
            for mask in range(1, rep):
                for h in held:
                    here = piece(fulls[w], w, flip(me, h ^ bit))
                    moved.append(sems.remote(here, here, "rep", mask))
            start_all(moved)
            relays.append(moved)
            pending += over[w]
        for moved in relays:
            for copy in moved:
                copy.wait_recv()
            pending += moved
        held = held + [h ^ bit for h in held]
    last = []
    for w in range(count):
        for h in held:
            src = shards[w] if h == 0 else fulls[w].at[flip(me, h)]
            last.append(sems.remote(src, fulls[w].at[flip(me, h)], "fsdp", 1))
    start_all(last)
    wait_all(into)
    start_all(outof)
    for copy in pending:
        copy.wait_send()
    wait_all(last)
    wait_all(blocks)
    wait_all(outof)


def enter(sizes, tokens, shards):
    fsdp, rep, seq = sizes
    count = len(shards)
    assert fsdp >= 2
    held, copies = 1, seq - 1
    for _ in bits_of(fsdp)[1:]:
        copies += count * held * rep
        held *= 2
    copies += count * held
    hbm = lambda shape: struct(bf16, *shape)
    return pl.pallas_call(
        functools.partial(enter_kernel, sizes, count),
        in_specs=[ANY] * (1 + count),
        out_specs=[ANY] * (1 + count),
        out_shape=[hbm(tokens.shape)] + [hbm((fsdp,) + s.shape) for s in shards],
        scratch_shapes=[pltpu.VMEM(tokens.shape[1:], bf16)]
        + [pltpu.VMEM(s.shape, bf16) for s in shards]
        + sem_shapes(copies, 2 * (1 + count)),
        compiler_params=pltpu.CompilerParams(collective_id=0, has_side_effects=True),
    )(tokens, *shards)


class Reducer:
    def __init__(self, parts_shape, sizes, order):
        self.fsdp, self.rows, self.cols = parts_shape
        self.steps = []
        held, rows, cols = list(range(self.fsdp)), self.rows, self.cols
        row_at, col_at = [], []
        for axis, bit in order:
            step = dict(axis=axis, bit=bit, row_at=list(row_at), col_at=list(col_at), rows=rows, cols=cols)
            if axis == "fsdp":
                step["send"] = [j for j in held if j & bit]
                held = [j for j in held if not j & bit]
                step["keep"] = held
                step["shape"] = (len(held), rows, cols)
                step["split"] = None
            else:
                step["keep"] = step["send"] = held
                if (rows // 2) % 16 == 0:
                    rows //= 2
                    row_at = row_at + [(axis, bit, rows)]
                    step["split"] = "rows"
                elif (cols // 2) % 128 == 0:
                    cols //= 2
                    col_at = col_at + [(axis, bit, cols)]
                    step["split"] = "cols"
                else:
                    step["split"] = "none"
                step["shape"] = (len(held), rows, cols)
            self.steps.append(step)
        self.down = len(self.steps)
        for step in reversed(self.steps[: self.down]):
            if step["split"] in ("rows", "cols"):
                self.steps.append(dict(step, up=True))

    @staticmethod
    def offset(terms, align, last=None):
        total = 0
        for i, (axis, bit, extent) in enumerate(terms):
            half = (lax.axis_index(axis) // bit) % 2
            if last == i:
                half = 1 - half
            total = total + half * extent
        return total if isinstance(total, int) else pl.multiple_of(total, align)

    def region(self, step, after, other=False):
        row_at, col_at, rows, cols = step["row_at"], step["col_at"], step["rows"], step["cols"]
        row_last = col_last = None
        if after:
            if step["split"] == "rows":
                rows //= 2
                row_at = row_at + [(step["axis"], step["bit"], rows)]
                row_last = len(row_at) - 1 if other else None
            elif step["split"] == "cols":
                cols //= 2
                col_at = col_at + [(step["axis"], step["bit"], cols)]
                col_last = len(col_at) - 1 if other else None
        return (
            pl.ds(self.offset(row_at, 16, row_last), rows),
            pl.ds(self.offset(col_at, 128, col_last), cols),
        )

    def scratch(self, first, last):
        return [pltpu.VMEM(s["shape"], bf16) for s in self.steps[first:last] if "up" not in s]

    def copies(self, first, last):
        return sum(1 if "up" in s else len(s["send"]) for s in self.steps[first:last])

    def bind(self, parts, lands, sems, first, last, final=None):
        self.parts, self.sems, self.final = parts, sems, final
        self.lands, self.moves = {}, {}
        lands = list(lands)
        for s in range(first, last):
            step = self.steps[s]
            moves = []
            if "up" in step:
                there = final.at[self.region(step, True)]
                moves.append(sems.remote(there, there, step["axis"], step["bit"]))
            else:
                land = self.lands[s] = lands.pop(0)
                for i, j in enumerate(step["send"]):
                    fsdp = step["axis"] == "fsdp"
                    src = self.parts(j).at[self.region(step, not fsdp, not fsdp)]
                    moves.append(sems.remote(src, land.at[i], step["axis"], step["bit"]))
            self.moves[s] = moves

    def start(self, s):
        start_all(self.moves[s])

    def finish(self, s):
        step = self.steps[s]
        for i, move in enumerate(self.moves[s]):
            move.wait()
            if "up" not in step:
                j = step["keep"][i]
                ref = self.parts(j)
                region = self.region(step, True)
                total = (ref[region].astype(f32) + self.lands[s][i].astype(f32)).astype(bf16)
                if s == self.down - 1:
                    self.final[region] = total
                else:
                    ref[region] = total


def give_back(slots, home, bounce, sems):
    me = lax.axis_index("seq")
    seq = slots.shape[0]
    return (
        sems.copy(slots.at[0], bounce),
        sems.copy(bounce, home.at[me]),
        [sems.remote(slots.at[k], home.at[me], "seq", k) for k in range(1, seq)],
    )


def body(sizes, tokens, segments, positions, gain_attn, w_qkv, w_out, gain_mlp, w_in, w_mlp_out, cotangent):
    fsdp, rep, seq = sizes
    micro, batch, rows, _ = tokens.shape
    assert micro * batch == seq and rows % TILE == 0
    length = seq * rows
    me_seq, me_fsdp = lax.axis_index("seq"), lax.axis_index("fsdp")

    own_gains = jnp.zeros((16, D), bf16)
    own_gains = lax.dynamic_update_slice(own_gains, jnp.stack([gain_attn, gain_mlp]), (0, me_fsdp * (D // fsdp)))
    x, gains, wq, wo, wm, wi = enter(
        sizes, tokens.reshape(seq, rows, D), [own_gains, w_qkv, w_out, w_mlp_out, w_in]
    )
    x = x.reshape(length, D)
    gains = jnp.sum(gains[:, :2].astype(f32), axis=0)
    gain_one, gain_two = gains[:1], gains[1:]
    wq, wo, wm, wi = (w.reshape(-1, w.shape[-1]) for w in (wq, wo, wm, wi))

    marks = take(segments.reshape(seq, length), me_seq)
    place = jnp.arange(length, dtype=jnp.int32) - jnp.sum(
        (marks[None, :] < marks[:, None]).astype(jnp.int32), axis=1
    )
    slot_order = [me_seq ^ k for k in range(seq)]
    marks = jnp.concatenate([take(marks.reshape(seq, rows), s) for s in slot_order])
    place = jnp.concatenate([take(place.reshape(seq, rows), s) for s in slot_order])
    half = jnp.arange(0, HDIM, 2).astype(f32) / HDIM
    angles = place.astype(f32)[:, None] * jnp.exp(-half * math.log(THETA))
    cosine, sine = jnp.cos(angles), jnp.sin(angles)
    cosine = jnp.concatenate([cosine] * 4, -1)
    sine = jnp.concatenate([-sine, sine] * 2, -1)

    tiles, pairs = length // TILE, HEADS // 2
    a, qkv = call(
        first_kernel, tiles,
        [rows_spec(D), whole_spec(1, D), whole_spec(D, 3 * D), rows_spec(PAIR), rows_spec(PAIR)],
        [rows_spec(D), rows_spec(3 * D)],
        [struct(bf16, length, D), struct(bf16, length, 3 * D)],
        2 * length * D * 3 * D,
    )(x, gain_one, wq, cosine, sine)

    prob_spec = pl.BlockSpec((2, length, length), lambda i: (i, 0, 0))
    o, probs, dy = call(
        functools.partial(attend_kernel, sizes), pairs,
        [pair_spec(length), pair_spec(length, pairs), pair_spec(length, 2 * pairs),
         whole_spec(length, 1), whole_spec(1, length), ANY],
        [pair_spec(length), prob_spec, ANY],
        [struct(bf16, length, D), struct(bf16, HEADS, length, length), struct(bf16, seq, rows, D)],
        16 * length * length * D,
        [pltpu.VMEM((rows, D), bf16)] + sem_shapes(seq - 1, 2), 1,
    )(qkv, qkv, qkv, marks[:, None], marks[None, :], cotangent.reshape(seq, rows, D))
    dy = dy.reshape(length, D)

    x1, b, m, slope, act, y = call(
        middle_kernel, tiles,
        [rows_spec(D), rows_spec(D), whole_spec(1, D), whole_spec(D, D), whole_spec(D, 2 * FF), whole_spec(FF, D)],
        [rows_spec(D), rows_spec(D), rows_spec(FF), rows_spec(FF), rows_spec(FF), rows_spec(D)],
        [struct(f32, length, D), struct(bf16, length, D), struct(bf16, length, FF),
         struct(bf16, length, FF), struct(bf16, length, FF), struct(bf16, length, D)],
        2 * length * (D * D + 3 * D * FF),
    )(o, x, gain_two, wo, wi, wm)
    dh, low, dx1, do, dgain_two = call(
        middle_back_kernel, tiles,
        [rows_spec(D), rows_spec(D), rows_spec(FF), rows_spec(FF), whole_spec(1, D),
         whole_spec(D, D), whole_spec(D, 2 * FF), whole_spec(FF, D)],
        [rows_spec(2 * FF), rows_spec(D), rows_spec(D), rows_spec(D), whole_spec(1, D)],
        [struct(bf16, length, 2 * FF), struct(bf16, length, D), struct(f32, length, D),
         struct(bf16, length, D), struct(f32, 1, D)],
        2 * length * (D * D + 3 * D * FF),
    )(dy, x1, slope, act, gain_two, wo, wi, wm)

    grads = [dot_tn(m, dy), dot_tn(o, low), dot_tn(b, dh)]
    grads = [g.astype(bf16).reshape(fsdp, g.shape[0] // fsdp, g.shape[1]) for g in grads]
    shapes = [g.shape for g in grads]
    reducers, early = early_reducers(sizes, shapes)
    halves = fsdp // 2
    quarter = lambda shape: struct(bf16, *shape[1:])
    dq, dk, dv, block_out, *sums = call(
        functools.partial(attend_back_kernel, sizes, shapes), pairs,
        [pair_spec(length), pair_spec(length, pairs), pair_spec(length, 2 * pairs),
         pair_spec(length), pair_spec(length), prob_spec, whole_spec(length, PAIR), whole_spec(length, PAIR)]
        + [ANY] * 4,
        [pair_spec(length)] * 3 + [ANY] * 4,
        [struct(bf16, length, D)] * 3 + [struct(bf16, seq, rows, D)] + [quarter(s) for s in shapes],
        32 * length * length * D,
        [pltpu.VMEM((length, PAIR), f32)] * 2 + [pltpu.VMEM((rows, D), bf16)]
        + [pltpu.VMEM((halves,) + s[1:], bf16) for s in shapes]
        + [land for r in reducers for land in r.scratch(0, early)]
        + sem_shapes(seq - 1 + sum(r.copies(0, early) for r in reducers), 2 + 3 * (halves + 1)), 2,
    )(qkv, qkv, qkv, o, do, probs, cosine, sine, y.reshape(seq, rows, D), *grads)

    dx, dgain_one = call(
        last_kernel, tiles,
        [rows_spec(D)] * 5 + [whole_spec(1, D), whole_spec(D, 3 * D)],
        [rows_spec(D), whole_spec(1, D)],
        [struct(bf16, length, D), struct(f32, 1, D)],
        2 * length * D * 3 * D,
    )(dq, dk, dv, x, dx1, gain_one, wq)
    late = [dot_tn(a, part).astype(bf16).reshape(fsdp, D // fsdp, D) for part in (dq, dk, dv)]
    late_shapes = [g.shape for g in late]
    whole = [Reducer(s, sizes, early_order(sizes, w == 1) + late_order(sizes)) for w, s in enumerate(late_shapes)]
    dgains = jnp.concatenate([dgain_one, dgain_two, jnp.zeros((6, D), f32)], 0)
    hops = sum(len(bits_of(n)) for n in sizes)
    vmem = pl.BlockSpec(memory_space=pltpu.VMEM)
    input_grad, *results, dgains = pl.pallas_call(
        functools.partial(leave_kernel, sizes, shapes, late_shapes),
        in_specs=[ANY, vmem] + [ANY] * 6,
        out_specs=[ANY] * 7 + [vmem],
        out_shape=[struct(bf16, seq, rows, D)] + [quarter(s) for s in shapes + late_shapes] + [struct(f32, 8, D)],
        scratch_shapes=[pltpu.VMEM((rows, D), bf16)]
        + [pltpu.VMEM(s[1:], bf16) for s in shapes]
        + [pltpu.VMEM((halves,) + s[1:], bf16) for s in late_shapes]
        + [pltpu.VMEM(s[1:], bf16) for s in shapes + late_shapes]
        + [land for r in reducers for land in r.scratch(early, len(r.steps))]
        + [land for r in whole for land in r.scratch(0, len(r.steps))]
        + [pltpu.VMEM((hops, 8, D), f32)]
        + sem_shapes(
            seq - 1 + hops + sum(r.copies(early, len(r.steps)) for r in reducers)
            + sum(r.copies(0, len(r.steps)) for r in whole),
            2 + 2 * len(shapes) + len(late_shapes) * (halves + 1),
        ),
        compiler_params=pltpu.CompilerParams(
            collective_id=3, has_side_effects=True, vmem_limit_bytes=VMEM_LIMIT
        ),
    )(dx.reshape(seq, rows, D), dgains, *sums, *late)
    dgains = lax.dynamic_slice_in_dim(dgains, me_fsdp * (D // fsdp), D // fsdp, 1)
    grad_mlp, grad_out, grad_in, grad_q, grad_k, grad_v = (r.astype(f32) for r in results)
    return (
        block_out.reshape(tokens.shape),
        input_grad.astype(f32).reshape(tokens.shape),
        dgains[0],
        jnp.concatenate([grad_q, grad_k, grad_v], 1),
        grad_out,
        dgains[1],
        grad_in,
        grad_mlp,
    )


def solution(mesh):
    sizes = (mesh.shape["fsdp"], mesh.shape["rep"], mesh.shape["seq"])
    wide = P(None, ("rep", "fsdp"), "seq", None)
    placed = (
        wide, P(None, ("rep", "fsdp"), None), P(None, ("rep", "fsdp"), "seq"),
        P("fsdp"), P("fsdp", None), P("fsdp", None), P("fsdp"), P("fsdp", None), P("fsdp", None), wide,
    )
    return jax.shard_map(
        functools.partial(body, sizes),
        mesh=mesh,
        in_specs=placed,
        out_specs=(
            wide, wide, P("fsdp"), P("fsdp", None), P("fsdp", None), P("fsdp"), P("fsdp", None), P("fsdp", None),
        ),
        check_vma=False,
    )
```

```python
import functools
import math

import jax
import jax.numpy as jnp
from jax import lax
from jax.experimental import pallas as pl
from jax.experimental.pallas import tpu as pltpu
from jax.sharding import PartitionSpec as P

D = 768
HEADS = 12
HDIM = 64
FF = 1152
EPS = 1e-05
THETA = 160000.0
MASKED = -1000000000.0
QUERY_SCALE = HDIM**-0.5 / math.log(2.0)
TILE = 256
PAIR = 2 * HDIM
HCHUNK = 384
f32 = jnp.float32
bf16 = jnp.bfloat16
VMEM_LIMIT = 62 * 2**20


def dot_nn(left, right):
    return lax.dot_general(left, right, (((1,), (0,)), ((), ())), preferred_element_type=f32)


def dot_nt(left, right):
    return lax.dot_general(left, right, (((1,), (1,)), ((), ())), preferred_element_type=f32)


def dot_tn(left, right):
    return lax.dot_general(left, right, (((0,), (0,)), ((), ())), preferred_element_type=f32)


def normalize(values):
    mean = jnp.mean(values, axis=-1, keepdims=True)
    centered = values - mean
    var = jnp.mean(centered * centered, axis=-1, keepdims=True)
    scale = lax.rsqrt(var + EPS)
    return centered * scale, scale


def norm_back(unit, scale, gain, grad):
    gain_terms = grad * unit
    inner = grad * gain
    first = jnp.mean(inner, axis=-1, keepdims=True)
    second = jnp.mean(inner * unit, axis=-1, keepdims=True)
    return scale * (inner - first - unit * second), gain_terms


def lane_halves(shape):
    lane = lax.broadcasted_iota(jnp.int32, shape, len(shape) - 1)
    return lane % HDIM < HDIM // 2


def rotate_pair(values, cosine, signed_sine):
    swapped = jnp.where(
        lane_halves(values.shape),
        pltpu.roll(values, PAIR - HDIM // 2, 1),
        pltpu.roll(values, HDIM // 2, 1),
    )
    return values * cosine + swapped * signed_sine


def first_kernel(x_ref, gain_ref, w_ref, cos_ref, sin_ref, a_ref, qkv_ref):
    unit, _ = normalize(x_ref[...].astype(f32))
    a = (unit * gain_ref[...]).astype(bf16)
    a_ref[...] = a
    cosine, sine = cos_ref[...], sin_ref[...]
    for column in range(0, 3 * D, TILE):
        part = dot_nn(a, w_ref[:, column : column + TILE])
        for half in range(0, TILE, PAIR):
            start = column + half
            piece = part[:, half : half + PAIR]
            if start < 2 * D:
                piece = rotate_pair(piece, cosine, sine)
            if start < D:
                piece = piece * QUERY_SCALE
            qkv_ref[:, start : start + PAIR] = piece.astype(bf16)


def head_lanes():
    lane = lax.broadcasted_iota(jnp.int32, (1, PAIR), 1)
    return [lane < HDIM, lane >= HDIM]


def attend_pair(q_ref, k_ref, v_ref, rows_ref, cols_ref, p_ref, inv_ref, write):
    k, v = k_ref[...], v_ref[...]
    length = k.shape[0]
    mine = head_lanes()
    zero, one = jnp.zeros((), bf16), jnp.ones((), bf16)
    summing = [jnp.where(m, v, one) for m in mine]
    items = [(tile, head) for tile in range(0, length, TILE) for head in range(2)]

    def score(item):
        tile, head = item
        return dot_nt(jnp.where(mine[head], q_ref[tile : tile + TILE, :], zero), k)

    ahead = score(items[0])
    kept = None
    for i, (tile, head) in enumerate(items):
        rows = slice(tile, tile + TILE)
        scores = ahead
        if i + 1 < len(items):
            ahead = score(items[i + 1])
        scores = jnp.where(rows_ref[rows, :] == cols_ref[...], scores, MASKED)
        probs = jnp.exp2(scores - jnp.max(scores, axis=-1, keepdims=True)).astype(bf16)
        p_ref[head, rows, :] = probs
        part = dot_nn(probs, summing[head])
        inv = 1.0 / pltpu.roll(part, HDIM, 1)
        if head == 0:
            kept = (part * inv, inv)
        else:
            inv_ref[rows, :] = jnp.where(mine[0], kept[1], inv)
            write(rows, jnp.where(mine[0], kept[0], part * inv).astype(bf16))


def forward_kernel(
    sizes, pairs, q_ref, k_ref, v_ref, rows_ref, cols_ref, x_ref, gain_ref, w_out_any, w_in_any, w_mlp_any, cot_ref,
    o_ref, p_ref, inv_ref, x1_ref, b_ref, m_ref, slope_ref, act_ref, y_ref, dy_ref,
    joined, w_out_ref, w_in_ref, w_mlp_ref, bounce, *sem_refs,
):
    seq = sizes[2]
    step, last = pl.program_id(0), pl.num_programs(0) - 1
    sems = Sems(*sem_refs)
    me_seq = lax.axis_index("seq")
    into = sems.copy(cot_ref.at[me_seq], bounce)
    outof = sems.copy(bounce, dy_ref.at[0])
    weights = [sems.copy(w_out_any, w_out_ref), sems.copy(w_in_any, w_in_ref), sems.copy(w_mlp_any, w_mlp_ref)]
    blocks = [sems.remote(cot_ref.at[flip(me_seq, k)], dy_ref.at[k], "seq", k) for k in range(1, seq)]

    @pl.when(step == 0)
    def _():
        into.start()
        start_all(weights)
        meet([("seq", k) for k in range(1, seq)])
        start_all(blocks)
        into.wait()
        outof.start()

    @pl.when(step < pairs)
    def _():
        def write(rows, value):
            o_ref[rows, :] = value
            joined[rows, pl.ds(pl.multiple_of(step * PAIR, PAIR), PAIR)] = value

        attend_pair(q_ref, k_ref, v_ref, rows_ref, cols_ref, p_ref, inv_ref, write)

    @pl.when(step == pairs)
    def _():
        wait_all(weights)

    @pl.when(step >= pairs)
    def _():
        start = pl.multiple_of((step - pairs) * TILE, TILE)
        x1 = x_ref[...].astype(f32) + dot_nn(joined[pl.ds(start, TILE), :], w_out_ref[...])
        x1_ref[...] = x1
        unit, _ = normalize(x1)
        b = (unit * gain_ref[...]).astype(bf16)
        b_ref[...] = b

        def hidden(column):
            return (
                dot_nn(b, w_in_ref[:, column : column + HCHUNK]),
                dot_nn(b, w_in_ref[:, FF + column : FF + column + HCHUNK]),
            )

        ahead = hidden(0)
        for column in range(0, FF, HCHUNK):
            hin, gate = ahead
            if column + HCHUNK < FF:
                ahead = hidden(column + HCHUNK)
            phi = 0.5 + 0.5 * lax.erf(hin * math.sqrt(0.5))
            act = hin * phi
            slope = phi + hin * (jnp.exp(hin * hin * -0.5) * (1.0 / math.sqrt(2.0 * math.pi)))
            m_ref[:, column : column + HCHUNK] = (act * gate).astype(bf16)
            act_ref[:, column : column + HCHUNK] = act.astype(bf16)
            slope_ref[:, column : column + HCHUNK] = (slope * gate).astype(bf16)
        y_ref[...] = (x1 + dot_nn(m_ref[...], w_mlp_ref[...])).astype(bf16)

    @pl.when(step == last)
    def _():
        outof.wait()
        wait_all(blocks)


def order_of(sizes, rep_first):
    fsdp, rep, seq = sizes
    core = [("fsdp", 1)]
    rest = [("fsdp", b) for b in bits_of(fsdp)[1:]]
    copies = [("rep", b) for b in bits_of(rep)]
    return core + (copies + rest if rep_first else rest + copies) + [("seq", b) for b in bits_of(seq)]


def all_partners(sizes):
    fsdp, rep, seq = sizes
    return [("seq", k) for k in range(1, seq)] + [("fsdp", b) for b in bits_of(fsdp)] + [("rep", b) for b in bits_of(rep)]


def early_reducers(sizes):
    fsdp, rep, seq = sizes
    shapes = [(fsdp, FF // fsdp, D), (fsdp, D // fsdp, FF), (fsdp, D // fsdp, FF), (fsdp, D // fsdp, D)]
    reducers = [Reducer(shape, sizes, order_of(sizes, w == 2)) for w, shape in enumerate(shapes)]
    across = len(bits_of(fsdp)) + len(bits_of(rep))
    return reducers, [reducers[0].down, across, across, across]


def late_reducers(sizes):
    fsdp = sizes[0]
    return [Reducer((fsdp, D // fsdp, D), sizes, order_of(sizes, w == 1)) for w in range(3)]


def spread(ref, wide, value):
    shards, rows, cols = ref.shape
    if rows % 16 == 0:
        for q in range(shards):
            ref[q] = value[q * rows : (q + 1) * rows].astype(bf16)
    else:
        wide[: shards * rows, :cols] = value
        for q in range(shards):
            ref[q] = wide[q * rows : (q + 1) * rows, :cols].astype(bf16)


def middle_back_tile(dy, x1_ref, slope_ref, act_ref, gain_ref, w_out_ref, w_in_ref, w_mlp_ref, dh_ref, dgain_ref, dx1_ref):
    ahead = dot_nt(dy, w_mlp_ref[:HCHUNK, :])
    for column in range(0, FF, HCHUNK):
        dm = ahead
        if column + HCHUNK < FF:
            ahead = dot_nt(dy, w_mlp_ref[column + HCHUNK : column + 2 * HCHUNK, :])
        dh_ref[:, column : column + HCHUNK] = (dm * slope_ref[:, column : column + HCHUNK].astype(f32)).astype(bf16)
        dh_ref[:, FF + column : FF + column + HCHUNK] = (
            dm * act_ref[:, column : column + HCHUNK].astype(f32)
        ).astype(bf16)
    db = dot_nt(dh_ref[...], w_in_ref[...])
    unit, scale = normalize(x1_ref[...])
    back, terms = norm_back(unit, scale, gain_ref[...], db)
    dgain_ref[...] += jnp.sum(terms, axis=0, keepdims=True)
    dx1 = dy.astype(f32) + back
    dx1_ref[...] = dx1
    return dx1.astype(bf16)


def attend_back_pair(q_ref, k_ref, v_ref, o_ref, inv_ref, do, p_ref, cos_ref, sin_ref, dq_ref, dk_ref, dv_ref):
    v = v_ref[...]
    length = v.shape[0]
    mine = head_lanes()
    zero = jnp.zeros((), bf16)
    do = (do.astype(f32) * inv_ref[...]).astype(bf16)
    inner = do.astype(f32) * o_ref[...].astype(f32)
    do_heads = [jnp.where(m, do, zero) for m in mine]
    q_heads = [jnp.where(m, q_ref[...], zero).T for m in mine]
    k_heads = [jnp.where(m, k_ref[...], zero) for m in mine]
    do_turned = [d.T for d in do_heads]
    cosine, sine = cos_ref[...], sin_ref[...]
    dv = dk = None
    for tile in range(0, length, TILE):
        rows = slice(tile, tile + TILE)
        dq = None
        for head in range(2):
            probs = p_ref[head, rows, :]
            delta = jnp.sum(jnp.where(mine[head], inner[rows], 0.0), axis=-1, keepdims=True)
            dp = dot_nt(do_heads[head][rows], v)
            ds = (probs.astype(f32) * (dp - delta)).astype(bf16)
            value_part = dot_nn(do_turned[head][:, rows], probs)
            key_part = dot_nn(q_heads[head][:, rows], ds)
            query_part = dot_nn(ds, k_heads[head])
            dv = value_part if dv is None else dv + value_part
            dk = key_part if dk is None else dk + key_part
            dq = query_part if dq is None else dq + query_part
        dq_ref[rows, :] = rotate_pair(dq * HDIM**-0.5, cosine[rows], -sine[rows]).astype(bf16)
    dk_ref[...] = rotate_pair(dk.T * math.log(2.0), cosine, -sine).astype(bf16)
    dv_ref[...] = dv.T.astype(bf16)


def backward_kernel(
    sizes, tiles, x1_ref, slope_ref, act_ref, gain_ref, q_ref, k_ref, v_ref, o_ref, inv_ref, p_ref, cos_ref, sin_ref,
    w_out_any, w_in_any, w_mlp_any, m_any, dy_any, b_any, o_any, y_ref, *refs,
):
    reducers, early = early_reducers(sizes)
    count = len(reducers)
    refs = list(refs)
    pop = lambda n: [refs.pop(0) for _ in range(n)]
    dx1_ref, dgain_ref, dq_ref, dk_ref, dv_ref, home_ref = pop(6)
    sums_out = pop(count)
    w_out_ref, w_in_ref, w_mlp_ref, m_ref, dy_ref, b_ref, all_o_ref = pop(7)
    dh_ref, low_ref, do_ref, wide, bounce = pop(5)
    grads = pop(count)
    lands = [pop(len(r.scratch(0, e))) for r, e in zip(reducers, early)]
    sems = Sems(*refs)
    me = lax.axis_index("fsdp")
    step, last = pl.program_id(0), pl.num_programs(0) - 1
    into, outof, blocks = give_back(y_ref, home_ref, bounce, sems)
    loads = [
        sems.copy(src, dst)
        for src, dst in [
            (m_any, m_ref), (dy_any, dy_ref), (w_mlp_any, w_mlp_ref), (w_in_any, w_in_ref), (w_out_any, w_out_ref),
            (b_any, b_ref), (o_any, all_o_ref),
        ]
    ]
    stores = [sems.copy(grads[w].at[me], sums_out[w]) for w in range(count)]
    for w, reducer in enumerate(reducers):
        reducer.bind(lambda j, w=w: grads[w].at[flip(me, j)], lands[w], sems, 0, early[w])
    mlp, first_half, second_half, out = reducers

    def at(when, *actions):
        @pl.when(step == when)
        def _():
            for action in actions:
                action()

    def advance(reducer, s, limit):
        def run():
            reducer.finish(s)
            if s + 1 < limit:
                reducer.start(s + 1)
        return run

    @pl.when(step == 0)
    def _():
        start_all(loads)
        into.start()
        meet(all_partners(sizes))
        start_all(blocks)
        dgain_ref[...] = jnp.zeros_like(dgain_ref)
        wait_all(loads[:2])
        spread(grads[0], wide, dot_tn(m_ref[...], dy_ref[...]))
        mlp.start(0)
        into.wait()
        outof.start()
        wait_all(loads[2:5])

    at(1, advance(mlp, 0, early[0]))

    @pl.when(step < tiles)
    def _():
        rows = pl.ds(pl.multiple_of(step * TILE, TILE), TILE)
        low = middle_back_tile(
            dy_ref[rows, :], x1_ref, slope_ref, act_ref, gain_ref, w_out_ref, w_in_ref, w_mlp_ref,
            dh_ref.at[rows, :], dgain_ref, dx1_ref,
        )
        low_ref[rows, :] = low
        do_ref[rows, :] = dot_nt(low, w_out_ref[...]).astype(bf16)

    inner_steps = len(bits_of(sizes[0])) - 1

    @pl.when(step == tiles)
    def _():
        for s in range(1, 1 + inner_steps):
            advance(mlp, s, early[0])()
        wait_all(loads[5:])
        spread(grads[1], wide, dot_tn(b_ref[...], dh_ref[:, :FF]))
        first_half.start(0)
        spread(grads[2], wide, dot_tn(b_ref[...], dh_ref[:, FF:]))
        second_half.start(0)
        spread(grads[3], wide, dot_tn(all_o_ref[...], low_ref[...]))
        out.start(0)

    for reducer, limit in zip(reducers[1:], early[1:]):
        at(tiles + 1, advance(reducer, 0, limit))
    at(tiles + 1, *[advance(mlp, s, early[0]) for s in range(1 + inner_steps, 2 + inner_steps)])
    for reducer, limit in zip(reducers[1:], early[1:]):
        for s in range(1, limit - 1):
            at(tiles + 4, advance(reducer, s, limit))
    at(tiles + 5, *[advance(mlp, s, early[0]) for s in range(2 + inner_steps, early[0] - 1)])

    @pl.when(step > tiles)
    def _():
        column = pl.multiple_of((step - tiles - 1) * PAIR, PAIR)
        attend_back_pair(
            q_ref, k_ref, v_ref, o_ref, inv_ref, do_ref[:, pl.ds(column, PAIR)], p_ref, cos_ref, sin_ref,
            dq_ref, dk_ref, dv_ref,
        )

    @pl.when(step == last)
    def _():
        for w, reducer in enumerate(reducers):
            reducer.finish(early[w] - 1)
            stores[w].start()
        wait_all(stores)
        outof.wait()
        wait_all(blocks)


def leave_kernel(
    sizes, gain_ref, other_gain_ref, dx1_ref, x_ref, dq_ref, dk_ref, dv_ref, a_ref, w_ref, *refs
):
    fsdp, rep, seq = sizes
    reducers, early = early_reducers(sizes)
    whole = late_reducers(sizes)
    count, more = len(reducers), len(whole)
    refs = list(refs)
    pop = lambda n: [refs.pop(0) for _ in range(n)]
    sums_in = pop(count)
    (home_ref,) = pop(1)
    sums_out, wholes_out = pop(count), pop(more)
    (gains_out,) = pop(1)
    slots, wide = pop(2)
    held, grads, finals = pop(count), pop(more), pop(count + more)
    lands = [pop(len(r.scratch(e, len(r.steps)))) for r, e in zip(reducers, early)]
    whole_lands = [pop(len(r.scratch(0, len(r.steps)))) for r in whole]
    (gain_lands,) = pop(1)
    sems = Sems(*refs)
    me, me_seq = lax.axis_index("fsdp"), lax.axis_index("seq")
    own = sems.copy(slots.at[0], home_ref.at[me_seq])
    blocks = {k: sems.remote(slots.at[k], home_ref.at[me_seq], "seq", k) for k in range(1, seq)}
    loads = [sems.copy(sums_in[w], held[w]) for w in range(count)]
    stores = [sems.copy(finals[w], out) for w, out in enumerate(sums_out + wholes_out)]
    for w, reducer in enumerate(reducers):
        reducer.bind(lambda j, w=w: held[w], lands[w], sems, early[w], len(reducer.steps), finals[w])
    for w, reducer in enumerate(whole):
        reducer.bind(
            lambda j, w=w: grads[w].at[flip(me, j)], whole_lands[w], sems, 0, len(reducer.steps), finals[count + w]
        )
    hops = [("fsdp", b) for b in bits_of(fsdp)] + [("rep", b) for b in bits_of(rep)] + [("seq", b) for b in bits_of(seq)]
    gain_moves = [sems.remote(gains_out, gain_lands.at[i], axis, bit) for i, (axis, bit) in enumerate(hops)]
    rows = slots.shape[1]

    def advance(reducer, s):
        if s < len(reducer.steps):
            reducer.finish(s)
            if s + 1 < len(reducer.steps):
                reducer.start(s + 1)

    gains_out[...] = jnp.zeros_like(gains_out)
    gains_out[1:2, :] = other_gain_ref[...]
    start_all(loads)
    meet(all_partners(sizes))
    wait_all(loads)
    for reducer, e in zip(reducers, early):
        reducer.start(e)

    def input_slot(k):
        piece = slice(k * rows, (k + 1) * rows)
        da = dot_nt(dq_ref[piece, :], w_ref[:, :D])
        da = da + dot_nt(dk_ref[piece, :], w_ref[:, D : 2 * D])
        da = da + dot_nt(dv_ref[piece, :], w_ref[:, 2 * D :])
        unit, scale = normalize(x_ref[piece, :].astype(f32))
        back, terms = norm_back(unit, scale, gain_ref[...], da)
        gains_out[0:1, :] += jnp.sum(terms, axis=0, keepdims=True)
        slots[k] = (dx1_ref[piece, :] + back).astype(bf16)

    for w, part in enumerate((dq_ref, dk_ref, dv_ref)):
        spread(grads[w], wide, dot_tn(a_ref[...], part[...]))
        whole[w].start(0)
        for earlier in range(w):
            advance(whole[earlier], w - 1 - earlier)
    for k in list(range(1, seq)) + [0]:
        input_slot(k)
        if k:
            blocks[k].start()
    own.start()
    gain_moves[0].start()
    for s in range(max(len(r.steps) for r in whole) + more):
        for w, reducer in enumerate(whole):
            at = s + more - 1 - w if s == 0 else s + more - 1 - w
            advance(reducer, at)
        for reducer, e in zip(reducers, early):
            advance(reducer, s + e)
        if s < len(hops):
            gain_moves[s].wait()
            gains_out[...] += gain_lands[s]
            if s + 1 < len(hops):
                gain_moves[s + 1].start()
    start_all(stores)
    wait_all(stores)
    own.wait()
    wait_all([blocks[k] for k in range(1, seq)])


def rows_spec(width):
    return pl.BlockSpec((TILE, width), lambda i: (i, 0))


def whole_spec(*shape):
    return pl.BlockSpec(shape, lambda i: (0,) * len(shape))


def pair_spec(length, offset=0):
    return pl.BlockSpec((length, PAIR), lambda i: (0, i + offset))


def struct(dtype, *shape):
    return jax.ShapeDtypeStruct(shape, dtype)


def call(kernel, grid, in_specs, out_specs, out_shape, flops, scratch=(), collective=None):
    return pl.pallas_call(
        kernel,
        grid=(grid,),
        in_specs=in_specs,
        out_specs=out_specs,
        out_shape=out_shape,
        scratch_shapes=list(scratch),
        compiler_params=pltpu.CompilerParams(
            dimension_semantics=("arbitrary",), vmem_limit_bytes=VMEM_LIMIT,
            collective_id=collective, has_side_effects=collective is not None,
        ),
        cost_estimate=pl.CostEstimate(flops=flops, bytes_accessed=10 * 2**20, transcendentals=0),
    )


MESH = pl.DeviceIdType.MESH
ANY = pl.BlockSpec(memory_space=pl.ANY)


def take(array, index):
    return lax.dynamic_index_in_dim(array, index, 0, keepdims=False)


def flip(index, mask):
    bit = 1
    while bit <= mask:
        if mask & bit:
            index = index + bit - 2 * bit * ((index // bit) % 2)
        bit *= 2
    return index


def bits_of(size):
    return [1 << i for i in range(size.bit_length() - 1)]


def meet(partners):
    barrier = pltpu.get_barrier_semaphore()
    for axis, mask in partners:
        pl.semaphore_signal(
            barrier, inc=1, device_id={axis: flip(lax.axis_index(axis), mask)}, device_id_type=MESH
        )
    pl.semaphore_wait(barrier, len(partners))


class Sems:
    def __init__(self, send, recv, local):
        self.send, self.recv, self.local = send, recv, local
        self.remote_used = self.local_used = 0

    def remote(self, src, dst, axis, mask):
        i = self.remote_used
        self.remote_used += 1
        return pltpu.make_async_remote_copy(
            src_ref=src, dst_ref=dst, send_sem=self.send.at[i], recv_sem=self.recv.at[i],
            device_id={axis: flip(lax.axis_index(axis), mask)}, device_id_type=MESH,
        )

    def copy(self, src, dst):
        i = self.local_used
        self.local_used += 1
        return pltpu.make_async_copy(src, dst, self.local.at[i])


def sem_shapes(remote, local):
    dma = pltpu.SemaphoreType.DMA
    return [dma((remote,)), dma((remote,)), dma((max(local, 1),))]


def start_all(copies):
    for copy in copies:
        copy.start()


def wait_all(copies):
    for copy in copies:
        copy.wait()


def enter_kernel(sizes, count, *refs):
    fsdp, rep, seq = sizes
    tokens, shards = refs[0], refs[1 : 1 + count]
    x_out, fulls = refs[1 + count], refs[2 + count : 2 + 2 * count]
    bounce_x, bounces = refs[2 + 2 * count], refs[3 + 2 * count : 3 + 3 * count]
    sems = Sems(*refs[3 + 3 * count :])
    me, me_seq, me_rep = lax.axis_index("fsdp"), lax.axis_index("seq"), lax.axis_index("rep")
    into = [sems.copy(tokens.at[me_seq], bounce_x)] + [sems.copy(shards[w], bounces[w]) for w in range(count)]
    outof = [sems.copy(bounce_x, x_out.at[0])] + [sems.copy(bounces[w], fulls[w].at[me]) for w in range(count)]
    start_all(into)
    meet([("seq", k) for k in range(1, seq)] + [("fsdp", b) for b in bits_of(fsdp)] + [("rep", b) for b in bits_of(rep)])
    blocks = [sems.remote(tokens.at[flip(me_seq, k)], x_out.at[k], "seq", k) for k in range(1, seq)]
    start_all(blocks)

    def piece(ref, w, index):
        width = shards[w].shape[-1] // rep
        return ref.at[index, :, pl.ds(pl.multiple_of(me_rep * width, 128), width)]

    def first_piece(w):
        width = shards[w].shape[-1] // rep
        return shards[w].at[:, pl.ds(pl.multiple_of(me_rep * width, 128), width)]

    held = [0]
    pending = []
    for bit in reversed(bits_of(fsdp)[1:]):
        over = []
        for w in range(count):
            moved = []
            for h in held:
                src = first_piece(w) if h == 0 else piece(fulls[w], w, flip(me, h))
                moved.append(sems.remote(src, piece(fulls[w], w, flip(me, h)), "fsdp", bit))
            start_all(moved)
            over.append(moved)
        relays = []
        for w in range(count):
            for copy in over[w]:
                copy.wait_recv()
            moved = []
            for mask in range(1, rep):
                for h in held:
                    here = piece(fulls[w], w, flip(me, h ^ bit))
                    moved.append(sems.remote(here, here, "rep", mask))
            start_all(moved)
            relays.append(moved)
            pending += over[w]
        for moved in relays:
            for copy in moved:
                copy.wait_recv()
            pending += moved
        held = held + [h ^ bit for h in held]
    last = []
    for w in range(count):
        for h in held:
            src = shards[w] if h == 0 else fulls[w].at[flip(me, h)]
            last.append(sems.remote(src, fulls[w].at[flip(me, h)], "fsdp", 1))
    start_all(last)
    wait_all(into)
    start_all(outof)
    for copy in pending:
        copy.wait_send()
    wait_all(last)
    wait_all(blocks)
    wait_all(outof)


def enter(sizes, tokens, shards):
    fsdp, rep, seq = sizes
    count = len(shards)
    assert fsdp >= 2
    held, copies = 1, seq - 1
    for _ in bits_of(fsdp)[1:]:
        copies += count * held * rep
        held *= 2
    copies += count * held
    hbm = lambda shape: struct(bf16, *shape)
    return pl.pallas_call(
        functools.partial(enter_kernel, sizes, count),
        in_specs=[ANY] * (1 + count),
        out_specs=[ANY] * (1 + count),
        out_shape=[hbm(tokens.shape)] + [hbm((fsdp,) + s.shape) for s in shards],
        scratch_shapes=[pltpu.VMEM(tokens.shape[1:], bf16)]
        + [pltpu.VMEM(s.shape, bf16) for s in shards]
        + sem_shapes(copies, 2 * (1 + count)),
        compiler_params=pltpu.CompilerParams(collective_id=0, has_side_effects=True),
    )(tokens, *shards)


class Reducer:
    def __init__(self, parts_shape, sizes, order):
        self.fsdp, self.rows, self.cols = parts_shape
        self.steps = []
        held, rows, cols = list(range(self.fsdp)), self.rows, self.cols
        row_at, col_at = [], []
        for axis, bit in order:
            step = dict(axis=axis, bit=bit, row_at=list(row_at), col_at=list(col_at), rows=rows, cols=cols)
            if axis == "fsdp":
                step["send"] = [j for j in held if j & bit]
                held = [j for j in held if not j & bit]
                step["keep"] = held
                step["shape"] = (len(held), rows, cols)
                step["split"] = None
            else:
                step["keep"] = step["send"] = held
                if (rows // 2) % 16 == 0:
                    rows //= 2
                    row_at = row_at + [(axis, bit, rows)]
                    step["split"] = "rows"
                elif (cols // 2) % 128 == 0:
                    cols //= 2
                    col_at = col_at + [(axis, bit, cols)]
                    step["split"] = "cols"
                else:
                    step["split"] = "none"
                step["shape"] = (len(held), rows, cols)
            self.steps.append(step)
        self.down = len(self.steps)
        for step in reversed(self.steps[: self.down]):
            if step["split"] in ("rows", "cols"):
                self.steps.append(dict(step, up=True))

    @staticmethod
    def offset(terms, align, last=None):
        total = 0
        for i, (axis, bit, extent) in enumerate(terms):
            half = (lax.axis_index(axis) // bit) % 2
            if last == i:
                half = 1 - half
            total = total + half * extent
        return total if isinstance(total, int) else pl.multiple_of(total, align)

    def region(self, step, after, other=False):
        row_at, col_at, rows, cols = step["row_at"], step["col_at"], step["rows"], step["cols"]
        row_last = col_last = None
        if after:
            if step["split"] == "rows":
                rows //= 2
                row_at = row_at + [(step["axis"], step["bit"], rows)]
                row_last = len(row_at) - 1 if other else None
            elif step["split"] == "cols":
                cols //= 2
                col_at = col_at + [(step["axis"], step["bit"], cols)]
                col_last = len(col_at) - 1 if other else None
        return (
            pl.ds(self.offset(row_at, 16, row_last), rows),
            pl.ds(self.offset(col_at, 128, col_last), cols),
        )

    def scratch(self, first, last):
        return [pltpu.VMEM(s["shape"], bf16) for s in self.steps[first:last] if "up" not in s]

    def copies(self, first, last):
        return sum(1 if "up" in s else len(s["send"]) for s in self.steps[first:last])

    def bind(self, parts, lands, sems, first, last, final=None):
        self.parts, self.sems, self.final = parts, sems, final
        self.lands, self.moves = {}, {}
        lands = list(lands)
        for s in range(first, last):
            step = self.steps[s]
            moves = []
            if "up" in step:
                there = final.at[self.region(step, True)]
                moves.append(sems.remote(there, there, step["axis"], step["bit"]))
            else:
                land = self.lands[s] = lands.pop(0)
                for i, j in enumerate(step["send"]):
                    fsdp = step["axis"] == "fsdp"
                    src = self.parts(j).at[self.region(step, not fsdp, not fsdp)]
                    moves.append(sems.remote(src, land.at[i], step["axis"], step["bit"]))
            self.moves[s] = moves

    def start(self, s):
        if s == self.down:
            region = self.region(self.steps[s - 1], True)
            self.final[region] = self.parts(0)[region]
        start_all(self.moves[s])

    def finish(self, s):
        step = self.steps[s]
        for i, move in enumerate(self.moves[s]):
            move.wait()
            if "up" not in step:
                j = step["keep"][i]
                ref = self.parts(j)
                region = self.region(step, True)
                ref[region] = (ref[region].astype(f32) + self.lands[s][i].astype(f32)).astype(bf16)


def give_back(slots, home, bounce, sems):
    me = lax.axis_index("seq")
    seq = slots.shape[0]
    return (
        sems.copy(slots.at[0], bounce),
        sems.copy(bounce, home.at[me]),
        [sems.remote(slots.at[k], home.at[me], "seq", k) for k in range(1, seq)],
    )


def body(sizes, tokens, segments, positions, gain_attn, w_qkv, w_out, gain_mlp, w_in, w_mlp_out, cotangent):
    fsdp, rep, seq = sizes
    micro, batch, rows, _ = tokens.shape
    assert micro * batch == seq and rows % TILE == 0
    length = seq * rows
    me_seq, me_fsdp = lax.axis_index("seq"), lax.axis_index("fsdp")

    own_gains = jnp.zeros((16, D), bf16)
    own_gains = lax.dynamic_update_slice(own_gains, jnp.stack([gain_attn, gain_mlp]), (0, me_fsdp * (D // fsdp)))
    x, gains, wq, wo, wm, wi = enter(
        sizes, tokens.reshape(seq, rows, D), [own_gains, w_qkv, w_out, w_mlp_out, w_in]
    )
    x = x.reshape(length, D)
    gains = jnp.sum(gains[:, :2].astype(f32), axis=0)
    gain_one, gain_two = gains[:1], gains[1:]
    wq, wo, wm, wi = (w.reshape(-1, w.shape[-1]) for w in (wq, wo, wm, wi))

    marks = take(segments.reshape(seq, length), me_seq)
    place = jnp.arange(length, dtype=jnp.int32) - jnp.sum(
        (marks[None, :] < marks[:, None]).astype(jnp.int32), axis=1
    )
    slot_order = [me_seq ^ k for k in range(seq)]
    marks = jnp.concatenate([take(marks.reshape(seq, rows), s) for s in slot_order])
    place = jnp.concatenate([take(place.reshape(seq, rows), s) for s in slot_order])
    half = jnp.arange(0, HDIM, 2).astype(f32) / HDIM
    angles = place.astype(f32)[:, None] * jnp.exp(-half * math.log(THETA))
    cosine, sine = jnp.cos(angles), jnp.sin(angles)
    cosine = jnp.concatenate([cosine] * 4, -1)
    sine = jnp.concatenate([-sine, sine] * 2, -1)

    tiles, pairs = length // TILE, HEADS // 2
    a, qkv = call(
        first_kernel, tiles,
        [rows_spec(D), whole_spec(1, D), whole_spec(D, 3 * D), rows_spec(PAIR), rows_spec(PAIR)],
        [rows_spec(D), rows_spec(3 * D)],
        [struct(bf16, length, D), struct(bf16, length, 3 * D)],
        2 * length * D * 3 * D,
    )(x, gain_one, wq, cosine, sine)

    vmem = pl.BlockSpec(memory_space=pltpu.VMEM)
    pair_at = lambda offset, lag, n: pl.BlockSpec(
        (length, PAIR), lambda i: (0, jnp.clip(i - lag, 0, n - 1) + offset)
    )
    prob_at = lambda lag: pl.BlockSpec((2, length, length), lambda i: (jnp.clip(i - lag, 0, pairs - 1), 0, 0))
    tile_at = lambda width, lag: pl.BlockSpec((TILE, width), lambda i: (jnp.clip(i - lag, 0, tiles - 1), 0))
    slots = struct(bf16, seq, rows, D)
    o, probs, inv, x1, b, m, slope, act, y, dy = call(
        functools.partial(forward_kernel, sizes, pairs), pairs + tiles,
        [pair_at(0, 0, pairs), pair_at(pairs, 0, pairs), pair_at(2 * pairs, 0, pairs),
         whole_spec(length, 1), whole_spec(1, length), tile_at(D, pairs), whole_spec(1, D)] + [ANY] * 4,
        [pair_at(0, 0, pairs), prob_at(0), pair_at(0, 0, pairs), tile_at(D, pairs), tile_at(D, pairs)]
        + [tile_at(FF, pairs)] * 3 + [tile_at(D, pairs), ANY],
        [struct(bf16, length, D), struct(bf16, HEADS, length, length), struct(f32, length, D),
         struct(f32, length, D), struct(bf16, length, D), struct(bf16, length, FF),
         struct(bf16, length, FF), struct(bf16, length, FF), struct(bf16, length, D), slots],
        16 * length * length * D,
        [pltpu.VMEM((length, D), bf16), pltpu.VMEM((D, D), bf16), pltpu.VMEM((D, 2 * FF), bf16), pltpu.VMEM((FF, D), bf16),
         pltpu.VMEM((rows, D), bf16)] + sem_shapes(seq - 1, 5), 1,
    )(qkv, qkv, qkv, marks[:, None], marks[None, :], x, gain_two, wo, wi, wm, cotangent.reshape(seq, rows, D))

    reducers, early = early_reducers(sizes)
    whole = late_reducers(sizes)
    own_shard = lambda r: struct(bf16, r.rows, r.cols)
    full_shard = lambda r: pltpu.VMEM((fsdp, r.rows, r.cols), bf16)
    odd = (FF // fsdp) % 16 or (D // fsdp) % 16
    wide = pltpu.VMEM((FF, FF) if odd else (8, 128), f32)
    dx1, dgain_two, dq, dk, dv, block_out, *sums = call(
        functools.partial(backward_kernel, sizes, tiles), tiles + 1 + pairs,
        [tile_at(D, 0), tile_at(FF, 0), tile_at(FF, 0), whole_spec(1, D)]
        + [pair_at(n * pairs, tiles + 1, pairs) for n in range(3)]
        + [pair_at(0, tiles + 1, pairs), pair_at(0, tiles + 1, pairs), prob_at(tiles + 1),
           whole_spec(length, PAIR), whole_spec(length, PAIR)] + [ANY] * 8,
        [tile_at(D, 0), whole_spec(1, D)] + [pair_at(0, tiles + 1, pairs)] * 3 + [ANY] * (1 + len(reducers)),
        [struct(f32, length, D), struct(f32, 1, D)] + [struct(bf16, length, D)] * 3 + [slots]
        + [own_shard(r) for r in reducers],
        32 * length * length * D,
        [pltpu.VMEM((D, D), bf16), pltpu.VMEM((D, 2 * FF), bf16), pltpu.VMEM((FF, D), bf16),
         pltpu.VMEM((length, FF), bf16)] + [pltpu.VMEM((length, D), bf16)] * 3
        + [pltpu.VMEM((length, 2 * FF), bf16), pltpu.VMEM((length, D), bf16), pltpu.VMEM((length, D), bf16),
           wide, pltpu.VMEM((rows, D), bf16)]
        + [full_shard(r) for r in reducers]
        + [land for r, e in zip(reducers, early) for land in r.scratch(0, e)]
        + sem_shapes(seq - 1 + sum(r.copies(0, e) for r, e in zip(reducers, early)), 9 + len(reducers)), 2,
    )(x1, slope, act, gain_two, qkv, qkv, qkv, o, inv, probs, cosine, sine,
      wo, wi, wm, m, dy.reshape(length, D), b, o, y.reshape(seq, rows, D))

    hops = sum(len(bits_of(n)) for n in sizes)
    input_grad, *results, dgains = pl.pallas_call(
        functools.partial(leave_kernel, sizes),
        in_specs=[vmem] * 9 + [ANY] * len(reducers),
        out_specs=[ANY] * (1 + len(reducers + whole)) + [vmem],
        out_shape=[slots] + [own_shard(r) for r in reducers + whole] + [struct(f32, 8, D)],
        scratch_shapes=[pltpu.VMEM((seq, rows, D), bf16), wide]
        + [pltpu.VMEM((r.rows, r.cols), bf16) for r in reducers]
        + [full_shard(r) for r in whole]
        + [pltpu.VMEM((r.rows, r.cols), bf16) for r in reducers + whole]
        + [land for r, e in zip(reducers, early) for land in r.scratch(e, len(r.steps))]
        + [land for r in whole for land in r.scratch(0, len(r.steps))]
        + [pltpu.VMEM((hops, 8, D), f32)]
        + sem_shapes(
            seq - 1 + hops + sum(r.copies(e, len(r.steps)) for r, e in zip(reducers, early))
            + sum(r.copies(0, len(r.steps)) for r in whole),
            1 + 2 * len(reducers) + len(whole),
        ),
        compiler_params=pltpu.CompilerParams(
            collective_id=3, has_side_effects=True, vmem_limit_bytes=VMEM_LIMIT
        ),
    )(gain_one, dgain_two, dx1, x, dq, dk, dv, a, wq, *sums)
    dgains = lax.dynamic_slice_in_dim(dgains, me_fsdp * (D // fsdp), D // fsdp, 1)
    grad_mlp, grad_in, grad_gate, grad_out, grad_q, grad_k, grad_v = (r.astype(f32) for r in results)
    return (
        block_out.reshape(tokens.shape),
        input_grad.astype(f32).reshape(tokens.shape),
        dgains[0],
        jnp.concatenate([grad_q, grad_k, grad_v], 1),
        grad_out,
        dgains[1],
        jnp.concatenate([grad_in, grad_gate], 1),
        grad_mlp,
    )


def solution(mesh):
    sizes = (mesh.shape["fsdp"], mesh.shape["rep"], mesh.shape["seq"])
    wide = P(None, ("rep", "fsdp"), "seq", None)
    placed = (
        wide, P(None, ("rep", "fsdp"), None), P(None, ("rep", "fsdp"), "seq"),
        P("fsdp"), P("fsdp", None), P("fsdp", None), P("fsdp"), P("fsdp", None), P("fsdp", None), wide,
    )
    return jax.shard_map(
        functools.partial(body, sizes),
        mesh=mesh,
        in_specs=placed,
        out_specs=(
            wide, wide, P("fsdp"), P("fsdp", None), P("fsdp", None), P("fsdp"), P("fsdp", None), P("fsdp", None),
        ),
        check_vma=False,
    )
```

```python
import functools
import math

import jax
import jax.numpy as jnp
from jax import lax
from jax.experimental import pallas as pl
from jax.experimental.pallas import tpu as pltpu
from jax.sharding import PartitionSpec as P

D = 768
HEADS = 12
HDIM = 64
FF = 1152
EPS = 1e-05
THETA = 160000.0
MASKED = -1000000000.0
QUERY_SCALE = HDIM**-0.5 / math.log(2.0)
TILE = 256
PAIR = 2 * HDIM
HCHUNK = 384
f32 = jnp.float32
bf16 = jnp.bfloat16
VMEM_LIMIT = 62 * 2**20


def dot_nn(left, right):
    return lax.dot_general(left, right, (((1,), (0,)), ((), ())), preferred_element_type=f32)


def dot_nt(left, right):
    return lax.dot_general(left, right, (((1,), (1,)), ((), ())), preferred_element_type=f32)


def dot_tn(left, right):
    return lax.dot_general(left, right, (((0,), (0,)), ((), ())), preferred_element_type=f32)


def normalize(values):
    mean = jnp.mean(values, axis=-1, keepdims=True)
    centered = values - mean
    var = jnp.mean(centered * centered, axis=-1, keepdims=True)
    scale = lax.rsqrt(var + EPS)
    return centered * scale, scale


def norm_back(unit, scale, gain, grad):
    gain_terms = grad * unit
    inner = grad * gain
    first = jnp.mean(inner, axis=-1, keepdims=True)
    second = jnp.mean(inner * unit, axis=-1, keepdims=True)
    return scale * (inner - first - unit * second), gain_terms


def lane_halves(shape):
    lane = lax.broadcasted_iota(jnp.int32, shape, len(shape) - 1)
    return lane % HDIM < HDIM // 2


def rotate_pair(values, cosine, signed_sine):
    swapped = jnp.where(
        lane_halves(values.shape),
        pltpu.roll(values, PAIR - HDIM // 2, 1),
        pltpu.roll(values, HDIM // 2, 1),
    )
    return values * cosine + swapped * signed_sine


def first_kernel(x_ref, gain_ref, w_ref, cos_ref, sin_ref, a_ref, qkv_ref):
    unit, _ = normalize(x_ref[...].astype(f32))
    a = (unit * gain_ref[...]).astype(bf16)
    a_ref[...] = a
    cosine, sine = cos_ref[...], sin_ref[...]
    for column in range(0, 3 * D, TILE):
        part = dot_nn(a, w_ref[:, column : column + TILE])
        for half in range(0, TILE, PAIR):
            start = column + half
            piece = part[:, half : half + PAIR]
            if start < 2 * D:
                piece = rotate_pair(piece, cosine, sine)
            if start < D:
                piece = piece * QUERY_SCALE
            qkv_ref[:, start : start + PAIR] = piece.astype(bf16)


def head_lanes():
    lane = lax.broadcasted_iota(jnp.int32, (1, PAIR), 1)
    return [lane < HDIM, lane >= HDIM]


def attend_pair(q_ref, k_ref, v_ref, rows_ref, cols_ref, p_ref, inv_ref, write):
    k, v = k_ref[...], v_ref[...]
    length = k.shape[0]
    mine = head_lanes()
    zero, one = jnp.zeros((), bf16), jnp.ones((), bf16)
    summing = [jnp.where(m, v, one) for m in mine]
    items = [(tile, head) for tile in range(0, length, TILE) for head in range(2)]

    def score(item):
        tile, head = item
        return dot_nt(jnp.where(mine[head], q_ref[tile : tile + TILE, :], zero), k)

    ahead = score(items[0])
    kept = None
    for i, (tile, head) in enumerate(items):
        rows = slice(tile, tile + TILE)
        scores = ahead
        if i + 1 < len(items):
            ahead = score(items[i + 1])
        scores = jnp.where(rows_ref[rows, :] == cols_ref[...], scores, MASKED)
        probs = jnp.exp2(scores - jnp.max(scores, axis=-1, keepdims=True)).astype(bf16)
        p_ref[head, rows, :] = probs
        part = dot_nn(probs, summing[head])
        inv = 1.0 / pltpu.roll(part, HDIM, 1)
        if head == 0:
            kept = (part * inv, inv)
        else:
            inv_ref[rows, :] = jnp.where(mine[0], kept[1], inv)
            write(rows, jnp.where(mine[0], kept[0], part * inv).astype(bf16))


def forward_kernel(
    sizes, pairs, q_ref, k_ref, v_ref, rows_ref, cols_ref, x_ref, gain_ref, w_out_any, w_in_any, w_mlp_any, cot_ref,
    o_ref, p_ref, inv_ref, x1_ref, b_ref, m_ref, slope_ref, act_ref, y_ref, dy_ref,
    joined, w_out_ref, w_in_ref, w_mlp_ref, bounce, *sem_refs,
):
    seq = sizes[2]
    step, last = pl.program_id(0), pl.num_programs(0) - 1
    sems = Sems(*sem_refs)
    me_seq = lax.axis_index("seq")
    into = sems.copy(cot_ref.at[me_seq], bounce)
    outof = sems.copy(bounce, dy_ref.at[0])
    weights = [sems.copy(w_out_any, w_out_ref), sems.copy(w_in_any, w_in_ref), sems.copy(w_mlp_any, w_mlp_ref)]
    blocks = [sems.remote(cot_ref.at[flip(me_seq, k)], dy_ref.at[k], "seq", k) for k in range(1, seq)]

    @pl.when(step == 0)
    def _():
        into.start()
        start_all(weights)
        meet([("seq", k) for k in range(1, seq)])
        start_all(blocks)
        into.wait()
        outof.start()

    @pl.when(step < pairs)
    def _():
        def write(rows, value):
            o_ref[rows, :] = value
            joined[rows, pl.ds(pl.multiple_of(step * PAIR, PAIR), PAIR)] = value

        attend_pair(q_ref, k_ref, v_ref, rows_ref, cols_ref, p_ref, inv_ref, write)

    @pl.when(step == pairs)
    def _():
        wait_all(weights)

    @pl.when(step >= pairs)
    def _():
        start = pl.multiple_of((step - pairs) * TILE, TILE)
        x1 = x_ref[...].astype(f32) + dot_nn(joined[pl.ds(start, TILE), :], w_out_ref[...])
        x1_ref[...] = x1
        unit, _ = normalize(x1)
        b = (unit * gain_ref[...]).astype(bf16)
        b_ref[...] = b

        def hidden(column):
            return (
                dot_nn(b, w_in_ref[:, column : column + HCHUNK]),
                dot_nn(b, w_in_ref[:, FF + column : FF + column + HCHUNK]),
            )

        ahead = hidden(0)
        for column in range(0, FF, HCHUNK):
            hin, gate = ahead
            if column + HCHUNK < FF:
                ahead = hidden(column + HCHUNK)
            phi = 0.5 + 0.5 * lax.erf(hin * math.sqrt(0.5))
            act = hin * phi
            slope = phi + hin * (jnp.exp(hin * hin * -0.5) * (1.0 / math.sqrt(2.0 * math.pi)))
            m_ref[:, column : column + HCHUNK] = (act * gate).astype(bf16)
            act_ref[:, column : column + HCHUNK] = act.astype(bf16)
            slope_ref[:, column : column + HCHUNK] = (slope * gate).astype(bf16)
        y_ref[...] = (x1 + dot_nn(m_ref[...], w_mlp_ref[...])).astype(bf16)

    @pl.when(step == last)
    def _():
        outof.wait()
        wait_all(blocks)


def order_of(sizes, rep_first):
    fsdp, rep, seq = sizes
    core = [("fsdp", 1)]
    rest = [("fsdp", b) for b in bits_of(fsdp)[1:]]
    copies = [("rep", b) for b in bits_of(rep)]
    return core + (copies + rest if rep_first else rest + copies) + [("seq", b) for b in bits_of(seq)]


def all_partners(sizes):
    fsdp, rep, seq = sizes
    return [("seq", k) for k in range(1, seq)] + [("fsdp", b) for b in bits_of(fsdp)] + [("rep", b) for b in bits_of(rep)]


def early_reducers(sizes):
    fsdp, rep, seq = sizes
    shapes = [(fsdp, FF // fsdp, D), (fsdp, D // fsdp, FF), (fsdp, D // fsdp, FF), (fsdp, D // fsdp, D)]
    reducers = [Reducer(shape, sizes, order_of(sizes, w == 2)) for w, shape in enumerate(shapes)]
    across = len(bits_of(fsdp)) + len(bits_of(rep))
    return reducers, [reducers[0].down] + [across + 1] * 3


def late_reducers(sizes):
    fsdp = sizes[0]
    return [Reducer((fsdp, D // fsdp, D), sizes, order_of(sizes, w == 1)) for w in range(3)]


def spread(ref, wide, value):
    shards, rows, cols = ref.shape
    if rows % 16 == 0:
        for q in range(shards):
            ref[q] = value[q * rows : (q + 1) * rows].astype(bf16)
    else:
        wide[: shards * rows, :cols] = value
        for q in range(shards):
            ref[q] = wide[q * rows : (q + 1) * rows, :cols].astype(bf16)


def middle_back_tile(dy, x1_ref, slope_ref, act_ref, gain_ref, w_out_ref, w_in_ref, w_mlp_ref, dh_ref, dgain_ref, dx1_ref):
    ahead = dot_nt(dy, w_mlp_ref[:HCHUNK, :])
    for column in range(0, FF, HCHUNK):
        dm = ahead
        if column + HCHUNK < FF:
            ahead = dot_nt(dy, w_mlp_ref[column + HCHUNK : column + 2 * HCHUNK, :])
        dh_ref[:, column : column + HCHUNK] = (dm * slope_ref[:, column : column + HCHUNK].astype(f32)).astype(bf16)
        dh_ref[:, FF + column : FF + column + HCHUNK] = (
            dm * act_ref[:, column : column + HCHUNK].astype(f32)
        ).astype(bf16)
    db = dot_nt(dh_ref[...], w_in_ref[...])
    unit, scale = normalize(x1_ref[...])
    back, terms = norm_back(unit, scale, gain_ref[...], db)
    dgain_ref[...] += jnp.sum(terms, axis=0, keepdims=True)
    dx1 = dy.astype(f32) + back
    dx1_ref[...] = dx1
    return dx1.astype(bf16)


def attend_back_pair(q_ref, k_ref, v_ref, o_ref, inv_ref, do, p_ref, cos_ref, sin_ref, dq_ref, dk_ref, dv_ref):
    v = v_ref[...]
    length = v.shape[0]
    mine = head_lanes()
    zero = jnp.zeros((), bf16)
    do = (do.astype(f32) * inv_ref[...]).astype(bf16)
    inner = do.astype(f32) * o_ref[...].astype(f32)
    do_heads = [jnp.where(m, do, zero) for m in mine]
    q_heads = [jnp.where(m, q_ref[...], zero).T for m in mine]
    k_heads = [jnp.where(m, k_ref[...], zero) for m in mine]
    do_turned = [d.T for d in do_heads]
    cosine, sine = cos_ref[...], sin_ref[...]
    dv = dk = None
    for tile in range(0, length, TILE):
        rows = slice(tile, tile + TILE)
        dq = None
        for head in range(2):
            probs = p_ref[head, rows, :]
            delta = jnp.sum(jnp.where(mine[head], inner[rows], 0.0), axis=-1, keepdims=True)
            dp = dot_nt(do_heads[head][rows], v)
            ds = (probs.astype(f32) * (dp - delta)).astype(bf16)
            value_part = dot_nn(do_turned[head][:, rows], probs)
            key_part = dot_nn(q_heads[head][:, rows], ds)
            query_part = dot_nn(ds, k_heads[head])
            dv = value_part if dv is None else dv + value_part
            dk = key_part if dk is None else dk + key_part
            dq = query_part if dq is None else dq + query_part
        dq_ref[rows, :] = rotate_pair(dq * HDIM**-0.5, cosine[rows], -sine[rows]).astype(bf16)
    dk_ref[...] = rotate_pair(dk.T * math.log(2.0), cosine, -sine).astype(bf16)
    dv_ref[...] = dv.T.astype(bf16)


def backward_kernel(
    sizes, tiles, x1_ref, slope_ref, act_ref, gain_ref, q_ref, k_ref, v_ref, o_ref, inv_ref, p_ref, cos_ref, sin_ref,
    w_out_any, w_in_any, w_mlp_any, m_any, dy_any, b_any, o_any, y_ref, *refs,
):
    reducers, early = early_reducers(sizes)
    count = len(reducers)
    refs = list(refs)
    pop = lambda n: [refs.pop(0) for _ in range(n)]
    dx1_ref, dgain_ref, dq_ref, dk_ref, dv_ref, home_ref = pop(6)
    sums_out = pop(count)
    w_out_ref, w_in_ref, w_mlp_ref, m_ref, dy_ref, b_ref, all_o_ref = pop(7)
    dh_ref, low_ref, do_ref, wide, bounce = pop(5)
    grads = pop(count)
    lands = [pop(len(r.scratch(0, e))) for r, e in zip(reducers, early)]
    sems = Sems(*refs)
    me = lax.axis_index("fsdp")
    step, last = pl.program_id(0), pl.num_programs(0) - 1
    into, outof, blocks = give_back(y_ref, home_ref, bounce, sems)
    loads = [
        sems.copy(src, dst)
        for src, dst in [
            (m_any, m_ref), (dy_any, dy_ref), (w_mlp_any, w_mlp_ref), (w_in_any, w_in_ref), (w_out_any, w_out_ref),
            (b_any, b_ref), (o_any, all_o_ref),
        ]
    ]
    stores = [sems.copy(grads[w].at[me], sums_out[w]) for w in range(count)]
    for w, reducer in enumerate(reducers):
        reducer.bind(lambda j, w=w: grads[w].at[flip(me, j)], lands[w], sems, 0, early[w])
    mlp, first_half, second_half, out = reducers

    def at(when, *actions):
        @pl.when(step == when)
        def _():
            for action in actions:
                action()

    def advance(reducer, s, limit):
        def run():
            reducer.finish(s)
            if s + 1 < limit:
                reducer.start(s + 1)
        return run

    @pl.when(step == 0)
    def _():
        start_all(loads)
        into.start()
        meet(all_partners(sizes))
        start_all(blocks)
        dgain_ref[...] = jnp.zeros_like(dgain_ref)
        wait_all(loads[:2])
        spread(grads[0], wide, dot_tn(m_ref[...], dy_ref[...]))
        mlp.start(0)
        into.wait()
        outof.start()
        wait_all(loads[2:5])

    at(1, advance(mlp, 0, early[0]))

    @pl.when(step < tiles)
    def _():
        rows = pl.ds(pl.multiple_of(step * TILE, TILE), TILE)
        low = middle_back_tile(
            dy_ref[rows, :], x1_ref, slope_ref, act_ref, gain_ref, w_out_ref, w_in_ref, w_mlp_ref,
            dh_ref.at[rows, :], dgain_ref, dx1_ref,
        )
        low_ref[rows, :] = low
        do_ref[rows, :] = dot_nt(low, w_out_ref[...]).astype(bf16)

    across = len(bits_of(sizes[0])) + len(bits_of(sizes[1]))

    @pl.when(step == tiles)
    def _():
        wait_all(loads[5:])
        spread(grads[1], wide, dot_tn(b_ref[...], dh_ref[:, :FF]))
        first_half.start(0)
        spread(grads[2], wide, dot_tn(b_ref[...], dh_ref[:, FF:]))
        second_half.start(0)
        for s in range(1, across - 1):
            advance(mlp, s, early[0])()
        spread(grads[3], wide, dot_tn(all_o_ref[...], low_ref[...]))
        out.start(0)

    last_pair = tiles + 6
    at(tiles + 1, *[advance(r, 0, e) for r, e in zip(reducers[1:], early[1:])])
    at(tiles + 2, advance(mlp, across - 1, early[0]))
    at(tiles + 4, *[advance(r, s, early[1]) for s in range(1, across - 1) for r in (first_half, second_half)])
    at(last_pair - 1, advance(out, 1, early[3]), advance(mlp, across, early[0]))
    at(
        last_pair,
        *[advance(out, s, early[3]) for s in range(2, across - 1)],
        *[advance(r, across - 1, early[1]) for r in (first_half, second_half)],
        *[advance(mlp, s, early[0]) for s in range(across + 1, early[0] - 1)],
        advance(out, across - 1, early[3]),
    )

    @pl.when(step > tiles)
    def _():
        column = pl.multiple_of((step - tiles - 1) * PAIR, PAIR)
        attend_back_pair(
            q_ref, k_ref, v_ref, o_ref, inv_ref, do_ref[:, pl.ds(column, PAIR)], p_ref, cos_ref, sin_ref,
            dq_ref, dk_ref, dv_ref,
        )

    @pl.when(step == last)
    def _():
        for w, reducer in enumerate(reducers):
            reducer.finish(early[w] - 1)
            stores[w].start()
        wait_all(stores)
        outof.wait()
        wait_all(blocks)


def leave_kernel(
    sizes, gain_ref, other_gain_ref, dx1_ref, x_ref, dq_ref, dk_ref, dv_ref, a_ref, w_ref, *refs
):
    fsdp, rep, seq = sizes
    reducers, early = early_reducers(sizes)
    whole = late_reducers(sizes)
    count, more = len(reducers), len(whole)
    refs = list(refs)
    pop = lambda n: [refs.pop(0) for _ in range(n)]
    sums_in = pop(count)
    (home_ref,) = pop(1)
    sums_out, wholes_out = pop(count), pop(more)
    (gains_out,) = pop(1)
    slots, wide = pop(2)
    held, grads, finals = pop(count), pop(more), pop(count + more)
    lands = [pop(len(r.scratch(e, len(r.steps)))) for r, e in zip(reducers, early)]
    whole_lands = [pop(len(r.scratch(0, len(r.steps)))) for r in whole]
    (gain_lands,) = pop(1)
    sems = Sems(*refs)
    me, me_seq = lax.axis_index("fsdp"), lax.axis_index("seq")
    own = sems.copy(slots.at[0], home_ref.at[me_seq])
    half = slots.shape[1] // 2
    blocks = {
        k: [
            sems.remote(slots.at[k, pl.ds(n * half, half)], home_ref.at[me_seq, pl.ds(n * half, half)], "seq", k)
            for n in range(2)
        ]
        for k in range(1, seq)
    }
    loads = [sems.copy(sums_in[w], held[w]) for w in range(count)]
    stores = [sems.copy(finals[w], out) for w, out in enumerate(sums_out + wholes_out)]
    for w, reducer in enumerate(reducers):
        reducer.bind(lambda j, w=w: held[w], lands[w], sems, early[w], len(reducer.steps), finals[w])
    for w, reducer in enumerate(whole):
        reducer.bind(
            lambda j, w=w: grads[w].at[flip(me, j)], whole_lands[w], sems, 0, len(reducer.steps), finals[count + w]
        )
    hops = [("fsdp", b) for b in bits_of(fsdp)] + [("rep", b) for b in bits_of(rep)] + [("seq", b) for b in bits_of(seq)]
    gain_moves = [sems.remote(gains_out, gain_lands.at[i], axis, bit) for i, (axis, bit) in enumerate(hops)]
    rows = slots.shape[1]

    def advance(some, s):
        for reducer in some:
            if s < len(reducer.steps):
                reducer.finish(s)
                if s + 1 < len(reducer.steps):
                    reducer.start(s + 1)

    def advance_gains(i):
        gain_moves[i].wait()
        gains_out[...] += gain_lands[i]
        if i + 1 < len(hops):
            gain_moves[i + 1].start()

    def input_slot(k):
        piece = slice(k * rows, (k + 1) * rows)
        da = dot_nt(dq_ref[piece, :], w_ref[:, :D])
        da = da + dot_nt(dk_ref[piece, :], w_ref[:, D : 2 * D])
        da = da + dot_nt(dv_ref[piece, :], w_ref[:, 2 * D :])
        unit, scale = normalize(x_ref[piece, :].astype(f32))
        back, terms = norm_back(unit, scale, gain_ref[...], da)
        gains_out[0:1, :] += jnp.sum(terms, axis=0, keepdims=True)
        slots[k] = (dx1_ref[piece, :] + back).astype(bf16)

    across = len(bits_of(fsdp)) + len(bits_of(rep))
    order = sorted(range(1, seq), key=lambda k: (k != 2, k == 1))
    far = [copy for k in order for copy in blocks[k]]
    late_blocks = far[2:]

    gains_out[...] = jnp.zeros_like(gains_out)
    gains_out[1:2, :] = other_gain_ref[...]
    start_all(loads)
    meet(all_partners(sizes))
    wait_all(loads)
    mlp = reducers[:1]
    others = reducers[1:]
    for reducer, e in zip(reducers, early):
        reducer.start(e)
    for w, part in enumerate((dq_ref, dk_ref, dv_ref)):
        spread(grads[w], wide, dot_tn(a_ref[...], part[...]))
        whole[w].start(0)
        if w < len(order):
            input_slot(order[w])
        if w == 0:
            start_all(blocks[order[0]])
        advance(whole[w : w + 1], 0)
        if w == 1:
            advance(mlp, early[0])
            advance(others, early[1])
    for k in order[3:] + [0]:
        input_slot(k)
    own.start()
    gain_moves[0].start()
    for s in range(1, across):
        advance(whole, s)
        advance_gains(s - 1)
        if late_blocks and s == across - 1:
            late_blocks.pop(0).start()
    for s in range(early[1] + 1, len(others[0].steps) - 1):
        advance(others, s)
    for s in range(across, len(whole[0].steps)):
        advance(whole, s)
        if late_blocks:
            late_blocks.pop(0).start()
        if across - 2 + s - across + 1 < len(hops):
            advance_gains(across - 1 + s - across)
    for i in range(len(whole[0].steps) - 1, len(hops)):
        advance_gains(i)
    start_all(late_blocks)
    for reducer, e in zip(reducers, early):
        for s in range(e + 1, len(reducer.steps)):
            if reducer in mlp or s == len(reducer.steps) - 1:
                advance([reducer], s)
    start_all(stores)
    wait_all(stores)
    own.wait()
    for k in range(1, seq):
        wait_all(blocks[k])


def rows_spec(width):
    return pl.BlockSpec((TILE, width), lambda i: (i, 0))


def whole_spec(*shape):
    return pl.BlockSpec(shape, lambda i: (0,) * len(shape))


def pair_spec(length, offset=0):
    return pl.BlockSpec((length, PAIR), lambda i: (0, i + offset))


def struct(dtype, *shape):
    return jax.ShapeDtypeStruct(shape, dtype)


def call(kernel, grid, in_specs, out_specs, out_shape, flops, scratch=(), collective=None):
    return pl.pallas_call(
        kernel,
        grid=(grid,),
        in_specs=in_specs,
        out_specs=out_specs,
        out_shape=out_shape,
        scratch_shapes=list(scratch),
        compiler_params=pltpu.CompilerParams(
            dimension_semantics=("arbitrary",), vmem_limit_bytes=VMEM_LIMIT,
            collective_id=collective, has_side_effects=collective is not None,
        ),
        cost_estimate=pl.CostEstimate(flops=flops, bytes_accessed=10 * 2**20, transcendentals=0),
    )


MESH = pl.DeviceIdType.MESH
ANY = pl.BlockSpec(memory_space=pl.ANY)


def take(array, index):
    return lax.dynamic_index_in_dim(array, index, 0, keepdims=False)


def flip(index, mask):
    bit = 1
    while bit <= mask:
        if mask & bit:
            index = index + bit - 2 * bit * ((index // bit) % 2)
        bit *= 2
    return index


def bits_of(size):
    return [1 << i for i in range(size.bit_length() - 1)]


def meet(partners):
    barrier = pltpu.get_barrier_semaphore()
    for axis, mask in partners:
        pl.semaphore_signal(
            barrier, inc=1, device_id={axis: flip(lax.axis_index(axis), mask)}, device_id_type=MESH
        )
    pl.semaphore_wait(barrier, len(partners))


class Sems:
    def __init__(self, send, recv, local):
        self.send, self.recv, self.local = send, recv, local
        self.remote_used = self.local_used = 0

    def remote(self, src, dst, axis, mask):
        i = self.remote_used
        self.remote_used += 1
        return pltpu.make_async_remote_copy(
            src_ref=src, dst_ref=dst, send_sem=self.send.at[i], recv_sem=self.recv.at[i],
            device_id={axis: flip(lax.axis_index(axis), mask)}, device_id_type=MESH,
        )

    def copy(self, src, dst):
        i = self.local_used
        self.local_used += 1
        return pltpu.make_async_copy(src, dst, self.local.at[i])


def sem_shapes(remote, local):
    dma = pltpu.SemaphoreType.DMA
    return [dma((remote,)), dma((remote,)), dma((max(local, 1),))]


def start_all(copies):
    for copy in copies:
        copy.start()


def wait_all(copies):
    for copy in copies:
        copy.wait()


def enter_kernel(sizes, count, *refs):
    fsdp, rep, seq = sizes
    tokens, shards = refs[0], refs[1 : 1 + count]
    x_out, fulls = refs[1 + count], refs[2 + count : 2 + 2 * count]
    bounce_x, bounces = refs[2 + 2 * count], refs[3 + 2 * count : 3 + 3 * count]
    sems = Sems(*refs[3 + 3 * count :])
    me, me_seq, me_rep = lax.axis_index("fsdp"), lax.axis_index("seq"), lax.axis_index("rep")
    into = [sems.copy(tokens.at[me_seq], bounce_x)] + [sems.copy(shards[w], bounces[w]) for w in range(count)]
    outof = [sems.copy(bounce_x, x_out.at[0])] + [sems.copy(bounces[w], fulls[w].at[me]) for w in range(count)]
    start_all(into)
    meet([("seq", k) for k in range(1, seq)] + [("fsdp", b) for b in bits_of(fsdp)] + [("rep", b) for b in bits_of(rep)])
    blocks = [sems.remote(tokens.at[flip(me_seq, k)], x_out.at[k], "seq", k) for k in range(1, seq)]
    start_all(blocks)

    def piece(ref, w, index):
        width = shards[w].shape[-1] // rep
        return ref.at[index, :, pl.ds(pl.multiple_of(me_rep * width, 128), width)]

    def first_piece(w):
        width = shards[w].shape[-1] // rep
        return shards[w].at[:, pl.ds(pl.multiple_of(me_rep * width, 128), width)]

    held = [0]
    pending = []
    for bit in reversed(bits_of(fsdp)[1:]):
        over = []
        for w in range(count):
            moved = []
            for h in held:
                src = first_piece(w) if h == 0 else piece(fulls[w], w, flip(me, h))
                moved.append(sems.remote(src, piece(fulls[w], w, flip(me, h)), "fsdp", bit))
            start_all(moved)
            over.append(moved)
        relays = []
        for w in range(count):
            for copy in over[w]:
                copy.wait_recv()
            moved = []
            for mask in range(1, rep):
                for h in held:
                    here = piece(fulls[w], w, flip(me, h ^ bit))
                    moved.append(sems.remote(here, here, "rep", mask))
            start_all(moved)
            relays.append(moved)
            pending += over[w]
        for moved in relays:
            for copy in moved:
                copy.wait_recv()
            pending += moved
        held = held + [h ^ bit for h in held]
    last = []
    for w in range(count):
        for h in held:
            src = shards[w] if h == 0 else fulls[w].at[flip(me, h)]
            last.append(sems.remote(src, fulls[w].at[flip(me, h)], "fsdp", 1))
    start_all(last)
    wait_all(into)
    start_all(outof)
    for copy in pending:
        copy.wait_send()
    wait_all(last)
    wait_all(blocks)
    wait_all(outof)


def enter(sizes, tokens, shards):
    fsdp, rep, seq = sizes
    count = len(shards)
    assert fsdp >= 2
    held, copies = 1, seq - 1
    for _ in bits_of(fsdp)[1:]:
        copies += count * held * rep
        held *= 2
    copies += count * held
    hbm = lambda shape: struct(bf16, *shape)
    return pl.pallas_call(
        functools.partial(enter_kernel, sizes, count),
        in_specs=[ANY] * (1 + count),
        out_specs=[ANY] * (1 + count),
        out_shape=[hbm(tokens.shape)] + [hbm((fsdp,) + s.shape) for s in shards],
        scratch_shapes=[pltpu.VMEM(tokens.shape[1:], bf16)]
        + [pltpu.VMEM(s.shape, bf16) for s in shards]
        + sem_shapes(copies, 2 * (1 + count)),
        compiler_params=pltpu.CompilerParams(collective_id=0, has_side_effects=True),
    )(tokens, *shards)


class Reducer:
    def __init__(self, parts_shape, sizes, order):
        self.fsdp, self.rows, self.cols = parts_shape
        self.steps = []
        held, rows, cols = list(range(self.fsdp)), self.rows, self.cols
        row_at, col_at = [], []
        for axis, bit in order:
            step = dict(axis=axis, bit=bit, row_at=list(row_at), col_at=list(col_at), rows=rows, cols=cols)
            if axis == "fsdp":
                step["send"] = [j for j in held if j & bit]
                held = [j for j in held if not j & bit]
                step["keep"] = held
                step["shape"] = (len(held), rows, cols)
                step["split"] = None
            else:
                step["keep"] = step["send"] = held
                if (axis, bit) == order[-1]:
                    step["split"] = "none"
                elif (rows // 2) % 16 == 0:
                    rows //= 2
                    row_at = row_at + [(axis, bit, rows)]
                    step["split"] = "rows"
                elif (cols // 2) % 128 == 0:
                    cols //= 2
                    col_at = col_at + [(axis, bit, cols)]
                    step["split"] = "cols"
                else:
                    step["split"] = "none"
                step["shape"] = (len(held), rows, cols)
            self.steps.append(step)
        self.down = len(self.steps)
        for step in reversed(self.steps[: self.down]):
            if step["split"] in ("rows", "cols"):
                self.steps.append(dict(step, up=True))

    @staticmethod
    def offset(terms, align, last=None):
        total = 0
        for i, (axis, bit, extent) in enumerate(terms):
            half = (lax.axis_index(axis) // bit) % 2
            if last == i:
                half = 1 - half
            total = total + half * extent
        return total if isinstance(total, int) else pl.multiple_of(total, align)

    def region(self, step, after, other=False):
        row_at, col_at, rows, cols = step["row_at"], step["col_at"], step["rows"], step["cols"]
        row_last = col_last = None
        if after:
            if step["split"] == "rows":
                rows //= 2
                row_at = row_at + [(step["axis"], step["bit"], rows)]
                row_last = len(row_at) - 1 if other else None
            elif step["split"] == "cols":
                cols //= 2
                col_at = col_at + [(step["axis"], step["bit"], cols)]
                col_last = len(col_at) - 1 if other else None
        return (
            pl.ds(self.offset(row_at, 16, row_last), rows),
            pl.ds(self.offset(col_at, 128, col_last), cols),
        )

    def scratch(self, first, last):
        return [pltpu.VMEM(s["shape"], bf16) for s in self.steps[first:last] if "up" not in s]

    def copies(self, first, last):
        return sum(1 if "up" in s else len(s["send"]) for s in self.steps[first:last])

    def bind(self, parts, lands, sems, first, last, final=None):
        self.parts, self.sems, self.final = parts, sems, final
        self.lands, self.moves = {}, {}
        lands = list(lands)
        for s in range(first, last):
            step = self.steps[s]
            moves = []
            if "up" in step:
                there = final.at[self.region(step, True)]
                moves.append(sems.remote(there, there, step["axis"], step["bit"]))
            else:
                land = self.lands[s] = lands.pop(0)
                for i, j in enumerate(step["send"]):
                    fsdp = step["axis"] == "fsdp"
                    src = self.parts(j).at[self.region(step, not fsdp, not fsdp)]
                    moves.append(sems.remote(src, land.at[i], step["axis"], step["bit"]))
            self.moves[s] = moves

    def start(self, s):
        if s == self.down:
            region = self.region(self.steps[s - 1], True)
            self.final[region] = self.parts(0)[region]
        start_all(self.moves[s])

    def finish(self, s):
        step = self.steps[s]
        for i, move in enumerate(self.moves[s]):
            move.wait()
            if "up" not in step:
                j = step["keep"][i]
                ref = self.parts(j)
                region = self.region(step, True)
                ref[region] = (ref[region].astype(f32) + self.lands[s][i].astype(f32)).astype(bf16)


def give_back(slots, home, bounce, sems):
    me = lax.axis_index("seq")
    seq = slots.shape[0]
    return (
        sems.copy(slots.at[0], bounce),
        sems.copy(bounce, home.at[me]),
        [sems.remote(slots.at[k], home.at[me], "seq", k) for k in range(1, seq)],
    )


def body(sizes, tokens, segments, positions, gain_attn, w_qkv, w_out, gain_mlp, w_in, w_mlp_out, cotangent):
    fsdp, rep, seq = sizes
    micro, batch, rows, _ = tokens.shape
    assert micro * batch == seq and rows % TILE == 0
    length = seq * rows
    me_seq, me_fsdp = lax.axis_index("seq"), lax.axis_index("fsdp")

    own_gains = jnp.zeros((16, D), bf16)
    own_gains = lax.dynamic_update_slice(own_gains, jnp.stack([gain_attn, gain_mlp]), (0, me_fsdp * (D // fsdp)))
    x, gains, wq, wo, wm, wi = enter(
        sizes, tokens.reshape(seq, rows, D), [own_gains, w_qkv, w_out, w_mlp_out, w_in]
    )
    x = x.reshape(length, D)
    gains = jnp.sum(gains[:, :2].astype(f32), axis=0)
    gain_one, gain_two = gains[:1], gains[1:]
    wq, wo, wm, wi = (w.reshape(-1, w.shape[-1]) for w in (wq, wo, wm, wi))

    marks = take(segments.reshape(seq, length), me_seq)
    place = jnp.arange(length, dtype=jnp.int32) - jnp.sum(
        (marks[None, :] < marks[:, None]).astype(jnp.int32), axis=1
    )
    slot_order = [me_seq ^ k for k in range(seq)]
    marks = jnp.concatenate([take(marks.reshape(seq, rows), s) for s in slot_order])
    place = jnp.concatenate([take(place.reshape(seq, rows), s) for s in slot_order])
    half = jnp.arange(0, HDIM, 2).astype(f32) / HDIM
    angles = place.astype(f32)[:, None] * jnp.exp(-half * math.log(THETA))
    cosine, sine = jnp.cos(angles), jnp.sin(angles)
    cosine = jnp.concatenate([cosine] * 4, -1)
    sine = jnp.concatenate([-sine, sine] * 2, -1)

    tiles, pairs = length // TILE, HEADS // 2
    a, qkv = call(
        first_kernel, tiles,
        [rows_spec(D), whole_spec(1, D), whole_spec(D, 3 * D), rows_spec(PAIR), rows_spec(PAIR)],
        [rows_spec(D), rows_spec(3 * D)],
        [struct(bf16, length, D), struct(bf16, length, 3 * D)],
        2 * length * D * 3 * D,
    )(x, gain_one, wq, cosine, sine)

    vmem = pl.BlockSpec(memory_space=pltpu.VMEM)
    pair_at = lambda offset, lag, n: pl.BlockSpec(
        (length, PAIR), lambda i: (0, jnp.clip(i - lag, 0, n - 1) + offset)
    )
    prob_at = lambda lag: pl.BlockSpec((2, length, length), lambda i: (jnp.clip(i - lag, 0, pairs - 1), 0, 0))
    tile_at = lambda width, lag: pl.BlockSpec((TILE, width), lambda i: (jnp.clip(i - lag, 0, tiles - 1), 0))
    slots = struct(bf16, seq, rows, D)
    o, probs, inv, x1, b, m, slope, act, y, dy = call(
        functools.partial(forward_kernel, sizes, pairs), pairs + tiles,
        [pair_at(0, 0, pairs), pair_at(pairs, 0, pairs), pair_at(2 * pairs, 0, pairs),
         whole_spec(length, 1), whole_spec(1, length), tile_at(D, pairs), whole_spec(1, D)] + [ANY] * 4,
        [pair_at(0, 0, pairs), prob_at(0), pair_at(0, 0, pairs), tile_at(D, pairs), tile_at(D, pairs)]
        + [tile_at(FF, pairs)] * 3 + [tile_at(D, pairs), ANY],
        [struct(bf16, length, D), struct(bf16, HEADS, length, length), struct(f32, length, D),
         struct(f32, length, D), struct(bf16, length, D), struct(bf16, length, FF),
         struct(bf16, length, FF), struct(bf16, length, FF), struct(bf16, length, D), slots],
        16 * length * length * D,
        [pltpu.VMEM((length, D), bf16), pltpu.VMEM((D, D), bf16), pltpu.VMEM((D, 2 * FF), bf16), pltpu.VMEM((FF, D), bf16),
         pltpu.VMEM((rows, D), bf16)] + sem_shapes(seq - 1, 5), 1,
    )(qkv, qkv, qkv, marks[:, None], marks[None, :], x, gain_two, wo, wi, wm, cotangent.reshape(seq, rows, D))

    reducers, early = early_reducers(sizes)
    whole = late_reducers(sizes)
    own_shard = lambda r: struct(bf16, r.rows, r.cols)
    full_shard = lambda r: pltpu.VMEM((fsdp, r.rows, r.cols), bf16)
    odd = (FF // fsdp) % 16 or (D // fsdp) % 16
    wide = pltpu.VMEM((FF, FF) if odd else (8, 128), f32)
    dx1, dgain_two, dq, dk, dv, block_out, *sums = call(
        functools.partial(backward_kernel, sizes, tiles), tiles + 1 + pairs,
        [tile_at(D, 0), tile_at(FF, 0), tile_at(FF, 0), whole_spec(1, D)]
        + [pair_at(n * pairs, tiles + 1, pairs) for n in range(3)]
        + [pair_at(0, tiles + 1, pairs), pair_at(0, tiles + 1, pairs), prob_at(tiles + 1),
           whole_spec(length, PAIR), whole_spec(length, PAIR)] + [ANY] * 8,
        [tile_at(D, 0), whole_spec(1, D)] + [pair_at(0, tiles + 1, pairs)] * 3 + [ANY] * (1 + len(reducers)),
        [struct(f32, length, D), struct(f32, 1, D)] + [struct(bf16, length, D)] * 3 + [slots]
        + [own_shard(r) for r in reducers],
        32 * length * length * D,
        [pltpu.VMEM((D, D), bf16), pltpu.VMEM((D, 2 * FF), bf16), pltpu.VMEM((FF, D), bf16),
         pltpu.VMEM((length, FF), bf16)] + [pltpu.VMEM((length, D), bf16)] * 3
        + [pltpu.VMEM((length, 2 * FF), bf16), pltpu.VMEM((length, D), bf16), pltpu.VMEM((length, D), bf16),
           wide, pltpu.VMEM((rows, D), bf16)]
        + [full_shard(r) for r in reducers]
        + [land for r, e in zip(reducers, early) for land in r.scratch(0, e)]
        + sem_shapes(seq - 1 + sum(r.copies(0, e) for r, e in zip(reducers, early)), 9 + len(reducers)), 2,
    )(x1, slope, act, gain_two, qkv, qkv, qkv, o, inv, probs, cosine, sine,
      wo, wi, wm, m, dy.reshape(length, D), b, o, y.reshape(seq, rows, D))

    hops = sum(len(bits_of(n)) for n in sizes)
    input_grad, *results, dgains = pl.pallas_call(
        functools.partial(leave_kernel, sizes),
        in_specs=[vmem] * 9 + [ANY] * len(reducers),
        out_specs=[ANY] * (1 + len(reducers + whole)) + [vmem],
        out_shape=[slots] + [own_shard(r) for r in reducers + whole] + [struct(f32, 8, D)],
        scratch_shapes=[pltpu.VMEM((seq, rows, D), bf16), wide]
        + [pltpu.VMEM((r.rows, r.cols), bf16) for r in reducers]
        + [full_shard(r) for r in whole]
        + [pltpu.VMEM((r.rows, r.cols), bf16) for r in reducers + whole]
        + [land for r, e in zip(reducers, early) for land in r.scratch(e, len(r.steps))]
        + [land for r in whole for land in r.scratch(0, len(r.steps))]
        + [pltpu.VMEM((hops, 8, D), f32)]
        + sem_shapes(
            2 * (seq - 1) + hops + sum(r.copies(e, len(r.steps)) for r, e in zip(reducers, early))
            + sum(r.copies(0, len(r.steps)) for r in whole),
            1 + 2 * len(reducers) + len(whole),
        ),
        compiler_params=pltpu.CompilerParams(
            collective_id=3, has_side_effects=True, vmem_limit_bytes=VMEM_LIMIT
        ),
    )(gain_one, dgain_two, dx1, x, dq, dk, dv, a, wq, *sums)
    dgains = lax.dynamic_slice_in_dim(dgains, me_fsdp * (D // fsdp), D // fsdp, 1)
    grad_mlp, grad_in, grad_gate, grad_out, grad_q, grad_k, grad_v = (r.astype(f32) for r in results)
    return (
        block_out.reshape(tokens.shape),
        input_grad.astype(f32).reshape(tokens.shape),
        dgains[0],
        jnp.concatenate([grad_q, grad_k, grad_v], 1),
        grad_out,
        dgains[1],
        jnp.concatenate([grad_in, grad_gate], 1),
        grad_mlp,
    )


def solution(mesh):
    sizes = (mesh.shape["fsdp"], mesh.shape["rep"], mesh.shape["seq"])
    wide = P(None, ("rep", "fsdp"), "seq", None)
    placed = (
        wide, P(None, ("rep", "fsdp"), None), P(None, ("rep", "fsdp"), "seq"),
        P("fsdp"), P("fsdp", None), P("fsdp", None), P("fsdp"), P("fsdp", None), P("fsdp", None), wide,
    )
    return jax.shard_map(
        functools.partial(body, sizes),
        mesh=mesh,
        in_specs=placed,
        out_specs=(
            wide, wide, P("fsdp"), P("fsdp", None), P("fsdp", None), P("fsdp"), P("fsdp", None), P("fsdp", None),
        ),
        check_vma=False,
    )
```

```python
import functools
import math

import jax
import jax.numpy as jnp
from jax import lax
from jax.experimental import pallas as pl
from jax.experimental.pallas import tpu as pltpu
from jax.sharding import PartitionSpec as P

D = 768
HEADS = 12
HDIM = 64
FF = 1152
EPS = 1e-05
THETA = 160000.0
MASKED = -1000000000.0
QUERY_SCALE = HDIM**-0.5 / math.log(2.0)
TILE = 256
PAIR = 2 * HDIM
HCHUNK = 384
f32 = jnp.float32
bf16 = jnp.bfloat16
VMEM_LIMIT = 62 * 2**20


def dot_nn(left, right):
    return lax.dot_general(left, right, (((1,), (0,)), ((), ())), preferred_element_type=f32)


def dot_nt(left, right):
    return lax.dot_general(left, right, (((1,), (1,)), ((), ())), preferred_element_type=f32)


def dot_tn(left, right):
    return lax.dot_general(left, right, (((0,), (0,)), ((), ())), preferred_element_type=f32)


def normalize(values):
    mean = jnp.mean(values, axis=-1, keepdims=True)
    centered = values - mean
    var = jnp.mean(centered * centered, axis=-1, keepdims=True)
    scale = lax.rsqrt(var + EPS)
    return centered * scale, scale


def norm_back(unit, scale, gain, grad):
    gain_terms = grad * unit
    inner = grad * gain
    first = jnp.mean(inner, axis=-1, keepdims=True)
    second = jnp.mean(inner * unit, axis=-1, keepdims=True)
    return scale * (inner - first - unit * second), gain_terms


def lane_halves(shape):
    lane = lax.broadcasted_iota(jnp.int32, shape, len(shape) - 1)
    return lane % HDIM < HDIM // 2


def rotate_pair(values, cosine, signed_sine):
    swapped = jnp.where(
        lane_halves(values.shape),
        pltpu.roll(values, PAIR - HDIM // 2, 1),
        pltpu.roll(values, HDIM // 2, 1),
    )
    return values * cosine + swapped * signed_sine


def first_kernel(x_ref, gain_ref, w_ref, cos_ref, sin_ref, a_ref, qkv_ref):
    unit, _ = normalize(x_ref[...].astype(f32))
    a = (unit * gain_ref[...]).astype(bf16)
    a_ref[...] = a
    cosine, sine = cos_ref[...], sin_ref[...]
    for column in range(0, 3 * D, TILE):
        part = dot_nn(a, w_ref[:, column : column + TILE])
        for half in range(0, TILE, PAIR):
            start = column + half
            piece = part[:, half : half + PAIR]
            if start < 2 * D:
                piece = rotate_pair(piece, cosine, sine)
            if start < D:
                piece = piece * QUERY_SCALE
            qkv_ref[:, start : start + PAIR] = piece.astype(bf16)


def head_lanes():
    lane = lax.broadcasted_iota(jnp.int32, (1, PAIR), 1)
    return [lane < HDIM, lane >= HDIM]


def attend_pair(q_ref, k_ref, v_ref, rows_ref, cols_ref, p_ref, inv_ref, write):
    k, v = k_ref[...], v_ref[...]
    length = k.shape[0]
    mine = head_lanes()
    zero, one = jnp.zeros((), bf16), jnp.ones((), bf16)
    summing = [jnp.where(m, v, one) for m in mine]
    items = [(tile, head) for tile in range(0, length, TILE) for head in range(2)]

    def score(item):
        tile, head = item
        return dot_nt(jnp.where(mine[head], q_ref[tile : tile + TILE, :], zero), k)

    ahead = score(items[0])
    kept = None
    for i, (tile, head) in enumerate(items):
        rows = slice(tile, tile + TILE)
        scores = ahead
        if i + 1 < len(items):
            ahead = score(items[i + 1])
        scores = jnp.where(rows_ref[rows, :] == cols_ref[...], scores, MASKED)
        probs = jnp.exp2(scores - jnp.max(scores, axis=-1, keepdims=True)).astype(bf16)
        p_ref[head, rows, :] = probs
        part = dot_nn(probs, summing[head])
        inv = 1.0 / pltpu.roll(part, HDIM, 1)
        if head == 0:
            kept = (part * inv, inv)
        else:
            inv_ref[rows, :] = jnp.where(mine[0], kept[1], inv)
            write(rows, jnp.where(mine[0], kept[0], part * inv).astype(bf16))


def forward_kernel(
    sizes, pairs, q_ref, k_ref, v_ref, rows_ref, cols_ref, x_ref, gain_ref, w_out_any, w_in_any, w_mlp_any, cot_ref,
    o_ref, p_ref, inv_ref, x1_ref, b_ref, m_ref, slope_ref, act_ref, y_ref, dy_ref,
    joined, w_out_ref, w_in_ref, w_mlp_ref, bounce, *sem_refs,
):
    seq = sizes[2]
    step, last = pl.program_id(0), pl.num_programs(0) - 1
    sems = Sems(*sem_refs)
    me_seq = lax.axis_index("seq")
    into = sems.copy(cot_ref.at[me_seq], bounce)
    outof = sems.copy(bounce, dy_ref.at[0])
    weights = [sems.copy(w_out_any, w_out_ref), sems.copy(w_in_any, w_in_ref), sems.copy(w_mlp_any, w_mlp_ref)]
    blocks = [sems.remote(cot_ref.at[flip(me_seq, k)], dy_ref.at[k], "seq", k) for k in range(1, seq)]

    @pl.when(step == 0)
    def _():
        into.start()
        start_all(weights)
        meet([("seq", k) for k in range(1, seq)])
        start_all(blocks)
        into.wait()
        outof.start()

    @pl.when(step < pairs)
    def _():
        def write(rows, value):
            o_ref[rows, :] = value
            joined[rows, pl.ds(pl.multiple_of(step * PAIR, PAIR), PAIR)] = value

        attend_pair(q_ref, k_ref, v_ref, rows_ref, cols_ref, p_ref, inv_ref, write)

    @pl.when(step == pairs)
    def _():
        wait_all(weights)

    @pl.when(step >= pairs)
    def _():
        start = pl.multiple_of((step - pairs) * TILE, TILE)
        x1 = x_ref[...].astype(f32) + dot_nn(joined[pl.ds(start, TILE), :], w_out_ref[...])
        x1_ref[...] = x1
        unit, _ = normalize(x1)
        b = (unit * gain_ref[...]).astype(bf16)
        b_ref[...] = b

        def hidden(column):
            return (
                dot_nn(b, w_in_ref[:, column : column + HCHUNK]),
                dot_nn(b, w_in_ref[:, FF + column : FF + column + HCHUNK]),
            )

        ahead = hidden(0)
        for column in range(0, FF, HCHUNK):
            hin, gate = ahead
            if column + HCHUNK < FF:
                ahead = hidden(column + HCHUNK)
            phi = 0.5 + 0.5 * lax.erf(hin * math.sqrt(0.5))
            act = hin * phi
            slope = phi + hin * (jnp.exp(hin * hin * -0.5) * (1.0 / math.sqrt(2.0 * math.pi)))
            m_ref[:, column : column + HCHUNK] = (act * gate).astype(bf16)
            act_ref[:, column : column + HCHUNK] = act.astype(bf16)
            slope_ref[:, column : column + HCHUNK] = (slope * gate).astype(bf16)
        y_ref[...] = (x1 + dot_nn(m_ref[...], w_mlp_ref[...])).astype(bf16)

    @pl.when(step == last)
    def _():
        outof.wait()
        wait_all(blocks)


def order_of(sizes, rep_first):
    fsdp, rep, seq = sizes
    core = [("fsdp", 1)]
    rest = [("fsdp", b) for b in bits_of(fsdp)[1:]]
    copies = [("rep", b) for b in bits_of(rep)]
    return core + (copies + rest if rep_first else rest + copies) + [("seq", b) for b in bits_of(seq)]


def all_partners(sizes):
    fsdp, rep, seq = sizes
    return [("seq", k) for k in range(1, seq)] + [("fsdp", b) for b in bits_of(fsdp)] + [("rep", b) for b in bits_of(rep)]


def early_reducers(sizes):
    fsdp, rep, seq = sizes
    shapes = [(fsdp, FF // fsdp, D), (fsdp, D // fsdp, FF), (fsdp, D // fsdp, FF), (fsdp, D // fsdp, D)]
    reducers = [Reducer(shape, sizes, order_of(sizes, w == 2)) for w, shape in enumerate(shapes)]
    across = len(bits_of(fsdp)) + len(bits_of(rep))
    return reducers, [reducers[0].down] + [across + 1] * 3


def late_reducers(sizes):
    fsdp = sizes[0]
    return [Reducer((fsdp, D // fsdp, D), sizes, order_of(sizes, w == 1)) for w in range(3)]


def spread(ref, wide, value):
    shards, rows, cols = ref.shape
    if rows % 16 == 0:
        for q in range(shards):
            ref[q] = value[q * rows : (q + 1) * rows].astype(bf16)
    else:
        wide[: shards * rows, :cols] = value
        for q in range(shards):
            ref[q] = wide[q * rows : (q + 1) * rows, :cols].astype(bf16)


def middle_back_tile(dy, x1_ref, slope_ref, act_ref, gain_ref, w_out_ref, w_in_ref, w_mlp_ref, dh_ref, dgain_ref, dx1_ref):
    ahead = dot_nt(dy, w_mlp_ref[:HCHUNK, :])
    for column in range(0, FF, HCHUNK):
        dm = ahead
        if column + HCHUNK < FF:
            ahead = dot_nt(dy, w_mlp_ref[column + HCHUNK : column + 2 * HCHUNK, :])
        dh_ref[:, column : column + HCHUNK] = (dm * slope_ref[:, column : column + HCHUNK].astype(f32)).astype(bf16)
        dh_ref[:, FF + column : FF + column + HCHUNK] = (
            dm * act_ref[:, column : column + HCHUNK].astype(f32)
        ).astype(bf16)
    db = dot_nt(dh_ref[...], w_in_ref[...])
    unit, scale = normalize(x1_ref[...])
    back, terms = norm_back(unit, scale, gain_ref[...], db)
    dgain_ref[...] += jnp.sum(terms, axis=0, keepdims=True)
    dx1 = dy.astype(f32) + back
    dx1_ref[...] = dx1
    return dx1.astype(bf16)


def attend_back_pair(q_ref, k_ref, v_ref, o_ref, inv_ref, do, p_ref, cos_ref, sin_ref, dq_ref, dk_ref, dv_ref):
    v = v_ref[...]
    length = v.shape[0]
    mine = head_lanes()
    zero = jnp.zeros((), bf16)
    do = (do.astype(f32) * inv_ref[...]).astype(bf16)
    inner = do.astype(f32) * o_ref[...].astype(f32)
    do_heads = [jnp.where(m, do, zero) for m in mine]
    q_heads = [jnp.where(m, q_ref[...], zero).T for m in mine]
    k_heads = [jnp.where(m, k_ref[...], zero) for m in mine]
    do_turned = [d.T for d in do_heads]
    cosine, sine = cos_ref[...], sin_ref[...]
    dv = dk = None
    for tile in range(0, length, TILE):
        rows = slice(tile, tile + TILE)
        dq = None
        for head in range(2):
            probs = p_ref[head, rows, :]
            delta = jnp.sum(jnp.where(mine[head], inner[rows], 0.0), axis=-1, keepdims=True)
            dp = dot_nt(do_heads[head][rows], v)
            ds = (probs.astype(f32) * (dp - delta)).astype(bf16)
            value_part = dot_nn(do_turned[head][:, rows], probs)
            key_part = dot_nn(q_heads[head][:, rows], ds)
            query_part = dot_nn(ds, k_heads[head])
            dv = value_part if dv is None else dv + value_part
            dk = key_part if dk is None else dk + key_part
            dq = query_part if dq is None else dq + query_part
        dq_ref[rows, :] = rotate_pair(dq * HDIM**-0.5, cosine[rows], -sine[rows]).astype(bf16)
    dk_ref[...] = rotate_pair(dk.T * math.log(2.0), cosine, -sine).astype(bf16)
    dv_ref[...] = dv.T.astype(bf16)


def backward_kernel(
    sizes, tiles, x1_ref, slope_ref, act_ref, gain_ref, q_ref, k_ref, v_ref, o_ref, inv_ref, p_ref, cos_ref, sin_ref,
    w_out_any, w_in_any, w_mlp_any, m_any, dy_any, b_any, o_any, y_ref, *refs,
):
    reducers, early = early_reducers(sizes)
    count = len(reducers)
    refs = list(refs)
    pop = lambda n: [refs.pop(0) for _ in range(n)]
    dx1_ref, dgain_ref, dq_ref, dk_ref, dv_ref, home_ref = pop(6)
    sums_out = pop(count)
    w_out_ref, w_in_ref, w_mlp_ref, m_ref, dy_ref, b_ref, all_o_ref = pop(7)
    dh_ref, low_ref, do_ref, wide, bounce = pop(5)
    grads = pop(count)
    lands = [pop(len(r.scratch(0, e))) for r, e in zip(reducers, early)]
    sems = Sems(*refs)
    me = lax.axis_index("fsdp")
    step, last = pl.program_id(0), pl.num_programs(0) - 1
    into, outof, blocks = give_back(y_ref, home_ref, bounce, sems)
    loads = [
        sems.copy(src, dst)
        for src, dst in [
            (m_any, m_ref), (dy_any, dy_ref), (w_mlp_any, w_mlp_ref), (w_in_any, w_in_ref), (w_out_any, w_out_ref),
            (b_any, b_ref), (o_any, all_o_ref),
        ]
    ]
    stores = [sems.copy(grads[w].at[me], sums_out[w]) for w in range(count)]
    for w, reducer in enumerate(reducers):
        reducer.bind(lambda j, w=w: grads[w].at[flip(me, j)], lands[w], sems, 0, early[w])
    mlp, first_half, second_half, out = reducers

    def at(when, *actions):
        @pl.when(step == when)
        def _():
            for action in actions:
                action()

    def advance(reducer, s, limit):
        def run():
            reducer.finish(s)
            if s + 1 < limit:
                reducer.start(s + 1)
        return run

    @pl.when(step == 0)
    def _():
        start_all(loads)
        into.start()
        meet(all_partners(sizes))
        start_all(blocks)
        dgain_ref[...] = jnp.zeros_like(dgain_ref)
        wait_all(loads[:2])
        spread(grads[0], wide, dot_tn(m_ref[...], dy_ref[...]))
        mlp.start(0)
        into.wait()
        outof.start()
        wait_all(loads[2:5])

    at(1, advance(mlp, 0, early[0]))

    @pl.when(step < tiles)
    def _():
        rows = pl.ds(pl.multiple_of(step * TILE, TILE), TILE)
        low = middle_back_tile(
            dy_ref[rows, :], x1_ref, slope_ref, act_ref, gain_ref, w_out_ref, w_in_ref, w_mlp_ref,
            dh_ref.at[rows, :], dgain_ref, dx1_ref,
        )
        low_ref[rows, :] = low
        do_ref[rows, :] = dot_nt(low, w_out_ref[...]).astype(bf16)

    across = len(bits_of(sizes[0])) + len(bits_of(sizes[1]))

    @pl.when(step == tiles)
    def _():
        wait_all(loads[5:])
        spread(grads[1], wide, dot_tn(b_ref[...], dh_ref[:, :FF]))
        first_half.start(0)
        spread(grads[2], wide, dot_tn(b_ref[...], dh_ref[:, FF:]))
        second_half.start(0)
        for s in range(1, across - 1):
            advance(mlp, s, early[0])()
        spread(grads[3], wide, dot_tn(all_o_ref[...], low_ref[...]))
        out.start(0)

    last_pair = tiles + 6
    at(tiles + 1, *[advance(r, 0, e) for r, e in zip(reducers[1:], early[1:])])
    at(tiles + 2, advance(mlp, across - 1, early[0]))
    at(tiles + 4, *[advance(r, s, early[1]) for s in range(1, across - 1) for r in (first_half, second_half)])
    at(last_pair - 1, advance(out, 1, early[3]), advance(mlp, across, early[0]))
    at(
        last_pair,
        *[advance(out, s, early[3]) for s in range(2, across - 1)],
        *[advance(r, across - 1, early[1]) for r in (first_half, second_half)],
        *[advance(mlp, s, early[0]) for s in range(across + 1, early[0] - 1)],
        advance(out, across - 1, early[3]),
    )

    @pl.when(step > tiles)
    def _():
        column = pl.multiple_of((step - tiles - 1) * PAIR, PAIR)
        attend_back_pair(
            q_ref, k_ref, v_ref, o_ref, inv_ref, do_ref[:, pl.ds(column, PAIR)], p_ref, cos_ref, sin_ref,
            dq_ref, dk_ref, dv_ref,
        )

    @pl.when(step == last)
    def _():
        for w, reducer in enumerate(reducers):
            reducer.finish(early[w] - 1)
            stores[w].start()
        wait_all(stores)
        outof.wait()
        wait_all(blocks)


def leave_kernel(
    sizes, gain_ref, other_gain_ref, dx1_ref, x_ref, dq_ref, dk_ref, dv_ref, a_ref, w_ref, *refs
):
    fsdp, rep, seq = sizes
    reducers, early = early_reducers(sizes)
    whole = late_reducers(sizes)
    count, more = len(reducers), len(whole)
    refs = list(refs)
    pop = lambda n: [refs.pop(0) for _ in range(n)]
    sums_in = pop(count)
    (home_ref,) = pop(1)
    sums_out, wholes_out = pop(count), pop(more)
    (gains_out,) = pop(1)
    slots, wide = pop(2)
    held, grads, finals = pop(count), pop(more), pop(count + more)
    lands = [pop(len(r.scratch(e, len(r.steps)))) for r, e in zip(reducers, early)]
    whole_lands = [pop(len(r.scratch(0, len(r.steps)))) for r in whole]
    (gain_lands,) = pop(1)
    sems = Sems(*refs)
    me, me_seq = lax.axis_index("fsdp"), lax.axis_index("seq")
    own = sems.copy(slots.at[0], home_ref.at[me_seq])
    half = slots.shape[1] // 2
    blocks = {
        k: [
            sems.remote(slots.at[k, pl.ds(n * half, half)], home_ref.at[me_seq, pl.ds(n * half, half)], "seq", k)
            for n in range(2)
        ]
        for k in range(1, seq)
    }
    loads = [sems.copy(sums_in[w], held[w]) for w in range(count)]
    stores = [sems.copy(finals[w], out) for w, out in enumerate(sums_out + wholes_out)]
    for w, reducer in enumerate(reducers):
        reducer.bind(lambda j, w=w: held[w], lands[w], sems, early[w], len(reducer.steps), finals[w])
    for w, reducer in enumerate(whole):
        reducer.bind(
            lambda j, w=w: grads[w].at[flip(me, j)], whole_lands[w], sems, 0, len(reducer.steps), finals[count + w]
        )
    hops = [("fsdp", b) for b in bits_of(fsdp)] + [("rep", b) for b in bits_of(rep)] + [("seq", b) for b in bits_of(seq)]
    gain_moves = [sems.remote(gains_out, gain_lands.at[i], axis, bit) for i, (axis, bit) in enumerate(hops)]
    rows = slots.shape[1]

    def advance(some, s):
        for reducer in some:
            if s < len(reducer.steps):
                reducer.finish(s)
                if s + 1 < len(reducer.steps):
                    reducer.start(s + 1)

    def advance_gains(i):
        gain_moves[i].wait()
        gains_out[...] += gain_lands[i]
        if i + 1 < len(hops):
            gain_moves[i + 1].start()

    def input_slot(k):
        piece = slice(k * rows, (k + 1) * rows)
        da = dot_nt(dq_ref[piece, :], w_ref[:, :D])
        da = da + dot_nt(dk_ref[piece, :], w_ref[:, D : 2 * D])
        da = da + dot_nt(dv_ref[piece, :], w_ref[:, 2 * D :])
        unit, scale = normalize(x_ref[piece, :].astype(f32))
        back, terms = norm_back(unit, scale, gain_ref[...], da)
        gains_out[0:1, :] += jnp.sum(terms, axis=0, keepdims=True)
        slots[k] = (dx1_ref[piece, :] + back).astype(bf16)

    across = len(bits_of(fsdp)) + len(bits_of(rep))
    order = sorted(range(1, seq), key=lambda k: (k != 2, k == 1))
    far = [copy for k in order for copy in blocks[k]]
    late_blocks = far[2:]

    gains_out[...] = jnp.zeros_like(gains_out)
    gains_out[1:2, :] = other_gain_ref[...]
    start_all(loads)
    meet(all_partners(sizes))
    wait_all(loads)
    mlp = reducers[:1]
    others = reducers[1:]
    for reducer, e in zip(reducers, early):
        reducer.start(e)
    for w, part in enumerate((dq_ref, dk_ref, dv_ref)):
        spread(grads[w], wide, dot_tn(a_ref[...], part[...]))
        whole[w].start(0)
        if w < len(order):
            input_slot(order[w])
        if w == 0:
            start_all(blocks[order[0]])
        advance(whole[w : w + 1], 0)
        if w == 1:
            advance(mlp, early[0])
            advance(others, early[1])
    for k in order[3:] + [0]:
        input_slot(k)
    own.start()
    gain_moves[0].start()
    for s in range(1, across):
        advance(whole, s)
        advance_gains(s - 1)
        if late_blocks and s == across - 1:
            late_blocks.pop(0).start()
    for s in range(early[1] + 1, len(others[0].steps) - 1):
        advance(others, s)
    for s in range(across, len(whole[0].steps)):
        advance(whole, s)
        if late_blocks:
            late_blocks.pop(0).start()
        if across - 2 + s - across + 1 < len(hops):
            advance_gains(across - 1 + s - across)
    for i in range(len(whole[0].steps) - 1, len(hops)):
        advance_gains(i)
    start_all(late_blocks)
    for reducer, e in zip(reducers, early):
        for s in range(e + 1, len(reducer.steps)):
            if reducer in mlp or s == len(reducer.steps) - 1:
                advance([reducer], s)
    start_all(stores)
    wait_all(stores)
    own.wait()
    for k in range(1, seq):
        wait_all(blocks[k])


def rows_spec(width):
    return pl.BlockSpec((TILE, width), lambda i: (i, 0))


def whole_spec(*shape):
    return pl.BlockSpec(shape, lambda i: (0,) * len(shape))


def pair_spec(length, offset=0):
    return pl.BlockSpec((length, PAIR), lambda i: (0, i + offset))


def struct(dtype, *shape):
    return jax.ShapeDtypeStruct(shape, dtype)


def call(kernel, grid, in_specs, out_specs, out_shape, flops, scratch=(), collective=None):
    return pl.pallas_call(
        kernel,
        grid=(grid,),
        in_specs=in_specs,
        out_specs=out_specs,
        out_shape=out_shape,
        scratch_shapes=list(scratch),
        compiler_params=pltpu.CompilerParams(
            dimension_semantics=("arbitrary",), vmem_limit_bytes=VMEM_LIMIT,
            collective_id=collective, has_side_effects=collective is not None,
        ),
        cost_estimate=pl.CostEstimate(flops=flops, bytes_accessed=10 * 2**20, transcendentals=0),
    )


MESH = pl.DeviceIdType.MESH
ANY = pl.BlockSpec(memory_space=pl.ANY)


def take(array, index):
    return lax.dynamic_index_in_dim(array, index, 0, keepdims=False)


def flip(index, mask):
    bit = 1
    while bit <= mask:
        if mask & bit:
            index = index + bit - 2 * bit * ((index // bit) % 2)
        bit *= 2
    return index


def bits_of(size):
    return [1 << i for i in range(size.bit_length() - 1)]


def meet(partners):
    barrier = pltpu.get_barrier_semaphore()
    for axis, mask in partners:
        pl.semaphore_signal(
            barrier, inc=1, device_id={axis: flip(lax.axis_index(axis), mask)}, device_id_type=MESH
        )
    pl.semaphore_wait(barrier, len(partners))


class Sems:
    def __init__(self, send, recv, local):
        self.send, self.recv, self.local = send, recv, local
        self.remote_used = self.local_used = 0

    def remote(self, src, dst, axis, mask):
        i = self.remote_used
        self.remote_used += 1
        return pltpu.make_async_remote_copy(
            src_ref=src, dst_ref=dst, send_sem=self.send.at[i], recv_sem=self.recv.at[i],
            device_id={axis: flip(lax.axis_index(axis), mask)}, device_id_type=MESH,
        )

    def copy(self, src, dst):
        i = self.local_used
        self.local_used += 1
        return pltpu.make_async_copy(src, dst, self.local.at[i])


def sem_shapes(remote, local):
    dma = pltpu.SemaphoreType.DMA
    return [dma((remote,)), dma((remote,)), dma((max(local, 1),))]


def start_all(copies):
    for copy in copies:
        copy.start()


def wait_all(copies):
    for copy in copies:
        copy.wait()


class Gather:
    def __init__(self, sizes, shards, place, sems, order):
        self.sizes, self.shards, self.place, self.sems = sizes, shards, place, sems
        self.pieces = order
        self.me, self.me_rep = lax.axis_index("fsdp"), lax.axis_index("rep")
        self.pending = []

    def part(self, ref, pieces, n):
        width = ref.shape[-1] // (self.sizes[1] * pieces)
        start = (self.me_rep * pieces + n) * width
        return ref.at[:, pl.ds(pl.multiple_of(start, 128), width)]

    def source(self, w, h):
        return self.shards[w] if h == 0 else self.place(w, flip(self.me, h))

    def start(self):
        self.held = [0]
        self.over = self.cross(self.far_bits()[0]) if self.far_bits() else []

    def far_bits(self):
        return list(reversed(bits_of(self.sizes[0])[1:]))

    def cross(self, bit):
        over = []
        for w, pieces, n in self.pieces:
            moved = [
                self.sems.remote(
                    self.part(self.source(w, h), pieces, n),
                    self.part(self.place(w, flip(self.me, h)), pieces, n), "fsdp", bit,
                )
                for h in self.held
            ]
            start_all(moved)
            over.append(moved)
        return over

    def relay(self, bit):
        for (w, pieces, n), moved in zip(self.pieces, self.over):
            for copy in moved:
                copy.wait_recv()
            self.pending += moved
            passed = []
            for mask in range(1, self.sizes[1]):
                for h in self.held:
                    here = self.part(self.place(w, flip(self.me, h ^ bit)), pieces, n)
                    passed.append(self.sems.remote(here, here, "rep", mask))
            start_all(passed)
            yield (w, passed)

    def finish_far(self):
        bits = self.far_bits()
        for i, bit in enumerate(bits):
            passed = list(self.relay(bit))
            self.held = self.held + [h ^ bit for h in self.held]
            if i + 1 < len(bits):
                for _, copies in passed:
                    for copy in copies:
                        copy.wait_recv()
                    self.pending += copies
                self.over = self.cross(bits[i + 1])
                continue
            left = {w: pieces for w, pieces, _ in self.pieces}
            for w, copies in passed:
                for copy in copies:
                    copy.wait_recv()
                self.pending += copies
                left[w] -= 1
                if left[w] == 0:
                    yield w, self.near(w)
        if not bits:
            for w in range(len(self.shards)):
                yield w, self.near(w)

    def near(self, w):
        copies = [
            self.sems.remote(self.source(w, h), self.place(w, flip(self.me, h)), "fsdp", 1) for h in self.held
        ]
        start_all(copies)
        return copies

    @staticmethod
    def count(sizes, order, weights):
        held, copies = 1, 0
        for _ in bits_of(sizes[0])[1:]:
            copies += len(order) * held * sizes[1]
            held *= 2
        return copies + weights * held


def gather_order(sizes, shards):
    fits = lambda w, n: shards[w].shape[-1] % (sizes[1] * n * 128) == 0
    split = lambda w, n: n if fits(w, n) else 1
    order = []
    for w, n in ((0, 1), (1, 3), (2, 1), (4, 3), (3, 1)):
        n = split(w, n)
        order += [(w, n, i) for i in range(n)]
    return order


def enter_kernel(sizes, count, tokens, *refs):
    fsdp, rep, seq = sizes
    refs = list(refs)
    pop = lambda n: [refs.pop(0) for _ in range(n)]
    shards = pop(count)
    (x_out,) = pop(1)
    fulls = pop(count)
    (bounce_x,) = pop(1)
    bounces = pop(count)
    sems = Sems(*refs)
    me, me_seq = lax.axis_index("fsdp"), lax.axis_index("seq")
    into = [sems.copy(tokens.at[me_seq], bounce_x)] + [sems.copy(shards[w], bounces[w]) for w in range(count)]
    outof = [sems.copy(bounce_x, x_out.at[0])] + [sems.copy(bounces[w], fulls[w].at[me]) for w in range(count)]
    gather = Gather(sizes, shards, lambda w, q: fulls[w].at[q], sems, gather_order(sizes, shards))
    start_all(into)
    meet(all_partners(sizes))
    blocks = [sems.remote(tokens.at[flip(me_seq, k)], x_out.at[k], "seq", k) for k in range(1, seq)]
    start_all(blocks)
    gather.start()
    last = []
    for _, copies in gather.finish_far():
        last += copies
    wait_all(into)
    start_all(outof)
    for copy in gather.pending:
        copy.wait_send()
    wait_all(last)
    wait_all(blocks)
    wait_all(outof)


def enter(sizes, tokens, shards):
    fsdp = sizes[0]
    count = len(shards)
    hbm = lambda shape: struct(bf16, *shape)
    copies = sizes[2] - 1 + Gather.count(sizes, gather_order(sizes, shards), count)
    return pl.pallas_call(
        functools.partial(enter_kernel, sizes, count),
        in_specs=[ANY] * (1 + count),
        out_specs=[ANY] * (1 + count),
        out_shape=[hbm(tokens.shape)] + [hbm((fsdp,) + s.shape) for s in shards],
        scratch_shapes=[pltpu.VMEM(tokens.shape[1:], bf16)]
        + [pltpu.VMEM(s.shape, bf16) for s in shards]
        + sem_shapes(copies, 2 * (1 + count)),
        compiler_params=pltpu.CompilerParams(collective_id=0, has_side_effects=True),
    )(tokens, *shards)


def turn(row):
    n = row.shape[1]
    diagonal = lax.broadcasted_iota(jnp.int32, (n, n), 0) == lax.broadcasted_iota(jnp.int32, (n, n), 1)
    return jnp.sum(jnp.where(diagonal, row, 0), axis=1, keepdims=True)


def enter_project_kernel(sizes, count, tokens, segments, *refs):
    fsdp, rep, seq = sizes
    refs = list(refs)
    pop = lambda n: [refs.pop(0) for _ in range(n)]
    shards = pop(count)
    x_out, a_out, qkv_out, cos_out, sin_out, marks_out, row_out, gains_out, wq_out = pop(9)
    fulls = [None, None] + pop(count - 2)
    xs, a, qkv, wq, gains = pop(5)
    bounces = pop(count)
    sems = Sems(*refs)
    me, me_seq = lax.axis_index("fsdp"), lax.axis_index("seq")
    shard_rows, rows = shards[1].shape[0], xs.shape[1]
    columns = wq.shape[1]

    def place(w, q):
        if w == 0:
            return gains.at[q]
        if w == 1:
            return wq.at[pl.ds(pl.multiple_of(q * shard_rows, 16), shard_rows)]
        return fulls[w].at[q]

    own = sems.copy(tokens.at[me_seq], xs.at[0])
    into = [sems.copy(shards[w], place(w, me) if w < 2 else bounces[w - 2]) for w in range(count)]
    outof = [sems.copy(bounces[w - 2], place(w, me)) for w in range(2, count)]
    blocks = [sems.remote(tokens.at[flip(me_seq, k)], xs.at[k], "seq", k) for k in range(1, seq)]
    stores = [
        [sems.copy(src.at[k], dst.at[k]) for src, dst in ((xs, x_out), (a, a_out), (qkv, qkv_out))] for k in range(seq)
    ]
    keep = sems.copy(wq, wq_out)
    gather = Gather(sizes, shards, place, sems, gather_order(sizes, shards))
    own.start()
    start_all(into)
    meet(all_partners(sizes))
    gather.start()
    start_all(blocks)

    lane = lax.broadcasted_iota(jnp.int32, (1, PAIR), 1)
    rate = jnp.exp((lane % (HDIM // 2)).astype(f32) * (-2.0 * math.log(THETA) / HDIM))
    sign = jnp.where(lane_halves((1, PAIR)), -1.0, 1.0)
    for k in range(seq):
        block = flip(me_seq, k)
        piece = slice(k * rows, (k + 1) * rows)
        row = segments[me_seq, block]
        column = turn(row)
        earlier = jnp.zeros((rows, 1), jnp.int32)
        for other in range(seq):
            earlier += jnp.sum((segments[me_seq, other] < column).astype(jnp.int32), axis=1, keepdims=True)
        index = block * rows + lax.broadcasted_iota(jnp.int32, (rows, 1), 0)
        angles = (index - earlier).astype(f32) * rate
        cos_out[piece, :] = jnp.cos(angles)
        sin_out[piece, :] = jnp.sin(angles) * sign
        marks_out[piece, :] = column
        row_out[:, piece] = row

    last = {}
    far = gather.finish_far()
    for w, copies in far:
        last[w] = copies
        if len(last) == 2:
            break
    assert sorted(last) == [0, 1]
    for copy in into[:2] + last[0] + last[1]:
        copy.wait()
    keep.start()
    total = gains[0, :2, :].astype(f32)
    for q in range(1, fsdp):
        total = total + gains[q, :2, :].astype(f32)
    gains_out[...] = total

    def project(k):
        if k == 0:
            own.wait()
        else:
            blocks[k - 1].wait()
        piece = slice(k * rows, (k + 1) * rows)
        unit, _ = normalize(xs[k].astype(f32))
        low = (unit * total[:1]).astype(bf16)
        a[k] = low
        cosine, sine = cos_out[piece, :], sin_out[piece, :]
        for at in range(0, columns, TILE):
            part = dot_nn(low, wq[:, at : at + TILE])
            for half in range(0, TILE, PAIR):
                start = at + half
                value = part[:, half : half + PAIR]
                if start < 2 * D:
                    value = rotate_pair(value, cosine, sine)
                if start < D:
                    value = value * QUERY_SCALE
                qkv[k, :, start : start + PAIR] = value.astype(bf16)
        start_all(stores[k])

    project(0)
    project(1)
    for w, copies in far:
        last[w] = copies
        if w == 2:
            wait_all(into[2:])
            start_all(outof)
    for k in range(2, seq):
        project(k)
    for copy in gather.pending:
        copy.wait_send()
    for w in range(2, count):
        wait_all(last[w])
    wait_all(outof)
    for group in stores:
        wait_all(group)
    keep.wait()


def enter_project(sizes, tokens, segments, shards):
    fsdp, rep, seq = sizes
    count, rows = len(shards), tokens.shape[1]
    length, columns = seq * rows, shards[1].shape[1]
    vmem = pl.BlockSpec(memory_space=pltpu.VMEM)
    copies = seq - 1 + Gather.count(sizes, gather_order(sizes, shards), count)
    return pl.pallas_call(
        functools.partial(enter_project_kernel, sizes, count),
        in_specs=[ANY, vmem] + [ANY] * count,
        out_specs=[ANY] * 3 + [vmem] * 5 + [ANY] * (count - 1),
        out_shape=[struct(bf16, seq, rows, D), struct(bf16, seq, rows, D), struct(bf16, seq, rows, columns),
                   struct(f32, length, PAIR), struct(f32, length, PAIR), struct(jnp.int32, length, 1),
                   struct(jnp.int32, 1, length), struct(f32, 2, D), struct(bf16, D, columns)]
        + [struct(bf16, fsdp, *s.shape) for s in shards[2:]],
        scratch_shapes=[pltpu.VMEM((seq, rows, D), bf16), pltpu.VMEM((seq, rows, D), bf16),
                        pltpu.VMEM((seq, rows, columns), bf16), pltpu.VMEM((D, columns), bf16),
                        pltpu.VMEM((fsdp,) + shards[0].shape, bf16)]
        + [pltpu.VMEM(s.shape, bf16) for s in shards[2:]] + [pltpu.VMEM((16, 128), bf16)] * 2
        + sem_shapes(copies, 2 + count + count - 2 + 3 * seq),
        compiler_params=pltpu.CompilerParams(
            collective_id=4, has_side_effects=True, vmem_limit_bytes=VMEM_LIMIT
        ),
    )(tokens, segments, *shards)


class Reducer:
    def __init__(self, parts_shape, sizes, order):
        self.fsdp, self.rows, self.cols = parts_shape
        self.steps = []
        held, rows, cols = list(range(self.fsdp)), self.rows, self.cols
        row_at, col_at = [], []
        for axis, bit in order:
            step = dict(axis=axis, bit=bit, row_at=list(row_at), col_at=list(col_at), rows=rows, cols=cols)
            if axis == "fsdp":
                step["send"] = [j for j in held if j & bit]
                held = [j for j in held if not j & bit]
                step["keep"] = held
                step["shape"] = (len(held), rows, cols)
                step["split"] = None
            else:
                step["keep"] = step["send"] = held
                if (axis, bit) == order[-1]:
                    step["split"] = "none"
                elif (rows // 2) % 16 == 0:
                    rows //= 2
                    row_at = row_at + [(axis, bit, rows)]
                    step["split"] = "rows"
                elif (cols // 2) % 128 == 0:
                    cols //= 2
                    col_at = col_at + [(axis, bit, cols)]
                    step["split"] = "cols"
                else:
                    step["split"] = "none"
                step["shape"] = (len(held), rows, cols)
            self.steps.append(step)
        self.down = len(self.steps)
        for step in reversed(self.steps[: self.down]):
            if step["split"] in ("rows", "cols"):
                self.steps.append(dict(step, up=True))

    @staticmethod
    def offset(terms, align, last=None):
        total = 0
        for i, (axis, bit, extent) in enumerate(terms):
            half = (lax.axis_index(axis) // bit) % 2
            if last == i:
                half = 1 - half
            total = total + half * extent
        return total if isinstance(total, int) else pl.multiple_of(total, align)

    def region(self, step, after, other=False):
        row_at, col_at, rows, cols = step["row_at"], step["col_at"], step["rows"], step["cols"]
        row_last = col_last = None
        if after:
            if step["split"] == "rows":
                rows //= 2
                row_at = row_at + [(step["axis"], step["bit"], rows)]
                row_last = len(row_at) - 1 if other else None
            elif step["split"] == "cols":
                cols //= 2
                col_at = col_at + [(step["axis"], step["bit"], cols)]
                col_last = len(col_at) - 1 if other else None
        return (
            pl.ds(self.offset(row_at, 16, row_last), rows),
            pl.ds(self.offset(col_at, 128, col_last), cols),
        )

    def scratch(self, first, last):
        return [pltpu.VMEM(s["shape"], bf16) for s in self.steps[first:last] if "up" not in s]

    def copies(self, first, last):
        return sum(1 if "up" in s else len(s["send"]) for s in self.steps[first:last])

    def bind(self, parts, lands, sems, first, last, final=None):
        self.parts, self.sems, self.final = parts, sems, final
        self.lands, self.moves = {}, {}
        lands = list(lands)
        for s in range(first, last):
            step = self.steps[s]
            moves = []
            if "up" in step:
                there = final.at[self.region(step, True)]
                moves.append(sems.remote(there, there, step["axis"], step["bit"]))
            else:
                land = self.lands[s] = lands.pop(0)
                for i, j in enumerate(step["send"]):
                    fsdp = step["axis"] == "fsdp"
                    src = self.parts(j).at[self.region(step, not fsdp, not fsdp)]
                    moves.append(sems.remote(src, land.at[i], step["axis"], step["bit"]))
            self.moves[s] = moves

    def start(self, s):
        if s == self.down:
            region = self.region(self.steps[s - 1], True)
            self.final[region] = self.parts(0)[region]
        start_all(self.moves[s])

    def finish(self, s):
        step = self.steps[s]
        for i, move in enumerate(self.moves[s]):
            move.wait()
            if "up" not in step:
                j = step["keep"][i]
                ref = self.parts(j)
                region = self.region(step, True)
                ref[region] = (ref[region].astype(f32) + self.lands[s][i].astype(f32)).astype(bf16)


def give_back(slots, home, bounce, sems):
    me = lax.axis_index("seq")
    seq = slots.shape[0]
    return (
        sems.copy(slots.at[0], bounce),
        sems.copy(bounce, home.at[me]),
        [sems.remote(slots.at[k], home.at[me], "seq", k) for k in range(1, seq)],
    )


def body(sizes, tokens, segments, positions, gain_attn, w_qkv, w_out, gain_mlp, w_in, w_mlp_out, cotangent):
    fsdp, rep, seq = sizes
    micro, batch, rows, _ = tokens.shape
    assert micro * batch == seq and rows % TILE == 0
    length = seq * rows
    me_seq, me_fsdp = lax.axis_index("seq"), lax.axis_index("fsdp")

    own_gains = jnp.zeros((16, D), bf16)
    own_gains = lax.dynamic_update_slice(own_gains, jnp.stack([gain_attn, gain_mlp]), (0, me_fsdp * (D // fsdp)))
    shards = [own_gains, w_qkv, w_out, w_mlp_out, w_in]
    tiles, pairs = length // TILE, HEADS // 2
    if (D // fsdp) % 16 == 0:
        x, a, qkv, cosine, sine, marks_column, marks_row, gains, wq, wo, wm, wi = enter_project(
            sizes, tokens.reshape(seq, rows, D), segments.reshape(seq, seq, 1, rows), shards
        )
        x, a, qkv = (v.reshape(length, -1) for v in (x, a, qkv))
        gain_one, gain_two = gains[:1], gains[1:]
        wo, wm, wi = (w.reshape(-1, w.shape[-1]) for w in (wo, wm, wi))
    else:
        x, gains, wq, wo, wm, wi = enter(sizes, tokens.reshape(seq, rows, D), shards)
        x = x.reshape(length, D)
        gains = jnp.sum(gains[:, :2].astype(f32), axis=0)
        gain_one, gain_two = gains[:1], gains[1:]
        wq, wo, wm, wi = (w.reshape(-1, w.shape[-1]) for w in (wq, wo, wm, wi))

        marks = take(segments.reshape(seq, length), me_seq)
        place = jnp.arange(length, dtype=jnp.int32) - jnp.sum(
            (marks[None, :] < marks[:, None]).astype(jnp.int32), axis=1
        )
        slot_order = [me_seq ^ k for k in range(seq)]
        marks = jnp.concatenate([take(marks.reshape(seq, rows), s) for s in slot_order])
        place = jnp.concatenate([take(place.reshape(seq, rows), s) for s in slot_order])
        half = jnp.arange(0, HDIM, 2).astype(f32) / HDIM
        angles = place.astype(f32)[:, None] * jnp.exp(-half * math.log(THETA))
        cosine, sine = jnp.cos(angles), jnp.sin(angles)
        cosine = jnp.concatenate([cosine] * 4, -1)
        sine = jnp.concatenate([-sine, sine] * 2, -1)

        a, qkv = call(
            first_kernel, tiles,
            [rows_spec(D), whole_spec(1, D), whole_spec(D, 3 * D), rows_spec(PAIR), rows_spec(PAIR)],
            [rows_spec(D), rows_spec(3 * D)],
            [struct(bf16, length, D), struct(bf16, length, 3 * D)],
            2 * length * D * 3 * D,
        )(x, gain_one, wq, cosine, sine)
        marks_column, marks_row = marks[:, None], marks[None, :]

    vmem = pl.BlockSpec(memory_space=pltpu.VMEM)
    pair_at = lambda offset, lag, n: pl.BlockSpec(
        (length, PAIR), lambda i: (0, jnp.clip(i - lag, 0, n - 1) + offset)
    )
    prob_at = lambda lag: pl.BlockSpec((2, length, length), lambda i: (jnp.clip(i - lag, 0, pairs - 1), 0, 0))
    tile_at = lambda width, lag: pl.BlockSpec((TILE, width), lambda i: (jnp.clip(i - lag, 0, tiles - 1), 0))
    slots = struct(bf16, seq, rows, D)
    o, probs, inv, x1, b, m, slope, act, y, dy = call(
        functools.partial(forward_kernel, sizes, pairs), pairs + tiles,
        [pair_at(0, 0, pairs), pair_at(pairs, 0, pairs), pair_at(2 * pairs, 0, pairs),
         whole_spec(length, 1), whole_spec(1, length), tile_at(D, pairs), whole_spec(1, D)] + [ANY] * 4,
        [pair_at(0, 0, pairs), prob_at(0), pair_at(0, 0, pairs), tile_at(D, pairs), tile_at(D, pairs)]
        + [tile_at(FF, pairs)] * 3 + [tile_at(D, pairs), ANY],
        [struct(bf16, length, D), struct(bf16, HEADS, length, length), struct(f32, length, D),
         struct(f32, length, D), struct(bf16, length, D), struct(bf16, length, FF),
         struct(bf16, length, FF), struct(bf16, length, FF), struct(bf16, length, D), slots],
        16 * length * length * D,
        [pltpu.VMEM((length, D), bf16), pltpu.VMEM((D, D), bf16), pltpu.VMEM((D, 2 * FF), bf16), pltpu.VMEM((FF, D), bf16),
         pltpu.VMEM((rows, D), bf16)] + sem_shapes(seq - 1, 5), 1,
    )(qkv, qkv, qkv, marks_column, marks_row, x, gain_two, wo, wi, wm, cotangent.reshape(seq, rows, D))

    reducers, early = early_reducers(sizes)
    whole = late_reducers(sizes)
    own_shard = lambda r: struct(bf16, r.rows, r.cols)
    full_shard = lambda r: pltpu.VMEM((fsdp, r.rows, r.cols), bf16)
    odd = (FF // fsdp) % 16 or (D // fsdp) % 16
    wide = pltpu.VMEM((FF, FF) if odd else (8, 128), f32)
    dx1, dgain_two, dq, dk, dv, block_out, *sums = call(
        functools.partial(backward_kernel, sizes, tiles), tiles + 1 + pairs,
        [tile_at(D, 0), tile_at(FF, 0), tile_at(FF, 0), whole_spec(1, D)]
        + [pair_at(n * pairs, tiles + 1, pairs) for n in range(3)]
        + [pair_at(0, tiles + 1, pairs), pair_at(0, tiles + 1, pairs), prob_at(tiles + 1),
           whole_spec(length, PAIR), whole_spec(length, PAIR)] + [ANY] * 8,
        [tile_at(D, 0), whole_spec(1, D)] + [pair_at(0, tiles + 1, pairs)] * 3 + [ANY] * (1 + len(reducers)),
        [struct(f32, length, D), struct(f32, 1, D)] + [struct(bf16, length, D)] * 3 + [slots]
        + [own_shard(r) for r in reducers],
        32 * length * length * D,
        [pltpu.VMEM((D, D), bf16), pltpu.VMEM((D, 2 * FF), bf16), pltpu.VMEM((FF, D), bf16),
         pltpu.VMEM((length, FF), bf16)] + [pltpu.VMEM((length, D), bf16)] * 3
        + [pltpu.VMEM((length, 2 * FF), bf16), pltpu.VMEM((length, D), bf16), pltpu.VMEM((length, D), bf16),
           wide, pltpu.VMEM((rows, D), bf16)]
        + [full_shard(r) for r in reducers]
        + [land for r, e in zip(reducers, early) for land in r.scratch(0, e)]
        + sem_shapes(seq - 1 + sum(r.copies(0, e) for r, e in zip(reducers, early)), 9 + len(reducers)), 2,
    )(x1, slope, act, gain_two, qkv, qkv, qkv, o, inv, probs, cosine, sine,
      wo, wi, wm, m, dy.reshape(length, D), b, o, y.reshape(seq, rows, D))

    hops = sum(len(bits_of(n)) for n in sizes)
    input_grad, *results, dgains = pl.pallas_call(
        functools.partial(leave_kernel, sizes),
        in_specs=[vmem] * 9 + [ANY] * len(reducers),
        out_specs=[ANY] * (1 + len(reducers + whole)) + [vmem],
        out_shape=[slots] + [own_shard(r) for r in reducers + whole] + [struct(f32, 8, D)],
        scratch_shapes=[pltpu.VMEM((seq, rows, D), bf16), wide]
        + [pltpu.VMEM((r.rows, r.cols), bf16) for r in reducers]
        + [full_shard(r) for r in whole]
        + [pltpu.VMEM((r.rows, r.cols), bf16) for r in reducers + whole]
        + [land for r, e in zip(reducers, early) for land in r.scratch(e, len(r.steps))]
        + [land for r in whole for land in r.scratch(0, len(r.steps))]
        + [pltpu.VMEM((hops, 8, D), f32)]
        + sem_shapes(
            2 * (seq - 1) + hops + sum(r.copies(e, len(r.steps)) for r, e in zip(reducers, early))
            + sum(r.copies(0, len(r.steps)) for r in whole),
            1 + 2 * len(reducers) + len(whole),
        ),
        compiler_params=pltpu.CompilerParams(
            collective_id=3, has_side_effects=True, vmem_limit_bytes=VMEM_LIMIT
        ),
    )(gain_one, dgain_two, dx1, x, dq, dk, dv, a, wq, *sums)
    dgains = lax.dynamic_slice_in_dim(dgains, me_fsdp * (D // fsdp), D // fsdp, 1)
    grad_mlp, grad_in, grad_gate, grad_out, grad_q, grad_k, grad_v = (r.astype(f32) for r in results)
    return (
        block_out.reshape(tokens.shape),
        input_grad.astype(f32).reshape(tokens.shape),
        dgains[0],
        jnp.concatenate([grad_q, grad_k, grad_v], 1),
        grad_out,
        dgains[1],
        jnp.concatenate([grad_in, grad_gate], 1),
        grad_mlp,
    )


def solution(mesh):
    sizes = (mesh.shape["fsdp"], mesh.shape["rep"], mesh.shape["seq"])
    wide = P(None, ("rep", "fsdp"), "seq", None)
    placed = (
        wide, P(None, ("rep", "fsdp"), None), P(None, ("rep", "fsdp"), "seq"),
        P("fsdp"), P("fsdp", None), P("fsdp", None), P("fsdp"), P("fsdp", None), P("fsdp", None), wide,
    )
    return jax.shard_map(
        functools.partial(body, sizes),
        mesh=mesh,
        in_specs=placed,
        out_specs=(
            wide, wide, P("fsdp"), P("fsdp", None), P("fsdp", None), P("fsdp"), P("fsdp", None), P("fsdp", None),
        ),
        check_vma=False,
    )
```

```python
import functools
import math

import jax
import jax.numpy as jnp
from jax import lax
from jax.experimental import pallas as pl
from jax.experimental.pallas import tpu as pltpu
from jax.sharding import PartitionSpec as P

D = 768
HEADS = 12
HDIM = 64
FF = 1152
EPS = 1e-05
THETA = 160000.0
MASKED = -1000000000.0
QUERY_SCALE = HDIM**-0.5 / math.log(2.0)
TILE = 256
PAIR = 2 * HDIM
WIDE = 384
HCHUNK = 384
f32 = jnp.float32
bf16 = jnp.bfloat16
VMEM_LIMIT = 62 * 2**20


def dot_nn(left, right):
    return lax.dot_general(left, right, (((1,), (0,)), ((), ())), preferred_element_type=f32)


def dot_nt(left, right):
    return lax.dot_general(left, right, (((1,), (1,)), ((), ())), preferred_element_type=f32)


def dot_tn(left, right):
    return lax.dot_general(left, right, (((0,), (0,)), ((), ())), preferred_element_type=f32)


def normalize(values):
    mean = jnp.mean(values, axis=-1, keepdims=True)
    centered = values - mean
    var = jnp.mean(centered * centered, axis=-1, keepdims=True)
    scale = lax.rsqrt(var + EPS)
    return centered * scale, scale


def norm_back(unit, scale, gain, grad):
    gain_terms = grad * unit
    inner = grad * gain
    first = jnp.mean(inner, axis=-1, keepdims=True)
    second = jnp.mean(inner * unit, axis=-1, keepdims=True)
    return scale * (inner - first - unit * second), gain_terms


def lane_halves(shape):
    lane = lax.broadcasted_iota(jnp.int32, shape, len(shape) - 1)
    return lane % HDIM < HDIM // 2


def rotate_pair(values, cosine, signed_sine):
    swapped = jnp.where(
        lane_halves(values.shape),
        pltpu.roll(values, PAIR - HDIM // 2, 1),
        pltpu.roll(values, HDIM // 2, 1),
    )
    return values * cosine + swapped * signed_sine


def first_kernel(x_ref, gain_ref, w_ref, cos_ref, sin_ref, a_ref, qkv_ref):
    unit, _ = normalize(x_ref[...].astype(f32))
    a = (unit * gain_ref[0:1, :]).astype(bf16)
    a_ref[...] = a
    cosine, sine = cos_ref[...], sin_ref[...]
    for column in range(0, 3 * D, TILE):
        part = dot_nn(a, w_ref[:, column : column + TILE])
        for half in range(0, TILE, PAIR):
            start = column + half
            piece = part[:, half : half + PAIR]
            if start < 2 * D:
                piece = rotate_pair(piece, cosine, sine)
            if start < D:
                piece = piece * QUERY_SCALE
            qkv_ref[:, start : start + PAIR] = piece.astype(bf16)


def head_lanes():
    lane = lax.broadcasted_iota(jnp.int32, (1, PAIR), 1)
    return [lane < HDIM, lane >= HDIM]


def attend_pair(q_ref, k_ref, v_ref, rows_ref, cols_ref, p_ref, inv_ref, write):
    k, v = k_ref[...], v_ref[...]
    length = k.shape[0]
    mine = head_lanes()
    zero, one = jnp.zeros((), bf16), jnp.ones((), bf16)
    summing = [jnp.where(m, v, one) for m in mine]
    items = [(tile, head) for tile in range(0, length, TILE) for head in range(2)]

    def score(item):
        tile, head = item
        return dot_nt(jnp.where(mine[head], q_ref[tile : tile + TILE, :], zero), k)

    ahead = score(items[0])
    kept = None
    for i, (tile, head) in enumerate(items):
        rows = slice(tile, tile + TILE)
        scores = ahead
        if i + 1 < len(items):
            ahead = score(items[i + 1])
        scores = jnp.where(rows_ref[rows, :] == cols_ref[...], scores, MASKED)
        probs = jnp.exp2(scores - jnp.max(scores, axis=-1, keepdims=True)).astype(bf16)
        p_ref[head, rows, :] = probs
        part = dot_nn(probs, summing[head])
        inv = 1.0 / pltpu.roll(part, HDIM, 1)
        if head == 0:
            kept = (part * inv, inv)
        else:
            inv_ref[rows, :] = jnp.where(mine[0], kept[1], inv)
            write(rows, jnp.where(mine[0], kept[0], part * inv).astype(bf16))


def forward_kernel(
    sizes, pairs, q_ref, k_ref, v_ref, rows_ref, cols_ref, x_ref, gain_ref, w_out_any, w_in_any, w_mlp_any, cot_ref,
    o_ref, p_ref, inv_ref, x1_ref, b_ref, m_ref, slope_ref, act_ref, y_ref, dy_ref,
    joined, w_out_ref, w_in_ref, w_mlp_ref, bounce, *sem_refs,
):
    seq = sizes[2]
    step, last = pl.program_id(0), pl.num_programs(0) - 1
    sems = Sems(*sem_refs)
    me_seq = lax.axis_index("seq")
    into = sems.copy(cot_ref.at[me_seq], bounce)
    outof = sems.copy(bounce, dy_ref.at[0])
    weights = [sems.copy(w_out_any, w_out_ref), sems.copy(w_in_any, w_in_ref), sems.copy(w_mlp_any, w_mlp_ref)]
    blocks = [sems.remote(cot_ref.at[flip(me_seq, k)], dy_ref.at[k], "seq", k) for k in range(1, seq)]

    @pl.when(step == 0)
    def _():
        into.start()
        start_all(weights)
        meet([("seq", k) for k in range(1, seq)])
        start_all(blocks)
        into.wait()
        outof.start()

    @pl.when(step < pairs)
    def _():
        def write(rows, value):
            o_ref[rows, :] = value
            joined[rows, pl.ds(pl.multiple_of(step * PAIR, PAIR), PAIR)] = value

        attend_pair(q_ref, k_ref, v_ref, rows_ref, cols_ref, p_ref, inv_ref, write)

    @pl.when(step == pairs)
    def _():
        wait_all(weights)

    @pl.when(step >= pairs)
    def _():
        start = pl.multiple_of((step - pairs) * TILE, TILE)
        x1 = x_ref[...].astype(f32) + dot_nn(joined[pl.ds(start, TILE), :], w_out_ref[...])
        x1_ref[...] = x1
        unit, _ = normalize(x1)
        b = (unit * gain_ref[1:2, :]).astype(bf16)
        b_ref[...] = b

        def hidden(column):
            return (
                dot_nn(b, w_in_ref[:, column : column + HCHUNK]),
                dot_nn(b, w_in_ref[:, FF + column : FF + column + HCHUNK]),
            )

        ahead = hidden(0)
        for column in range(0, FF, HCHUNK):
            hin, gate = ahead
            if column + HCHUNK < FF:
                ahead = hidden(column + HCHUNK)
            phi = 0.5 + 0.5 * lax.erf(hin * math.sqrt(0.5))
            act = hin * phi
            slope = phi + hin * (jnp.exp(hin * hin * -0.5) * (1.0 / math.sqrt(2.0 * math.pi)))
            m_ref[:, column : column + HCHUNK] = (act * gate).astype(bf16)
            act_ref[:, column : column + HCHUNK] = act.astype(bf16)
            slope_ref[:, column : column + HCHUNK] = (slope * gate).astype(bf16)
        y_ref[...] = (x1 + dot_nn(m_ref[...], w_mlp_ref[...])).astype(bf16)

    @pl.when(step == last)
    def _():
        outof.wait()
        wait_all(blocks)


def order_of(sizes, rep_first):
    fsdp, rep, seq = sizes
    core = [("fsdp", 1)]
    rest = [("fsdp", b) for b in bits_of(fsdp)[1:]]
    copies = [("rep", b) for b in bits_of(rep)]
    return core + (copies + rest if rep_first else rest + copies) + [("seq", b) for b in bits_of(seq)]


def all_partners(sizes):
    fsdp, rep, seq = sizes
    return [("seq", k) for k in range(1, seq)] + [("fsdp", b) for b in bits_of(fsdp)] + [("rep", b) for b in bits_of(rep)]


def early_reducers(sizes):
    fsdp, rep, seq = sizes
    shapes = [(fsdp, FF // fsdp, D), (fsdp, D // fsdp, FF), (fsdp, D // fsdp, FF), (fsdp, D // fsdp, D)]
    reducers = [Reducer(shape, sizes, order_of(sizes, w == 2)) for w, shape in enumerate(shapes)]
    across = len(bits_of(fsdp)) + len(bits_of(rep))
    return reducers, [len(reducers[0].steps)] + [across + 2] * 2 + [across + 1]


def late_reducers(sizes):
    fsdp = sizes[0]
    return [Reducer((fsdp, D // fsdp, D), sizes, order_of(sizes, w == 1)) for w in range(3)]


def weight_gradient(ref, wide, left, right):
    shards, rows, cols = ref.shape
    if rows % 16 == 0:
        @pl.loop(0, cols // HCHUNK)
        def _(i):
            at = pl.ds(pl.multiple_of(i * HCHUNK, HCHUNK), HCHUNK)
            value = dot_tn(left, right(at))
            for q in range(shards):
                ref[q, :, at] = value[q * rows : (q + 1) * rows].astype(bf16)
    else:
        wide[: shards * rows, :cols] = dot_tn(left, right(pl.ds(0, cols)))
        for q in range(shards):
            ref[q] = wide[q * rows : (q + 1) * rows, :cols].astype(bf16)


def middle_back_tile(dy, x1_ref, slope_ref, act_ref, gain_ref, w_out_ref, w_in_ref, w_mlp_ref, dh_ref, dgain_ref, dx1_ref):
    ahead = dot_nt(dy, w_mlp_ref[:HCHUNK, :])
    for column in range(0, FF, HCHUNK):
        dm = ahead
        if column + HCHUNK < FF:
            ahead = dot_nt(dy, w_mlp_ref[column + HCHUNK : column + 2 * HCHUNK, :])
        dh_ref[:, column : column + HCHUNK] = (dm * slope_ref[:, column : column + HCHUNK].astype(f32)).astype(bf16)
        dh_ref[:, FF + column : FF + column + HCHUNK] = (
            dm * act_ref[:, column : column + HCHUNK].astype(f32)
        ).astype(bf16)
    db = dot_nt(dh_ref[...], w_in_ref[...])
    unit, scale = normalize(x1_ref[...])
    back, terms = norm_back(unit, scale, gain_ref[1:2, :], db)
    dgain_ref[...] += jnp.sum(terms, axis=0, keepdims=True)
    dx1 = dy.astype(f32) + back
    dx1_ref[...] = dx1
    return dx1.astype(bf16)


def attend_back_pair(q_ref, k_ref, v_ref, o_ref, inv_ref, do, p_ref, cos_ref, sin_ref, dq_ref, dk_ref, dv_ref):
    v = v_ref[...]
    length = v.shape[0]
    mine = head_lanes()
    zero = jnp.zeros((), bf16)
    do = (do.astype(f32) * inv_ref[...]).astype(bf16)
    inner = do.astype(f32) * o_ref[...].astype(f32)
    do_heads = [jnp.where(m, do, zero) for m in mine]
    q_heads = [jnp.where(m, q_ref[...], zero).T for m in mine]
    k_heads = [jnp.where(m, k_ref[...], zero) for m in mine]
    do_turned = [d.T for d in do_heads]
    cosine, sine = cos_ref[...], sin_ref[...]
    dv = dk = None
    for tile in range(0, length, TILE):
        rows = slice(tile, tile + TILE)
        dq = None
        for head in range(2):
            probs = p_ref[head, rows, :]
            delta = jnp.sum(jnp.where(mine[head], inner[rows], 0.0), axis=-1, keepdims=True)
            dp = dot_nt(do_heads[head][rows], v)
            ds = (probs.astype(f32) * (dp - delta)).astype(bf16)
            value_part = dot_nn(do_turned[head][:, rows], probs)
            key_part = dot_nn(q_heads[head][:, rows], ds)
            query_part = dot_nn(ds, k_heads[head])
            dv = value_part if dv is None else dv + value_part
            dk = key_part if dk is None else dk + key_part
            dq = query_part if dq is None else dq + query_part
        dq_ref[rows, :] = rotate_pair(dq * HDIM**-0.5, cosine[rows], -sine[rows]).astype(bf16)
    dk_ref[...] = rotate_pair(dk.T * math.log(2.0), cosine, -sine).astype(bf16)
    dv_ref[...] = dv.T.astype(bf16)


def backward_kernel(
    sizes, tiles, x1_ref, slope_ref, act_ref, gain_ref, q_ref, k_ref, v_ref, o_ref, inv_ref, p_ref, cos_ref, sin_ref,
    w_out_any, w_in_any, w_mlp_any, m_any, dy_any, b_any, o_any, y_ref, *refs,
):
    reducers, early = early_reducers(sizes)
    count = len(reducers)
    refs = list(refs)
    pop = lambda n: [refs.pop(0) for _ in range(n)]
    dx1_ref, dgain_ref, dq_ref, dk_ref, dv_ref, home_ref = pop(6)
    sums_out = pop(count)
    w_out_ref, w_in_ref, w_mlp_ref, m_ref, dy_ref, b_ref, all_o_ref = pop(7)
    dh_ref, low_ref, do_ref, wide, bounce = pop(5)
    grads = pop(count)
    (mlp_final,) = pop(1)
    lands = [pop(len(r.scratch(0, e))) for r, e in zip(reducers, early)]
    sems = Sems(*refs)
    me = lax.axis_index("fsdp")
    step, last = pl.program_id(0), pl.num_programs(0) - 1
    into, outof, blocks = give_back(y_ref, home_ref, bounce, sems)
    loads = [
        sems.copy(src, dst)
        for src, dst in [
            (m_any, m_ref), (dy_any, dy_ref), (w_mlp_any, w_mlp_ref), (w_in_any, w_in_ref), (w_out_any, w_out_ref),
            (b_any, b_ref), (o_any, all_o_ref),
        ]
    ]
    stores = [sems.copy(mlp_final if w == 0 else grads[w].at[me], sums_out[w]) for w in range(count)]
    for w, reducer in enumerate(reducers):
        reducer.bind(lambda j, w=w: grads[w].at[flip(me, j)], lands[w], sems, 0, early[w], mlp_final if w == 0 else None)
    mlp, first_half, second_half, out = reducers

    def at(when, *actions):
        @pl.when(step == when)
        def _():
            for action in actions:
                action()

    def advance(reducer, s, limit):
        def run():
            reducer.finish(s)
            if s + 1 < limit:
                reducer.start(s + 1)
        return run

    @pl.when(step == 0)
    def _():
        start_all(loads)
        into.start()
        meet(all_partners(sizes))
        start_all(blocks)
        dgain_ref[...] = jnp.zeros_like(dgain_ref)
        wait_all(loads[:2])
        weight_gradient(grads[0], wide, m_ref[...], lambda at: dy_ref[:, at])
        mlp.start(0)
        into.wait()
        outof.start()
        wait_all(loads[2:5])

    at(1, advance(mlp, 0, early[0]))

    @pl.when(step < tiles)
    def _():
        rows = pl.ds(pl.multiple_of(step * TILE, TILE), TILE)
        low = middle_back_tile(
            dy_ref[rows, :], x1_ref, slope_ref, act_ref, gain_ref, w_out_ref, w_in_ref, w_mlp_ref,
            dh_ref.at[rows, :], dgain_ref, dx1_ref,
        )
        low_ref[rows, :] = low
        do_ref[rows, :] = dot_nt(low, w_out_ref[...]).astype(bf16)

    across = len(bits_of(sizes[0])) + len(bits_of(sizes[1]))

    @pl.when(step == tiles)
    def _():
        wait_all(loads[5:])
        weight_gradient(grads[1], wide, b_ref[...], lambda at: dh_ref.at[:, :FF][:, at])
        first_half.start(0)
        weight_gradient(grads[2], wide, b_ref[...], lambda at: dh_ref.at[:, FF:][:, at])
        second_half.start(0)
        for s in range(1, across - 1):
            advance(mlp, s, early[0])()
        weight_gradient(grads[3], wide, all_o_ref[...], lambda at: low_ref[:, at])
        out.start(0)

    halves = (first_half, second_half)
    steps = lambda reducer, limit, *which: [advance(reducer, s, limit) for s in which]
    half_steps = lambda *which: [advance(r, s, early[1]) for s in which for r in halves]
    middle = range(1, across - 1)
    at(tiles + 1, *steps(mlp, early[0], across - 1), *half_steps(0))
    at(tiles + 2, *steps(out, early[3], 0))
    at(tiles + 3, *half_steps(*middle))
    at(tiles + 4, *steps(mlp, early[0], across), *steps(out, early[3], *middle))
    at(tiles + 5, *steps(mlp, early[0], across + 1), *half_steps(across - 1))
    at(tiles + 6, *steps(mlp, early[0], *range(across + 2, early[0] - 1)), *half_steps(across), *steps(out, early[3], across - 1))

    @pl.when(step > tiles)
    def _():
        column = pl.multiple_of((step - tiles - 1) * PAIR, PAIR)
        attend_back_pair(
            q_ref, k_ref, v_ref, o_ref, inv_ref, do_ref[:, pl.ds(column, PAIR)], p_ref, cos_ref, sin_ref,
            dq_ref, dk_ref, dv_ref,
        )

    @pl.when(step == last)
    def _():
        for w, reducer in enumerate(reducers):
            reducer.finish(early[w] - 1)
            stores[w].start()
        wait_all(stores)
        outof.wait()
        wait_all(blocks)


PIECES = 4


def leave_kernel(sizes, gain_ref, other_gain_ref, *refs):
    fsdp, rep, seq = sizes
    reducers, early = (some[1:] for some in early_reducers(sizes))
    whole = late_reducers(sizes)
    count, more = len(reducers), len(whole)
    refs = list(refs)
    pop = lambda n: [refs.pop(0) for _ in range(n)]
    anys = pop(7)
    sums_in = pop(count)
    (home_ref,) = pop(1)
    in_out, out_out, qkv_out, gains_out = pop(4)
    dq_ref, a_ref, dk_ref, dv_ref, w_ref, x_ref, dx1_ref = local = pop(7)
    slots, wide, in_final, out_final, qkv_final = pop(5)
    held, grads = pop(count), pop(more)
    lands = [pop(len(r.scratch(e, len(r.steps)))) for r, e in zip(reducers, early)]
    whole_lands = [pop(len(r.scratch(0, len(r.steps)))) for r in whole]
    (gain_lands,) = pop(1)
    sems = Sems(*refs)
    me, me_seq = lax.axis_index("fsdp"), lax.axis_index("seq")
    own = sems.copy(slots.at[0], home_ref.at[me_seq])
    height = slots.shape[1] // PIECES
    blocks = {
        k: [
            sems.remote(slots.at[k, pl.ds(n * height, height)], home_ref.at[me_seq, pl.ds(n * height, height)], "seq", k)
            for n in range(PIECES)
        ]
        for k in range(1, seq)
    }
    order = sorted(range(1, seq), key=lambda k: (k != 2, k == 1))
    ready = []

    def send_piece(n=1):
        for _ in range(n):
            if ready:
                ready.pop(0).start()

    operands = [sems.copy(src, dst) for src, dst in zip(anys, local)]
    loads = [sems.copy(sums_in[w], held[w]) for w in range(count)]
    stores = [
        sems.copy(src, dst)
        for src, dst in ((in_final, in_out), (out_final, out_out), (qkv_final, qkv_out))
    ]
    finals = [in_final.at[:, pl.ds(0, FF)], in_final.at[:, pl.ds(FF, FF)], out_final]
    for w, reducer in enumerate(reducers):
        reducer.bind(lambda j, w=w: held[w], lands[w], sems, early[w], len(reducer.steps), finals[w])
    for w, reducer in enumerate(whole):
        reducer.bind(
            lambda j, w=w: grads[w].at[flip(me, j)], whole_lands[w], sems, 0, len(reducer.steps),
            qkv_final.at[:, pl.ds(w * D, D)],
        )
    hops = [("fsdp", b) for b in bits_of(fsdp)] + [("rep", b) for b in bits_of(rep)] + [("seq", b) for b in bits_of(seq)]
    gain_moves = [sems.remote(gains_out, gain_lands.at[i], axis, bit) for i, (axis, bit) in enumerate(hops)]
    rows = slots.shape[1]

    def advance(some, s):
        for reducer in some:
            if s < len(reducer.steps):
                reducer.finish(s)
                if s + 1 < len(reducer.steps):
                    reducer.start(s + 1)

    def advance_gains(i):
        if i < len(hops):
            gain_moves[i].wait()
            gains_out[...] += gain_lands[i]
            if i + 1 < len(hops):
                gain_moves[i + 1].start()

    def input_slot(k):
        piece = slice(k * rows, (k + 1) * rows)
        da = dot_nt(dq_ref[piece, :], w_ref[:, :D])
        da = da + dot_nt(dk_ref[piece, :], w_ref[:, D : 2 * D])
        da = da + dot_nt(dv_ref[piece, :], w_ref[:, 2 * D :])
        unit, scale = normalize(x_ref[piece, :].astype(f32))
        back, terms = norm_back(unit, scale, gain_ref[0:1, :], da)
        gains_out[0:1, :] += jnp.sum(terms, axis=0, keepdims=True)
        slots[k] = (dx1_ref[piece, :] + back).astype(bf16)
        if k:
            ready.extend(blocks[k])

    def gradient(w, part):
        weight_gradient(grads[w], wide, a_ref[...], lambda at: part[:, at])
        whole[w].start(0)

    across = len(bits_of(fsdp)) + len(bits_of(rep))
    halves, out, last = reducers[:2], reducers[2:], len(whole[0].steps)
    start_all(operands[:2])
    start_all(loads)
    start_all(operands[2:])
    gains_out[...] = jnp.zeros_like(gains_out)
    gains_out[1:2, :] = other_gain_ref[...]
    meet(all_partners(sizes))
    wait_all(loads)
    for w, (reducer, s) in enumerate(zip(reducers, early)):
        if s < len(reducer.steps):
            reducer.start(s)
        else:
            finals[w][...] = held[w][...]
    wait_all(operands[:2])
    gradient(0, dq_ref)
    wait_all(operands[2:])
    input_slot(order[0])
    send_piece(PIECES // 2)
    advance(whole[:1], 0)
    advance(halves, early[0])
    gradient(1, dk_ref)
    for k in order[1:2]:
        input_slot(k)
    advance(whole[1:2], 0)
    advance(out, early[2])
    send_piece()
    gradient(2, dv_ref)
    for k in order[2:]:
        input_slot(k)
    advance(whole[:1], 1)
    advance(whole[2:], 0)
    send_piece()
    input_slot(0)
    own.start()
    gain_moves[0].start()
    advance(whole[1:2], 1)
    advance(out, early[2] + 1)
    send_piece()
    for s in range(2, across):
        advance(whole[:1], s)
        advance(whole[2:], s - 1)
        advance(whole[1:2], s)
        send_piece()
    advance(whole[2:], across - 1)
    send_piece()
    i = 0
    for s in range(across, last):
        for reducer in whole:
            advance([reducer], s)
            send_piece()
        for _ in range(2):
            advance_gains(i)
            i += 1
    while i < len(hops):
        advance_gains(i)
        i += 1
    send_piece(len(ready))
    for s in range(early[0] + 1, len(halves[0].steps)):
        advance(halves, s)
    for s in range(early[2] + 2, len(out[0].steps)):
        advance(out, s)
    start_all(stores)
    wait_all(stores)
    own.wait()
    for k in range(1, seq):
        wait_all(blocks[k])


def rows_spec(width):
    return pl.BlockSpec((TILE, width), lambda i: (i, 0))


def whole_spec(*shape):
    return pl.BlockSpec(shape, lambda i: (0,) * len(shape))


def pair_spec(length, offset=0):
    return pl.BlockSpec((length, PAIR), lambda i: (0, i + offset))


def struct(dtype, *shape):
    return jax.ShapeDtypeStruct(shape, dtype)


def call(kernel, grid, in_specs, out_specs, out_shape, flops, scratch=(), collective=None):
    return pl.pallas_call(
        kernel,
        grid=(grid,),
        in_specs=in_specs,
        out_specs=out_specs,
        out_shape=out_shape,
        scratch_shapes=list(scratch),
        compiler_params=pltpu.CompilerParams(
            dimension_semantics=("arbitrary",), vmem_limit_bytes=VMEM_LIMIT,
            collective_id=collective, has_side_effects=collective is not None,
        ),
        cost_estimate=pl.CostEstimate(flops=flops, bytes_accessed=10 * 2**20, transcendentals=0),
    )


MESH = pl.DeviceIdType.MESH
ANY = pl.BlockSpec(memory_space=pl.ANY)


def take(array, index):
    return lax.dynamic_index_in_dim(array, index, 0, keepdims=False)


def flip(index, mask):
    bit = 1
    while bit <= mask:
        if mask & bit:
            index = index + bit - 2 * bit * ((index // bit) % 2)
        bit *= 2
    return index


def bits_of(size):
    return [1 << i for i in range(size.bit_length() - 1)]


def meet(partners):
    barrier = pltpu.get_barrier_semaphore()
    for axis, mask in partners:
        pl.semaphore_signal(
            barrier, inc=1, device_id={axis: flip(lax.axis_index(axis), mask)}, device_id_type=MESH
        )
    pl.semaphore_wait(barrier, len(partners))


class Sems:
    def __init__(self, send, recv, local):
        self.send, self.recv, self.local = send, recv, local
        self.remote_used = self.local_used = 0

    def remote(self, src, dst, axis, mask):
        i = self.remote_used
        self.remote_used += 1
        return pltpu.make_async_remote_copy(
            src_ref=src, dst_ref=dst, send_sem=self.send.at[i], recv_sem=self.recv.at[i],
            device_id={axis: flip(lax.axis_index(axis), mask)}, device_id_type=MESH,
        )

    def copy(self, src, dst):
        i = self.local_used
        self.local_used += 1
        return pltpu.make_async_copy(src, dst, self.local.at[i])


def sem_shapes(remote, local):
    dma = pltpu.SemaphoreType.DMA
    return [dma((remote,)), dma((remote,)), dma((max(local, 1),))]


def start_all(copies):
    for copy in copies:
        copy.start()


def wait_all(copies):
    for copy in copies:
        copy.wait()


class Gather:
    def __init__(self, sizes, shards, place, sems, order):
        self.sizes, self.shards, self.place, self.sems = sizes, shards, place, sems
        self.pieces = order
        self.me, self.me_rep = lax.axis_index("fsdp"), lax.axis_index("rep")
        self.pending = []

    def part(self, ref, pieces, n):
        width = ref.shape[-1] // (self.sizes[1] * pieces)
        start = (self.me_rep * pieces + n) * width
        return ref.at[:, pl.ds(pl.multiple_of(start, 128), width)]

    def source(self, w, h):
        return self.shards[w] if h == 0 else self.place(w, flip(self.me, h))

    def start(self):
        self.held = [0]
        self.over = self.cross(self.far_bits()[0]) if self.far_bits() else []

    def far_bits(self):
        return list(reversed(bits_of(self.sizes[0])[1:]))

    def cross(self, bit):
        over = []
        for w, pieces, n in self.pieces:
            moved = [
                self.sems.remote(
                    self.part(self.source(w, h), pieces, n),
                    self.part(self.place(w, flip(self.me, h)), pieces, n), "fsdp", bit,
                )
                for h in self.held
            ]
            start_all(moved)
            over.append(moved)
        return over

    def relay(self, bit):
        for (w, pieces, n), moved in zip(self.pieces, self.over):
            for copy in moved:
                copy.wait_recv()
            self.pending += moved
            passed = []
            for mask in range(1, self.sizes[1]):
                for h in self.held:
                    here = self.part(self.place(w, flip(self.me, h ^ bit)), pieces, n)
                    passed.append(self.sems.remote(here, here, "rep", mask))
            start_all(passed)
            yield (w, passed)

    def finish_far(self):
        bits = self.far_bits()
        for i, bit in enumerate(bits):
            passed = list(self.relay(bit))
            self.held = self.held + [h ^ bit for h in self.held]
            if i + 1 < len(bits):
                for _, copies in passed:
                    for copy in copies:
                        copy.wait_recv()
                    self.pending += copies
                self.over = self.cross(bits[i + 1])
                continue
            left = {w: pieces for w, pieces, _ in self.pieces}
            for w, copies in passed:
                for copy in copies:
                    copy.wait_recv()
                self.pending += copies
                left[w] -= 1
                if left[w] == 0:
                    yield w, self.near(w)
        if not bits:
            for w in range(len(self.shards)):
                yield w, self.near(w)

    def near(self, w):
        copies = [
            self.sems.remote(self.source(w, h), self.place(w, flip(self.me, h)), "fsdp", 1) for h in self.held
        ]
        start_all(copies)
        return copies

    @staticmethod
    def count(sizes, order, weights):
        held, copies = 1, 0
        for _ in bits_of(sizes[0])[1:]:
            copies += len(order) * held * sizes[1]
            held *= 2
        return copies + weights * held


def gather_order(sizes, shards):
    fits = lambda w, n: shards[w].shape[-1] % (sizes[1] * n * 128) == 0
    split = lambda w, n: n if fits(w, n) else 1
    order = []
    for w, n in ((0, 1), (1, 3), (2, 1), (4, 3), (3, 1)):
        n = split(w, n)
        order += [(w, n, i) for i in range(n)]
    return order


def enter_kernel(sizes, count, tokens, *refs):
    fsdp, rep, seq = sizes
    refs = list(refs)
    pop = lambda n: [refs.pop(0) for _ in range(n)]
    shards = pop(count)
    (x_out,) = pop(1)
    fulls = pop(count)
    (bounce_x,) = pop(1)
    bounces = pop(count)
    sems = Sems(*refs)
    me, me_seq = lax.axis_index("fsdp"), lax.axis_index("seq")
    into = [sems.copy(tokens.at[me_seq], bounce_x)] + [sems.copy(shards[w], bounces[w]) for w in range(count)]
    outof = [sems.copy(bounce_x, x_out.at[0])] + [sems.copy(bounces[w], fulls[w].at[me]) for w in range(count)]
    gather = Gather(sizes, shards, lambda w, q: fulls[w].at[q], sems, gather_order(sizes, shards))
    start_all(into)
    meet(all_partners(sizes))
    blocks = [sems.remote(tokens.at[flip(me_seq, k)], x_out.at[k], "seq", k) for k in range(1, seq)]
    start_all(blocks)
    gather.start()
    last = []
    for _, copies in gather.finish_far():
        last += copies
    wait_all(into)
    start_all(outof)
    for copy in gather.pending:
        copy.wait_send()
    wait_all(last)
    wait_all(blocks)
    wait_all(outof)


def enter(sizes, tokens, shards):
    fsdp = sizes[0]
    count = len(shards)
    hbm = lambda shape: struct(bf16, *shape)
    copies = sizes[2] - 1 + Gather.count(sizes, gather_order(sizes, shards), count)
    return pl.pallas_call(
        functools.partial(enter_kernel, sizes, count),
        in_specs=[ANY] * (1 + count),
        out_specs=[ANY] * (1 + count),
        out_shape=[hbm(tokens.shape)] + [hbm((fsdp,) + s.shape) for s in shards],
        scratch_shapes=[pltpu.VMEM(tokens.shape[1:], bf16)]
        + [pltpu.VMEM(s.shape, bf16) for s in shards]
        + sem_shapes(copies, 2 * (1 + count)),
        compiler_params=pltpu.CompilerParams(collective_id=0, has_side_effects=True),
    )(tokens, *shards)


def turn(row):
    n = row.shape[1]
    diagonal = lax.broadcasted_iota(jnp.int32, (n, n), 0) == lax.broadcasted_iota(jnp.int32, (n, n), 1)
    return jnp.sum(jnp.where(diagonal, row, 0), axis=1, keepdims=True)


def enter_project_kernel(sizes, count, tokens, segments, *refs):
    fsdp, rep, seq = sizes
    refs = list(refs)
    pop = lambda n: [refs.pop(0) for _ in range(n)]
    shards = pop(count)
    x_out, a_out, qkv_out, cos_out, sin_out, marks_out, row_out, gains_out, wq_out = pop(9)
    fulls = [None, None] + pop(count - 2)
    xs, a, qkv, wq, gains = pop(5)
    bounces = pop(count)
    sems = Sems(*refs)
    me, me_seq = lax.axis_index("fsdp"), lax.axis_index("seq")
    shard_rows, rows = shards[1].shape[0], xs.shape[1]
    columns = wq.shape[1]

    def place(w, q):
        if w == 0:
            return gains.at[q]
        if w == 1:
            return wq.at[pl.ds(pl.multiple_of(q * shard_rows, 16), shard_rows)]
        return fulls[w].at[q]

    own = sems.copy(tokens.at[me_seq], xs.at[0])
    into = [sems.copy(shards[w], place(w, me) if w < 2 else bounces[w - 2]) for w in range(count)]
    outof = [sems.copy(bounces[w - 2], place(w, me)) for w in range(2, count)]
    blocks = [sems.remote(tokens.at[flip(me_seq, k)], xs.at[k], "seq", k) for k in range(1, seq)]
    stores = [
        [sems.copy(src.at[k], dst.at[k]) for src, dst in ((xs, x_out), (a, a_out), (qkv, qkv_out))] for k in range(seq)
    ]
    keep = sems.copy(wq, wq_out)
    gather = Gather(sizes, shards, place, sems, gather_order(sizes, shards))
    own.start()
    start_all(into)
    meet(all_partners(sizes))
    gather.start()
    start_all(blocks)

    lane = lax.broadcasted_iota(jnp.int32, (1, PAIR), 1)
    rate = jnp.exp((lane % (HDIM // 2)).astype(f32) * (-2.0 * math.log(THETA) / HDIM))
    sign = jnp.where(lane_halves((1, PAIR)), -1.0, 1.0)
    batch = segments.shape[1]

    def own_segments(block):
        at = pl.multiple_of(block * rows, 128)
        return segments[me_seq // batch, pl.ds(me_seq % batch, 1), pl.ds(at, rows)]

    for k in range(seq):
        block = flip(me_seq, k)
        piece = slice(k * rows, (k + 1) * rows)
        row = own_segments(block)
        column = turn(row)
        earlier = jnp.zeros((rows, 1), jnp.int32)
        for other in range(seq):
            earlier += jnp.sum((own_segments(other) < column).astype(jnp.int32), axis=1, keepdims=True)
        index = block * rows + lax.broadcasted_iota(jnp.int32, (rows, 1), 0)
        angles = (index - earlier).astype(f32) * rate
        cos_out[piece, :] = jnp.cos(angles)
        sin_out[piece, :] = jnp.sin(angles) * sign
        marks_out[piece, :] = column
        row_out[:, piece] = row

    last = {}
    far = gather.finish_far()
    for w, copies in far:
        last[w] = copies
        if len(last) == 2:
            break
    assert sorted(last) == [0, 1]
    for copy in into[:2] + last[0] + last[1]:
        copy.wait()
    keep.start()
    total = gains[0, :2, :].astype(f32)
    for q in range(1, fsdp):
        total = total + gains[q, :2, :].astype(f32)
    gains_out[...] = total

    def project(k):
        if k == 0:
            own.wait()
        else:
            blocks[k - 1].wait()
        piece = slice(k * rows, (k + 1) * rows)
        unit, _ = normalize(xs[k].astype(f32))
        low = (unit * total[:1]).astype(bf16)
        a[k] = low
        cosine, sine = cos_out[piece, :], sin_out[piece, :]

        @pl.loop(0, 2 * D // WIDE)
        def _(i):
            at = pl.multiple_of(i * WIDE, WIDE)
            part = dot_nn(low, wq[:, pl.ds(at, WIDE)])
            scale = jnp.where(at < D, QUERY_SCALE, 1.0)
            for half in range(0, WIDE, PAIR):
                value = rotate_pair(part[:, half : half + PAIR], cosine, sine) * scale
                qkv[k, :, pl.ds(at + half, PAIR)] = value.astype(bf16)

        qkv[k, :, 2 * D :] = dot_nn(low, wq[:, 2 * D :]).astype(bf16)
        start_all(stores[k])

    project(0)
    project(1)
    for w, copies in far:
        last[w] = copies
        if w == 2:
            wait_all(into[2:])
            start_all(outof)
    for k in range(2, seq):
        project(k)
    for copy in gather.pending:
        copy.wait_send()
    for w in range(2, count):
        wait_all(last[w])
    wait_all(outof)
    for group in stores:
        wait_all(group)
    keep.wait()


def enter_project(sizes, tokens, segments, shards):
    fsdp, rep, seq = sizes
    count, rows = len(shards), tokens.shape[1]
    length, columns = seq * rows, shards[1].shape[1]
    vmem = pl.BlockSpec(memory_space=pltpu.VMEM)
    copies = seq - 1 + Gather.count(sizes, gather_order(sizes, shards), count)
    return pl.pallas_call(
        functools.partial(enter_project_kernel, sizes, count),
        in_specs=[ANY, vmem] + [ANY] * count,
        out_specs=[ANY] * 3 + [vmem] * 5 + [ANY] * (count - 1),
        out_shape=[struct(bf16, seq, rows, D), struct(bf16, seq, rows, D), struct(bf16, seq, rows, columns),
                   struct(f32, length, PAIR), struct(f32, length, PAIR), struct(jnp.int32, length, 1),
                   struct(jnp.int32, 1, length), struct(f32, 2, D), struct(bf16, D, columns)]
        + [struct(bf16, fsdp, *s.shape) for s in shards[2:]],
        scratch_shapes=[pltpu.VMEM((seq, rows, D), bf16), pltpu.VMEM((seq, rows, D), bf16),
                        pltpu.VMEM((seq, rows, columns), bf16), pltpu.VMEM((D, columns), bf16),
                        pltpu.VMEM((fsdp,) + shards[0].shape, bf16)]
        + [pltpu.VMEM(s.shape, bf16) for s in shards[2:]] + [pltpu.VMEM((16, 128), bf16)] * 2
        + sem_shapes(copies, 2 + count + count - 2 + 3 * seq),
        compiler_params=pltpu.CompilerParams(
            collective_id=4, has_side_effects=True, vmem_limit_bytes=VMEM_LIMIT
        ),
    )(tokens, segments, *shards)


class Reducer:
    def __init__(self, parts_shape, sizes, order):
        self.fsdp, self.rows, self.cols = parts_shape
        self.steps = []
        held, rows, cols = list(range(self.fsdp)), self.rows, self.cols
        row_at, col_at = [], []
        for axis, bit in order:
            step = dict(axis=axis, bit=bit, row_at=list(row_at), col_at=list(col_at), rows=rows, cols=cols)
            if axis == "fsdp":
                step["send"] = [j for j in held if j & bit]
                held = [j for j in held if not j & bit]
                step["keep"] = held
                step["shape"] = (len(held), rows, cols)
                step["split"] = None
            else:
                step["keep"] = step["send"] = held
                if (axis, bit) == order[-1]:
                    step["split"] = "none"
                elif (rows // 2) % 16 == 0:
                    rows //= 2
                    row_at = row_at + [(axis, bit, rows)]
                    step["split"] = "rows"
                elif (cols // 2) % 128 == 0:
                    cols //= 2
                    col_at = col_at + [(axis, bit, cols)]
                    step["split"] = "cols"
                else:
                    step["split"] = "none"
                step["shape"] = (len(held), rows, cols)
            self.steps.append(step)
        self.down = len(self.steps)
        for step in reversed(self.steps[: self.down]):
            if step["split"] in ("rows", "cols"):
                self.steps.append(dict(step, up=True))

    @staticmethod
    def offset(terms, align, last=None):
        total = 0
        for i, (axis, bit, extent) in enumerate(terms):
            half = (lax.axis_index(axis) // bit) % 2
            if last == i:
                half = 1 - half
            total = total + half * extent
        return total if isinstance(total, int) else pl.multiple_of(total, align)

    def region(self, step, after, other=False):
        row_at, col_at, rows, cols = step["row_at"], step["col_at"], step["rows"], step["cols"]
        row_last = col_last = None
        if after:
            if step["split"] == "rows":
                rows //= 2
                row_at = row_at + [(step["axis"], step["bit"], rows)]
                row_last = len(row_at) - 1 if other else None
            elif step["split"] == "cols":
                cols //= 2
                col_at = col_at + [(step["axis"], step["bit"], cols)]
                col_last = len(col_at) - 1 if other else None
        return (
            pl.ds(self.offset(row_at, 16, row_last), rows),
            pl.ds(self.offset(col_at, 128, col_last), cols),
        )

    def scratch(self, first, last):
        return [pltpu.VMEM(s["shape"], bf16) for s in self.steps[first:last] if "up" not in s]

    def copies(self, first, last):
        return sum(1 if "up" in s else len(s["send"]) for s in self.steps[first:last])

    def bind(self, parts, lands, sems, first, last, final=None):
        self.parts, self.sems, self.final = parts, sems, final
        self.lands, self.moves = {}, {}
        lands = list(lands)
        for s in range(first, last):
            step = self.steps[s]
            moves = []
            if "up" in step:
                there = final.at[self.region(step, True)]
                moves.append(sems.remote(there, there, step["axis"], step["bit"]))
            else:
                land = self.lands[s] = lands.pop(0)
                for i, j in enumerate(step["send"]):
                    fsdp = step["axis"] == "fsdp"
                    src = self.parts(j).at[self.region(step, not fsdp, not fsdp)]
                    moves.append(sems.remote(src, land.at[i], step["axis"], step["bit"]))
            self.moves[s] = moves

    def start(self, s):
        if s == self.down:
            region = self.region(self.steps[s - 1], True)
            self.final[region] = self.parts(0)[region]
        start_all(self.moves.get(s, []))

    def finish(self, s):
        step = self.steps[s]
        self.finish_step(s, step)
        if s + 1 == len(self.steps) == self.down and self.final is not None:
            self.final[...] = self.parts(0)[...]

    def finish_step(self, s, step):
        for i, move in enumerate(self.moves[s]):
            move.wait()
            if "up" not in step:
                j = step["keep"][i]
                ref = self.parts(j)
                region = self.region(step, True)
                ref[region] = (ref[region].astype(f32) + self.lands[s][i].astype(f32)).astype(bf16)


def give_back(slots, home, bounce, sems):
    me = lax.axis_index("seq")
    seq = slots.shape[0]
    return (
        sems.copy(slots.at[0], bounce),
        sems.copy(bounce, home.at[me]),
        [sems.remote(slots.at[k], home.at[me], "seq", k) for k in range(1, seq)],
    )


def body(sizes, tokens, segments, positions, gain_attn, w_qkv, w_out, gain_mlp, w_in, w_mlp_out, cotangent):
    fsdp, rep, seq = sizes
    micro, batch, rows, _ = tokens.shape
    assert micro * batch == seq and rows % TILE == 0
    length = seq * rows
    me_seq, me_fsdp = lax.axis_index("seq"), lax.axis_index("fsdp")

    own_gains = jnp.zeros((16, D), bf16)
    own_gains = lax.dynamic_update_slice(own_gains, jnp.stack([gain_attn, gain_mlp]), (0, me_fsdp * (D // fsdp)))
    shards = [own_gains, w_qkv, w_out, w_mlp_out, w_in]
    tiles, pairs = length // TILE, HEADS // 2
    if (D // fsdp) % 16 == 0:
        x, a, qkv, cosine, sine, marks_column, marks_row, gains, wq, wo, wm, wi = enter_project(
            sizes, tokens.reshape(seq, rows, D), segments, shards
        )
        x, a, qkv = (v.reshape(length, -1) for v in (x, a, qkv))
        wo, wm, wi = (w.reshape(-1, w.shape[-1]) for w in (wo, wm, wi))
    else:
        x, gains, wq, wo, wm, wi = enter(sizes, tokens.reshape(seq, rows, D), shards)
        x = x.reshape(length, D)
        gains = jnp.sum(gains[:, :2].astype(f32), axis=0)
        wq, wo, wm, wi = (w.reshape(-1, w.shape[-1]) for w in (wq, wo, wm, wi))

        marks = take(segments.reshape(seq, length), me_seq)
        place = jnp.arange(length, dtype=jnp.int32) - jnp.sum(
            (marks[None, :] < marks[:, None]).astype(jnp.int32), axis=1
        )
        slot_order = [me_seq ^ k for k in range(seq)]
        marks = jnp.concatenate([take(marks.reshape(seq, rows), s) for s in slot_order])
        place = jnp.concatenate([take(place.reshape(seq, rows), s) for s in slot_order])
        half = jnp.arange(0, HDIM, 2).astype(f32) / HDIM
        angles = place.astype(f32)[:, None] * jnp.exp(-half * math.log(THETA))
        cosine, sine = jnp.cos(angles), jnp.sin(angles)
        cosine = jnp.concatenate([cosine] * 4, -1)
        sine = jnp.concatenate([-sine, sine] * 2, -1)

        a, qkv = call(
            first_kernel, tiles,
            [rows_spec(D), whole_spec(2, D), whole_spec(D, 3 * D), rows_spec(PAIR), rows_spec(PAIR)],
            [rows_spec(D), rows_spec(3 * D)],
            [struct(bf16, length, D), struct(bf16, length, 3 * D)],
            2 * length * D * 3 * D,
        )(x, gains, wq, cosine, sine)
        marks_column, marks_row = marks[:, None], marks[None, :]

    vmem = pl.BlockSpec(memory_space=pltpu.VMEM)
    pair_at = lambda offset, lag, n: pl.BlockSpec(
        (length, PAIR), lambda i: (0, jnp.clip(i - lag, 0, n - 1) + offset)
    )
    prob_at = lambda lag: pl.BlockSpec((2, length, length), lambda i: (jnp.clip(i - lag, 0, pairs - 1), 0, 0))
    tile_at = lambda width, lag: pl.BlockSpec((TILE, width), lambda i: (jnp.clip(i - lag, 0, tiles - 1), 0))
    slots = struct(bf16, seq, rows, D)
    o, probs, inv, x1, b, m, slope, act, y, dy = call(
        functools.partial(forward_kernel, sizes, pairs), pairs + tiles,
        [pair_at(0, 0, pairs), pair_at(pairs, 0, pairs), pair_at(2 * pairs, 0, pairs),
         whole_spec(length, 1), whole_spec(1, length), tile_at(D, pairs), whole_spec(2, D)] + [ANY] * 4,
        [pair_at(0, 0, pairs), prob_at(0), pair_at(0, 0, pairs), tile_at(D, pairs), tile_at(D, pairs)]
        + [tile_at(FF, pairs)] * 3 + [tile_at(D, pairs), ANY],
        [struct(bf16, length, D), struct(bf16, HEADS, length, length), struct(f32, length, D),
         struct(f32, length, D), struct(bf16, length, D), struct(bf16, length, FF),
         struct(bf16, length, FF), struct(bf16, length, FF), struct(bf16, length, D), slots],
        16 * length * length * D,
        [pltpu.VMEM((length, D), bf16), pltpu.VMEM((D, D), bf16), pltpu.VMEM((D, 2 * FF), bf16), pltpu.VMEM((FF, D), bf16),
         pltpu.VMEM((rows, D), bf16)] + sem_shapes(seq - 1, 5), 1,
    )(qkv, qkv, qkv, marks_column, marks_row, x, gains, wo, wi, wm, cotangent.reshape(seq, rows, D))

    reducers, early = early_reducers(sizes)
    whole = late_reducers(sizes)
    own_shard = lambda r: struct(bf16, r.rows, r.cols)
    full_shard = lambda r: pltpu.VMEM((fsdp, r.rows, r.cols), bf16)
    odd = (FF // fsdp) % 16 or (D // fsdp) % 16
    wide = pltpu.VMEM((FF, FF) if odd else (8, 128), f32)
    dx1, dgain_two, dq, dk, dv, block_out, *sums = call(
        functools.partial(backward_kernel, sizes, tiles), tiles + 1 + pairs,
        [tile_at(D, 0), tile_at(FF, 0), tile_at(FF, 0), whole_spec(2, D)]
        + [pair_at(n * pairs, tiles + 1, pairs) for n in range(3)]
        + [pair_at(0, tiles + 1, pairs), pair_at(0, tiles + 1, pairs), prob_at(tiles + 1),
           whole_spec(length, PAIR), whole_spec(length, PAIR)] + [ANY] * 8,
        [tile_at(D, 0), whole_spec(1, D)] + [pair_at(0, tiles + 1, pairs)] * 3 + [ANY] * (1 + len(reducers)),
        [struct(f32, length, D), struct(f32, 1, D)] + [struct(bf16, length, D)] * 3 + [slots]
        + [own_shard(r) for r in reducers],
        32 * length * length * D,
        [pltpu.VMEM((D, D), bf16), pltpu.VMEM((D, 2 * FF), bf16), pltpu.VMEM((FF, D), bf16),
         pltpu.VMEM((length, FF), bf16)] + [pltpu.VMEM((length, D), bf16)] * 3
        + [pltpu.VMEM((length, 2 * FF), bf16), pltpu.VMEM((length, D), bf16), pltpu.VMEM((length, D), bf16),
           wide, pltpu.VMEM((rows, D), bf16)]
        + [full_shard(r) for r in reducers] + [pltpu.VMEM((reducers[0].rows, reducers[0].cols), bf16)]
        + [land for r, e in zip(reducers, early) for land in r.scratch(0, e)]
        + sem_shapes(seq - 1 + sum(r.copies(0, e) for r, e in zip(reducers, early)), 9 + len(reducers)), 2,
    )(x1, slope, act, gains, qkv, qkv, qkv, o, inv, probs, cosine, sine,
      wo, wi, wm, m, dy.reshape(length, D), b, o, y.reshape(seq, rows, D))

    hops = sum(len(bits_of(n)) for n in sizes)
    shard = lambda n, width: struct(bf16, n // fsdp, width)
    finals = [shard(D, 2 * FF), shard(D, D), shard(D, 3 * D)]
    operands = [dq, a, dk, dv, wq, x, dx1]
    grad_mlp, *sums = sums
    reducers, early = reducers[1:], early[1:]
    input_grad, grad_in, grad_out, grad_qkv, dgains = pl.pallas_call(
        functools.partial(leave_kernel, sizes),
        in_specs=[vmem] * 2 + [ANY] * (len(operands) + len(reducers)),
        out_specs=[ANY] * 4 + [vmem],
        out_shape=[slots] + finals + [struct(f32, 8, D)],
        scratch_shapes=[pltpu.VMEM(v.shape, v.dtype) for v in operands]
        + [pltpu.VMEM((seq, rows, D), bf16), wide]
        + [pltpu.VMEM(v.shape, v.dtype) for v in finals]
        + [pltpu.VMEM((r.rows, r.cols), bf16) for r in reducers]
        + [full_shard(r) for r in whole]
        + [land for r, e in zip(reducers, early) for land in r.scratch(e, len(r.steps))]
        + [land for r in whole for land in r.scratch(0, len(r.steps))]
        + [pltpu.VMEM((hops, 8, D), f32)]
        + sem_shapes(
            PIECES * (seq - 1) + hops + sum(r.copies(e, len(r.steps)) for r, e in zip(reducers, early))
            + sum(r.copies(0, len(r.steps)) for r in whole),
            1 + len(operands) + len(reducers) + len(finals),
        ),
        compiler_params=pltpu.CompilerParams(
            collective_id=3, has_side_effects=True, vmem_limit_bytes=VMEM_LIMIT
        ),
    )(gains, dgain_two, *operands, *sums)
    dgains = lax.dynamic_slice_in_dim(dgains, me_fsdp * (D // fsdp), D // fsdp, 1)
    return (
        block_out.reshape(tokens.shape),
        input_grad.astype(f32).reshape(tokens.shape),
        dgains[0],
        grad_qkv.astype(f32),
        grad_out.astype(f32),
        dgains[1],
        grad_in.astype(f32),
        grad_mlp.astype(f32),
    )


def solution(mesh):
    sizes = (mesh.shape["fsdp"], mesh.shape["rep"], mesh.shape["seq"])
    wide = P(None, ("rep", "fsdp"), "seq", None)
    placed = (
        wide, P(None, ("rep", "fsdp"), None), P(None, ("rep", "fsdp"), "seq"),
        P("fsdp"), P("fsdp", None), P("fsdp", None), P("fsdp"), P("fsdp", None), P("fsdp", None), wide,
    )
    return jax.shard_map(
        functools.partial(body, sizes),
        mesh=mesh,
        in_specs=placed,
        out_specs=(
            wide, wide, P("fsdp"), P("fsdp", None), P("fsdp", None), P("fsdp"), P("fsdp", None), P("fsdp", None),
        ),
        check_vma=False,
    )
```

```python
import functools
import math

import jax
import jax.numpy as jnp
from jax import lax
from jax.experimental import pallas as pl
from jax.experimental.pallas import tpu as pltpu
from jax.sharding import PartitionSpec as P

D = 768
HEADS = 12
HDIM = 64
FF = 1152
EPS = 1e-05
THETA = 160000.0
MASKED = -1000000000.0
QUERY_SCALE = HDIM**-0.5 / math.log(2.0)
TILE = 256
PAIR = 2 * HDIM
WIDE = 384
HCHUNK = 384
f32 = jnp.float32
bf16 = jnp.bfloat16
VMEM_LIMIT = 62 * 2**20


def dot_nn(left, right):
    return lax.dot_general(left, right, (((1,), (0,)), ((), ())), preferred_element_type=f32)


def dot_nt(left, right):
    return lax.dot_general(left, right, (((1,), (1,)), ((), ())), preferred_element_type=f32)


def dot_tn(left, right):
    return lax.dot_general(left, right, (((0,), (0,)), ((), ())), preferred_element_type=f32)


def normalize(values):
    mean = jnp.mean(values, axis=-1, keepdims=True)
    centered = values - mean
    var = jnp.mean(centered * centered, axis=-1, keepdims=True)
    scale = lax.rsqrt(var + EPS)
    return centered * scale, scale


def norm_back(unit, scale, gain, grad):
    gain_terms = grad * unit
    inner = grad * gain
    first = jnp.mean(inner, axis=-1, keepdims=True)
    second = jnp.mean(inner * unit, axis=-1, keepdims=True)
    return scale * (inner - first - unit * second), gain_terms


def lane_halves(shape):
    lane = lax.broadcasted_iota(jnp.int32, shape, len(shape) - 1)
    return lane % HDIM < HDIM // 2


def rotate_pair(values, cosine, signed_sine):
    swapped = jnp.where(
        lane_halves(values.shape),
        pltpu.roll(values, PAIR - HDIM // 2, 1),
        pltpu.roll(values, HDIM // 2, 1),
    )
    return values * cosine + swapped * signed_sine


def first_kernel(x_ref, gain_ref, w_ref, cos_ref, sin_ref, a_ref, qkv_ref):
    unit, _ = normalize(x_ref[...].astype(f32))
    a = (unit * gain_ref[0:1, :]).astype(bf16)
    a_ref[...] = a
    cosine, sine = cos_ref[...], sin_ref[...]
    for column in range(0, 3 * D, TILE):
        part = dot_nn(a, w_ref[:, column : column + TILE])
        for half in range(0, TILE, PAIR):
            start = column + half
            piece = part[:, half : half + PAIR]
            if start < 2 * D:
                piece = rotate_pair(piece, cosine, sine)
            if start < D:
                piece = piece * QUERY_SCALE
            qkv_ref[:, start : start + PAIR] = piece.astype(bf16)


def head_lanes():
    lane = lax.broadcasted_iota(jnp.int32, (1, PAIR), 1)
    return [lane < HDIM, lane >= HDIM]


def attend_pair(q_ref, k_ref, v_ref, rows_ref, cols_ref, p_ref, inv_ref, write):
    k, v = k_ref[...], v_ref[...]
    length = k.shape[0]
    mine = head_lanes()
    zero, one = jnp.zeros((), bf16), jnp.ones((), bf16)
    summing = [jnp.where(m, v, one) for m in mine]
    items = [(tile, head) for tile in range(0, length, TILE) for head in range(2)]

    def score(item):
        tile, head = item
        return dot_nt(jnp.where(mine[head], q_ref[tile : tile + TILE, :], zero), k)

    ahead = score(items[0])
    kept = None
    for i, (tile, head) in enumerate(items):
        rows = slice(tile, tile + TILE)
        scores = ahead
        if i + 1 < len(items):
            ahead = score(items[i + 1])
        scores = jnp.where(rows_ref[rows, :] == cols_ref[...], scores, MASKED)
        probs = jnp.exp2(scores - jnp.max(scores, axis=-1, keepdims=True)).astype(bf16)
        p_ref[head, rows, :] = probs
        part = dot_nn(probs, summing[head])
        inv = 1.0 / pltpu.roll(part, HDIM, 1)
        if head == 0:
            kept = (part * inv, inv)
        else:
            inv_ref[rows, :] = jnp.where(mine[0], kept[1], inv)
            write(rows, jnp.where(mine[0], kept[0], part * inv).astype(bf16))


def forward_kernel(
    sizes, pairs, late, q_ref, k_ref, v_ref, rows_ref, cols_ref, x_ref, gain_ref, w_out_any, w_in_any, w_mlp_any, cot_ref,
    o_ref, p_ref, inv_ref, x1_ref, b_ref, m_ref, slope_ref, act_ref, y_ref, dy_ref, *refs,
):
    seq = sizes[2]
    refs = list(refs)
    outs = [refs.pop(0) for _ in range(2 * late)]
    joined, w_out_ref, w_in_ref, w_mlp_ref, bounce, *sem_refs = refs
    step, last = pl.program_id(0), pl.num_programs(0) - 1
    sems = Sems(*sem_refs)
    me_seq = lax.axis_index("seq")
    into = sems.copy(cot_ref.at[me_seq], bounce)
    outof = sems.copy(bounce, dy_ref.at[0])
    weights = [sems.copy(w_out_any, w_out_ref)]
    partners = [("seq", k) for k in range(1, seq)]
    if late:
        gather = LateGather(sizes, [w_in_any, w_mlp_any], [w_in_ref, w_mlp_ref], sems)
        weights += gather.own
        keeps = [sems.copy(w_in_ref, outs[0]), sems.copy(w_mlp_ref, outs[1])]
        partners = all_partners(sizes)
    else:
        weights += [sems.copy(w_in_any, w_in_ref), sems.copy(w_mlp_any, w_mlp_ref)]
    blocks = [sems.remote(cot_ref.at[flip(me_seq, k)], dy_ref.at[k], "seq", k) for k in range(1, seq)]

    @pl.when(step == 0)
    def _():
        into.start()
        start_all(weights)
        meet(partners)
        if late:
            start_all(gather.far)
        start_all(blocks)
        into.wait()
        outof.start()

    if late:
        for when in range(1, pairs + 1):
            @pl.when(step == when)
            def _(when=when):
                gather.advance(when)

    @pl.when(step < pairs)
    def _():
        def write(rows, value):
            o_ref[rows, :] = value
            joined[rows, pl.ds(pl.multiple_of(step * PAIR, PAIR), PAIR)] = value

        attend_pair(q_ref, k_ref, v_ref, rows_ref, cols_ref, p_ref, inv_ref, write)

    @pl.when(step == pairs)
    def _():
        if late:
            wait_all(weights[:1])
            gather.finish(0)
            keeps[0].start()
        else:
            wait_all(weights)

    @pl.when(step >= pairs)
    def _():
        start = pl.multiple_of((step - pairs) * TILE, TILE)
        x1 = x_ref[...].astype(f32) + dot_nn(joined[pl.ds(start, TILE), :], w_out_ref[...])
        x1_ref[...] = x1
        unit, _ = normalize(x1)
        b = (unit * gain_ref[1:2, :]).astype(bf16)
        b_ref[...] = b

        def hidden(column):
            return (
                dot_nn(b, w_in_ref[:, column : column + HCHUNK]),
                dot_nn(b, w_in_ref[:, FF + column : FF + column + HCHUNK]),
            )

        ahead = hidden(0)
        for column in range(0, FF, HCHUNK):
            hin, gate = ahead
            if column + HCHUNK < FF:
                ahead = hidden(column + HCHUNK)
            phi = 0.5 + 0.5 * lax.erf(hin * math.sqrt(0.5))
            act = hin * phi
            slope = phi + hin * (jnp.exp(hin * hin * -0.5) * (1.0 / math.sqrt(2.0 * math.pi)))
            m_ref[:, column : column + HCHUNK] = (act * gate).astype(bf16)
            act_ref[:, column : column + HCHUNK] = act.astype(bf16)
            slope_ref[:, column : column + HCHUNK] = (slope * gate).astype(bf16)
        if late:
            @pl.when(step == pairs)
            def _():
                gather.finish(1)
                keeps[1].start()

        y_ref[...] = (x1_ref[...] + dot_nn(m_ref[...], w_mlp_ref[...])).astype(bf16)

    @pl.when(step == last)
    def _():
        if late:
            wait_all(keeps)
        outof.wait()
        wait_all(blocks)


def order_of(sizes, rep_first):
    fsdp, rep, seq = sizes
    core = [("fsdp", 1)]
    rest = [("fsdp", b) for b in bits_of(fsdp)[1:]]
    copies = [("rep", b) for b in bits_of(rep)]
    return core + (copies + rest if rep_first else rest + copies) + [("seq", b) for b in bits_of(seq)]


def all_partners(sizes):
    fsdp, rep, seq = sizes
    return [("seq", k) for k in range(1, seq)] + [("fsdp", b) for b in bits_of(fsdp)] + [("rep", b) for b in bits_of(rep)]


def early_reducers(sizes):
    fsdp, rep, seq = sizes
    shapes = [(fsdp, FF // fsdp, D), (fsdp, D // fsdp, FF), (fsdp, D // fsdp, FF), (fsdp, D // fsdp, D)]
    reducers = [Reducer(shape, sizes, order_of(sizes, w == 2)) for w, shape in enumerate(shapes)]
    across = len(bits_of(fsdp)) + len(bits_of(rep))
    return reducers, [len(reducers[0].steps)] + [across + 2] * 2 + [across + 1]


def late_reducers(sizes):
    fsdp = sizes[0]
    return [Reducer((fsdp, D // fsdp, D), sizes, order_of(sizes, w == 1)) for w in range(3)]


def flat(rows):
    return rows % 16 == 0


def shard_of(ref, rows, q):
    return ref.at[pl.ds(pl.multiple_of(q * rows, 16), rows)] if flat(rows) else ref.at[q]


def weight_gradient(ref, wide, left, right):
    if len(ref.shape) == 2:
        @pl.loop(0, ref.shape[0] // HCHUNK)
        def _(i):
            at = pl.ds(pl.multiple_of(i * HCHUNK, HCHUNK), HCHUNK)
            ref[at, :] = dot_tn(left[:, at], right[...]).astype(bf16)
    else:
        shards, rows, cols = ref.shape
        wide[: shards * rows, :cols] = dot_tn(left[...], right[...])
        for q in range(shards):
            ref[q] = wide[q * rows : (q + 1) * rows, :cols].astype(bf16)


def middle_back_tile(dy, x1_ref, slope_ref, act_ref, gain_ref, w_out_ref, w_in_ref, w_mlp_ref, dh_ref, dgain_ref, dx1_ref):
    ahead = dot_nt(dy, w_mlp_ref[:HCHUNK, :])
    for column in range(0, FF, HCHUNK):
        dm = ahead
        if column + HCHUNK < FF:
            ahead = dot_nt(dy, w_mlp_ref[column + HCHUNK : column + 2 * HCHUNK, :])
        dh_ref[:, column : column + HCHUNK] = (dm * slope_ref[:, column : column + HCHUNK].astype(f32)).astype(bf16)
        dh_ref[:, FF + column : FF + column + HCHUNK] = (
            dm * act_ref[:, column : column + HCHUNK].astype(f32)
        ).astype(bf16)
    db = dot_nt(dh_ref[...], w_in_ref[...])
    unit, scale = normalize(x1_ref[...])
    back, terms = norm_back(unit, scale, gain_ref[1:2, :], db)
    dgain_ref[...] += jnp.sum(terms, axis=0, keepdims=True)
    dx1 = dy.astype(f32) + back
    dx1_ref[...] = dx1
    return dx1.astype(bf16)


def attend_back_pair(q_ref, k_ref, v_ref, o_ref, inv_ref, do, p_ref, cos_ref, sin_ref, dq_ref, dk_ref, dv_ref):
    v = v_ref[...]
    length = v.shape[0]
    mine = head_lanes()
    zero = jnp.zeros((), bf16)
    do = (do.astype(f32) * inv_ref[...]).astype(bf16)
    inner = do.astype(f32) * o_ref[...].astype(f32)
    do_heads = [jnp.where(m, do, zero) for m in mine]
    q_heads = [jnp.where(m, q_ref[...], zero).T for m in mine]
    k_heads = [jnp.where(m, k_ref[...], zero) for m in mine]
    do_turned = [d.T for d in do_heads]
    cosine, sine = cos_ref[...], sin_ref[...]
    dv = dk = None
    for tile in range(0, length, TILE):
        rows = slice(tile, tile + TILE)
        dq = None
        for head in range(2):
            probs = p_ref[head, rows, :]
            delta = jnp.sum(jnp.where(mine[head], inner[rows], 0.0), axis=-1, keepdims=True)
            dp = dot_nt(do_heads[head][rows], v)
            ds = (probs.astype(f32) * (dp - delta)).astype(bf16)
            value_part = dot_nn(do_turned[head][:, rows], probs)
            key_part = dot_nn(q_heads[head][:, rows], ds)
            query_part = dot_nn(ds, k_heads[head])
            dv = value_part if dv is None else dv + value_part
            dk = key_part if dk is None else dk + key_part
            dq = query_part if dq is None else dq + query_part
        dq_ref[rows, :] = rotate_pair(dq * HDIM**-0.5, cosine[rows], -sine[rows]).astype(bf16)
    dk_ref[...] = rotate_pair(dk.T * math.log(2.0), cosine, -sine).astype(bf16)
    dv_ref[...] = dv.T.astype(bf16)


def backward_kernel(
    sizes, tiles, x1_ref, slope_ref, act_ref, gain_ref, q_ref, k_ref, v_ref, o_ref, inv_ref,
    p_any, cos_any, sin_any, w_out_any, w_in_any, w_mlp_any, m_any, dy_any, b_any, o_any, y_ref, *refs,
):
    reducers, early = early_reducers(sizes)
    count = len(reducers)
    refs = list(refs)
    pop = lambda n: [refs.pop(0) for _ in range(n)]
    dx1_ref, dgain_ref, dq_ref, dk_ref, dv_ref, home_ref = pop(6)
    sums_out = pop(count)
    w_out_ref, w_in_ref, w_mlp_ref, m_ref, dy_ref, b_ref, all_o_ref = pop(7)
    dh_ref, low_ref, do_ref, wide, bounce, probs_ref, cos_ref, sin_ref = pop(8)
    grads = pop(count)
    (mlp_final,) = pop(1)
    lands = [pop(len(r.scratch(0, e))) for r, e in zip(reducers, early)]
    sems = Sems(*refs)
    me = lax.axis_index("fsdp")
    step, last = pl.program_id(0), pl.num_programs(0) - 1
    into, outof, blocks = give_back(y_ref, home_ref, bounce, sems)
    loads = [
        sems.copy(src, dst)
        for src, dst in [
            (m_any, m_ref), (dy_any, dy_ref), (w_mlp_any, w_mlp_ref), (w_in_any, w_in_ref), (w_out_any, w_out_ref),
            (b_any, b_ref), (o_any, all_o_ref), (cos_any, cos_ref), (sin_any, sin_ref),
        ]
    ]
    pair, pairs = step - tiles - 1, last - tiles
    slot_sems = [sems.local.at[sems.local_used + i] for i in range(2)]
    sems.local_used += 2

    def fetch(which, slot):
        return pltpu.make_async_copy(p_any.at[pl.ds(which * 2, 2)], probs_ref.at[slot], slot_sems[slot])
    stores = [sems.copy(mlp_final if w == 0 else shard_of(grads[w], reducers[w].rows, me), sums_out[w]) for w in range(count)]
    for w, reducer in enumerate(reducers):
        reducer.bind(lambda j, w=w: shard_of(grads[w], reducers[w].rows, flip(me, j)), lands[w], sems, 0, early[w], mlp_final if w == 0 else None)
    mlp, first_half, second_half, out = reducers

    def at(when, *actions):
        @pl.when(step == when)
        def _():
            for action in actions:
                action()

    def advance(reducer, s, limit):
        def run():
            reducer.finish(s)
            if s + 1 < limit:
                reducer.start(s + 1)
        return run

    @pl.when(step == 0)
    def _():
        start_all(loads)
        into.start()
        meet(all_partners(sizes))
        start_all(blocks)
        dgain_ref[...] = jnp.zeros_like(dgain_ref)
        wait_all(loads[:2])
        weight_gradient(grads[0], wide, m_ref, dy_ref)
        mlp.start(0)
        into.wait()
        outof.start()
        wait_all(loads[2:5])

    at(1, advance(mlp, 0, early[0]))

    @pl.when(step < tiles)
    def _():
        rows = pl.ds(pl.multiple_of(step * TILE, TILE), TILE)
        low = middle_back_tile(
            dy_ref[rows, :], x1_ref, slope_ref, act_ref, gain_ref, w_out_ref, w_in_ref, w_mlp_ref,
            dh_ref.at[rows, :], dgain_ref, dx1_ref,
        )
        low_ref[rows, :] = low
        do_ref[rows, :] = dot_nt(low, w_out_ref[...]).astype(bf16)

    across = len(bits_of(sizes[0])) + len(bits_of(sizes[1]))

    @pl.when(step == tiles)
    def _():
        wait_all(loads[5:])
        weight_gradient(grads[1], wide, b_ref, dh_ref.at[:, :FF])
        first_half.start(0)
        weight_gradient(grads[2], wide, b_ref, dh_ref.at[:, FF:])
        second_half.start(0)
        for s in range(1, across - 1):
            advance(mlp, s, early[0])()
        weight_gradient(grads[3], wide, all_o_ref, low_ref)
        out.start(0)

    @pl.when(step == tiles - 1)
    def _():
        fetch(0, 0).start()

    for slot in range(2):
        @pl.when((step > tiles) & (pair % 2 == slot))
        def _(slot=slot):
            fetch(pair, slot).wait()

            @pl.when(pair + 1 < pairs)
            def _():
                fetch(pair + 1, 1 - slot).start()

    halves = (first_half, second_half)
    steps = lambda reducer, limit, *which: [advance(reducer, s, limit) for s in which]
    half_steps = lambda *which: [advance(r, s, early[1]) for s in which for r in halves]
    middle = range(1, across - 1)
    at(tiles + 1, *steps(mlp, early[0], across - 1), *half_steps(0))
    at(tiles + 2, *steps(out, early[3], 0))
    at(tiles + 3, *half_steps(*middle))
    at(tiles + 4, *steps(mlp, early[0], across), *steps(out, early[3], *middle))
    at(tiles + 5, *steps(mlp, early[0], across + 1), *half_steps(across - 1))
    at(tiles + 6, *steps(mlp, early[0], *range(across + 2, early[0] - 1)), *half_steps(across), *steps(out, early[3], across - 1))

    @pl.when(step > tiles)
    def _():
        column = pl.multiple_of(pair * PAIR, PAIR)
        attend_back_pair(
            q_ref, k_ref, v_ref, o_ref, inv_ref, do_ref[:, pl.ds(column, PAIR)], probs_ref.at[pair % 2], cos_ref, sin_ref,
            dq_ref, dk_ref, dv_ref,
        )

    @pl.when(step == last)
    def _():
        for w, reducer in enumerate(reducers):
            reducer.finish(early[w] - 1)
            stores[w].start()
        wait_all(stores)
        outof.wait()
        wait_all(blocks)


PIECES = 4


def leave_kernel(sizes, gain_ref, other_gain_ref, *refs):
    fsdp, rep, seq = sizes
    reducers, early = (some[1:] for some in early_reducers(sizes))
    whole = late_reducers(sizes)
    count, more = len(reducers), len(whole)
    refs = list(refs)
    pop = lambda n: [refs.pop(0) for _ in range(n)]
    anys = pop(7)
    sums_in = pop(count)
    (home_ref,) = pop(1)
    in_out, out_out, qkv_out, gains_out = pop(4)
    dq_ref, a_ref, dk_ref, dv_ref, w_ref, x_ref, dx1_ref = local = pop(7)
    slots, wide, in_final, out_final, qkv_final = pop(5)
    held, grads = pop(count), pop(more)
    lands = [pop(len(r.scratch(e, len(r.steps)))) for r, e in zip(reducers, early)]
    whole_lands = [pop(len(r.scratch(0, len(r.steps)))) for r in whole]
    (gain_lands,) = pop(1)
    sems = Sems(*refs)
    me, me_seq = lax.axis_index("fsdp"), lax.axis_index("seq")
    own = sems.copy(slots.at[0], home_ref.at[me_seq])
    height = slots.shape[1] // PIECES
    blocks = {
        k: [
            sems.remote(slots.at[k, pl.ds(n * height, height)], home_ref.at[me_seq, pl.ds(n * height, height)], "seq", k)
            for n in range(PIECES)
        ]
        for k in range(1, seq)
    }
    order = sorted(range(1, seq), key=lambda k: (k != 2, k == 1))
    ready = []

    def send_piece(n=1):
        for _ in range(n):
            if ready:
                ready.pop(0).start()

    operands = [sems.copy(src, dst) for src, dst in zip(anys, local)]
    loads = [sems.copy(sums_in[w], held[w]) for w in range(count)]
    stores = [
        sems.copy(src, dst)
        for src, dst in ((in_final, in_out), (out_final, out_out), (qkv_final, qkv_out))
    ]
    finals = [in_final.at[:, pl.ds(0, FF)], in_final.at[:, pl.ds(FF, FF)], out_final]
    for w, reducer in enumerate(reducers):
        reducer.bind(lambda j, w=w: held[w], lands[w], sems, early[w], len(reducer.steps), finals[w])
    for w, reducer in enumerate(whole):
        reducer.bind(
            lambda j, w=w: shard_of(grads[w], whole[w].rows, flip(me, j)), whole_lands[w], sems, 0, len(reducer.steps),
            qkv_final.at[:, pl.ds(w * D, D)],
        )
    hops = [("fsdp", b) for b in bits_of(fsdp)] + [("rep", b) for b in bits_of(rep)] + [("seq", b) for b in bits_of(seq)]
    gain_moves = [sems.remote(gains_out, gain_lands.at[i], axis, bit) for i, (axis, bit) in enumerate(hops)]
    rows = slots.shape[1]

    def advance(some, s):
        for reducer in some:
            if s < len(reducer.steps):
                reducer.finish(s)
                if s + 1 < len(reducer.steps):
                    reducer.start(s + 1)

    def advance_gains(i):
        if i < len(hops):
            gain_moves[i].wait()
            gains_out[...] += gain_lands[i]
            if i + 1 < len(hops):
                gain_moves[i + 1].start()

    def input_slot(k):
        piece = slice(k * rows, (k + 1) * rows)
        da = dot_nt(dq_ref[piece, :], w_ref[:, :D])
        da = da + dot_nt(dk_ref[piece, :], w_ref[:, D : 2 * D])
        da = da + dot_nt(dv_ref[piece, :], w_ref[:, 2 * D :])
        unit, scale = normalize(x_ref[piece, :].astype(f32))
        back, terms = norm_back(unit, scale, gain_ref[0:1, :], da)
        gains_out[0:1, :] += jnp.sum(terms, axis=0, keepdims=True)
        slots[k] = (dx1_ref[piece, :] + back).astype(bf16)
        if k:
            ready.extend(blocks[k])

    def gradient(w, part):
        weight_gradient(grads[w], wide, a_ref, part)
        whole[w].start(0)

    across = len(bits_of(fsdp)) + len(bits_of(rep))
    halves, out, last = reducers[:2], reducers[2:], len(whole[0].steps)
    start_all(operands[:2])
    start_all(loads)
    start_all(operands[2:])
    gains_out[...] = jnp.zeros_like(gains_out)
    gains_out[1:2, :] = other_gain_ref[...]
    meet(all_partners(sizes))
    wait_all(loads)
    for w, (reducer, s) in enumerate(zip(reducers, early)):
        if s < len(reducer.steps):
            reducer.start(s)
        else:
            finals[w][...] = held[w][...]
    wait_all(operands[:2])
    gradient(0, dq_ref)
    wait_all(operands[2:])
    input_slot(order[0])
    send_piece(PIECES // 2)
    advance(whole[:1], 0)
    advance(halves, early[0])
    gradient(1, dk_ref)
    for k in order[1:2]:
        input_slot(k)
    advance(whole[1:2], 0)
    advance(out, early[2])
    send_piece()
    gradient(2, dv_ref)
    for k in order[2:]:
        input_slot(k)
    advance(whole[:1], 1)
    advance(whole[2:], 0)
    send_piece()
    input_slot(0)
    own.start()
    gain_moves[0].start()
    advance(whole[1:2], 1)
    advance(out, early[2] + 1)
    send_piece()
    for s in range(2, across):
        advance(whole[:1], s)
        advance(whole[2:], s - 1)
        advance(whole[1:2], s)
        send_piece()
    advance(whole[2:], across - 1)
    send_piece()
    i = 0
    for s in range(across, last):
        for reducer in whole:
            advance([reducer], s)
            send_piece()
        for _ in range(2):
            advance_gains(i)
            i += 1
    while i < len(hops):
        advance_gains(i)
        i += 1
    send_piece(len(ready))
    for s in range(early[0] + 1, len(halves[0].steps)):
        advance(halves, s)
    for s in range(early[2] + 2, len(out[0].steps)):
        advance(out, s)
    start_all(stores)
    wait_all(stores)
    own.wait()
    for k in range(1, seq):
        wait_all(blocks[k])


def rows_spec(width):
    return pl.BlockSpec((TILE, width), lambda i: (i, 0))


def whole_spec(*shape):
    return pl.BlockSpec(shape, lambda i: (0,) * len(shape))


def pair_spec(length, offset=0):
    return pl.BlockSpec((length, PAIR), lambda i: (0, i + offset))


def struct(dtype, *shape):
    return jax.ShapeDtypeStruct(shape, dtype)


def call(kernel, grid, in_specs, out_specs, out_shape, flops, scratch=(), collective=None):
    return pl.pallas_call(
        kernel,
        grid=(grid,),
        in_specs=in_specs,
        out_specs=out_specs,
        out_shape=out_shape,
        scratch_shapes=list(scratch),
        compiler_params=pltpu.CompilerParams(
            dimension_semantics=("arbitrary",), vmem_limit_bytes=VMEM_LIMIT,
            collective_id=collective, has_side_effects=collective is not None,
        ),
        cost_estimate=pl.CostEstimate(flops=flops, bytes_accessed=10 * 2**20, transcendentals=0),
    )


MESH = pl.DeviceIdType.MESH
ANY = pl.BlockSpec(memory_space=pl.ANY)


def take(array, index):
    return lax.dynamic_index_in_dim(array, index, 0, keepdims=False)


def flip(index, mask):
    bit = 1
    while bit <= mask:
        if mask & bit:
            index = index + bit - 2 * bit * ((index // bit) % 2)
        bit *= 2
    return index


def bits_of(size):
    return [1 << i for i in range(size.bit_length() - 1)]


def meet(partners):
    barrier = pltpu.get_barrier_semaphore()
    for axis, mask in partners:
        pl.semaphore_signal(
            barrier, inc=1, device_id={axis: flip(lax.axis_index(axis), mask)}, device_id_type=MESH
        )
    pl.semaphore_wait(barrier, len(partners))


class Sems:
    def __init__(self, send, recv, local):
        self.send, self.recv, self.local = send, recv, local
        self.remote_used = self.local_used = 0

    def remote(self, src, dst, axis, mask):
        i = self.remote_used
        self.remote_used += 1
        return pltpu.make_async_remote_copy(
            src_ref=src, dst_ref=dst, send_sem=self.send.at[i], recv_sem=self.recv.at[i],
            device_id={axis: flip(lax.axis_index(axis), mask)}, device_id_type=MESH,
        )

    def copy(self, src, dst):
        i = self.local_used
        self.local_used += 1
        return pltpu.make_async_copy(src, dst, self.local.at[i])


def sem_shapes(remote, local):
    dma = pltpu.SemaphoreType.DMA
    return [dma((remote,)), dma((remote,)), dma((max(local, 1),))]


def start_all(copies):
    for copy in copies:
        copy.start()


def wait_all(copies):
    for copy in copies:
        copy.wait()


class Gather:
    def __init__(self, sizes, shards, place, sems, order):
        self.sizes, self.shards, self.place, self.sems = sizes, shards, place, sems
        self.pieces = order
        self.me, self.me_rep = lax.axis_index("fsdp"), lax.axis_index("rep")
        self.pending = []

    def part(self, ref, pieces, n):
        width = ref.shape[-1] // (self.sizes[1] * pieces)
        start = (self.me_rep * pieces + n) * width
        return ref.at[:, pl.ds(pl.multiple_of(start, 128), width)]

    def source(self, w, h):
        return self.shards[w] if h == 0 else self.place(w, flip(self.me, h))

    def start(self):
        self.held = [0]
        self.over = self.cross(self.far_bits()[0]) if self.far_bits() else []

    def far_bits(self):
        return list(reversed(bits_of(self.sizes[0])[1:]))

    def cross(self, bit):
        over = []
        for w, pieces, n in self.pieces:
            moved = [
                self.sems.remote(
                    self.part(self.source(w, h), pieces, n),
                    self.part(self.place(w, flip(self.me, h)), pieces, n), "fsdp", bit,
                )
                for h in self.held
            ]
            start_all(moved)
            over.append(moved)
        return over

    def pass_on(self, i, bit):
        w, pieces, n = self.pieces[i]
        for copy in self.over[i]:
            copy.wait_recv()
        self.pending += self.over[i]
        passed = []
        for mask in range(1, self.sizes[1]):
            for h in self.held:
                here = self.part(self.place(w, flip(self.me, h ^ bit)), pieces, n)
                passed.append(self.sems.remote(here, here, "rep", mask))
        start_all(passed)
        self.pending += passed
        return passed

    def events(self, lag=2):
        bits = self.far_bits()
        count = len(self.pieces)
        for bit in bits[:-1]:
            passed = [self.pass_on(i, bit) for i in range(count)]
            self.held = self.held + [h ^ bit for h in self.held]
            for copies in passed:
                for copy in copies:
                    copy.wait_recv()
            self.over = self.cross(bits[bits.index(bit) + 1])
        end = {w: i for i, (w, _, _) in enumerate(self.pieces)}
        passed, near_held = [], self.held + [h ^ bit for bit in bits[-1:] for h in self.held]
        for i in range(count + lag):
            if i < count:
                if bits:
                    passed.append(self.pass_on(i, bits[-1]))
                yield None
            for w, last in end.items():
                if last == i - lag:
                    if bits:
                        for j, (other, _, _) in enumerate(self.pieces):
                            if other == w:
                                for copy in passed[j]:
                                    copy.wait_recv()
                    yield w, self.near(w, near_held)

    def near(self, w, held):
        copies = [self.sems.remote(self.source(w, h), self.place(w, flip(self.me, h)), "fsdp", 1) for h in held]
        start_all(copies)
        return copies

    @staticmethod
    def count(sizes, order, weights):
        held, copies = 1, 0
        for _ in bits_of(sizes[0])[1:]:
            copies += len(order) * held * sizes[1]
            held *= 2
        return copies + weights * held


PASSED = (0, 1, 2, 4, 6, 6, 6)
CROSSED = (4, 5)


class LateGather:
    def __init__(self, sizes, shards, wholes, sems):
        fsdp, rep, _ = sizes
        me, me_rep = lax.axis_index("fsdp"), lax.axis_index("rep")
        place = lambda w, q: shard_of(wholes[w], shards[w].shape[0], q)
        self.own = [sems.copy(shards[w], place(w, me)) for w in range(2)]
        self.far, self.passed, self.near = [], [], [[], []]
        for w in range(2):
            fits = shards[w].shape[-1] % (rep * 3 * 128) == 0
            pieces = 3 if fits else 1
            width = shards[w].shape[-1] // (rep * pieces)
            for n in range(pieces if fsdp > 2 else 0):
                cols = pl.ds(pl.multiple_of((me_rep * pieces + n) * width, 128), width)
                self.far.append(sems.remote(shards[w].at[:, cols], place(w, me).at[:, cols], "fsdp", 2))
                here = place(w, flip(me, 2)).at[:, cols]
                self.passed.append([sems.remote(here, here, "rep", mask) for mask in range(1, rep)])
            for h in range(0, fsdp, 2):
                src = shards[w] if h == 0 else place(w, flip(me, h))
                self.near[w].append(sems.remote(src, place(w, flip(me, h)), "fsdp", 1))
        self.pieces = len(self.far) // 2
        self.count = len(self.far)

    @staticmethod
    def copies(sizes):
        return 2 * (3 * sizes[1] + sizes[0] // 2)

    def pass_on(self, i):
        self.far[i].wait_recv()
        start_all(self.passed[i])

    def cross_core(self, w):
        for copies in self.passed[w * self.pieces : (w + 1) * self.pieces]:
            for copy in copies:
                copy.wait_recv()
        start_all(self.near[w])

    def advance(self, step):
        upto = lambda n: min(n, self.count)
        for i in range(upto(PASSED[step - 1]), upto(PASSED[step])):
            self.pass_on(i)
        for w in range(2):
            if step == CROSSED[w]:
                self.cross_core(w)

    def finish(self, w):
        wait_all(self.own[w : w + 1])
        for i in range(w * self.pieces, (w + 1) * self.pieces):
            self.far[i].wait_send()
            for copy in self.passed[i]:
                copy.wait_send()
        wait_all(self.near[w])


def gather_order(sizes, shards):
    fits = lambda w, n: shards[w].shape[-1] % (sizes[1] * n * 128) == 0
    split = lambda w, n: n if fits(w, n) else 1
    order = []
    for w, n in ((0, 1), (1, 3), (2, 3), (4, 3), (3, 3)):
        if w >= len(shards):
            continue
        n = split(w, n)
        order += [(w, n, i) for i in range(n)]
    return order


def enter_kernel(sizes, count, tokens, *refs):
    fsdp, rep, seq = sizes
    refs = list(refs)
    pop = lambda n: [refs.pop(0) for _ in range(n)]
    shards = pop(count)
    (x_out,) = pop(1)
    fulls = pop(count)
    (bounce_x,) = pop(1)
    bounces = pop(count)
    sems = Sems(*refs)
    me, me_seq = lax.axis_index("fsdp"), lax.axis_index("seq")
    into = [sems.copy(tokens.at[me_seq], bounce_x)] + [sems.copy(shards[w], bounces[w]) for w in range(count)]
    outof = [sems.copy(bounce_x, x_out.at[0])] + [sems.copy(bounces[w], fulls[w].at[me]) for w in range(count)]
    gather = Gather(sizes, shards, lambda w, q: fulls[w].at[q], sems, gather_order(sizes, shards))
    start_all(into)
    meet(all_partners(sizes))
    blocks = [sems.remote(tokens.at[flip(me_seq, k)], x_out.at[k], "seq", k) for k in range(1, seq)]
    start_all(blocks)
    gather.start()
    last = []
    for event in gather.events():
        if event:
            last += event[1]
    wait_all(into)
    start_all(outof)
    for copy in gather.pending:
        copy.wait_send()
    wait_all(last)
    wait_all(blocks)
    wait_all(outof)


def enter(sizes, tokens, shards):
    fsdp = sizes[0]
    count = len(shards)
    hbm = lambda shape: struct(bf16, *shape)
    copies = sizes[2] - 1 + Gather.count(sizes, gather_order(sizes, shards), count)
    return pl.pallas_call(
        functools.partial(enter_kernel, sizes, count),
        in_specs=[ANY] * (1 + count),
        out_specs=[ANY] * (1 + count),
        out_shape=[hbm(tokens.shape)] + [hbm((fsdp,) + s.shape) for s in shards],
        scratch_shapes=[pltpu.VMEM(tokens.shape[1:], bf16)]
        + [pltpu.VMEM(s.shape, bf16) for s in shards]
        + sem_shapes(copies, 2 * (1 + count)),
        compiler_params=pltpu.CompilerParams(collective_id=0, has_side_effects=True),
    )(tokens, *shards)


def turn(row):
    n = row.shape[1]
    diagonal = lax.broadcasted_iota(jnp.int32, (n, n), 0) == lax.broadcasted_iota(jnp.int32, (n, n), 1)
    return jnp.sum(jnp.where(diagonal, row, 0), axis=1, keepdims=True)


def enter_project_kernel(sizes, count, tokens, segments, *refs):
    fsdp, rep, seq = sizes
    refs = list(refs)
    pop = lambda n: [refs.pop(0) for _ in range(n)]
    shards = pop(count)
    x_out, a_out, qkv_out, cos_out, sin_out, marks_out, row_out, gains_out, wq_out = pop(9)
    fulls = [None, None] + pop(count - 2)
    xs, a, qkv, wq, gains = pop(5)
    bounces = pop(count)
    sems = Sems(*refs)
    me, me_seq = lax.axis_index("fsdp"), lax.axis_index("seq")
    shard_rows, rows = shards[1].shape[0], xs.shape[1]
    columns = wq.shape[1]

    def place(w, q):
        if w == 0:
            return gains.at[q]
        if w == 1:
            return wq.at[pl.ds(pl.multiple_of(q * shard_rows, 16), shard_rows)]
        return fulls[w].at[q]

    own = sems.copy(tokens.at[me_seq], xs.at[0])
    into = [sems.copy(shards[w], place(w, me) if w < 2 else bounces[w - 2]) for w in range(count)]
    outof = [sems.copy(bounces[w - 2], place(w, me)) for w in range(2, count)]
    blocks = [sems.remote(tokens.at[flip(me_seq, k)], xs.at[k], "seq", k) for k in range(1, seq)]
    stores = [
        [sems.copy(src.at[k], dst.at[k]) for src, dst in ((xs, x_out), (a, a_out), (qkv, qkv_out))] for k in range(seq)
    ]
    keep = sems.copy(wq, wq_out)
    gather = Gather(sizes, shards, place, sems, gather_order(sizes, shards))
    own.start()
    start_all(into)
    meet(all_partners(sizes))
    gather.start()
    start_all(blocks)

    lane = lax.broadcasted_iota(jnp.int32, (1, PAIR), 1)
    rate = jnp.exp((lane % (HDIM // 2)).astype(f32) * (-2.0 * math.log(THETA) / HDIM))
    sign = jnp.where(lane_halves((1, PAIR)), -1.0, 1.0)
    batch = segments.shape[1]

    def own_segments(block):
        at = pl.multiple_of(block * rows, 128)
        return segments[me_seq // batch, pl.ds(me_seq % batch, 1), pl.ds(at, rows)]

    def tables(k):
        block = flip(me_seq, k)
        piece = slice(k * rows, (k + 1) * rows)
        row = own_segments(block)
        column = turn(row)
        earlier = jnp.zeros((rows, 1), jnp.int32)
        for other in range(seq):
            earlier += jnp.sum((own_segments(other) < column).astype(jnp.int32), axis=1, keepdims=True)
        index = block * rows + lax.broadcasted_iota(jnp.int32, (rows, 1), 0)
        angles = (index - earlier).astype(f32) * rate
        cos_out[piece, :] = jnp.cos(angles)
        sin_out[piece, :] = jnp.sin(angles) * sign
        marks_out[piece, :] = column
        row_out[:, piece] = row

    def project(k):
        if k == 0:
            own.wait()
        else:
            blocks[k - 1].wait()
        piece = slice(k * rows, (k + 1) * rows)
        unit, _ = normalize(xs[k].astype(f32))
        low = (unit * gains_out[0:1, :]).astype(bf16)
        a[k] = low
        cosine, sine = cos_out[piece, :], sin_out[piece, :]

        @pl.loop(0, 2 * D // WIDE)
        def _(i):
            at = pl.multiple_of(i * WIDE, WIDE)
            part = dot_nn(low, wq[:, pl.ds(at, WIDE)])
            scale = jnp.where(at < D, QUERY_SCALE, 1.0)
            for half in range(0, WIDE, PAIR):
                value = rotate_pair(part[:, half : half + PAIR], cosine, sine) * scale
                qkv[k, :, pl.ds(at + half, PAIR)] = value.astype(bf16)

        qkv[k, :, 2 * D :] = dot_nn(low, wq[:, 2 * D :]).astype(bf16)
        start_all(stores[k])

    last, queue, since, untabled = {}, list(range(seq)), 0, list(range(seq))
    for event in gather.events():
        if event:
            last[event[0]] = event[1]
            if event[0] == 1:
                while untabled:
                    tables(untabled.pop(0))
                for copy in into[:2] + last[0] + last[1]:
                    copy.wait()
                keep.start()
                total = gains[0, :2, :].astype(f32)
                for q in range(1, fsdp):
                    total = total + gains[q, :2, :].astype(f32)
                gains_out[...] = total
                wait_all(into[2:])
                start_all(outof)
                project(queue.pop(0))
        elif untabled and 1 not in last:
            tables(untabled.pop(0))
        elif 1 in last:
            since += 1
            if since % 2 == 0 and len(queue) > 1:
                project(queue.pop(0))
    for k in queue:
        project(k)
    for copy in gather.pending:
        copy.wait_send()
    for w in range(2, count):
        wait_all(last[w])
    wait_all(outof)
    for group in stores:
        wait_all(group)
    keep.wait()


def enter_project(sizes, tokens, segments, shards):
    fsdp, rep, seq = sizes
    count, rows = len(shards), tokens.shape[1]
    length, columns = seq * rows, shards[1].shape[1]
    vmem = pl.BlockSpec(memory_space=pltpu.VMEM)
    copies = seq - 1 + Gather.count(sizes, gather_order(sizes, shards), count)
    return pl.pallas_call(
        functools.partial(enter_project_kernel, sizes, count),
        in_specs=[ANY, vmem] + [ANY] * count,
        out_specs=[ANY] * 3 + [vmem] * 5 + [ANY] * (count - 1),
        out_shape=[struct(bf16, seq, rows, D), struct(bf16, seq, rows, D), struct(bf16, seq, rows, columns),
                   struct(f32, length, PAIR), struct(f32, length, PAIR), struct(jnp.int32, length, 1),
                   struct(jnp.int32, 1, length), struct(f32, 2, D), struct(bf16, D, columns)]
        + [struct(bf16, fsdp, *s.shape) for s in shards[2:]],
        scratch_shapes=[pltpu.VMEM((seq, rows, D), bf16), pltpu.VMEM((seq, rows, D), bf16),
                        pltpu.VMEM((seq, rows, columns), bf16), pltpu.VMEM((D, columns), bf16),
                        pltpu.VMEM((fsdp,) + shards[0].shape, bf16)]
        + [pltpu.VMEM(s.shape, bf16) for s in shards[2:]] + [pltpu.VMEM((16, 128), bf16)] * 2
        + sem_shapes(copies, 2 + count + count - 2 + 3 * seq),
        compiler_params=pltpu.CompilerParams(
            collective_id=4, has_side_effects=True, vmem_limit_bytes=VMEM_LIMIT
        ),
    )(tokens, segments, *shards)


class Reducer:
    def __init__(self, parts_shape, sizes, order):
        self.fsdp, self.rows, self.cols = parts_shape
        self.steps = []
        held, rows, cols = list(range(self.fsdp)), self.rows, self.cols
        row_at, col_at = [], []
        for axis, bit in order:
            step = dict(axis=axis, bit=bit, row_at=list(row_at), col_at=list(col_at), rows=rows, cols=cols)
            if axis == "fsdp":
                step["send"] = [j for j in held if j & bit]
                held = [j for j in held if not j & bit]
                step["keep"] = held
                step["shape"] = (len(held), rows, cols)
                step["split"] = None
            else:
                step["keep"] = step["send"] = held
                if (axis, bit) == order[-1]:
                    step["split"] = "none"
                elif (rows // 2) % 16 == 0:
                    rows //= 2
                    row_at = row_at + [(axis, bit, rows)]
                    step["split"] = "rows"
                elif (cols // 2) % 128 == 0:
                    cols //= 2
                    col_at = col_at + [(axis, bit, cols)]
                    step["split"] = "cols"
                else:
                    step["split"] = "none"
                step["shape"] = (len(held), rows, cols)
            self.steps.append(step)
        self.down = len(self.steps)
        for step in reversed(self.steps[: self.down]):
            if step["split"] in ("rows", "cols"):
                self.steps.append(dict(step, up=True))

    @staticmethod
    def offset(terms, align, last=None):
        total = 0
        for i, (axis, bit, extent) in enumerate(terms):
            half = (lax.axis_index(axis) // bit) % 2
            if last == i:
                half = 1 - half
            total = total + half * extent
        return total if isinstance(total, int) else pl.multiple_of(total, align)

    def region(self, step, after, other=False):
        row_at, col_at, rows, cols = step["row_at"], step["col_at"], step["rows"], step["cols"]
        row_last = col_last = None
        if after:
            if step["split"] == "rows":
                rows //= 2
                row_at = row_at + [(step["axis"], step["bit"], rows)]
                row_last = len(row_at) - 1 if other else None
            elif step["split"] == "cols":
                cols //= 2
                col_at = col_at + [(step["axis"], step["bit"], cols)]
                col_last = len(col_at) - 1 if other else None
        return (
            pl.ds(self.offset(row_at, 16, row_last), rows),
            pl.ds(self.offset(col_at, 128, col_last), cols),
        )

    def scratch(self, first, last):
        return [pltpu.VMEM(s["shape"], bf16) for s in self.steps[first:last] if "up" not in s]

    def copies(self, first, last):
        return sum(1 if "up" in s else len(s["send"]) for s in self.steps[first:last])

    def bind(self, parts, lands, sems, first, last, final=None):
        self.parts, self.sems, self.final = parts, sems, final
        self.lands, self.moves = {}, {}
        lands = list(lands)
        for s in range(first, last):
            step = self.steps[s]
            moves = []
            if "up" in step:
                there = final.at[self.region(step, True)]
                moves.append(sems.remote(there, there, step["axis"], step["bit"]))
            else:
                land = self.lands[s] = lands.pop(0)
                for i, j in enumerate(step["send"]):
                    fsdp = step["axis"] == "fsdp"
                    src = self.parts(j).at[self.region(step, not fsdp, not fsdp)]
                    moves.append(sems.remote(src, land.at[i], step["axis"], step["bit"]))
            self.moves[s] = moves

    def start(self, s):
        if s == self.down:
            region = self.region(self.steps[s - 1], True)
            self.final[region] = self.parts(0)[region]
        start_all(self.moves.get(s, []))

    def finish(self, s):
        step = self.steps[s]
        self.finish_step(s, step)
        if s + 1 == len(self.steps) == self.down and self.final is not None:
            self.final[...] = self.parts(0)[...]

    def finish_step(self, s, step):
        for i, move in enumerate(self.moves[s]):
            move.wait()
            if "up" not in step:
                j = step["keep"][i]
                ref = self.parts(j)
                region = self.region(step, True)
                ref[region] = (ref[region].astype(f32) + self.lands[s][i].astype(f32)).astype(bf16)


def give_back(slots, home, bounce, sems):
    me = lax.axis_index("seq")
    seq = slots.shape[0]
    return (
        sems.copy(slots.at[0], bounce),
        sems.copy(bounce, home.at[me]),
        [sems.remote(slots.at[k], home.at[me], "seq", k) for k in range(1, seq)],
    )


def body(sizes, tokens, segments, positions, gain_attn, w_qkv, w_out, gain_mlp, w_in, w_mlp_out, cotangent):
    fsdp, rep, seq = sizes
    micro, batch, rows, _ = tokens.shape
    assert micro * batch == seq and rows % TILE == 0
    length = seq * rows
    me_seq, me_fsdp = lax.axis_index("seq"), lax.axis_index("fsdp")

    own_gains = jnp.zeros((16, D), bf16)
    own_gains = lax.dynamic_update_slice(own_gains, jnp.stack([gain_attn, gain_mlp]), (0, me_fsdp * (D // fsdp)))
    shards = [own_gains, w_qkv, w_out, w_mlp_out, w_in]
    tiles, pairs = length // TILE, HEADS // 2
    late = fsdp in (2, 4) and pairs >= 6 and flat(D // fsdp) and flat(FF // fsdp)
    if (D // fsdp) % 16 == 0:
        x, a, qkv, cosine, sine, marks_column, marks_row, gains, wq, *rest = enter_project(
            sizes, tokens.reshape(seq, rows, D), segments, shards[:3] if late else shards
        )
        x, a, qkv = (v.reshape(length, -1) for v in (x, a, qkv))
        wo, *rest = (w.reshape(-1, w.shape[-1]) for w in rest)
        wm, wi = (w_mlp_out, w_in) if late else rest
    else:
        x, gains, wq, wo, wm, wi = enter(sizes, tokens.reshape(seq, rows, D), shards)
        x = x.reshape(length, D)
        gains = jnp.sum(gains[:, :2].astype(f32), axis=0)
        wq, wo, wm, wi = (w.reshape(-1, w.shape[-1]) for w in (wq, wo, wm, wi))

        marks = take(segments.reshape(seq, length), me_seq)
        place = jnp.arange(length, dtype=jnp.int32) - jnp.sum(
            (marks[None, :] < marks[:, None]).astype(jnp.int32), axis=1
        )
        slot_order = [me_seq ^ k for k in range(seq)]
        marks = jnp.concatenate([take(marks.reshape(seq, rows), s) for s in slot_order])
        place = jnp.concatenate([take(place.reshape(seq, rows), s) for s in slot_order])
        half = jnp.arange(0, HDIM, 2).astype(f32) / HDIM
        angles = place.astype(f32)[:, None] * jnp.exp(-half * math.log(THETA))
        cosine, sine = jnp.cos(angles), jnp.sin(angles)
        cosine = jnp.concatenate([cosine] * 4, -1)
        sine = jnp.concatenate([-sine, sine] * 2, -1)

        a, qkv = call(
            first_kernel, tiles,
            [rows_spec(D), whole_spec(2, D), whole_spec(D, 3 * D), rows_spec(PAIR), rows_spec(PAIR)],
            [rows_spec(D), rows_spec(3 * D)],
            [struct(bf16, length, D), struct(bf16, length, 3 * D)],
            2 * length * D * 3 * D,
        )(x, gains, wq, cosine, sine)
        marks_column, marks_row = marks[:, None], marks[None, :]

    vmem = pl.BlockSpec(memory_space=pltpu.VMEM)
    pair_at = lambda offset, lag, n: pl.BlockSpec(
        (length, PAIR), lambda i: (0, jnp.clip(i - lag, 0, n - 1) + offset)
    )
    prob_at = lambda lag: pl.BlockSpec((2, length, length), lambda i: (jnp.clip(i - lag, 0, pairs - 1), 0, 0))
    tile_at = lambda width, lag: pl.BlockSpec((TILE, width), lambda i: (jnp.clip(i - lag, 0, tiles - 1), 0))
    slots = struct(bf16, seq, rows, D)
    o, probs, inv, x1, b, m, slope, act, y, dy, *wholes = call(
        functools.partial(forward_kernel, sizes, pairs, late), pairs + tiles,
        [pair_at(0, 0, pairs), pair_at(pairs, 0, pairs), pair_at(2 * pairs, 0, pairs),
         whole_spec(length, 1), whole_spec(1, length), tile_at(D, pairs), whole_spec(2, D)] + [ANY] * 4,
        [pair_at(0, 0, pairs), prob_at(0), pair_at(0, 0, pairs), tile_at(D, pairs), tile_at(D, pairs)]
        + [tile_at(FF, pairs)] * 3 + [tile_at(D, pairs), ANY] + [ANY] * (2 * late),
        [struct(bf16, length, D), struct(bf16, HEADS, length, length), struct(f32, length, D),
         struct(f32, length, D), struct(bf16, length, D), struct(bf16, length, FF),
         struct(bf16, length, FF), struct(bf16, length, FF), struct(bf16, length, D), slots]
        + [struct(bf16, D, 2 * FF), struct(bf16, FF, D)] * late,
        16 * length * length * D,
        [pltpu.VMEM((length, D), bf16), pltpu.VMEM((D, D), bf16), pltpu.VMEM((D, 2 * FF), bf16), pltpu.VMEM((FF, D), bf16),
         pltpu.VMEM((rows, D), bf16)] + sem_shapes(seq - 1 + LateGather.copies(sizes) * late, 5 + 2 * late), 1,
    )(qkv, qkv, qkv, marks_column, marks_row, x, gains, wo, wi, wm, cotangent.reshape(seq, rows, D))

    if late:
        wi, wm = wholes
    reducers, early = early_reducers(sizes)
    whole = late_reducers(sizes)
    own_shard = lambda r: struct(bf16, r.rows, r.cols)
    full_shard = lambda r: pltpu.VMEM((fsdp * r.rows, r.cols) if flat(r.rows) else (fsdp, r.rows, r.cols), bf16)
    odd = (FF // fsdp) % 16 or (D // fsdp) % 16
    wide = pltpu.VMEM((FF, FF) if odd else (8, 128), f32)
    dx1, dgain_two, dq, dk, dv, block_out, *sums = call(
        functools.partial(backward_kernel, sizes, tiles), tiles + 1 + pairs,
        [tile_at(D, 0), tile_at(FF, 0), tile_at(FF, 0), whole_spec(2, D)]
        + [pair_at(n * pairs, tiles + 1, pairs) for n in range(3)]
        + [pair_at(0, tiles + 1, pairs), pair_at(0, tiles + 1, pairs)] + [ANY] * 11,
        [tile_at(D, 0), whole_spec(1, D)] + [pair_at(0, tiles + 1, pairs)] * 3 + [ANY] * (1 + len(reducers)),
        [struct(f32, length, D), struct(f32, 1, D)] + [struct(bf16, length, D)] * 3 + [slots]
        + [own_shard(r) for r in reducers],
        32 * length * length * D,
        [pltpu.VMEM((D, D), bf16), pltpu.VMEM((D, 2 * FF), bf16), pltpu.VMEM((FF, D), bf16),
         pltpu.VMEM((length, FF), bf16)] + [pltpu.VMEM((length, D), bf16)] * 3
        + [pltpu.VMEM((length, 2 * FF), bf16), pltpu.VMEM((length, D), bf16), pltpu.VMEM((length, D), bf16),
           wide, pltpu.VMEM((rows, D), bf16),
           pltpu.VMEM((2, 2, length, length), bf16)] + [pltpu.VMEM((length, PAIR), f32)] * 2
        + [full_shard(r) for r in reducers] + [pltpu.VMEM((reducers[0].rows, reducers[0].cols), bf16)]
        + [land for r, e in zip(reducers, early) for land in r.scratch(0, e)]
        + sem_shapes(seq - 1 + sum(r.copies(0, e) for r, e in zip(reducers, early)), 13 + len(reducers)), 2,
    )(x1, slope, act, gains, qkv, qkv, qkv, o, inv, probs, cosine, sine,
      wo, wi, wm, m, dy.reshape(length, D), b, o, y.reshape(seq, rows, D))

    hops = sum(len(bits_of(n)) for n in sizes)
    shard = lambda n, width: struct(bf16, n // fsdp, width)
    finals = [shard(D, 2 * FF), shard(D, D), shard(D, 3 * D)]
    operands = [dq, a, dk, dv, wq, x, dx1]
    grad_mlp, *sums = sums
    reducers, early = reducers[1:], early[1:]
    input_grad, grad_in, grad_out, grad_qkv, dgains = pl.pallas_call(
        functools.partial(leave_kernel, sizes),
        in_specs=[vmem] * 2 + [ANY] * (len(operands) + len(reducers)),
        out_specs=[ANY] * 4 + [vmem],
        out_shape=[slots] + finals + [struct(f32, 8, D)],
        scratch_shapes=[pltpu.VMEM(v.shape, v.dtype) for v in operands]
        + [pltpu.VMEM((seq, rows, D), bf16), wide]
        + [pltpu.VMEM(v.shape, v.dtype) for v in finals]
        + [pltpu.VMEM((r.rows, r.cols), bf16) for r in reducers]
        + [full_shard(r) for r in whole]
        + [land for r, e in zip(reducers, early) for land in r.scratch(e, len(r.steps))]
        + [land for r in whole for land in r.scratch(0, len(r.steps))]
        + [pltpu.VMEM((hops, 8, D), f32)]
        + sem_shapes(
            PIECES * (seq - 1) + hops + sum(r.copies(e, len(r.steps)) for r, e in zip(reducers, early))
            + sum(r.copies(0, len(r.steps)) for r in whole),
            1 + len(operands) + len(reducers) + len(finals),
        ),
        compiler_params=pltpu.CompilerParams(
            collective_id=3, has_side_effects=True, vmem_limit_bytes=VMEM_LIMIT
        ),
    )(gains, dgain_two, *operands, *sums)
    dgains = lax.dynamic_slice_in_dim(dgains, me_fsdp * (D // fsdp), D // fsdp, 1)
    return (
        block_out.reshape(tokens.shape),
        input_grad.astype(f32).reshape(tokens.shape),
        dgains[0],
        grad_qkv.astype(f32),
        grad_out.astype(f32),
        dgains[1],
        grad_in.astype(f32),
        grad_mlp.astype(f32),
    )


def solution(mesh):
    sizes = (mesh.shape["fsdp"], mesh.shape["rep"], mesh.shape["seq"])
    wide = P(None, ("rep", "fsdp"), "seq", None)
    placed = (
        wide, P(None, ("rep", "fsdp"), None), P(None, ("rep", "fsdp"), "seq"),
        P("fsdp"), P("fsdp", None), P("fsdp", None), P("fsdp"), P("fsdp", None), P("fsdp", None), wide,
    )
    return jax.shard_map(
        functools.partial(body, sizes),
        mesh=mesh,
        in_specs=placed,
        out_specs=(
            wide, wide, P("fsdp"), P("fsdp", None), P("fsdp", None), P("fsdp"), P("fsdp", None), P("fsdp", None),
        ),
        check_vma=False,
    )
```

```python
import functools
import math

import jax
import jax.numpy as jnp
from jax import lax
from jax.experimental import pallas as pl
from jax.experimental.pallas import tpu as pltpu
from jax.sharding import PartitionSpec as P

D = 768
HEADS = 12
HDIM = 64
FF = 1152
EPS = 1e-05
THETA = 160000.0
MASKED = -1000000000.0
QUERY_SCALE = HDIM**-0.5 / math.log(2.0)
TILE = 256
PAIR = 2 * HDIM
WIDE = 384
HCHUNK = 384
f32 = jnp.float32
bf16 = jnp.bfloat16
VMEM_LIMIT = 62 * 2**20


def dot_nn(left, right):
    return lax.dot_general(left, right, (((1,), (0,)), ((), ())), preferred_element_type=f32)


def dot_nt(left, right):
    return lax.dot_general(left, right, (((1,), (1,)), ((), ())), preferred_element_type=f32)


def dot_tn(left, right):
    return lax.dot_general(left, right, (((0,), (0,)), ((), ())), preferred_element_type=f32)


def normalize(values):
    mean = jnp.mean(values, axis=-1, keepdims=True)
    centered = values - mean
    var = jnp.mean(centered * centered, axis=-1, keepdims=True)
    scale = lax.rsqrt(var + EPS)
    return centered * scale, scale


def norm_back(unit, scale, gain, grad):
    gain_terms = grad * unit
    inner = grad * gain
    first = jnp.mean(inner, axis=-1, keepdims=True)
    second = jnp.mean(inner * unit, axis=-1, keepdims=True)
    return scale * (inner - first - unit * second), gain_terms


def lane_halves(shape):
    lane = lax.broadcasted_iota(jnp.int32, shape, len(shape) - 1)
    return lane % HDIM < HDIM // 2


def rotate_pair(values, cosine, signed_sine):
    swapped = jnp.where(
        lane_halves(values.shape),
        pltpu.roll(values, PAIR - HDIM // 2, 1),
        pltpu.roll(values, HDIM // 2, 1),
    )
    return values * cosine + swapped * signed_sine


def first_kernel(x_ref, gain_ref, w_ref, cos_ref, sin_ref, a_ref, qkv_ref):
    unit, _ = normalize(x_ref[...].astype(f32))
    a = (unit * gain_ref[0:1, :]).astype(bf16)
    a_ref[...] = a
    cosine, sine = cos_ref[...], sin_ref[...]
    for column in range(0, 3 * D, TILE):
        part = dot_nn(a, w_ref[:, column : column + TILE])
        for half in range(0, TILE, PAIR):
            start = column + half
            piece = part[:, half : half + PAIR]
            if start < 2 * D:
                piece = rotate_pair(piece, cosine, sine)
            if start < D:
                piece = piece * QUERY_SCALE
            qkv_ref[:, start : start + PAIR] = piece.astype(bf16)


def head_lanes():
    lane = lax.broadcasted_iota(jnp.int32, (1, PAIR), 1)
    return [lane < HDIM, lane >= HDIM]


def attend_pair(q_ref, k_ref, v_ref, rows_ref, cols_ref, p_ref, inv_ref, write):
    k, v = k_ref[...], v_ref[...]
    length = k.shape[0]
    mine = head_lanes()
    zero, one = jnp.zeros((), bf16), jnp.ones((), bf16)
    summing = [jnp.where(m, v, one) for m in mine]
    items = [(tile, head) for tile in range(0, length, TILE) for head in range(2)]

    def score(item):
        tile, head = item
        return dot_nt(jnp.where(mine[head], q_ref[tile : tile + TILE, :], zero), k)

    ahead = score(items[0])
    kept = None
    for i, (tile, head) in enumerate(items):
        rows = slice(tile, tile + TILE)
        scores = ahead
        if i + 1 < len(items):
            ahead = score(items[i + 1])
        scores = jnp.where(rows_ref[rows, :] == cols_ref[...], scores, MASKED)
        probs = jnp.exp2(scores - jnp.max(scores, axis=-1, keepdims=True)).astype(bf16)
        p_ref[head, rows, :] = probs
        part = dot_nn(probs, summing[head])
        inv = 1.0 / pltpu.roll(part, HDIM, 1)
        if head == 0:
            kept = (part * inv, inv)
        else:
            inv_ref[rows, :] = jnp.where(mine[0], kept[1], inv)
            write(rows, jnp.where(mine[0], kept[0], part * inv).astype(bf16))


def forward_kernel(
    sizes, pairs, late, q_ref, k_ref, v_ref, rows_ref, cols_ref, x_ref, gain_ref, w_out_any, w_in_any, w_mlp_any, cot_ref,
    o_ref, p_ref, inv_ref, x1_ref, b_ref, m_ref, slope_ref, act_ref, y_ref, dy_ref, *refs,
):
    seq = sizes[2]
    refs = list(refs)
    outs = [refs.pop(0) for _ in range(2 * late)]
    joined, w_out_ref, w_in_ref, w_mlp_ref, bounce, *sem_refs = refs
    step, last = pl.program_id(0), pl.num_programs(0) - 1
    sems = Sems(*sem_refs)
    me_seq = lax.axis_index("seq")
    into = sems.copy(cot_ref.at[me_seq], bounce)
    outof = sems.copy(bounce, dy_ref.at[0])
    weights = [sems.copy(w_out_any, w_out_ref)]
    partners = [("seq", k) for k in range(1, seq)]
    if late:
        gather = LateGather(sizes, [w_in_any, w_mlp_any], [w_in_ref, w_mlp_ref], sems)
        weights += gather.own
        keeps = [sems.copy(w_in_ref, outs[0]), sems.copy(w_mlp_ref, outs[1])]
        partners = all_partners(sizes)
    else:
        weights += [sems.copy(w_in_any, w_in_ref), sems.copy(w_mlp_any, w_mlp_ref)]
    blocks = [sems.remote(cot_ref.at[flip(me_seq, k)], dy_ref.at[k], "seq", k) for k in range(1, seq)]

    @pl.when(step == 0)
    def _():
        into.start()
        start_all(weights)
        meet(partners)
        if late:
            start_all(gather.far)
        start_all(blocks)
        into.wait()
        outof.start()

    if late:
        for when in range(1, pairs + 1):
            @pl.when(step == when)
            def _(when=when):
                gather.advance(when)

    @pl.when(step < pairs)
    def _():
        def write(rows, value):
            o_ref[rows, :] = value
            joined[rows, pl.ds(pl.multiple_of(step * PAIR, PAIR), PAIR)] = value

        attend_pair(q_ref, k_ref, v_ref, rows_ref, cols_ref, p_ref, inv_ref, write)

    @pl.when(step == pairs)
    def _():
        if late:
            wait_all(weights[:1])
            gather.finish(0)
            keeps[0].start()
        else:
            wait_all(weights)

    @pl.when(step >= pairs)
    def _():
        start = pl.multiple_of((step - pairs) * TILE, TILE)
        x1 = x_ref[...].astype(f32) + dot_nn(joined[pl.ds(start, TILE), :], w_out_ref[...])
        x1_ref[...] = x1
        unit, _ = normalize(x1)
        b = (unit * gain_ref[1:2, :]).astype(bf16)
        b_ref[...] = b

        def hidden(column):
            return (
                dot_nn(b, w_in_ref[:, column : column + HCHUNK]),
                dot_nn(b, w_in_ref[:, FF + column : FF + column + HCHUNK]),
            )

        ahead = hidden(0)
        for column in range(0, FF, HCHUNK):
            hin, gate = ahead
            if column + HCHUNK < FF:
                ahead = hidden(column + HCHUNK)
            phi = 0.5 + 0.5 * lax.erf(hin * math.sqrt(0.5))
            act = hin * phi
            slope = phi + hin * (jnp.exp(hin * hin * -0.5) * (1.0 / math.sqrt(2.0 * math.pi)))
            m_ref[:, column : column + HCHUNK] = (act * gate).astype(bf16)
            act_ref[:, column : column + HCHUNK] = act.astype(bf16)
            slope_ref[:, column : column + HCHUNK] = (slope * gate).astype(bf16)
        if late:
            @pl.when(step == pairs)
            def _():
                gather.finish(1)
                keeps[1].start()

        y_ref[...] = (x1_ref[...] + dot_nn(m_ref[...], w_mlp_ref[...])).astype(bf16)

    @pl.when(step == last)
    def _():
        if late:
            wait_all(keeps)
        outof.wait()
        wait_all(blocks)


def order_of(sizes, rep_first):
    fsdp, rep, seq = sizes
    core = [("fsdp", 1)]
    rest = [("fsdp", b) for b in bits_of(fsdp)[1:]]
    copies = [("rep", b) for b in bits_of(rep)]
    return core + (copies + rest if rep_first else rest + copies) + [("seq", b) for b in bits_of(seq)]


def all_partners(sizes):
    fsdp, rep, seq = sizes
    return [("seq", k) for k in range(1, seq)] + [("fsdp", b) for b in bits_of(fsdp)] + [("rep", b) for b in bits_of(rep)]


def early_reducers(sizes):
    fsdp, rep, seq = sizes
    shapes = [(fsdp, FF // fsdp, D), (fsdp, D // fsdp, FF), (fsdp, D // fsdp, FF), (fsdp, D // fsdp, D)]
    reducers = [Reducer(shape, sizes, order_of(sizes, w == 2)) for w, shape in enumerate(shapes)]
    across = len(bits_of(fsdp)) + len(bits_of(rep))
    return reducers, [len(reducers[0].steps)] + [across + 2] * 2 + [across + 1]


class Tiles:
    def __init__(self, buffer, rows, columns):
        self.buffer, self.rows, self.columns = buffer, rows, columns

    @property
    def at(self):
        return self

    def __getitem__(self, i):
        return self.buffer.at[pl.ds(i * self.rows, self.rows), self.columns]


def begun(sizes):
    return 1 if flat(D // sizes[0]) and sizes[0] <= 4 else 0


def late_reducers(sizes):
    fsdp = sizes[0]
    return [Reducer((fsdp, D // fsdp, D), sizes, order_of(sizes, w == 1)) for w in range(3)]


def flat(rows):
    return rows % 16 == 0


def shard_of(ref, rows, q):
    return ref.at[pl.ds(pl.multiple_of(q * rows, 16), rows)] if flat(rows) else ref.at[q]


def weight_gradient(ref, wide, left, right):
    if len(ref.shape) == 2:
        @pl.loop(0, ref.shape[0] // HCHUNK)
        def _(i):
            at = pl.ds(pl.multiple_of(i * HCHUNK, HCHUNK), HCHUNK)
            ref[at, :] = dot_tn(left[:, at], right[...]).astype(bf16)
    else:
        shards, rows, cols = ref.shape
        wide[: shards * rows, :cols] = dot_tn(left[...], right[...])
        for q in range(shards):
            ref[q] = wide[q * rows : (q + 1) * rows, :cols].astype(bf16)


def middle_back_tile(dy, x1_ref, slope_ref, act_ref, gain_ref, w_out_ref, w_in_ref, w_mlp_ref, dh_ref, dgain_ref, dx1_ref):
    ahead = dot_nt(dy, w_mlp_ref[:HCHUNK, :])
    for column in range(0, FF, HCHUNK):
        dm = ahead
        if column + HCHUNK < FF:
            ahead = dot_nt(dy, w_mlp_ref[column + HCHUNK : column + 2 * HCHUNK, :])
        dh_ref[:, column : column + HCHUNK] = (dm * slope_ref[:, column : column + HCHUNK].astype(f32)).astype(bf16)
        dh_ref[:, FF + column : FF + column + HCHUNK] = (
            dm * act_ref[:, column : column + HCHUNK].astype(f32)
        ).astype(bf16)
    db = dot_nt(dh_ref[...], w_in_ref[...])
    unit, scale = normalize(x1_ref[...])
    back, terms = norm_back(unit, scale, gain_ref[1:2, :], db)
    dgain_ref[...] += jnp.sum(terms, axis=0, keepdims=True)
    dx1 = dy.astype(f32) + back
    dx1_ref[...] = dx1
    return dx1.astype(bf16)


def attend_back_pair(q_ref, k_ref, v_ref, o_ref, inv_ref, do, p_ref, cos_ref, sin_ref, dq_ref, dk_ref, dv_ref):
    v = v_ref[...]
    length = v.shape[0]
    mine = head_lanes()
    zero = jnp.zeros((), bf16)
    do = (do.astype(f32) * inv_ref[...]).astype(bf16)
    inner = do.astype(f32) * o_ref[...].astype(f32)
    do_heads = [jnp.where(m, do, zero) for m in mine]
    q_heads = [jnp.where(m, q_ref[...], zero).T for m in mine]
    k_heads = [jnp.where(m, k_ref[...], zero) for m in mine]
    do_turned = [d.T for d in do_heads]
    cosine, sine = cos_ref[...], sin_ref[...]
    dv = dk = None
    for tile in range(0, length, TILE):
        rows = slice(tile, tile + TILE)
        dq = None
        for head in range(2):
            probs = p_ref[head, rows, :]
            delta = jnp.sum(jnp.where(mine[head], inner[rows], 0.0), axis=-1, keepdims=True)
            dp = dot_nt(do_heads[head][rows], v)
            ds = (probs.astype(f32) * (dp - delta)).astype(bf16)
            value_part = dot_nn(do_turned[head][:, rows], probs)
            key_part = dot_nn(q_heads[head][:, rows], ds)
            query_part = dot_nn(ds, k_heads[head])
            dv = value_part if dv is None else dv + value_part
            dk = key_part if dk is None else dk + key_part
            dq = query_part if dq is None else dq + query_part
        dq_ref[rows, :] = rotate_pair(dq * HDIM**-0.5, cosine[rows], -sine[rows]).astype(bf16)
    dk_ref[...] = rotate_pair(dk.T * math.log(2.0), cosine, -sine).astype(bf16)
    dv_ref[...] = dv.T.astype(bf16)


def backward_kernel(
    sizes, tiles, x1_ref, slope_ref, act_ref, gain_ref, q_ref, k_ref, v_ref, o_ref, inv_ref,
    p_any, cos_any, sin_any, w_out_any, w_in_any, w_mlp_any, m_any, dy_any, b_any, o_any, a_any, y_ref, *refs,
):
    reducers, early = early_reducers(sizes)
    count = len(reducers)
    refs = list(refs)
    pop = lambda n: [refs.pop(0) for _ in range(n)]
    dx1_ref, dgain_ref, dq_ref, dk_ref, dv_ref, home_ref = pop(6)
    sums_out = pop(count)
    whole = late_reducers(sizes) if begun(sizes) else []
    wholes_out = pop(len(whole))
    w_out_ref, w_in_ref, w_mlp_ref, m_ref, dy_ref, b_ref, all_o_ref = pop(7)
    dh_ref, low_ref, do_ref, wide, bounce, probs_ref, cos_ref, sin_ref = pop(8)
    grads = pop(count)
    (mlp_final,) = pop(1)
    lands = [pop(len(r.scratch(0, e))) for r, e in zip(reducers, early)]
    sems = Sems(*refs)
    me = lax.axis_index("fsdp")
    step, last = pl.program_id(0), pl.num_programs(0) - 1
    into, outof, blocks = give_back(y_ref, home_ref, bounce, sems)
    loads = [
        sems.copy(src, dst)
        for src, dst in [
            (m_any, m_ref), (dy_any, dy_ref), (w_mlp_any, w_mlp_ref), (w_in_any, w_in_ref), (w_out_any, w_out_ref),
            (b_any, b_ref), (o_any, all_o_ref), (cos_any, cos_ref), (sin_any, sin_ref),
        ]
    ]
    stores = [sems.copy(mlp_final if w == 0 else shard_of(grads[w], reducers[w].rows, me), sums_out[w]) for w in range(count)]
    load_a = sems.copy(a_any, b_ref)
    whole_grads = [ref.at[pl.ds(0, D)] for ref in (dy_ref, all_o_ref, low_ref)]
    for w, reducer in enumerate(whole):
        part = lambda j, w=w: shard_of(whole_grads[w], whole[w].rows, flip(me, j))
        reducer.bind(part, [Tiles(w_in_ref, reducer.rows, pl.ds(w * D, D))], sems, 0, 1)
        stores += [sems.copy(part(j), wholes_out[w].at[i]) for i, j in enumerate(reducer.steps[0]["keep"])]
    pair, pairs = step - tiles - 1, last - tiles
    slot_sems = [sems.local.at[sems.local_used + i] for i in range(2)]
    sems.local_used += 2

    def fetch(which, slot):
        return pltpu.make_async_copy(p_any.at[pl.ds(which * 2, 2)], probs_ref.at[slot], slot_sems[slot])
    for w, reducer in enumerate(reducers):
        reducer.bind(lambda j, w=w: shard_of(grads[w], reducers[w].rows, flip(me, j)), lands[w], sems, 0, early[w], mlp_final if w == 0 else None)
    mlp, first_half, second_half, out = reducers

    def at(when, *actions):
        @pl.when(step == when)
        def _():
            for action in actions:
                action()

    def advance(reducer, s, limit):
        def run():
            reducer.finish(s)
            if s + 1 < limit:
                reducer.start(s + 1)
        return run

    @pl.when(step == 0)
    def _():
        start_all(loads)
        into.start()
        meet(all_partners(sizes))
        start_all(blocks)
        dgain_ref[...] = jnp.zeros_like(dgain_ref)
        wait_all(loads[:2])
        weight_gradient(grads[0], wide, m_ref, dy_ref)
        mlp.start(0)
        into.wait()
        outof.start()
        wait_all(loads[2:5])

    at(1, advance(mlp, 0, early[0]))

    @pl.when(step < tiles)
    def _():
        rows = pl.ds(pl.multiple_of(step * TILE, TILE), TILE)
        low = middle_back_tile(
            dy_ref[rows, :], x1_ref, slope_ref, act_ref, gain_ref, w_out_ref, w_in_ref, w_mlp_ref,
            dh_ref.at[rows, :], dgain_ref, dx1_ref,
        )
        low_ref[rows, :] = low
        do_ref[rows, :] = dot_nt(low, w_out_ref[...]).astype(bf16)

    across = len(bits_of(sizes[0])) + len(bits_of(sizes[1]))

    @pl.when(step == tiles)
    def _():
        wait_all(loads[5:])
        weight_gradient(grads[1], wide, b_ref, dh_ref.at[:, :FF])
        first_half.start(0)
        weight_gradient(grads[2], wide, b_ref, dh_ref.at[:, FF:])
        second_half.start(0)
        for s in range(1, across - 1):
            advance(mlp, s, early[0])()
        weight_gradient(grads[3], wide, all_o_ref, low_ref)
        out.start(0)

    @pl.when(step == tiles - 1)
    def _():
        fetch(0, 0).start()

    for slot in range(2):
        @pl.when((step > tiles) & (pair % 2 == slot))
        def _(slot=slot):
            fetch(pair, slot).wait()

            @pl.when(pair + 1 < pairs)
            def _():
                fetch(pair + 1, 1 - slot).start()

    halves = (first_half, second_half)
    steps = lambda reducer, limit, *which: [advance(reducer, s, limit) for s in which]
    half_steps = lambda *which: [advance(r, s, early[1]) for s in which for r in halves]
    middle = range(1, across - 1)
    at(tiles + 1, *steps(mlp, early[0], across - 1), *half_steps(0))
    at(tiles + 2, *steps(out, early[3], 0))
    at(tiles + 3, *half_steps(*middle))
    at(tiles + 4, *steps(mlp, early[0], across), *steps(out, early[3], *middle))
    at(tiles + 5, *steps(mlp, early[0], across + 1), *half_steps(across - 1))
    at(tiles + 6, *steps(mlp, early[0], *range(across + 2, early[0] - 1)), *half_steps(across), *steps(out, early[3], across - 1))

    @pl.when(step > tiles)
    def _():
        column = pl.multiple_of(pair * PAIR, PAIR)
        attend_back_pair(
            q_ref, k_ref, v_ref, o_ref, inv_ref, do_ref[:, pl.ds(column, PAIR)], probs_ref.at[pair % 2], cos_ref, sin_ref,
            dq_ref, dk_ref, dv_ref,
        )
        for w, part in enumerate((dq_ref, dk_ref, dv_ref)):
            dh_ref[:, pl.ds(w * D + column, PAIR)] = part[...]

    if whole:
        at(tiles + 1, load_a.start)

    @pl.when(step == last)
    def _():
        if whole:
            load_a.wait()
        for w, reducer in enumerate(whole):
            weight_gradient(whole_grads[w], wide, b_ref, dh_ref.at[:, w * D : (w + 1) * D])
            reducer.start(0)
        for w, reducer in enumerate(reducers):
            reducer.finish(early[w] - 1)
            stores[w].start()
        for reducer in whole:
            reducer.finish(0)
        start_all(stores[count:])
        wait_all(stores)
        outof.wait()
        wait_all(blocks)


PIECES = 4


def leave_kernel(sizes, gain_ref, other_gain_ref, *refs):
    fsdp, rep, seq = sizes
    reducers, early = (some[1:] for some in early_reducers(sizes))
    whole = late_reducers(sizes)
    count, more = len(reducers), len(whole)
    refs = list(refs)
    pop = lambda n: [refs.pop(0) for _ in range(n)]
    first = begun(sizes)
    anys = pop(6 if first else 7)
    sums_in = pop(count)
    wholes_in = pop(more * first)
    (home_ref,) = pop(1)
    in_out, out_out, qkv_out, gains_out = pop(4)
    dq_ref, dk_ref, dv_ref, w_ref, x_ref, dx1_ref, *a_ref = local = pop(len(anys))
    slots, wide, in_final, out_final, qkv_final = pop(5)
    held, grads = pop(count), pop(more)
    lands = [pop(len(r.scratch(e, len(r.steps)))) for r, e in zip(reducers, early)]
    whole_lands = [pop(len(r.scratch(first, len(r.steps)))) for r in whole]
    (gain_lands,) = pop(1)
    sems = Sems(*refs)
    me, me_seq = lax.axis_index("fsdp"), lax.axis_index("seq")
    own = sems.copy(slots.at[0], home_ref.at[me_seq])
    height = slots.shape[1] // PIECES
    blocks = {
        k: [
            sems.remote(slots.at[k, pl.ds(n * height, height)], home_ref.at[me_seq, pl.ds(n * height, height)], "seq", k)
            for n in range(PIECES)
        ]
        for k in range(1, seq)
    }
    order = sorted(range(1, seq), key=lambda k: (k != 2, k == 1))
    ready = []

    def send_piece(n=1):
        for _ in range(n):
            if ready:
                ready.pop(0).start()

    operands = [sems.copy(src, dst) for src, dst in zip(anys, local)]
    loads = [sems.copy(sums_in[w], held[w]) for w in range(count)]
    loads += [sems.copy(wholes_in[w], grads[w]) for w in range(more * first)]
    stores = [
        sems.copy(src, dst)
        for src, dst in ((in_final, in_out), (out_final, out_out), (qkv_final, qkv_out))
    ]
    finals = [in_final.at[:, pl.ds(0, FF)], in_final.at[:, pl.ds(FF, FF)], out_final]
    for w, reducer in enumerate(reducers):
        reducer.bind(lambda j, w=w: held[w], lands[w], sems, early[w], len(reducer.steps), finals[w])
    for w, reducer in enumerate(whole):
        if first:
            parts = lambda j, w=w: grads[w].at[whole[w].steps[0]["keep"].index(j)]
        else:
            parts = lambda j, w=w: shard_of(grads[w], whole[w].rows, flip(me, j))
        reducer.bind(parts, whole_lands[w], sems, first, len(reducer.steps), qkv_final.at[:, pl.ds(w * D, D)])
    hops = [("fsdp", b) for b in bits_of(fsdp)] + [("rep", b) for b in bits_of(rep)] + [("seq", b) for b in bits_of(seq)]
    gain_moves = [sems.remote(gains_out, gain_lands.at[i], axis, bit) for i, (axis, bit) in enumerate(hops)]
    rows = slots.shape[1]

    def advance(some, s):
        for reducer in some:
            if s < len(reducer.steps):
                reducer.finish(s)
                if s + 1 < len(reducer.steps):
                    reducer.start(s + 1)

    def advance_gains(i):
        if i < len(hops):
            gain_moves[i].wait()
            gains_out[...] += gain_lands[i]
            if i + 1 < len(hops):
                gain_moves[i + 1].start()

    def input_slot(k):
        piece = slice(k * rows, (k + 1) * rows)
        da = dot_nt(dq_ref[piece, :], w_ref[:, :D])
        da = da + dot_nt(dk_ref[piece, :], w_ref[:, D : 2 * D])
        da = da + dot_nt(dv_ref[piece, :], w_ref[:, 2 * D :])
        unit, scale = normalize(x_ref[piece, :].astype(f32))
        back, terms = norm_back(unit, scale, gain_ref[0:1, :], da)
        gains_out[0:1, :] += jnp.sum(terms, axis=0, keepdims=True)
        slots[k] = (dx1_ref[piece, :] + back).astype(bf16)
        if k:
            ready.extend(blocks[k])

    def gradient(w, part):
        weight_gradient(grads[w], wide, a_ref[0], part)
        whole[w].start(0)

    across = len(bits_of(fsdp)) + len(bits_of(rep))
    halves, out, last = reducers[:2], reducers[2:], len(whole[0].steps)
    start_all(loads)
    start_all(operands)
    gains_out[...] = jnp.zeros_like(gains_out)
    gains_out[1:2, :] = other_gain_ref[...]
    meet(all_partners(sizes))
    wait_all(loads)
    for w, (reducer, s) in enumerate(zip(reducers, early)):
        if s < len(reducer.steps):
            reducer.start(s)
        else:
            finals[w][...] = held[w][...]
    for reducer in whole[: more * first]:
        reducer.start(1)
    wait_all(operands)

    def begin(w, part):
        if not first:
            gradient(w, part)

    begin(0, dq_ref)
    input_slot(order[0])
    send_piece(PIECES // 2)
    if not first:
        advance(whole[:1], 0)
    advance(halves, early[0])
    begin(1, dk_ref)
    for k in order[1:2]:
        input_slot(k)
    if not first:
        advance(whole[1:2], 0)
    advance(out, early[2])
    send_piece()
    begin(2, dv_ref)
    advance(whole[:1], 1)
    for k in order[2:]:
        input_slot(k)
    if not first:
        advance(whole[2:], 0)
    send_piece()
    advance(whole[1:2], 1)
    input_slot(0)
    own.start()
    gain_moves[0].start()
    advance(out, early[2] + 1)
    send_piece()
    for s in range(2, across):
        advance(whole[:1], s)
        advance(whole[2:], s - 1)
        advance(whole[1:2], s)
        send_piece()
    advance(whole[2:], across - 1)
    send_piece()
    i = 0
    for s in range(across, last):
        for reducer in whole:
            advance([reducer], s)
            send_piece()
        for _ in range(2):
            advance_gains(i)
            i += 1
    while i < len(hops):
        advance_gains(i)
        i += 1
    send_piece(len(ready))
    for s in range(early[0] + 1, len(halves[0].steps)):
        advance(halves, s)
    for s in range(early[2] + 2, len(out[0].steps)):
        advance(out, s)
    start_all(stores)
    wait_all(stores)
    own.wait()
    for k in range(1, seq):
        wait_all(blocks[k])


def rows_spec(width):
    return pl.BlockSpec((TILE, width), lambda i: (i, 0))


def whole_spec(*shape):
    return pl.BlockSpec(shape, lambda i: (0,) * len(shape))


def pair_spec(length, offset=0):
    return pl.BlockSpec((length, PAIR), lambda i: (0, i + offset))


def struct(dtype, *shape):
    return jax.ShapeDtypeStruct(shape, dtype)


def call(kernel, grid, in_specs, out_specs, out_shape, flops, scratch=(), collective=None):
    return pl.pallas_call(
        kernel,
        grid=(grid,),
        in_specs=in_specs,
        out_specs=out_specs,
        out_shape=out_shape,
        scratch_shapes=list(scratch),
        compiler_params=pltpu.CompilerParams(
            dimension_semantics=("arbitrary",), vmem_limit_bytes=VMEM_LIMIT,
            collective_id=collective, has_side_effects=collective is not None,
        ),
        cost_estimate=pl.CostEstimate(flops=flops, bytes_accessed=10 * 2**20, transcendentals=0),
    )


MESH = pl.DeviceIdType.MESH
ANY = pl.BlockSpec(memory_space=pl.ANY)


def take(array, index):
    return lax.dynamic_index_in_dim(array, index, 0, keepdims=False)


def flip(index, mask):
    bit = 1
    while bit <= mask:
        if mask & bit:
            index = index + bit - 2 * bit * ((index // bit) % 2)
        bit *= 2
    return index


def flip_by(index, mask, size):
    total = 0
    for bit in bits_of(size):
        ours, theirs = (index // bit) % 2, (mask // bit) % 2
        total = total + bit * (ours + theirs - 2 * ours * theirs)
    return total


def bits_of(size):
    return [1 << i for i in range(size.bit_length() - 1)]


def meet(partners):
    barrier = pltpu.get_barrier_semaphore()
    for axis, mask in partners:
        pl.semaphore_signal(
            barrier, inc=1, device_id={axis: flip(lax.axis_index(axis), mask)}, device_id_type=MESH
        )
    pl.semaphore_wait(barrier, len(partners))


class Sems:
    def __init__(self, send, recv, local):
        self.send, self.recv, self.local = send, recv, local
        self.remote_used = self.local_used = 0

    def remote(self, src, dst, axis, mask):
        i = self.remote_used
        self.remote_used += 1
        return pltpu.make_async_remote_copy(
            src_ref=src, dst_ref=dst, send_sem=self.send.at[i], recv_sem=self.recv.at[i],
            device_id={axis: flip(lax.axis_index(axis), mask)}, device_id_type=MESH,
        )

    def copy(self, src, dst):
        i = self.local_used
        self.local_used += 1
        return pltpu.make_async_copy(src, dst, self.local.at[i])


def sem_shapes(remote, local):
    dma = pltpu.SemaphoreType.DMA
    return [dma((remote,)), dma((remote,)), dma((max(local, 1),))]


def start_all(copies):
    for copy in copies:
        copy.start()


def wait_all(copies):
    for copy in copies:
        copy.wait()


class Gather:
    def __init__(self, sizes, shards, place, sems, order):
        self.sizes, self.shards, self.place, self.sems = sizes, shards, place, sems
        self.pieces = order
        self.me, self.me_rep = lax.axis_index("fsdp"), lax.axis_index("rep")
        self.pending = []

    def part(self, ref, pieces, n):
        width = ref.shape[-1] // (self.sizes[1] * pieces)
        start = (self.me_rep * pieces + n) * width
        return ref.at[:, pl.ds(pl.multiple_of(start, 128), width)]

    def source(self, w, h):
        return self.shards[w] if h == 0 else self.place(w, flip(self.me, h))

    def start(self):
        self.held = [0]
        self.over = self.cross(self.far_bits()[0]) if self.far_bits() else []

    def far_bits(self):
        return list(reversed(bits_of(self.sizes[0])[1:]))

    def cross(self, bit):
        over = []
        for w, pieces, n in self.pieces:
            moved = [
                self.sems.remote(
                    self.part(self.source(w, h), pieces, n),
                    self.part(self.place(w, flip(self.me, h)), pieces, n), "fsdp", bit,
                )
                for h in self.held
            ]
            start_all(moved)
            over.append(moved)
        return over

    def pass_on(self, i, bit):
        w, pieces, n = self.pieces[i]
        for copy in self.over[i]:
            copy.wait_recv()
        self.pending += self.over[i]
        passed = []
        for mask in range(1, self.sizes[1]):
            for h in self.held:
                here = self.part(self.place(w, flip(self.me, h ^ bit)), pieces, n)
                passed.append(self.sems.remote(here, here, "rep", mask))
        start_all(passed)
        self.pending += passed
        return passed

    def events(self, lag=2):
        bits = self.far_bits()
        count = len(self.pieces)
        for bit in bits[:-1]:
            passed = [self.pass_on(i, bit) for i in range(count)]
            self.held = self.held + [h ^ bit for h in self.held]
            for copies in passed:
                for copy in copies:
                    copy.wait_recv()
            self.over = self.cross(bits[bits.index(bit) + 1])
        end = {w: i for i, (w, _, _) in enumerate(self.pieces)}
        passed, near_held = [], self.held + [h ^ bit for bit in bits[-1:] for h in self.held]
        for i in range(count + lag):
            if i < count:
                if bits:
                    passed.append(self.pass_on(i, bits[-1]))
                yield None
            for w, last in end.items():
                if last == i - lag:
                    if bits:
                        for j, (other, _, _) in enumerate(self.pieces):
                            if other == w:
                                for copy in passed[j]:
                                    copy.wait_recv()
                    yield w, self.near(w, near_held)

    def near(self, w, held):
        copies = [self.sems.remote(self.source(w, h), self.place(w, flip(self.me, h)), "fsdp", 1) for h in held]
        start_all(copies)
        return copies

    @staticmethod
    def count(sizes, order, weights):
        held, copies = 1, 0
        for _ in bits_of(sizes[0])[1:]:
            copies += len(order) * held * sizes[1]
            held *= 2
        return copies + weights * held


PASSED = (0, 1, 2, 4, 6, 6, 6)
CROSSED = (4, 5)


class LateGather:
    def __init__(self, sizes, shards, wholes, sems):
        fsdp, rep, _ = sizes
        me, me_rep = lax.axis_index("fsdp"), lax.axis_index("rep")
        place = lambda w, q: shard_of(wholes[w], shards[w].shape[0], q)
        self.own = [sems.copy(shards[w], place(w, me)) for w in range(2)]
        self.far, self.passed, self.near = [], [], [[], []]
        for w in range(2):
            fits = shards[w].shape[-1] % (rep * 3 * 128) == 0
            pieces = 3 if fits else 1
            width = shards[w].shape[-1] // (rep * pieces)
            for n in range(pieces if fsdp > 2 else 0):
                cols = pl.ds(pl.multiple_of((me_rep * pieces + n) * width, 128), width)
                self.far.append(sems.remote(shards[w].at[:, cols], place(w, me).at[:, cols], "fsdp", 2))
                here = place(w, flip(me, 2)).at[:, cols]
                self.passed.append([sems.remote(here, here, "rep", mask) for mask in range(1, rep)])
            for h in range(0, fsdp, 2):
                src = shards[w] if h == 0 else place(w, flip(me, h))
                self.near[w].append(sems.remote(src, place(w, flip(me, h)), "fsdp", 1))
        self.pieces = len(self.far) // 2
        self.count = len(self.far)

    @staticmethod
    def copies(sizes):
        return 2 * (3 * sizes[1] + sizes[0] // 2)

    def pass_on(self, i):
        self.far[i].wait_recv()
        start_all(self.passed[i])

    def cross_core(self, w):
        for copies in self.passed[w * self.pieces : (w + 1) * self.pieces]:
            for copy in copies:
                copy.wait_recv()
        start_all(self.near[w])

    def advance(self, step):
        upto = lambda n: min(n, self.count)
        for i in range(upto(PASSED[step - 1]), upto(PASSED[step])):
            self.pass_on(i)
        for w in range(2):
            if step == CROSSED[w]:
                self.cross_core(w)

    def finish(self, w):
        wait_all(self.own[w : w + 1])
        for i in range(w * self.pieces, (w + 1) * self.pieces):
            self.far[i].wait_send()
            for copy in self.passed[i]:
                copy.wait_send()
        wait_all(self.near[w])


def gather_order(sizes, shards):
    fits = lambda w, n: shards[w].shape[-1] % (sizes[1] * n * 128) == 0
    split = lambda w, n: n if fits(w, n) else 1
    order = []
    for w, n in ((0, 1), (1, 3), (2, 3), (4, 3), (3, 3)):
        if w >= len(shards):
            continue
        n = split(w, n)
        order += [(w, n, i) for i in range(n)]
    return order


def enter_kernel(sizes, count, tokens, *refs):
    fsdp, rep, seq = sizes
    refs = list(refs)
    pop = lambda n: [refs.pop(0) for _ in range(n)]
    shards = pop(count)
    (x_out,) = pop(1)
    fulls = pop(count)
    (bounce_x,) = pop(1)
    bounces = pop(count)
    sems = Sems(*refs)
    me, me_seq = lax.axis_index("fsdp"), lax.axis_index("seq")
    into = [sems.copy(tokens.at[me_seq], bounce_x)] + [sems.copy(shards[w], bounces[w]) for w in range(count)]
    outof = [sems.copy(bounce_x, x_out.at[0])] + [sems.copy(bounces[w], fulls[w].at[me]) for w in range(count)]
    gather = Gather(sizes, shards, lambda w, q: fulls[w].at[q], sems, gather_order(sizes, shards))
    start_all(into)
    meet(all_partners(sizes))
    blocks = [sems.remote(tokens.at[flip(me_seq, k)], x_out.at[k], "seq", k) for k in range(1, seq)]
    start_all(blocks)
    gather.start()
    last = []
    for event in gather.events():
        if event:
            last += event[1]
    wait_all(into)
    start_all(outof)
    for copy in gather.pending:
        copy.wait_send()
    wait_all(last)
    wait_all(blocks)
    wait_all(outof)


def enter(sizes, tokens, shards):
    fsdp = sizes[0]
    count = len(shards)
    hbm = lambda shape: struct(bf16, *shape)
    copies = sizes[2] - 1 + Gather.count(sizes, gather_order(sizes, shards), count)
    return pl.pallas_call(
        functools.partial(enter_kernel, sizes, count),
        in_specs=[ANY] * (1 + count),
        out_specs=[ANY] * (1 + count),
        out_shape=[hbm(tokens.shape)] + [hbm((fsdp,) + s.shape) for s in shards],
        scratch_shapes=[pltpu.VMEM(tokens.shape[1:], bf16)]
        + [pltpu.VMEM(s.shape, bf16) for s in shards]
        + sem_shapes(copies, 2 * (1 + count)),
        compiler_params=pltpu.CompilerParams(collective_id=0, has_side_effects=True),
    )(tokens, *shards)


def turn(row):
    n = row.shape[1]
    diagonal = lax.broadcasted_iota(jnp.int32, (n, n), 0) == lax.broadcasted_iota(jnp.int32, (n, n), 1)
    return jnp.sum(jnp.where(diagonal, row, 0), axis=1, keepdims=True)


def enter_project_kernel(sizes, count, tokens, segments, *refs):
    fsdp, rep, seq = sizes
    refs = list(refs)
    pop = lambda n: [refs.pop(0) for _ in range(n)]
    shards = pop(count)
    x_out, a_out, qkv_out, cos_out, sin_out, marks_out, row_out, gains_out, wq_out = pop(9)
    fulls = [None, None] + pop(count - 2)
    xs, a, qkv, wq, gains = pop(5)
    bounces = pop(count)
    sems = Sems(*refs)
    me, me_seq = lax.axis_index("fsdp"), lax.axis_index("seq")
    shard_rows, rows = shards[1].shape[0], xs.shape[1]
    columns = wq.shape[1]

    def place(w, q):
        if w == 0:
            return gains.at[q]
        if w == 1:
            return wq.at[pl.ds(pl.multiple_of(q * shard_rows, 16), shard_rows)]
        return fulls[w].at[q]

    own = sems.copy(tokens.at[me_seq], xs.at[0])
    into = [sems.copy(shards[w], place(w, me) if w < 2 else bounces[w - 2]) for w in range(count)]
    outof = [sems.copy(bounces[w - 2], place(w, me)) for w in range(2, count)]
    blocks = [sems.remote(tokens.at[flip(me_seq, k)], xs.at[k], "seq", k) for k in range(1, seq)]
    stores = [
        [sems.copy(src.at[k], dst.at[k]) for src, dst in ((xs, x_out), (a, a_out), (qkv, qkv_out))] for k in range(seq)
    ]
    keep = sems.copy(wq, wq_out)
    gather = Gather(sizes, shards, place, sems, gather_order(sizes, shards))
    own.start()
    start_all(into)
    meet(all_partners(sizes))
    gather.start()
    start_all(blocks)

    lane = lax.broadcasted_iota(jnp.int32, (1, PAIR), 1)
    rate = jnp.exp((lane % (HDIM // 2)).astype(f32) * (-2.0 * math.log(THETA) / HDIM))
    sign = jnp.where(lane_halves((1, PAIR)), -1.0, 1.0)
    batch = segments.shape[1]

    def own_segments(block):
        at = pl.multiple_of(block * rows, 128)
        return segments[me_seq // batch, pl.ds(me_seq % batch, 1), pl.ds(at, rows)]

    @pl.loop(0, seq)
    def _(k):
        block = flip_by(me_seq, k, seq)
        piece = pl.ds(pl.multiple_of(k * rows, 128), rows)
        row = own_segments(block)
        column = turn(row)
        earlier = jnp.zeros((rows, 1), jnp.int32)
        for other in range(seq):
            earlier += jnp.sum((own_segments(other) < column).astype(jnp.int32), axis=1, keepdims=True)
        index = block * rows + lax.broadcasted_iota(jnp.int32, (rows, 1), 0)
        angles = (index - earlier).astype(f32) * rate
        cos_out[piece, :] = jnp.cos(angles)
        sin_out[piece, :] = jnp.sin(angles) * sign
        marks_out[piece, :] = column
        row_out[:, piece] = row

    def project(k):
        if k == 0:
            own.wait()
        else:
            blocks[k - 1].wait()
        piece = slice(k * rows, (k + 1) * rows)
        unit, _ = normalize(xs[k].astype(f32))
        low = (unit * gains_out[0:1, :]).astype(bf16)
        a[k] = low
        cosine, sine = cos_out[piece, :], sin_out[piece, :]

        @pl.loop(0, 2 * D // WIDE)
        def _(i):
            at = pl.multiple_of(i * WIDE, WIDE)
            part = dot_nn(low, wq[:, pl.ds(at, WIDE)])
            scale = jnp.where(at < D, QUERY_SCALE, 1.0)
            for half in range(0, WIDE, PAIR):
                value = rotate_pair(part[:, half : half + PAIR], cosine, sine) * scale
                qkv[k, :, pl.ds(at + half, PAIR)] = value.astype(bf16)

        qkv[k, :, 2 * D :] = dot_nn(low, wq[:, 2 * D :]).astype(bf16)
        start_all(stores[k])

    last, queue, since = {}, list(range(seq)), 0
    for event in gather.events():
        if event:
            last[event[0]] = event[1]
            if event[0] == 1:
                for copy in into[:2] + last[0] + last[1]:
                    copy.wait()
                keep.start()
                total = gains[0, :2, :].astype(f32)
                for q in range(1, fsdp):
                    total = total + gains[q, :2, :].astype(f32)
                gains_out[...] = total
                wait_all(into[2:])
                start_all(outof)
                project(queue.pop(0))
        elif 1 in last:
            since += 1
            if since % 2 == 0 and len(queue) > 1:
                project(queue.pop(0))
    for k in queue:
        project(k)
    for copy in gather.pending:
        copy.wait_send()
    for w in range(2, count):
        wait_all(last[w])
    wait_all(outof)
    for group in stores:
        wait_all(group)
    keep.wait()


def enter_project(sizes, tokens, segments, shards):
    fsdp, rep, seq = sizes
    count, rows = len(shards), tokens.shape[1]
    length, columns = seq * rows, shards[1].shape[1]
    vmem = pl.BlockSpec(memory_space=pltpu.VMEM)
    copies = seq - 1 + Gather.count(sizes, gather_order(sizes, shards), count)
    return pl.pallas_call(
        functools.partial(enter_project_kernel, sizes, count),
        in_specs=[ANY, vmem] + [ANY] * count,
        out_specs=[ANY] * 3 + [vmem] * 5 + [ANY] * (count - 1),
        out_shape=[struct(bf16, seq, rows, D), struct(bf16, seq, rows, D), struct(bf16, seq, rows, columns),
                   struct(f32, length, PAIR), struct(f32, length, PAIR), struct(jnp.int32, length, 1),
                   struct(jnp.int32, 1, length), struct(f32, 2, D), struct(bf16, D, columns)]
        + [struct(bf16, fsdp, *s.shape) for s in shards[2:]],
        scratch_shapes=[pltpu.VMEM((seq, rows, D), bf16), pltpu.VMEM((seq, rows, D), bf16),
                        pltpu.VMEM((seq, rows, columns), bf16), pltpu.VMEM((D, columns), bf16),
                        pltpu.VMEM((fsdp,) + shards[0].shape, bf16)]
        + [pltpu.VMEM(s.shape, bf16) for s in shards[2:]] + [pltpu.VMEM((16, 128), bf16)] * 2
        + sem_shapes(copies, 2 + count + count - 2 + 3 * seq),
        compiler_params=pltpu.CompilerParams(
            collective_id=4, has_side_effects=True, vmem_limit_bytes=VMEM_LIMIT
        ),
    )(tokens, segments, *shards)


def add_into(total, term):
    rows = total.shape[0]
    height = 48 if rows % 48 == 0 else rows

    @pl.loop(0, rows // height)
    def _(i):
        at = pl.ds(pl.multiple_of(i * height, 16), height) if height < rows else pl.ds(0, rows)
        total[at, :] = (total[at, :].astype(f32) + term[at, :].astype(f32)).astype(bf16)


class Reducer:
    def __init__(self, parts_shape, sizes, order):
        self.fsdp, self.rows, self.cols = parts_shape
        self.steps = []
        held, rows, cols = list(range(self.fsdp)), self.rows, self.cols
        row_at, col_at = [], []
        for axis, bit in order:
            step = dict(axis=axis, bit=bit, row_at=list(row_at), col_at=list(col_at), rows=rows, cols=cols)
            if axis == "fsdp":
                step["send"] = [j for j in held if j & bit]
                held = [j for j in held if not j & bit]
                step["keep"] = held
                step["shape"] = (len(held), rows, cols)
                step["split"] = None
            else:
                step["keep"] = step["send"] = held
                if (axis, bit) == order[-1]:
                    step["split"] = "none"
                elif (rows // 2) % 16 == 0:
                    rows //= 2
                    row_at = row_at + [(axis, bit, rows)]
                    step["split"] = "rows"
                elif (cols // 2) % 128 == 0:
                    cols //= 2
                    col_at = col_at + [(axis, bit, cols)]
                    step["split"] = "cols"
                else:
                    step["split"] = "none"
                step["shape"] = (len(held), rows, cols)
            self.steps.append(step)
        self.down = len(self.steps)
        for step in reversed(self.steps[: self.down]):
            if step["split"] in ("rows", "cols"):
                self.steps.append(dict(step, up=True))

    @staticmethod
    def offset(terms, align, last=None):
        total = 0
        for i, (axis, bit, extent) in enumerate(terms):
            half = (lax.axis_index(axis) // bit) % 2
            if last == i:
                half = 1 - half
            total = total + half * extent
        return total if isinstance(total, int) else pl.multiple_of(total, align)

    def region(self, step, after, other=False):
        row_at, col_at, rows, cols = step["row_at"], step["col_at"], step["rows"], step["cols"]
        row_last = col_last = None
        if after:
            if step["split"] == "rows":
                rows //= 2
                row_at = row_at + [(step["axis"], step["bit"], rows)]
                row_last = len(row_at) - 1 if other else None
            elif step["split"] == "cols":
                cols //= 2
                col_at = col_at + [(step["axis"], step["bit"], cols)]
                col_last = len(col_at) - 1 if other else None
        return (
            pl.ds(self.offset(row_at, 16, row_last), rows),
            pl.ds(self.offset(col_at, 128, col_last), cols),
        )

    def scratch(self, first, last):
        return [pltpu.VMEM(s["shape"], bf16) for s in self.steps[first:last] if "up" not in s]

    def copies(self, first, last):
        return sum(1 if "up" in s else len(s["send"]) for s in self.steps[first:last])

    def bind(self, parts, lands, sems, first, last, final=None):
        self.parts, self.sems, self.final = parts, sems, final
        self.lands, self.moves = {}, {}
        lands = list(lands)
        for s in range(first, last):
            step = self.steps[s]
            moves = []
            if "up" in step:
                there = final.at[self.region(step, True)]
                moves.append(sems.remote(there, there, step["axis"], step["bit"]))
            else:
                land = self.lands[s] = lands.pop(0)
                for i, j in enumerate(step["send"]):
                    fsdp = step["axis"] == "fsdp"
                    src = self.parts(j).at[self.region(step, not fsdp, not fsdp)]
                    moves.append(sems.remote(src, land.at[i], step["axis"], step["bit"]))
            self.moves[s] = moves

    def start(self, s):
        if s == self.down:
            region = self.region(self.steps[s - 1], True)
            self.final[region] = self.parts(0)[region]
        start_all(self.moves.get(s, []))

    def finish(self, s):
        step = self.steps[s]
        self.finish_step(s, step)
        if s + 1 == len(self.steps) == self.down and self.final is not None:
            self.final[...] = self.parts(0)[...]

    def finish_step(self, s, step):
        for i, move in enumerate(self.moves[s]):
            move.wait()
            if "up" not in step:
                j = step["keep"][i]
                ref = self.parts(j)
                add_into(ref.at[self.region(step, True)], self.lands[s].at[i])


def give_back(slots, home, bounce, sems):
    me = lax.axis_index("seq")
    seq = slots.shape[0]
    return (
        sems.copy(slots.at[0], bounce),
        sems.copy(bounce, home.at[me]),
        [sems.remote(slots.at[k], home.at[me], "seq", k) for k in range(1, seq)],
    )


def body(sizes, tokens, segments, positions, gain_attn, w_qkv, w_out, gain_mlp, w_in, w_mlp_out, cotangent):
    fsdp, rep, seq = sizes
    micro, batch, rows, _ = tokens.shape
    assert micro * batch == seq and rows % TILE == 0
    length = seq * rows
    me_seq, me_fsdp = lax.axis_index("seq"), lax.axis_index("fsdp")

    own_gains = jnp.zeros((16, D), bf16)
    own_gains = lax.dynamic_update_slice(own_gains, jnp.stack([gain_attn, gain_mlp]), (0, me_fsdp * (D // fsdp)))
    shards = [own_gains, w_qkv, w_out, w_mlp_out, w_in]
    tiles, pairs = length // TILE, HEADS // 2
    late = fsdp in (2, 4) and pairs >= 6 and flat(D // fsdp) and flat(FF // fsdp)
    if (D // fsdp) % 16 == 0:
        x, a, qkv, cosine, sine, marks_column, marks_row, gains, wq, *rest = enter_project(
            sizes, tokens.reshape(seq, rows, D), segments, shards[:3] if late else shards
        )
        x, a, qkv = (v.reshape(length, -1) for v in (x, a, qkv))
        wo, *rest = (w.reshape(-1, w.shape[-1]) for w in rest)
        wm, wi = (w_mlp_out, w_in) if late else rest
    else:
        x, gains, wq, wo, wm, wi = enter(sizes, tokens.reshape(seq, rows, D), shards)
        x = x.reshape(length, D)
        gains = jnp.sum(gains[:, :2].astype(f32), axis=0)
        wq, wo, wm, wi = (w.reshape(-1, w.shape[-1]) for w in (wq, wo, wm, wi))

        marks = take(segments.reshape(seq, length), me_seq)
        place = jnp.arange(length, dtype=jnp.int32) - jnp.sum(
            (marks[None, :] < marks[:, None]).astype(jnp.int32), axis=1
        )
        slot_order = [me_seq ^ k for k in range(seq)]
        marks = jnp.concatenate([take(marks.reshape(seq, rows), s) for s in slot_order])
        place = jnp.concatenate([take(place.reshape(seq, rows), s) for s in slot_order])
        half = jnp.arange(0, HDIM, 2).astype(f32) / HDIM
        angles = place.astype(f32)[:, None] * jnp.exp(-half * math.log(THETA))
        cosine, sine = jnp.cos(angles), jnp.sin(angles)
        cosine = jnp.concatenate([cosine] * 4, -1)
        sine = jnp.concatenate([-sine, sine] * 2, -1)

        a, qkv = call(
            first_kernel, tiles,
            [rows_spec(D), whole_spec(2, D), whole_spec(D, 3 * D), rows_spec(PAIR), rows_spec(PAIR)],
            [rows_spec(D), rows_spec(3 * D)],
            [struct(bf16, length, D), struct(bf16, length, 3 * D)],
            2 * length * D * 3 * D,
        )(x, gains, wq, cosine, sine)
        marks_column, marks_row = marks[:, None], marks[None, :]

    vmem = pl.BlockSpec(memory_space=pltpu.VMEM)
    pair_at = lambda offset, lag, n: pl.BlockSpec(
        (length, PAIR), lambda i: (0, jnp.clip(i - lag, 0, n - 1) + offset)
    )
    prob_at = lambda lag: pl.BlockSpec((2, length, length), lambda i: (jnp.clip(i - lag, 0, pairs - 1), 0, 0))
    tile_at = lambda width, lag: pl.BlockSpec((TILE, width), lambda i: (jnp.clip(i - lag, 0, tiles - 1), 0))
    slots = struct(bf16, seq, rows, D)
    o, probs, inv, x1, b, m, slope, act, y, dy, *wholes = call(
        functools.partial(forward_kernel, sizes, pairs, late), pairs + tiles,
        [pair_at(0, 0, pairs), pair_at(pairs, 0, pairs), pair_at(2 * pairs, 0, pairs),
         whole_spec(length, 1), whole_spec(1, length), tile_at(D, pairs), whole_spec(2, D)] + [ANY] * 4,
        [pair_at(0, 0, pairs), prob_at(0), pair_at(0, 0, pairs), tile_at(D, pairs), tile_at(D, pairs)]
        + [tile_at(FF, pairs)] * 3 + [tile_at(D, pairs), ANY] + [ANY] * (2 * late),
        [struct(bf16, length, D), struct(bf16, HEADS, length, length), struct(f32, length, D),
         struct(f32, length, D), struct(bf16, length, D), struct(bf16, length, FF),
         struct(bf16, length, FF), struct(bf16, length, FF), struct(bf16, length, D), slots]
        + [struct(bf16, D, 2 * FF), struct(bf16, FF, D)] * late,
        16 * length * length * D,
        [pltpu.VMEM((length, D), bf16), pltpu.VMEM((D, D), bf16), pltpu.VMEM((D, 2 * FF), bf16), pltpu.VMEM((FF, D), bf16),
         pltpu.VMEM((rows, D), bf16)] + sem_shapes(seq - 1 + LateGather.copies(sizes) * late, 5 + 2 * late), 1,
    )(qkv, qkv, qkv, marks_column, marks_row, x, gains, wo, wi, wm, cotangent.reshape(seq, rows, D))

    if late:
        wi, wm = wholes
    reducers, early = early_reducers(sizes)
    whole = late_reducers(sizes)
    own_shard = lambda r: struct(bf16, r.rows, r.cols)
    full_shard = lambda r: pltpu.VMEM((fsdp * r.rows, r.cols) if flat(r.rows) else (fsdp, r.rows, r.cols), bf16)
    first = begun(sizes)
    partial = lambda r: struct(bf16, len(r.steps[0]["keep"]), r.rows, r.cols)
    odd = (FF // fsdp) % 16 or (D // fsdp) % 16
    wide = pltpu.VMEM((FF, FF) if odd else (8, 128), f32)
    dx1, dgain_two, dq, dk, dv, block_out, *sums = call(
        functools.partial(backward_kernel, sizes, tiles), tiles + 1 + pairs,
        [tile_at(D, 0), tile_at(FF, 0), tile_at(FF, 0), whole_spec(2, D)]
        + [pair_at(n * pairs, tiles + 1, pairs) for n in range(3)]
        + [pair_at(0, tiles + 1, pairs), pair_at(0, tiles + 1, pairs)] + [ANY] * 12,
        [tile_at(D, 0), whole_spec(1, D)] + [pair_at(0, tiles + 1, pairs)] * 3 + [ANY] * (1 + len(reducers) + first * len(whole)),
        [struct(f32, length, D), struct(f32, 1, D)] + [struct(bf16, length, D)] * 3 + [slots]
        + [own_shard(r) for r in reducers] + [partial(r) for r in whole] * first,
        32 * length * length * D,
        [pltpu.VMEM((D, D), bf16), pltpu.VMEM((D, 2 * FF), bf16), pltpu.VMEM((FF, D), bf16),
         pltpu.VMEM((length, FF), bf16)] + [pltpu.VMEM((length, D), bf16)] * 3
        + [pltpu.VMEM((length, 2 * FF), bf16), pltpu.VMEM((length, D), bf16), pltpu.VMEM((length, D), bf16),
           wide, pltpu.VMEM((rows, D), bf16),
           pltpu.VMEM((2, 2, length, length), bf16)] + [pltpu.VMEM((length, PAIR), f32)] * 2
        + [full_shard(r) for r in reducers] + [pltpu.VMEM((reducers[0].rows, reducers[0].cols), bf16)]
        + [land for r, e in zip(reducers, early) for land in r.scratch(0, e)]
        + sem_shapes(
            seq - 1 + sum(r.copies(0, e) for r, e in zip(reducers, early)) + sum(r.copies(0, first) for r in whole),
            14 + len(reducers) + first * len(whole) * fsdp // 2,
        ), 2,
    )(x1, slope, act, gains, qkv, qkv, qkv, o, inv, probs, cosine, sine,
      wo, wi, wm, m, dy.reshape(length, D), b, o, a, y.reshape(seq, rows, D))

    hops = sum(len(bits_of(n)) for n in sizes)
    shard = lambda n, width: struct(bf16, n // fsdp, width)
    finals = [shard(D, 2 * FF), shard(D, D), shard(D, 3 * D)]
    operands = [dq, dk, dv, wq, x, dx1] + ([] if first else [a])
    grad_mlp, *sums = sums
    reducers, early = reducers[1:], early[1:]
    input_grad, grad_in, grad_out, grad_qkv, dgains = pl.pallas_call(
        functools.partial(leave_kernel, sizes),
        in_specs=[vmem] * 2 + [ANY] * (len(operands) + len(sums)),
        out_specs=[ANY] * 4 + [vmem],
        out_shape=[slots] + finals + [struct(f32, 8, D)],
        scratch_shapes=[pltpu.VMEM(v.shape, v.dtype) for v in operands]
        + [pltpu.VMEM((seq, rows, D), bf16), wide]
        + [pltpu.VMEM(v.shape, v.dtype) for v in finals]
        + [pltpu.VMEM((r.rows, r.cols), bf16) for r in reducers]
        + [pltpu.VMEM(partial(r).shape, bf16) if first else full_shard(r) for r in whole]
        + [land for r, e in zip(reducers, early) for land in r.scratch(e, len(r.steps))]
        + [land for r in whole for land in r.scratch(first, len(r.steps))]
        + [pltpu.VMEM((hops, 8, D), f32)]
        + sem_shapes(
            PIECES * (seq - 1) + hops + sum(r.copies(e, len(r.steps)) for r, e in zip(reducers, early))
            + sum(r.copies(first, len(r.steps)) for r in whole),
            1 + len(operands) + len(sums) + len(finals),
        ),
        compiler_params=pltpu.CompilerParams(
            collective_id=3, has_side_effects=True, vmem_limit_bytes=VMEM_LIMIT
        ),
    )(gains, dgain_two, *operands, *sums)
    dgains = lax.dynamic_slice_in_dim(dgains, me_fsdp * (D // fsdp), D // fsdp, 1)
    return (
        block_out.reshape(tokens.shape),
        input_grad.astype(f32).reshape(tokens.shape),
        dgains[0],
        grad_qkv.astype(f32),
        grad_out.astype(f32),
        dgains[1],
        grad_in.astype(f32),
        grad_mlp.astype(f32),
    )


def solution(mesh):
    sizes = (mesh.shape["fsdp"], mesh.shape["rep"], mesh.shape["seq"])
    wide = P(None, ("rep", "fsdp"), "seq", None)
    placed = (
        wide, P(None, ("rep", "fsdp"), None), P(None, ("rep", "fsdp"), "seq"),
        P("fsdp"), P("fsdp", None), P("fsdp", None), P("fsdp"), P("fsdp", None), P("fsdp", None), wide,
    )
    return jax.shard_map(
        functools.partial(body, sizes),
        mesh=mesh,
        in_specs=placed,
        out_specs=(
            wide, wide, P("fsdp"), P("fsdp", None), P("fsdp", None), P("fsdp"), P("fsdp", None), P("fsdp", None),
        ),
        check_vma=False,
    )
```

```python
import functools
import math

import jax
import jax.numpy as jnp
from jax import lax
from jax.experimental import pallas as pl
from jax.experimental.pallas import tpu as pltpu
from jax.sharding import PartitionSpec as P

D = 768
HEADS = 12
HDIM = 64
FF = 1152
EPS = 1e-05
THETA = 160000.0
MASKED = -1000000000.0
QUERY_SCALE = HDIM**-0.5 / math.log(2.0)
TILE = 256
PAIR = 2 * HDIM
WIDE = 384
HCHUNK = 384
f32 = jnp.float32
bf16 = jnp.bfloat16
VMEM_LIMIT = 62 * 2**20


def dot_nn(left, right):
    return lax.dot_general(left, right, (((1,), (0,)), ((), ())), preferred_element_type=f32)


def dot_nt(left, right):
    return lax.dot_general(left, right, (((1,), (1,)), ((), ())), preferred_element_type=f32)


def dot_tn(left, right):
    return lax.dot_general(left, right, (((0,), (0,)), ((), ())), preferred_element_type=f32)


def normalize(values):
    mean = jnp.mean(values, axis=-1, keepdims=True)
    centered = values - mean
    var = jnp.mean(centered * centered, axis=-1, keepdims=True)
    scale = lax.rsqrt(var + EPS)
    return centered * scale, scale


def norm_back(unit, scale, gain, grad):
    gain_terms = grad * unit
    inner = grad * gain
    first = jnp.mean(inner, axis=-1, keepdims=True)
    second = jnp.mean(inner * unit, axis=-1, keepdims=True)
    return scale * (inner - first - unit * second), gain_terms


def lane_halves(shape):
    lane = lax.broadcasted_iota(jnp.int32, shape, len(shape) - 1)
    return lane % HDIM < HDIM // 2


def rotate_pair(values, cosine, signed_sine):
    swapped = jnp.where(
        lane_halves(values.shape),
        pltpu.roll(values, PAIR - HDIM // 2, 1),
        pltpu.roll(values, HDIM // 2, 1),
    )
    return values * cosine + swapped * signed_sine


def first_kernel(x_ref, gain_ref, w_ref, cos_ref, sin_ref, a_ref, qkv_ref):
    unit, _ = normalize(x_ref[...].astype(f32))
    a = (unit * gain_ref[0:1, :]).astype(bf16)
    a_ref[...] = a
    cosine, sine = cos_ref[...], sin_ref[...]
    for column in range(0, 3 * D, TILE):
        part = dot_nn(a, w_ref[:, column : column + TILE])
        for half in range(0, TILE, PAIR):
            start = column + half
            piece = part[:, half : half + PAIR]
            if start < 2 * D:
                piece = rotate_pair(piece, cosine, sine)
            if start < D:
                piece = piece * QUERY_SCALE
            qkv_ref[:, start : start + PAIR] = piece.astype(bf16)


def head_lanes():
    lane = lax.broadcasted_iota(jnp.int32, (1, PAIR), 1)
    return [lane < HDIM, lane >= HDIM]


def attend_pair(q_ref, k_ref, v_ref, rows_ref, cols_ref, p_ref, inv_ref, write):
    k, v = k_ref[...], v_ref[...]
    length = k.shape[0]
    mine = head_lanes()
    zero, one = jnp.zeros((), bf16), jnp.ones((), bf16)
    summing = [jnp.where(m, v, one) for m in mine]
    items = [(tile, head) for tile in range(0, length, TILE) for head in range(2)]

    def score(item):
        tile, head = item
        return dot_nt(jnp.where(mine[head], q_ref[tile : tile + TILE, :], zero), k)

    ahead = score(items[0])
    kept = None
    for i, (tile, head) in enumerate(items):
        rows = slice(tile, tile + TILE)
        scores = ahead
        if i + 1 < len(items):
            ahead = score(items[i + 1])
        scores = jnp.where(rows_ref[rows, :] == cols_ref[...], scores, MASKED)
        probs = jnp.exp2(scores - jnp.max(scores, axis=-1, keepdims=True)).astype(bf16)
        p_ref[head, rows, :] = probs
        part = dot_nn(probs, summing[head])
        inv = 1.0 / pltpu.roll(part, HDIM, 1)
        if head == 0:
            kept = (part * inv, inv)
        else:
            inv_ref[rows, :] = jnp.where(mine[0], kept[1], inv)
            write(rows, jnp.where(mine[0], kept[0], part * inv).astype(bf16))


def forward_kernel(
    sizes, pairs, late, q_ref, k_ref, v_ref, rows_ref, cols_ref, x_ref, gain_ref, w_out_any, w_in_any, w_mlp_any, cot_ref,
    o_ref, p_ref, inv_ref, x1_ref, b_ref, m_ref, slope_ref, act_ref, y_ref, dy_ref, *refs,
):
    seq = sizes[2]
    refs = list(refs)
    outs = [refs.pop(0) for _ in range(2 * late)]
    joined, w_out_ref, w_in_ref, w_mlp_ref, bounce, *sem_refs = refs
    step, last = pl.program_id(0), pl.num_programs(0) - 1
    sems = Sems(*sem_refs)
    me_seq = lax.axis_index("seq")
    into = sems.copy(cot_ref.at[me_seq], bounce)
    outof = sems.copy(bounce, dy_ref.at[0])
    weights = [sems.copy(w_out_any, w_out_ref)]
    partners = [("seq", k) for k in range(1, seq)]
    if late:
        gather = LateGather(sizes, [w_in_any, w_mlp_any], [w_in_ref, w_mlp_ref], sems)
        weights += gather.own
        keeps = [sems.copy(w_in_ref, outs[0]), sems.copy(w_mlp_ref, outs[1])]
        partners = all_partners(sizes)
    else:
        weights += [sems.copy(w_in_any, w_in_ref), sems.copy(w_mlp_any, w_mlp_ref)]
    blocks = [sems.remote(cot_ref.at[flip(me_seq, k)], dy_ref.at[k], "seq", k) for k in range(1, seq)]

    @pl.when(step == 0)
    def _():
        into.start()
        start_all(weights)
        meet(partners)
        if late:
            start_all(gather.far)
        start_all(blocks)
        into.wait()
        outof.start()

    if late:
        for when in range(1, pairs + 1):
            @pl.when(step == when)
            def _(when=when):
                gather.advance(when)

    @pl.when(step < pairs)
    def _():
        def write(rows, value):
            o_ref[rows, :] = value
            joined[rows, pl.ds(pl.multiple_of(step * PAIR, PAIR), PAIR)] = value

        attend_pair(q_ref, k_ref, v_ref, rows_ref, cols_ref, p_ref, inv_ref, write)

    @pl.when(step == pairs)
    def _():
        if late:
            wait_all(weights[:1])
            gather.finish(0)
            keeps[0].start()
        else:
            wait_all(weights)

    @pl.when(step >= pairs)
    def _():
        start = pl.multiple_of((step - pairs) * TILE, TILE)
        x1 = x_ref[...].astype(f32) + dot_nn(joined[pl.ds(start, TILE), :], w_out_ref[...])
        x1_ref[...] = x1
        unit, _ = normalize(x1)
        b = (unit * gain_ref[1:2, :]).astype(bf16)
        b_ref[...] = b

        def hidden(column):
            return (
                dot_nn(b, w_in_ref[:, column : column + HCHUNK]),
                dot_nn(b, w_in_ref[:, FF + column : FF + column + HCHUNK]),
            )

        ahead = hidden(0)
        for column in range(0, FF, HCHUNK):
            hin, gate = ahead
            if column + HCHUNK < FF:
                ahead = hidden(column + HCHUNK)
            phi = 0.5 + 0.5 * lax.erf(hin * math.sqrt(0.5))
            act = hin * phi
            slope = phi + hin * (jnp.exp(hin * hin * -0.5) * (1.0 / math.sqrt(2.0 * math.pi)))
            m_ref[:, column : column + HCHUNK] = (act * gate).astype(bf16)
            act_ref[:, column : column + HCHUNK] = act.astype(bf16)
            slope_ref[:, column : column + HCHUNK] = (slope * gate).astype(bf16)
        if late:
            @pl.when(step == pairs)
            def _():
                gather.finish(1)
                keeps[1].start()

        y_ref[...] = (x1_ref[...] + dot_nn(m_ref[...], w_mlp_ref[...])).astype(bf16)

    @pl.when(step == last)
    def _():
        if late:
            wait_all(keeps)
        outof.wait()
        wait_all(blocks)


def order_of(sizes, rep_first):
    fsdp, rep, seq = sizes
    core = [("fsdp", 1)]
    rest = [("fsdp", b) for b in bits_of(fsdp)[1:]]
    copies = [("rep", b) for b in bits_of(rep)]
    return core + (copies + rest if rep_first else rest + copies) + [("seq", b) for b in bits_of(seq)]


def all_partners(sizes):
    fsdp, rep, seq = sizes
    return [("seq", k) for k in range(1, seq)] + [("fsdp", b) for b in bits_of(fsdp)] + [("rep", b) for b in bits_of(rep)]


def early_reducers(sizes):
    fsdp, rep, seq = sizes
    shapes = [(fsdp, FF // fsdp, D), (fsdp, D // fsdp, FF), (fsdp, D // fsdp, FF), (fsdp, D // fsdp, D)]
    reducers = [Reducer(shape, sizes, order_of(sizes, w == 2)) for w, shape in enumerate(shapes)]
    across = len(bits_of(fsdp)) + len(bits_of(rep))
    return reducers, [len(reducers[0].steps)] + [across + 2] * 2 + [across + 1]


def late_reducers(sizes):
    fsdp = sizes[0]
    return [Reducer((fsdp, D // fsdp, D), sizes, order_of(sizes, w == 1)) for w in range(3)]


def flat(rows):
    return rows % 16 == 0


def shard_of(ref, rows, q):
    return ref.at[pl.ds(pl.multiple_of(q * rows, 16), rows)] if flat(rows) else ref.at[q]


def weight_gradient(ref, wide, left, right):
    if len(ref.shape) == 2:
        @pl.loop(0, ref.shape[0] // HCHUNK)
        def _(i):
            at = pl.ds(pl.multiple_of(i * HCHUNK, HCHUNK), HCHUNK)
            ref[at, :] = dot_tn(left[:, at], right[...]).astype(bf16)
    else:
        shards, rows, cols = ref.shape
        wide[: shards * rows, :cols] = dot_tn(left[...], right[...])
        for q in range(shards):
            ref[q] = wide[q * rows : (q + 1) * rows, :cols].astype(bf16)


def middle_back_tile(dy, x1_ref, slope_ref, act_ref, gain_ref, w_out_ref, w_in_ref, w_mlp_ref, dh_ref, dgain_ref, dx1_ref):
    ahead = dot_nt(dy, w_mlp_ref[:HCHUNK, :])
    for column in range(0, FF, HCHUNK):
        dm = ahead
        if column + HCHUNK < FF:
            ahead = dot_nt(dy, w_mlp_ref[column + HCHUNK : column + 2 * HCHUNK, :])
        dh_ref[:, column : column + HCHUNK] = (dm * slope_ref[:, column : column + HCHUNK].astype(f32)).astype(bf16)
        dh_ref[:, FF + column : FF + column + HCHUNK] = (
            dm * act_ref[:, column : column + HCHUNK].astype(f32)
        ).astype(bf16)
    db = dot_nt(dh_ref[...], w_in_ref[...])
    unit, scale = normalize(x1_ref[...])
    back, terms = norm_back(unit, scale, gain_ref[1:2, :], db)
    dgain_ref[...] += jnp.sum(terms, axis=0, keepdims=True)
    dx1 = dy.astype(f32) + back
    dx1_ref[...] = dx1
    return dx1.astype(bf16)


def attend_back_pair(q_ref, k_ref, v_ref, o_ref, inv_ref, do, p_ref, cos_ref, sin_ref, dq_ref, dk_ref, dv_ref):
    v = v_ref[...]
    length = v.shape[0]
    mine = head_lanes()
    zero = jnp.zeros((), bf16)
    do = (do.astype(f32) * inv_ref[...]).astype(bf16)
    inner = do.astype(f32) * o_ref[...].astype(f32)
    do_heads = [jnp.where(m, do, zero) for m in mine]
    q_heads = [jnp.where(m, q_ref[...], zero).T for m in mine]
    k_heads = [jnp.where(m, k_ref[...], zero) for m in mine]
    do_turned = [d.T for d in do_heads]
    cosine, sine = cos_ref[...], sin_ref[...]
    dv = dk = None
    for tile in range(0, length, TILE):
        rows = slice(tile, tile + TILE)
        dq = None
        for head in range(2):
            probs = p_ref[head, rows, :]
            delta = jnp.sum(jnp.where(mine[head], inner[rows], 0.0), axis=-1, keepdims=True)
            dp = dot_nt(do_heads[head][rows], v)
            ds = (probs.astype(f32) * (dp - delta)).astype(bf16)
            value_part = dot_nn(do_turned[head][:, rows], probs)
            key_part = dot_nn(q_heads[head][:, rows], ds)
            query_part = dot_nn(ds, k_heads[head])
            dv = value_part if dv is None else dv + value_part
            dk = key_part if dk is None else dk + key_part
            dq = query_part if dq is None else dq + query_part
        dq_ref[rows, :] = rotate_pair(dq * HDIM**-0.5, cosine[rows], -sine[rows]).astype(bf16)
    dk_ref[...] = rotate_pair(dk.T * math.log(2.0), cosine, -sine).astype(bf16)
    dv_ref[...] = dv.T.astype(bf16)


def backward_kernel(
    sizes, tiles, x1_ref, slope_ref, act_ref, gain_ref, q_ref, k_ref, v_ref, o_ref, inv_ref,
    p_any, cos_any, sin_any, w_out_any, w_in_any, w_mlp_any, m_any, dy_any, b_any, o_any, y_ref, *refs,
):
    reducers, early = early_reducers(sizes)
    count = len(reducers)
    refs = list(refs)
    pop = lambda n: [refs.pop(0) for _ in range(n)]
    dx1_ref, dgain_ref, dq_ref, dk_ref, dv_ref, home_ref = pop(6)
    sums_out = pop(count)
    w_out_ref, w_in_ref, w_mlp_ref, m_ref, dy_ref, b_ref, all_o_ref = pop(7)
    dh_ref, low_ref, do_ref, wide, bounce, probs_ref, cos_ref, sin_ref = pop(8)
    grads = pop(count)
    (mlp_final,) = pop(1)
    lands = [pop(len(r.scratch(0, e))) for r, e in zip(reducers, early)]
    sems = Sems(*refs)
    me = lax.axis_index("fsdp")
    step, last = pl.program_id(0), pl.num_programs(0) - 1
    into, outof, blocks = give_back(y_ref, home_ref, bounce, sems)
    loads = [
        sems.copy(src, dst)
        for src, dst in [
            (m_any, m_ref), (dy_any, dy_ref), (w_mlp_any, w_mlp_ref), (w_in_any, w_in_ref), (w_out_any, w_out_ref),
            (b_any, b_ref), (o_any, all_o_ref), (cos_any, cos_ref), (sin_any, sin_ref),
        ]
    ]
    pair, pairs = step - tiles - 1, last - tiles
    slot_sems = [sems.local.at[sems.local_used + i] for i in range(2)]
    sems.local_used += 2

    def fetch(which, slot):
        return pltpu.make_async_copy(p_any.at[pl.ds(which * 2, 2)], probs_ref.at[slot], slot_sems[slot])
    stores = [sems.copy(mlp_final if w == 0 else shard_of(grads[w], reducers[w].rows, me), sums_out[w]) for w in range(count)]
    for w, reducer in enumerate(reducers):
        reducer.bind(lambda j, w=w: shard_of(grads[w], reducers[w].rows, flip(me, j)), lands[w], sems, 0, early[w], mlp_final if w == 0 else None)
    mlp, first_half, second_half, out = reducers

    def at(when, *actions):
        @pl.when(step == when)
        def _():
            for action in actions:
                action()

    def advance(reducer, s, limit):
        def run():
            reducer.finish(s)
            if s + 1 < limit:
                reducer.start(s + 1)
        return run

    @pl.when(step == 0)
    def _():
        start_all(loads)
        into.start()
        meet(all_partners(sizes))
        start_all(blocks)
        dgain_ref[...] = jnp.zeros_like(dgain_ref)
        wait_all(loads[:2])
        weight_gradient(grads[0], wide, m_ref, dy_ref)
        mlp.start(0)
        into.wait()
        outof.start()
        wait_all(loads[2:5])

    at(1, advance(mlp, 0, early[0]))

    @pl.when(step < tiles)
    def _():
        rows = pl.ds(pl.multiple_of(step * TILE, TILE), TILE)
        low = middle_back_tile(
            dy_ref[rows, :], x1_ref, slope_ref, act_ref, gain_ref, w_out_ref, w_in_ref, w_mlp_ref,
            dh_ref.at[rows, :], dgain_ref, dx1_ref,
        )
        low_ref[rows, :] = low
        do_ref[rows, :] = dot_nt(low, w_out_ref[...]).astype(bf16)

    across = len(bits_of(sizes[0])) + len(bits_of(sizes[1]))

    @pl.when(step == tiles)
    def _():
        wait_all(loads[5:])
        weight_gradient(grads[1], wide, b_ref, dh_ref.at[:, :FF])
        first_half.start(0)
        weight_gradient(grads[2], wide, b_ref, dh_ref.at[:, FF:])
        second_half.start(0)
        for s in range(1, across - 1):
            advance(mlp, s, early[0])()
        weight_gradient(grads[3], wide, all_o_ref, low_ref)
        out.start(0)

    @pl.when(step == tiles - 1)
    def _():
        fetch(0, 0).start()

    for slot in range(2):
        @pl.when((step > tiles) & (pair % 2 == slot))
        def _(slot=slot):
            fetch(pair, slot).wait()

            @pl.when(pair + 1 < pairs)
            def _():
                fetch(pair + 1, 1 - slot).start()

    halves = (first_half, second_half)
    steps = lambda reducer, limit, *which: [advance(reducer, s, limit) for s in which]
    half_steps = lambda *which: [advance(r, s, early[1]) for s in which for r in halves]
    middle = range(1, across - 1)
    at(tiles + 1, *steps(mlp, early[0], across - 1), *half_steps(0))
    at(tiles + 2, *steps(out, early[3], 0))
    at(tiles + 3, *half_steps(*middle))
    at(tiles + 4, *steps(mlp, early[0], across), *steps(out, early[3], *middle))
    at(tiles + 5, *steps(mlp, early[0], across + 1), *half_steps(across - 1))
    at(tiles + 6, *steps(mlp, early[0], *range(across + 2, early[0] - 1)), *half_steps(across), *steps(out, early[3], across - 1))

    @pl.when(step > tiles)
    def _():
        column = pl.multiple_of(pair * PAIR, PAIR)
        attend_back_pair(
            q_ref, k_ref, v_ref, o_ref, inv_ref, do_ref[:, pl.ds(column, PAIR)], probs_ref.at[pair % 2], cos_ref, sin_ref,
            dq_ref, dk_ref, dv_ref,
        )

    @pl.when(step == last)
    def _():
        for w, reducer in enumerate(reducers):
            reducer.finish(early[w] - 1)
            stores[w].start()
        wait_all(stores)
        outof.wait()
        wait_all(blocks)


PIECES = 4


def leave_kernel(sizes, gain_ref, other_gain_ref, *refs):
    fsdp, rep, seq = sizes
    reducers, early = (some[1:] for some in early_reducers(sizes))
    whole = late_reducers(sizes)
    count, more = len(reducers), len(whole)
    refs = list(refs)
    pop = lambda n: [refs.pop(0) for _ in range(n)]
    anys = pop(7)
    sums_in = pop(count)
    (home_ref,) = pop(1)
    in_out, out_out, qkv_out, gains_out = pop(4)
    dq_ref, a_ref, dk_ref, dv_ref, w_ref, x_ref, dx1_ref = local = pop(7)
    slots, wide, in_final, out_final, qkv_final = pop(5)
    held, grads = pop(count), pop(more)
    lands = [pop(len(r.scratch(e, len(r.steps)))) for r, e in zip(reducers, early)]
    whole_lands = [pop(len(r.scratch(0, len(r.steps)))) for r in whole]
    (gain_lands,) = pop(1)
    sems = Sems(*refs)
    me, me_seq = lax.axis_index("fsdp"), lax.axis_index("seq")
    own = sems.copy(slots.at[0], home_ref.at[me_seq])
    height = slots.shape[1] // PIECES
    blocks = {
        k: [
            sems.remote(slots.at[k, pl.ds(n * height, height)], home_ref.at[me_seq, pl.ds(n * height, height)], "seq", k)
            for n in range(PIECES)
        ]
        for k in range(1, seq)
    }
    order = sorted(range(1, seq), key=lambda k: (k != 2, k == 1))
    ready = []

    def send_piece(n=1):
        for _ in range(n):
            if ready:
                ready.pop(0).start()

    operands = [sems.copy(src, dst) for src, dst in zip(anys, local)]
    loads = [sems.copy(sums_in[w], held[w]) for w in range(count)]
    stores = [
        sems.copy(src, dst)
        for src, dst in ((in_final, in_out), (out_final, out_out), (qkv_final, qkv_out))
    ]
    finals = [in_final.at[:, pl.ds(0, FF)], in_final.at[:, pl.ds(FF, FF)], out_final]
    for w, reducer in enumerate(reducers):
        reducer.bind(lambda j, w=w: held[w], lands[w], sems, early[w], len(reducer.steps), finals[w])
    for w, reducer in enumerate(whole):
        reducer.bind(
            lambda j, w=w: shard_of(grads[w], whole[w].rows, flip(me, j)), whole_lands[w], sems, 0, len(reducer.steps),
            qkv_final.at[:, pl.ds(w * D, D)],
        )
    hops = [("fsdp", b) for b in bits_of(fsdp)] + [("rep", b) for b in bits_of(rep)] + [("seq", b) for b in bits_of(seq)]
    gain_moves = [sems.remote(gains_out, gain_lands.at[i], axis, bit) for i, (axis, bit) in enumerate(hops)]
    rows = slots.shape[1]

    def advance(some, s):
        for reducer in some:
            if s < len(reducer.steps):
                reducer.finish(s)
                if s + 1 < len(reducer.steps):
                    reducer.start(s + 1)

    def advance_gains(i):
        if i < len(hops):
            gain_moves[i].wait()
            gains_out[...] += gain_lands[i]
            if i + 1 < len(hops):
                gain_moves[i + 1].start()

    def input_slot(k):
        piece = slice(k * rows, (k + 1) * rows)
        da = dot_nt(dq_ref[piece, :], w_ref[:, :D])
        da = da + dot_nt(dk_ref[piece, :], w_ref[:, D : 2 * D])
        da = da + dot_nt(dv_ref[piece, :], w_ref[:, 2 * D :])
        unit, scale = normalize(x_ref[piece, :].astype(f32))
        back, terms = norm_back(unit, scale, gain_ref[0:1, :], da)
        gains_out[0:1, :] += jnp.sum(terms, axis=0, keepdims=True)
        slots[k] = (dx1_ref[piece, :] + back).astype(bf16)
        if k:
            ready.extend(blocks[k])

    def gradient(w, part):
        weight_gradient(grads[w], wide, a_ref, part)
        whole[w].start(0)

    across = len(bits_of(fsdp)) + len(bits_of(rep))
    halves, out, last = reducers[:2], reducers[2:], len(whole[0].steps)
    start_all(operands[:2])
    start_all(loads)
    start_all(operands[2:])
    gains_out[...] = jnp.zeros_like(gains_out)
    gains_out[1:2, :] = other_gain_ref[...]
    meet(all_partners(sizes))
    wait_all(loads)
    for w, (reducer, s) in enumerate(zip(reducers, early)):
        if s < len(reducer.steps):
            reducer.start(s)
        else:
            finals[w][...] = held[w][...]
    wait_all(operands[:2])
    gradient(0, dq_ref)
    wait_all(operands[2:])
    input_slot(order[0])
    send_piece(PIECES // 2)
    advance(whole[:1], 0)
    advance(halves, early[0])
    gradient(1, dk_ref)
    for k in order[1:2]:
        input_slot(k)
    advance(whole[1:2], 0)
    advance(out, early[2])
    send_piece()
    gradient(2, dv_ref)
    for k in order[2:]:
        input_slot(k)
    advance(whole[:1], 1)
    advance(whole[2:], 0)
    send_piece()
    input_slot(0)
    own.start()
    gain_moves[0].start()
    advance(whole[1:2], 1)
    advance(out, early[2] + 1)
    send_piece()
    for s in range(2, across):
        advance(whole[:1], s)
        advance(whole[2:], s - 1)
        advance(whole[1:2], s)
        send_piece()
    advance(whole[2:], across - 1)
    send_piece()
    i = 0
    for s in range(across, last):
        for reducer in whole:
            advance([reducer], s)
            send_piece()
        for _ in range(2):
            advance_gains(i)
            i += 1
    while i < len(hops):
        advance_gains(i)
        i += 1
    send_piece(len(ready))
    for s in range(early[0] + 1, len(halves[0].steps)):
        advance(halves, s)
    for s in range(early[2] + 2, len(out[0].steps)):
        advance(out, s)
    start_all(stores)
    wait_all(stores)
    own.wait()
    for k in range(1, seq):
        wait_all(blocks[k])


def rows_spec(width):
    return pl.BlockSpec((TILE, width), lambda i: (i, 0))


def whole_spec(*shape):
    return pl.BlockSpec(shape, lambda i: (0,) * len(shape))


def pair_spec(length, offset=0):
    return pl.BlockSpec((length, PAIR), lambda i: (0, i + offset))


def struct(dtype, *shape):
    return jax.ShapeDtypeStruct(shape, dtype)


def call(kernel, grid, in_specs, out_specs, out_shape, flops, scratch=(), collective=None):
    return pl.pallas_call(
        kernel,
        grid=(grid,),
        in_specs=in_specs,
        out_specs=out_specs,
        out_shape=out_shape,
        scratch_shapes=list(scratch),
        compiler_params=pltpu.CompilerParams(
            dimension_semantics=("arbitrary",), vmem_limit_bytes=VMEM_LIMIT,
            collective_id=collective, has_side_effects=collective is not None,
        ),
        cost_estimate=pl.CostEstimate(flops=flops, bytes_accessed=10 * 2**20, transcendentals=0),
    )


MESH = pl.DeviceIdType.MESH
ANY = pl.BlockSpec(memory_space=pl.ANY)


def take(array, index):
    return lax.dynamic_index_in_dim(array, index, 0, keepdims=False)


def flip(index, mask):
    bit = 1
    while bit <= mask:
        if mask & bit:
            index = index + bit - 2 * bit * ((index // bit) % 2)
        bit *= 2
    return index


def flip_by(index, mask, size):
    total = 0
    for bit in bits_of(size):
        ours, theirs = (index // bit) % 2, (mask // bit) % 2
        total = total + bit * (ours + theirs - 2 * ours * theirs)
    return total


def bits_of(size):
    return [1 << i for i in range(size.bit_length() - 1)]


def meet(partners):
    barrier = pltpu.get_barrier_semaphore()
    for axis, mask in partners:
        pl.semaphore_signal(
            barrier, inc=1, device_id={axis: flip(lax.axis_index(axis), mask)}, device_id_type=MESH
        )
    pl.semaphore_wait(barrier, len(partners))


class Sems:
    def __init__(self, send, recv, local):
        self.send, self.recv, self.local = send, recv, local
        self.remote_used = self.local_used = 0

    def remote(self, src, dst, axis, mask):
        i = self.remote_used
        self.remote_used += 1
        return pltpu.make_async_remote_copy(
            src_ref=src, dst_ref=dst, send_sem=self.send.at[i], recv_sem=self.recv.at[i],
            device_id={axis: flip(lax.axis_index(axis), mask)}, device_id_type=MESH,
        )

    def copy(self, src, dst):
        i = self.local_used
        self.local_used += 1
        return pltpu.make_async_copy(src, dst, self.local.at[i])


def sem_shapes(remote, local):
    dma = pltpu.SemaphoreType.DMA
    return [dma((remote,)), dma((remote,)), dma((max(local, 1),))]


def start_all(copies):
    for copy in copies:
        copy.start()


def wait_all(copies):
    for copy in copies:
        copy.wait()


class Gather:
    def __init__(self, sizes, shards, place, sems, order):
        self.sizes, self.shards, self.place, self.sems = sizes, shards, place, sems
        self.pieces = order
        self.me, self.me_rep = lax.axis_index("fsdp"), lax.axis_index("rep")
        self.pending = []

    def part(self, ref, pieces, n):
        width = ref.shape[-1] // (self.sizes[1] * pieces)
        start = (self.me_rep * pieces + n) * width
        return ref.at[:, pl.ds(pl.multiple_of(start, 128), width)]

    def source(self, w, h):
        return self.shards[w] if h == 0 else self.place(w, flip(self.me, h))

    def start(self):
        self.held = [0]
        self.over = self.cross(self.far_bits()[0]) if self.far_bits() else []

    def far_bits(self):
        return list(reversed(bits_of(self.sizes[0])[1:]))

    def cross(self, bit):
        over = []
        for w, pieces, n in self.pieces:
            moved = [
                self.sems.remote(
                    self.part(self.source(w, h), pieces, n),
                    self.part(self.place(w, flip(self.me, h)), pieces, n), "fsdp", bit,
                )
                for h in self.held
            ]
            start_all(moved)
            over.append(moved)
        return over

    def pass_on(self, i, bit):
        w, pieces, n = self.pieces[i]
        for copy in self.over[i]:
            copy.wait_recv()
        self.pending += self.over[i]
        passed = []
        for mask in range(1, self.sizes[1]):
            for h in self.held:
                here = self.part(self.place(w, flip(self.me, h ^ bit)), pieces, n)
                passed.append(self.sems.remote(here, here, "rep", mask))
        start_all(passed)
        self.pending += passed
        return passed

    def events(self, lag=2):
        bits = self.far_bits()
        count = len(self.pieces)
        for bit in bits[:-1]:
            passed = [self.pass_on(i, bit) for i in range(count)]
            self.held = self.held + [h ^ bit for h in self.held]
            for copies in passed:
                for copy in copies:
                    copy.wait_recv()
            self.over = self.cross(bits[bits.index(bit) + 1])
        end = {w: i for i, (w, _, _) in enumerate(self.pieces)}
        passed, near_held = [], self.held + [h ^ bit for bit in bits[-1:] for h in self.held]
        for i in range(count + lag):
            if i < count:
                if bits:
                    passed.append(self.pass_on(i, bits[-1]))
                yield None
            for w, last in end.items():
                if last == i - lag:
                    if bits:
                        for j, (other, _, _) in enumerate(self.pieces):
                            if other == w:
                                for copy in passed[j]:
                                    copy.wait_recv()
                    yield w, self.near(w, near_held)

    def near(self, w, held):
        copies = [self.sems.remote(self.source(w, h), self.place(w, flip(self.me, h)), "fsdp", 1) for h in held]
        start_all(copies)
        return copies

    @staticmethod
    def count(sizes, order, weights):
        held, copies = 1, 0
        for _ in bits_of(sizes[0])[1:]:
            copies += len(order) * held * sizes[1]
            held *= 2
        return copies + weights * held


PASSED = (0, 1, 2, 4, 6, 6, 6)
CROSSED = (4, 5)


class LateGather:
    def __init__(self, sizes, shards, wholes, sems):
        fsdp, rep, _ = sizes
        me, me_rep = lax.axis_index("fsdp"), lax.axis_index("rep")
        place = lambda w, q: shard_of(wholes[w], shards[w].shape[0], q)
        self.own = [sems.copy(shards[w], place(w, me)) for w in range(2)]
        self.far, self.passed, self.near = [], [], [[], []]
        for w in range(2):
            fits = shards[w].shape[-1] % (rep * 3 * 128) == 0
            pieces = 3 if fits else 1
            width = shards[w].shape[-1] // (rep * pieces)
            for n in range(pieces if fsdp > 2 else 0):
                cols = pl.ds(pl.multiple_of((me_rep * pieces + n) * width, 128), width)
                self.far.append(sems.remote(shards[w].at[:, cols], place(w, me).at[:, cols], "fsdp", 2))
                here = place(w, flip(me, 2)).at[:, cols]
                self.passed.append([sems.remote(here, here, "rep", mask) for mask in range(1, rep)])
            for h in range(0, fsdp, 2):
                src = shards[w] if h == 0 else place(w, flip(me, h))
                self.near[w].append(sems.remote(src, place(w, flip(me, h)), "fsdp", 1))
        self.pieces = len(self.far) // 2
        self.count = len(self.far)

    @staticmethod
    def copies(sizes):
        return 2 * (3 * sizes[1] + sizes[0] // 2)

    def pass_on(self, i):
        self.far[i].wait_recv()
        start_all(self.passed[i])

    def cross_core(self, w):
        for copies in self.passed[w * self.pieces : (w + 1) * self.pieces]:
            for copy in copies:
                copy.wait_recv()
        start_all(self.near[w])

    def advance(self, step):
        upto = lambda n: min(n, self.count)
        for i in range(upto(PASSED[step - 1]), upto(PASSED[step])):
            self.pass_on(i)
        for w in range(2):
            if step == CROSSED[w]:
                self.cross_core(w)

    def finish(self, w):
        wait_all(self.own[w : w + 1])
        for i in range(w * self.pieces, (w + 1) * self.pieces):
            self.far[i].wait_send()
            for copy in self.passed[i]:
                copy.wait_send()
        wait_all(self.near[w])


def gather_order(sizes, shards):
    fits = lambda w, n: shards[w].shape[-1] % (sizes[1] * n * 128) == 0
    split = lambda w, n: n if fits(w, n) else 1
    order = []
    for w, n in ((0, 1), (1, 3), (2, 3), (4, 3), (3, 3)):
        if w >= len(shards):
            continue
        n = split(w, n)
        order += [(w, n, i) for i in range(n)]
    return order


def enter_kernel(sizes, count, tokens, *refs):
    fsdp, rep, seq = sizes
    refs = list(refs)
    pop = lambda n: [refs.pop(0) for _ in range(n)]
    shards = pop(count)
    (x_out,) = pop(1)
    fulls = pop(count)
    (bounce_x,) = pop(1)
    bounces = pop(count)
    sems = Sems(*refs)
    me, me_seq = lax.axis_index("fsdp"), lax.axis_index("seq")
    into = [sems.copy(tokens.at[me_seq], bounce_x)] + [sems.copy(shards[w], bounces[w]) for w in range(count)]
    outof = [sems.copy(bounce_x, x_out.at[0])] + [sems.copy(bounces[w], fulls[w].at[me]) for w in range(count)]
    gather = Gather(sizes, shards, lambda w, q: fulls[w].at[q], sems, gather_order(sizes, shards))
    start_all(into)
    meet(all_partners(sizes))
    blocks = [sems.remote(tokens.at[flip(me_seq, k)], x_out.at[k], "seq", k) for k in range(1, seq)]
    start_all(blocks)
    gather.start()
    last = []
    for event in gather.events():
        if event:
            last += event[1]
    wait_all(into)
    start_all(outof)
    for copy in gather.pending:
        copy.wait_send()
    wait_all(last)
    wait_all(blocks)
    wait_all(outof)


def enter(sizes, tokens, shards):
    fsdp = sizes[0]
    count = len(shards)
    hbm = lambda shape: struct(bf16, *shape)
    copies = sizes[2] - 1 + Gather.count(sizes, gather_order(sizes, shards), count)
    return pl.pallas_call(
        functools.partial(enter_kernel, sizes, count),
        in_specs=[ANY] * (1 + count),
        out_specs=[ANY] * (1 + count),
        out_shape=[hbm(tokens.shape)] + [hbm((fsdp,) + s.shape) for s in shards],
        scratch_shapes=[pltpu.VMEM(tokens.shape[1:], bf16)]
        + [pltpu.VMEM(s.shape, bf16) for s in shards]
        + sem_shapes(copies, 2 * (1 + count)),
        compiler_params=pltpu.CompilerParams(collective_id=0, has_side_effects=True),
    )(tokens, *shards)


def turn(row):
    n = row.shape[1]
    diagonal = lax.broadcasted_iota(jnp.int32, (n, n), 0) == lax.broadcasted_iota(jnp.int32, (n, n), 1)
    return jnp.sum(jnp.where(diagonal, row, 0), axis=1, keepdims=True)


def enter_project_kernel(sizes, count, tokens, segments, *refs):
    fsdp, rep, seq = sizes
    refs = list(refs)
    pop = lambda n: [refs.pop(0) for _ in range(n)]
    shards = pop(count)
    x_out, a_out, qkv_out, cos_out, sin_out, marks_out, row_out, gains_out, wq_out = pop(9)
    fulls = [None, None] + pop(count - 2)
    xs, a, qkv, wq, gains = pop(5)
    bounces = pop(count)
    sems = Sems(*refs)
    me, me_seq = lax.axis_index("fsdp"), lax.axis_index("seq")
    shard_rows, rows = shards[1].shape[0], xs.shape[1]
    columns = wq.shape[1]

    def place(w, q):
        if w == 0:
            return gains.at[q]
        if w == 1:
            return wq.at[pl.ds(pl.multiple_of(q * shard_rows, 16), shard_rows)]
        return fulls[w].at[q]

    own = sems.copy(tokens.at[me_seq], xs.at[0])
    into = [sems.copy(shards[w], place(w, me) if w < 2 else bounces[w - 2]) for w in range(count)]
    outof = [sems.copy(bounces[w - 2], place(w, me)) for w in range(2, count)]
    blocks = [sems.remote(tokens.at[flip(me_seq, k)], xs.at[k], "seq", k) for k in range(1, seq)]
    stores = [
        [sems.copy(src.at[k], dst.at[k]) for src, dst in ((xs, x_out), (a, a_out), (qkv, qkv_out))] for k in range(seq)
    ]
    keep = sems.copy(wq, wq_out)
    gather = Gather(sizes, shards, place, sems, gather_order(sizes, shards))
    own.start()
    start_all(into)
    meet(all_partners(sizes))
    gather.start()
    start_all(blocks)

    lane = lax.broadcasted_iota(jnp.int32, (1, PAIR), 1)
    rate = jnp.exp((lane % (HDIM // 2)).astype(f32) * (-2.0 * math.log(THETA) / HDIM))
    sign = jnp.where(lane_halves((1, PAIR)), -1.0, 1.0)
    batch = segments.shape[1]

    def own_segments(block):
        at = pl.multiple_of(block * rows, 128)
        return segments[me_seq // batch, pl.ds(me_seq % batch, 1), pl.ds(at, rows)]

    @pl.loop(0, seq)
    def _(k):
        block = flip_by(me_seq, k, seq)
        piece = pl.ds(pl.multiple_of(k * rows, 128), rows)
        row = own_segments(block)
        column = turn(row)
        earlier = jnp.zeros((rows, 1), jnp.int32)
        for other in range(seq):
            earlier += jnp.sum((own_segments(other) < column).astype(jnp.int32), axis=1, keepdims=True)
        index = block * rows + lax.broadcasted_iota(jnp.int32, (rows, 1), 0)
        angles = (index - earlier).astype(f32) * rate
        cos_out[piece, :] = jnp.cos(angles)
        sin_out[piece, :] = jnp.sin(angles) * sign
        marks_out[piece, :] = column
        row_out[:, piece] = row

    def project(k):
        if k == 0:
            own.wait()
        else:
            blocks[k - 1].wait()
        piece = slice(k * rows, (k + 1) * rows)
        unit, _ = normalize(xs[k].astype(f32))
        low = (unit * gains_out[0:1, :]).astype(bf16)
        a[k] = low
        cosine, sine = cos_out[piece, :], sin_out[piece, :]

        @pl.loop(0, 2 * D // WIDE)
        def _(i):
            at = pl.multiple_of(i * WIDE, WIDE)
            part = dot_nn(low, wq[:, pl.ds(at, WIDE)])
            scale = jnp.where(at < D, QUERY_SCALE, 1.0)
            for half in range(0, WIDE, PAIR):
                value = rotate_pair(part[:, half : half + PAIR], cosine, sine) * scale
                qkv[k, :, pl.ds(at + half, PAIR)] = value.astype(bf16)

        qkv[k, :, 2 * D :] = dot_nn(low, wq[:, 2 * D :]).astype(bf16)
        start_all(stores[k])

    last, queue, since = {}, list(range(seq)), 0
    for event in gather.events():
        if event:
            last[event[0]] = event[1]
            if event[0] == 1:
                for copy in into[:2] + last[0] + last[1]:
                    copy.wait()
                keep.start()
                total = gains[0, :2, :].astype(f32)
                for q in range(1, fsdp):
                    total = total + gains[q, :2, :].astype(f32)
                gains_out[...] = total
                wait_all(into[2:])
                start_all(outof)
                project(queue.pop(0))
        elif 1 in last:
            since += 1
            if since % 2 == 0 and len(queue) > 1:
                project(queue.pop(0))
    for k in queue:
        project(k)
    for copy in gather.pending:
        copy.wait_send()
    for w in range(2, count):
        wait_all(last[w])
    wait_all(outof)
    for group in stores:
        wait_all(group)
    keep.wait()


def enter_project(sizes, tokens, segments, shards):
    fsdp, rep, seq = sizes
    count, rows = len(shards), tokens.shape[1]
    length, columns = seq * rows, shards[1].shape[1]
    vmem = pl.BlockSpec(memory_space=pltpu.VMEM)
    copies = seq - 1 + Gather.count(sizes, gather_order(sizes, shards), count)
    return pl.pallas_call(
        functools.partial(enter_project_kernel, sizes, count),
        in_specs=[ANY, vmem] + [ANY] * count,
        out_specs=[ANY] * 3 + [vmem] * 5 + [ANY] * (count - 1),
        out_shape=[struct(bf16, seq, rows, D), struct(bf16, seq, rows, D), struct(bf16, seq, rows, columns),
                   struct(f32, length, PAIR), struct(f32, length, PAIR), struct(jnp.int32, length, 1),
                   struct(jnp.int32, 1, length), struct(f32, 2, D), struct(bf16, D, columns)]
        + [struct(bf16, fsdp, *s.shape) for s in shards[2:]],
        scratch_shapes=[pltpu.VMEM((seq, rows, D), bf16), pltpu.VMEM((seq, rows, D), bf16),
                        pltpu.VMEM((seq, rows, columns), bf16), pltpu.VMEM((D, columns), bf16),
                        pltpu.VMEM((fsdp,) + shards[0].shape, bf16)]
        + [pltpu.VMEM(s.shape, bf16) for s in shards[2:]] + [pltpu.VMEM((16, 128), bf16)] * 2
        + sem_shapes(copies, 2 + count + count - 2 + 3 * seq),
        compiler_params=pltpu.CompilerParams(
            collective_id=4, has_side_effects=True, vmem_limit_bytes=VMEM_LIMIT
        ),
    )(tokens, segments, *shards)


def add_into(total, term):
    rows = total.shape[0]
    height = 48 if rows % 48 == 0 else rows

    @pl.loop(0, rows // height)
    def _(i):
        at = pl.ds(pl.multiple_of(i * height, 16), height) if height < rows else pl.ds(0, rows)
        total[at, :] = (total[at, :].astype(f32) + term[at, :].astype(f32)).astype(bf16)


class Reducer:
    def __init__(self, parts_shape, sizes, order):
        self.fsdp, self.rows, self.cols = parts_shape
        self.steps = []
        held, rows, cols = list(range(self.fsdp)), self.rows, self.cols
        row_at, col_at = [], []
        for axis, bit in order:
            step = dict(axis=axis, bit=bit, row_at=list(row_at), col_at=list(col_at), rows=rows, cols=cols)
            if axis == "fsdp":
                step["send"] = [j for j in held if j & bit]
                held = [j for j in held if not j & bit]
                step["keep"] = held
                step["shape"] = (len(held), rows, cols)
                step["split"] = None
            else:
                step["keep"] = step["send"] = held
                if (axis, bit) == order[-1]:
                    step["split"] = "none"
                elif (rows // 2) % 16 == 0:
                    rows //= 2
                    row_at = row_at + [(axis, bit, rows)]
                    step["split"] = "rows"
                elif (cols // 2) % 128 == 0:
                    cols //= 2
                    col_at = col_at + [(axis, bit, cols)]
                    step["split"] = "cols"
                else:
                    step["split"] = "none"
                step["shape"] = (len(held), rows, cols)
            self.steps.append(step)
        self.down = len(self.steps)
        for step in reversed(self.steps[: self.down]):
            if step["split"] in ("rows", "cols"):
                self.steps.append(dict(step, up=True))

    @staticmethod
    def offset(terms, align, last=None):
        total = 0
        for i, (axis, bit, extent) in enumerate(terms):
            half = (lax.axis_index(axis) // bit) % 2
            if last == i:
                half = 1 - half
            total = total + half * extent
        return total if isinstance(total, int) else pl.multiple_of(total, align)

    def region(self, step, after, other=False):
        row_at, col_at, rows, cols = step["row_at"], step["col_at"], step["rows"], step["cols"]
        row_last = col_last = None
        if after:
            if step["split"] == "rows":
                rows //= 2
                row_at = row_at + [(step["axis"], step["bit"], rows)]
                row_last = len(row_at) - 1 if other else None
            elif step["split"] == "cols":
                cols //= 2
                col_at = col_at + [(step["axis"], step["bit"], cols)]
                col_last = len(col_at) - 1 if other else None
        return (
            pl.ds(self.offset(row_at, 16, row_last), rows),
            pl.ds(self.offset(col_at, 128, col_last), cols),
        )

    def scratch(self, first, last):
        return [pltpu.VMEM(s["shape"], bf16) for s in self.steps[first:last] if "up" not in s]

    def copies(self, first, last):
        return sum(1 if "up" in s else len(s["send"]) for s in self.steps[first:last])

    def bind(self, parts, lands, sems, first, last, final=None):
        self.parts, self.sems, self.final = parts, sems, final
        self.lands, self.moves = {}, {}
        lands = list(lands)
        for s in range(first, last):
            step = self.steps[s]
            moves = []
            if "up" in step:
                there = final.at[self.region(step, True)]
                moves.append(sems.remote(there, there, step["axis"], step["bit"]))
            else:
                land = self.lands[s] = lands.pop(0)
                for i, j in enumerate(step["send"]):
                    fsdp = step["axis"] == "fsdp"
                    src = self.parts(j).at[self.region(step, not fsdp, not fsdp)]
                    moves.append(sems.remote(src, land.at[i], step["axis"], step["bit"]))
            self.moves[s] = moves

    def start(self, s):
        if s == self.down:
            region = self.region(self.steps[s - 1], True)
            self.final[region] = self.parts(0)[region]
        start_all(self.moves.get(s, []))

    def finish(self, s):
        step = self.steps[s]
        self.finish_step(s, step)
        if s + 1 == len(self.steps) == self.down and self.final is not None:
            self.final[...] = self.parts(0)[...]

    def finish_step(self, s, step):
        for i, move in enumerate(self.moves[s]):
            move.wait()
            if "up" not in step:
                j = step["keep"][i]
                ref = self.parts(j)
                add_into(ref.at[self.region(step, True)], self.lands[s].at[i])


def give_back(slots, home, bounce, sems):
    me = lax.axis_index("seq")
    seq = slots.shape[0]
    return (
        sems.copy(slots.at[0], bounce),
        sems.copy(bounce, home.at[me]),
        [sems.remote(slots.at[k], home.at[me], "seq", k) for k in range(1, seq)],
    )


def body(sizes, tokens, segments, positions, gain_attn, w_qkv, w_out, gain_mlp, w_in, w_mlp_out, cotangent):
    fsdp, rep, seq = sizes
    micro, batch, rows, _ = tokens.shape
    assert micro * batch == seq and rows % TILE == 0
    length = seq * rows
    me_seq, me_fsdp = lax.axis_index("seq"), lax.axis_index("fsdp")

    own_gains = jnp.zeros((16, D), bf16)
    own_gains = lax.dynamic_update_slice(own_gains, jnp.stack([gain_attn, gain_mlp]), (0, me_fsdp * (D // fsdp)))
    shards = [own_gains, w_qkv, w_out, w_mlp_out, w_in]
    tiles, pairs = length // TILE, HEADS // 2
    late = fsdp in (2, 4) and pairs >= 6 and flat(D // fsdp) and flat(FF // fsdp)
    if (D // fsdp) % 16 == 0:
        x, a, qkv, cosine, sine, marks_column, marks_row, gains, wq, *rest = enter_project(
            sizes, tokens.reshape(seq, rows, D), segments, shards[:3] if late else shards
        )
        x, a, qkv = (v.reshape(length, -1) for v in (x, a, qkv))
        wo, *rest = (w.reshape(-1, w.shape[-1]) for w in rest)
        wm, wi = (w_mlp_out, w_in) if late else rest
    else:
        x, gains, wq, wo, wm, wi = enter(sizes, tokens.reshape(seq, rows, D), shards)
        x = x.reshape(length, D)
        gains = jnp.sum(gains[:, :2].astype(f32), axis=0)
        wq, wo, wm, wi = (w.reshape(-1, w.shape[-1]) for w in (wq, wo, wm, wi))

        marks = take(segments.reshape(seq, length), me_seq)
        place = jnp.arange(length, dtype=jnp.int32) - jnp.sum(
            (marks[None, :] < marks[:, None]).astype(jnp.int32), axis=1
        )
        slot_order = [me_seq ^ k for k in range(seq)]
        marks = jnp.concatenate([take(marks.reshape(seq, rows), s) for s in slot_order])
        place = jnp.concatenate([take(place.reshape(seq, rows), s) for s in slot_order])
        half = jnp.arange(0, HDIM, 2).astype(f32) / HDIM
        angles = place.astype(f32)[:, None] * jnp.exp(-half * math.log(THETA))
        cosine, sine = jnp.cos(angles), jnp.sin(angles)
        cosine = jnp.concatenate([cosine] * 4, -1)
        sine = jnp.concatenate([-sine, sine] * 2, -1)

        a, qkv = call(
            first_kernel, tiles,
            [rows_spec(D), whole_spec(2, D), whole_spec(D, 3 * D), rows_spec(PAIR), rows_spec(PAIR)],
            [rows_spec(D), rows_spec(3 * D)],
            [struct(bf16, length, D), struct(bf16, length, 3 * D)],
            2 * length * D * 3 * D,
        )(x, gains, wq, cosine, sine)
        marks_column, marks_row = marks[:, None], marks[None, :]

    vmem = pl.BlockSpec(memory_space=pltpu.VMEM)
    pair_at = lambda offset, lag, n: pl.BlockSpec(
        (length, PAIR), lambda i: (0, jnp.clip(i - lag, 0, n - 1) + offset)
    )
    prob_at = lambda lag: pl.BlockSpec((2, length, length), lambda i: (jnp.clip(i - lag, 0, pairs - 1), 0, 0))
    tile_at = lambda width, lag: pl.BlockSpec((TILE, width), lambda i: (jnp.clip(i - lag, 0, tiles - 1), 0))
    slots = struct(bf16, seq, rows, D)
    o, probs, inv, x1, b, m, slope, act, y, dy, *wholes = call(
        functools.partial(forward_kernel, sizes, pairs, late), pairs + tiles,
        [pair_at(0, 0, pairs), pair_at(pairs, 0, pairs), pair_at(2 * pairs, 0, pairs),
         whole_spec(length, 1), whole_spec(1, length), tile_at(D, pairs), whole_spec(2, D)] + [ANY] * 4,
        [pair_at(0, 0, pairs), prob_at(0), pair_at(0, 0, pairs), tile_at(D, pairs), tile_at(D, pairs)]
        + [tile_at(FF, pairs)] * 3 + [tile_at(D, pairs), ANY] + [ANY] * (2 * late),
        [struct(bf16, length, D), struct(bf16, HEADS, length, length), struct(f32, length, D),
         struct(f32, length, D), struct(bf16, length, D), struct(bf16, length, FF),
         struct(bf16, length, FF), struct(bf16, length, FF), struct(bf16, length, D), slots]
        + [struct(bf16, D, 2 * FF), struct(bf16, FF, D)] * late,
        16 * length * length * D,
        [pltpu.VMEM((length, D), bf16), pltpu.VMEM((D, D), bf16), pltpu.VMEM((D, 2 * FF), bf16), pltpu.VMEM((FF, D), bf16),
         pltpu.VMEM((rows, D), bf16)] + sem_shapes(seq - 1 + LateGather.copies(sizes) * late, 5 + 2 * late), 1,
    )(qkv, qkv, qkv, marks_column, marks_row, x, gains, wo, wi, wm, cotangent.reshape(seq, rows, D))

    if late:
        wi, wm = wholes
    reducers, early = early_reducers(sizes)
    whole = late_reducers(sizes)
    own_shard = lambda r: struct(bf16, r.rows, r.cols)
    full_shard = lambda r: pltpu.VMEM((fsdp * r.rows, r.cols) if flat(r.rows) else (fsdp, r.rows, r.cols), bf16)
    odd = (FF // fsdp) % 16 or (D // fsdp) % 16
    wide = pltpu.VMEM((FF, FF) if odd else (8, 128), f32)
    dx1, dgain_two, dq, dk, dv, block_out, *sums = call(
        functools.partial(backward_kernel, sizes, tiles), tiles + 1 + pairs,
        [tile_at(D, 0), tile_at(FF, 0), tile_at(FF, 0), whole_spec(2, D)]
        + [pair_at(n * pairs, tiles + 1, pairs) for n in range(3)]
        + [pair_at(0, tiles + 1, pairs), pair_at(0, tiles + 1, pairs)] + [ANY] * 11,
        [tile_at(D, 0), whole_spec(1, D)] + [pair_at(0, tiles + 1, pairs)] * 3 + [ANY] * (1 + len(reducers)),
        [struct(f32, length, D), struct(f32, 1, D)] + [struct(bf16, length, D)] * 3 + [slots]
        + [own_shard(r) for r in reducers],
        32 * length * length * D,
        [pltpu.VMEM((D, D), bf16), pltpu.VMEM((D, 2 * FF), bf16), pltpu.VMEM((FF, D), bf16),
         pltpu.VMEM((length, FF), bf16)] + [pltpu.VMEM((length, D), bf16)] * 3
        + [pltpu.VMEM((length, 2 * FF), bf16), pltpu.VMEM((length, D), bf16), pltpu.VMEM((length, D), bf16),
           wide, pltpu.VMEM((rows, D), bf16),
           pltpu.VMEM((2, 2, length, length), bf16)] + [pltpu.VMEM((length, PAIR), f32)] * 2
        + [full_shard(r) for r in reducers] + [pltpu.VMEM((reducers[0].rows, reducers[0].cols), bf16)]
        + [land for r, e in zip(reducers, early) for land in r.scratch(0, e)]
        + sem_shapes(seq - 1 + sum(r.copies(0, e) for r, e in zip(reducers, early)), 13 + len(reducers)), 2,
    )(x1, slope, act, gains, qkv, qkv, qkv, o, inv, probs, cosine, sine,
      wo, wi, wm, m, dy.reshape(length, D), b, o, y.reshape(seq, rows, D))

    hops = sum(len(bits_of(n)) for n in sizes)
    shard = lambda n, width: struct(bf16, n // fsdp, width)
    finals = [shard(D, 2 * FF), shard(D, D), shard(D, 3 * D)]
    operands = [dq, a, dk, dv, wq, x, dx1]
    grad_mlp, *sums = sums
    reducers, early = reducers[1:], early[1:]
    input_grad, grad_in, grad_out, grad_qkv, dgains = pl.pallas_call(
        functools.partial(leave_kernel, sizes),
        in_specs=[vmem] * 2 + [ANY] * (len(operands) + len(reducers)),
        out_specs=[ANY] * 4 + [vmem],
        out_shape=[slots] + finals + [struct(f32, 8, D)],
        scratch_shapes=[pltpu.VMEM(v.shape, v.dtype) for v in operands]
        + [pltpu.VMEM((seq, rows, D), bf16), wide]
        + [pltpu.VMEM(v.shape, v.dtype) for v in finals]
        + [pltpu.VMEM((r.rows, r.cols), bf16) for r in reducers]
        + [full_shard(r) for r in whole]
        + [land for r, e in zip(reducers, early) for land in r.scratch(e, len(r.steps))]
        + [land for r in whole for land in r.scratch(0, len(r.steps))]
        + [pltpu.VMEM((hops, 8, D), f32)]
        + sem_shapes(
            PIECES * (seq - 1) + hops + sum(r.copies(e, len(r.steps)) for r, e in zip(reducers, early))
            + sum(r.copies(0, len(r.steps)) for r in whole),
            1 + len(operands) + len(reducers) + len(finals),
        ),
        compiler_params=pltpu.CompilerParams(
            collective_id=3, has_side_effects=True, vmem_limit_bytes=VMEM_LIMIT
        ),
    )(gains, dgain_two, *operands, *sums)
    dgains = lax.dynamic_slice_in_dim(dgains, me_fsdp * (D // fsdp), D // fsdp, 1)
    return (
        block_out.reshape(tokens.shape),
        input_grad.astype(f32).reshape(tokens.shape),
        dgains[0],
        grad_qkv.astype(f32),
        grad_out.astype(f32),
        dgains[1],
        grad_in.astype(f32),
        grad_mlp.astype(f32),
    )


def solution(mesh):
    sizes = (mesh.shape["fsdp"], mesh.shape["rep"], mesh.shape["seq"])
    wide = P(None, ("rep", "fsdp"), "seq", None)
    placed = (
        wide, P(None, ("rep", "fsdp"), None), P(None, ("rep", "fsdp"), "seq"),
        P("fsdp"), P("fsdp", None), P("fsdp", None), P("fsdp"), P("fsdp", None), P("fsdp", None), wide,
    )
    return jax.shard_map(
        functools.partial(body, sizes),
        mesh=mesh,
        in_specs=placed,
        out_specs=(
            wide, wide, P("fsdp"), P("fsdp", None), P("fsdp", None), P("fsdp"), P("fsdp", None), P("fsdp", None),
        ),
        check_vma=False,
    )
```

```python
import functools
import math

import jax
import jax.numpy as jnp
from jax import lax
from jax.experimental import pallas as pl
from jax.experimental.pallas import tpu as pltpu
from jax.sharding import PartitionSpec as P

D = 768
HEADS = 12
HDIM = 64
FF = 1152
EPS = 1e-05
THETA = 160000.0
MASKED = -1000000000.0
QUERY_SCALE = HDIM**-0.5 / math.log(2.0)
TILE = 256
PAIR = 2 * HDIM
WIDE = 384
HCHUNK = 384
f32 = jnp.float32
bf16 = jnp.bfloat16
VMEM_LIMIT = 62 * 2**20


def dot_nn(left, right):
    return lax.dot_general(left, right, (((1,), (0,)), ((), ())), preferred_element_type=f32)


def dot_nt(left, right):
    return lax.dot_general(left, right, (((1,), (1,)), ((), ())), preferred_element_type=f32)


def dot_tn(left, right):
    return lax.dot_general(left, right, (((0,), (0,)), ((), ())), preferred_element_type=f32)


def normalize(values):
    mean = jnp.mean(values, axis=-1, keepdims=True)
    centered = values - mean
    var = jnp.mean(centered * centered, axis=-1, keepdims=True)
    scale = lax.rsqrt(var + EPS)
    return centered * scale, scale


def norm_back(unit, scale, gain, grad):
    gain_terms = grad * unit
    inner = grad * gain
    first = jnp.mean(inner, axis=-1, keepdims=True)
    second = jnp.mean(inner * unit, axis=-1, keepdims=True)
    return scale * (inner - first - unit * second), gain_terms


def lane_halves(shape):
    lane = lax.broadcasted_iota(jnp.int32, shape, len(shape) - 1)
    return lane % HDIM < HDIM // 2


def rotate_pair(values, cosine, signed_sine):
    swapped = jnp.where(
        lane_halves(values.shape),
        pltpu.roll(values, PAIR - HDIM // 2, 1),
        pltpu.roll(values, HDIM // 2, 1),
    )
    return values * cosine + swapped * signed_sine


def first_kernel(x_ref, gain_ref, w_ref, cos_ref, sin_ref, a_ref, qkv_ref):
    unit, _ = normalize(x_ref[...].astype(f32))
    a = (unit * gain_ref[0:1, :]).astype(bf16)
    a_ref[...] = a
    cosine, sine = cos_ref[...], sin_ref[...]
    for column in range(0, 3 * D, TILE):
        part = dot_nn(a, w_ref[:, column : column + TILE])
        for half in range(0, TILE, PAIR):
            start = column + half
            piece = part[:, half : half + PAIR]
            if start < 2 * D:
                piece = rotate_pair(piece, cosine, sine)
            if start < D:
                piece = piece * QUERY_SCALE
            qkv_ref[:, start : start + PAIR] = piece.astype(bf16)


def head_lanes():
    lane = lax.broadcasted_iota(jnp.int32, (1, PAIR), 1)
    return [lane < HDIM, lane >= HDIM]


def attend_pair(q_ref, k_ref, v_ref, rows_ref, cols_ref, p_ref, inv_ref, write):
    k, v = k_ref[...], v_ref[...]
    length = k.shape[0]
    mine = head_lanes()
    zero, one = jnp.zeros((), bf16), jnp.ones((), bf16)
    summing = [jnp.where(m, v, one) for m in mine]
    items = [(tile, head) for tile in range(0, length, TILE) for head in range(2)]

    def score(item):
        tile, head = item
        return dot_nt(jnp.where(mine[head], q_ref[tile : tile + TILE, :], zero), k)

    ahead = score(items[0])
    kept = None
    for i, (tile, head) in enumerate(items):
        rows = slice(tile, tile + TILE)
        scores = ahead
        if i + 1 < len(items):
            ahead = score(items[i + 1])
        scores = jnp.where(rows_ref[rows, :] == cols_ref[...], scores, MASKED)
        probs = jnp.exp2(scores - jnp.max(scores, axis=-1, keepdims=True)).astype(bf16)
        p_ref[head, rows, :] = probs
        part = dot_nn(probs, summing[head])
        inv = 1.0 / pltpu.roll(part, HDIM, 1)
        if head == 0:
            kept = (part * inv, inv)
        else:
            inv_ref[rows, :] = jnp.where(mine[0], kept[1], inv)
            write(rows, jnp.where(mine[0], kept[0], part * inv).astype(bf16))


def forward_kernel(
    sizes, pairs, late, q_ref, k_ref, v_ref, rows_ref, cols_ref, x_ref, gain_ref, w_out_any, w_in_any, w_mlp_any, cot_ref,
    o_ref, p_ref, inv_ref, x1_ref, b_ref, m_ref, slope_ref, act_ref, y_ref, dy_ref, *refs,
):
    seq = sizes[2]
    refs = list(refs)
    outs = [refs.pop(0) for _ in range(2 * late)]
    joined, w_out_ref, w_in_ref, w_mlp_ref, bounce, *sem_refs = refs
    step, last = pl.program_id(0), pl.num_programs(0) - 1
    sems = Sems(*sem_refs)
    me_seq = lax.axis_index("seq")
    into = sems.copy(cot_ref.at[me_seq], bounce)
    outof = sems.copy(bounce, dy_ref.at[0])
    weights = [sems.copy(w_out_any, w_out_ref)]
    partners = [("seq", k) for k in range(1, seq)]
    if late:
        gather = LateGather(sizes, [w_in_any, w_mlp_any], [w_in_ref, w_mlp_ref], sems)
        weights += gather.own
        keeps = [sems.copy(w_in_ref, outs[0]), sems.copy(w_mlp_ref, outs[1])]
        partners = all_partners(sizes)
    else:
        weights += [sems.copy(w_in_any, w_in_ref), sems.copy(w_mlp_any, w_mlp_ref)]
    blocks = [sems.remote(cot_ref.at[flip(me_seq, k)], dy_ref.at[k], "seq", k) for k in range(1, seq)]

    @pl.when(step == 0)
    def _():
        into.start()
        start_all(weights)
        meet(partners)
        if late:
            start_all(gather.far)
        start_all(blocks)
        into.wait()
        outof.start()

    if late:
        for when in range(1, pairs + 1):
            @pl.when(step == when)
            def _(when=when):
                gather.advance(when)

    @pl.when(step < pairs)
    def _():
        def write(rows, value):
            o_ref[rows, :] = value
            joined[rows, pl.ds(pl.multiple_of(step * PAIR, PAIR), PAIR)] = value

        attend_pair(q_ref, k_ref, v_ref, rows_ref, cols_ref, p_ref, inv_ref, write)

    @pl.when(step == pairs)
    def _():
        if late:
            wait_all(weights[:1])
            gather.finish(0)
            keeps[0].start()
        else:
            wait_all(weights)

    @pl.when(step >= pairs)
    def _():
        start = pl.multiple_of((step - pairs) * TILE, TILE)
        x1 = x_ref[...].astype(f32) + dot_nn(joined[pl.ds(start, TILE), :], w_out_ref[...])
        x1_ref[...] = x1
        unit, _ = normalize(x1)
        b = (unit * gain_ref[1:2, :]).astype(bf16)
        b_ref[...] = b

        def hidden(column):
            return (
                dot_nn(b, w_in_ref[:, column : column + HCHUNK]),
                dot_nn(b, w_in_ref[:, FF + column : FF + column + HCHUNK]),
            )

        ahead = hidden(0)
        for column in range(0, FF, HCHUNK):
            hin, gate = ahead
            if column + HCHUNK < FF:
                ahead = hidden(column + HCHUNK)
            phi = 0.5 + 0.5 * lax.erf(hin * math.sqrt(0.5))
            act = hin * phi
            slope = phi + hin * (jnp.exp(hin * hin * -0.5) * (1.0 / math.sqrt(2.0 * math.pi)))
            m_ref[:, column : column + HCHUNK] = (act * gate).astype(bf16)
            act_ref[:, column : column + HCHUNK] = act.astype(bf16)
            slope_ref[:, column : column + HCHUNK] = (slope * gate).astype(bf16)
        if late:
            @pl.when(step == pairs)
            def _():
                gather.finish(1)
                keeps[1].start()

        y_ref[...] = (x1_ref[...] + dot_nn(m_ref[...], w_mlp_ref[...])).astype(bf16)

    @pl.when(step == last)
    def _():
        if late:
            wait_all(keeps)
        outof.wait()
        wait_all(blocks)


def order_of(sizes, rep_first):
    fsdp, rep, seq = sizes
    core = [("fsdp", 1)]
    rest = [("fsdp", b) for b in bits_of(fsdp)[1:]]
    copies = [("rep", b) for b in bits_of(rep)]
    return core + (copies + rest if rep_first else rest + copies) + [("seq", b) for b in bits_of(seq)]


def all_partners(sizes):
    fsdp, rep, seq = sizes
    return [("seq", k) for k in range(1, seq)] + [("fsdp", b) for b in bits_of(fsdp)] + [("rep", b) for b in bits_of(rep)]


def early_reducers(sizes):
    fsdp, rep, seq = sizes
    shapes = [(fsdp, FF // fsdp, D), (fsdp, D // fsdp, FF), (fsdp, D // fsdp, FF), (fsdp, D // fsdp, D)]
    reducers = [Reducer(shape, sizes, order_of(sizes, w == 2)) for w, shape in enumerate(shapes)]
    across = len(bits_of(fsdp)) + len(bits_of(rep))
    return reducers, [len(reducers[0].steps)] + [across + 2] * 2 + [across + 1]


def late_reducers(sizes):
    fsdp = sizes[0]
    return [Reducer((fsdp, D // fsdp, D), sizes, order_of(sizes, w == 1)) for w in range(3)]


def flat(rows):
    return rows % 16 == 0


def shard_of(ref, rows, q):
    return ref.at[pl.ds(pl.multiple_of(q * rows, 16), rows)] if flat(rows) else ref.at[q]


def weight_gradient(ref, wide, left, right):
    if len(ref.shape) == 2:
        @pl.loop(0, ref.shape[0] // HCHUNK)
        def _(i):
            at = pl.ds(pl.multiple_of(i * HCHUNK, HCHUNK), HCHUNK)
            ref[at, :] = dot_tn(left[:, at], right[...]).astype(bf16)
    else:
        shards, rows, cols = ref.shape
        wide[: shards * rows, :cols] = dot_tn(left[...], right[...])
        for q in range(shards):
            ref[q] = wide[q * rows : (q + 1) * rows, :cols].astype(bf16)


def middle_back_tile(dy, x1_ref, slope_ref, act_ref, gain_ref, w_out_ref, w_in_ref, w_mlp_ref, dh_ref, dgain_ref, dx1_ref):
    ahead = dot_nt(dy, w_mlp_ref[:HCHUNK, :])
    for column in range(0, FF, HCHUNK):
        dm = ahead
        if column + HCHUNK < FF:
            ahead = dot_nt(dy, w_mlp_ref[column + HCHUNK : column + 2 * HCHUNK, :])
        dh_ref[:, column : column + HCHUNK] = (dm * slope_ref[:, column : column + HCHUNK].astype(f32)).astype(bf16)
        dh_ref[:, FF + column : FF + column + HCHUNK] = (
            dm * act_ref[:, column : column + HCHUNK].astype(f32)
        ).astype(bf16)
    db = dot_nt(dh_ref[...], w_in_ref[...])
    unit, scale = normalize(x1_ref[...])
    back, terms = norm_back(unit, scale, gain_ref[1:2, :], db)
    dgain_ref[...] += jnp.sum(terms, axis=0, keepdims=True)
    dx1 = dy.astype(f32) + back
    dx1_ref[...] = dx1
    return dx1.astype(bf16)


def attend_back_pair(q_ref, k_ref, v_ref, o_ref, inv_ref, do, p_ref, cos_ref, sin_ref, dq_ref, dk_ref, dv_ref):
    v = v_ref[...]
    length = v.shape[0]
    mine = head_lanes()
    zero = jnp.zeros((), bf16)
    do = (do.astype(f32) * inv_ref[...]).astype(bf16)
    inner = do.astype(f32) * o_ref[...].astype(f32)
    do_heads = [jnp.where(m, do, zero) for m in mine]
    q_heads = [jnp.where(m, q_ref[...], zero).T for m in mine]
    k_heads = [jnp.where(m, k_ref[...], zero) for m in mine]
    do_turned = [d.T for d in do_heads]
    cosine, sine = cos_ref[...], sin_ref[...]
    dv = dk = None
    for tile in range(0, length, TILE):
        rows = slice(tile, tile + TILE)
        dq = None
        for head in range(2):
            probs = p_ref[head, rows, :]
            delta = jnp.sum(jnp.where(mine[head], inner[rows], 0.0), axis=-1, keepdims=True)
            dp = dot_nt(do_heads[head][rows], v)
            ds = (probs.astype(f32) * (dp - delta)).astype(bf16)
            value_part = dot_nn(do_turned[head][:, rows], probs)
            key_part = dot_nn(q_heads[head][:, rows], ds)
            query_part = dot_nn(ds, k_heads[head])
            dv = value_part if dv is None else dv + value_part
            dk = key_part if dk is None else dk + key_part
            dq = query_part if dq is None else dq + query_part
        dq_ref[rows, :] = rotate_pair(dq * HDIM**-0.5, cosine[rows], -sine[rows]).astype(bf16)
    dk_ref[...] = rotate_pair(dk.T * math.log(2.0), cosine, -sine).astype(bf16)
    dv_ref[...] = dv.T.astype(bf16)


def backward_kernel(
    sizes, tiles, x1_ref, slope_ref, act_ref, gain_ref, q_ref, k_ref, v_ref, o_ref, inv_ref,
    p_any, cos_any, sin_any, w_out_any, w_in_any, w_mlp_any, m_any, dy_any, b_any, o_any, y_ref, *refs,
):
    reducers, early = early_reducers(sizes)
    count = len(reducers)
    refs = list(refs)
    pop = lambda n: [refs.pop(0) for _ in range(n)]
    dx1_ref, dgain_ref, dq_ref, dk_ref, dv_ref, home_ref = pop(6)
    sums_out = pop(count)
    w_out_ref, w_in_ref, w_mlp_ref, m_ref, dy_ref, b_ref, all_o_ref = pop(7)
    dh_ref, low_ref, do_ref, wide, bounce, probs_ref, cos_ref, sin_ref = pop(8)
    grads = pop(count)
    (mlp_final,) = pop(1)
    lands = [pop(len(r.scratch(0, e))) for r, e in zip(reducers, early)]
    sems = Sems(*refs)
    me = lax.axis_index("fsdp")
    step, last = pl.program_id(0), pl.num_programs(0) - 1
    into, outof, blocks = give_back(y_ref, home_ref, bounce, sems)
    loads = [
        sems.copy(src, dst)
        for src, dst in [
            (m_any, m_ref), (dy_any, dy_ref), (w_mlp_any, w_mlp_ref), (w_in_any, w_in_ref), (w_out_any, w_out_ref),
            (b_any, b_ref), (o_any, all_o_ref), (cos_any, cos_ref), (sin_any, sin_ref),
        ]
    ]
    pair, pairs = step - tiles - 1, last - tiles
    slot_sems = [sems.local.at[sems.local_used + i] for i in range(2)]
    sems.local_used += 2

    def fetch(which, slot):
        return pltpu.make_async_copy(p_any.at[pl.ds(which * 2, 2)], probs_ref.at[slot], slot_sems[slot])
    stores = [sems.copy(mlp_final if w == 0 else shard_of(grads[w], reducers[w].rows, me), sums_out[w]) for w in range(count)]
    for w, reducer in enumerate(reducers):
        reducer.bind(lambda j, w=w: shard_of(grads[w], reducers[w].rows, flip(me, j)), lands[w], sems, 0, early[w], mlp_final if w == 0 else None)
    mlp, first_half, second_half, out = reducers

    def at(when, *actions):
        @pl.when(step == when)
        def _():
            for action in actions:
                action()

    def advance(reducer, s, limit):
        def run():
            reducer.finish(s)
            if s + 1 < limit:
                reducer.start(s + 1)
        return run

    @pl.when(step == 0)
    def _():
        start_all(loads)
        into.start()
        meet(all_partners(sizes))
        start_all(blocks)
        dgain_ref[...] = jnp.zeros_like(dgain_ref)
        wait_all(loads[:2])
        weight_gradient(grads[0], wide, m_ref, dy_ref)
        mlp.start(0)
        into.wait()
        outof.start()
        wait_all(loads[2:5])

    at(1, advance(mlp, 0, early[0]))

    @pl.when(step < tiles)
    def _():
        rows = pl.ds(pl.multiple_of(step * TILE, TILE), TILE)
        low = middle_back_tile(
            dy_ref[rows, :], x1_ref, slope_ref, act_ref, gain_ref, w_out_ref, w_in_ref, w_mlp_ref,
            dh_ref.at[rows, :], dgain_ref, dx1_ref,
        )
        low_ref[rows, :] = low
        do_ref[rows, :] = dot_nt(low, w_out_ref[...]).astype(bf16)

    across = len(bits_of(sizes[0])) + len(bits_of(sizes[1]))

    @pl.when(step == tiles)
    def _():
        wait_all(loads[5:])
        weight_gradient(grads[1], wide, b_ref, dh_ref.at[:, :FF])
        first_half.start(0)
        weight_gradient(grads[2], wide, b_ref, dh_ref.at[:, FF:])
        second_half.start(0)
        for s in range(1, across - 1):
            advance(mlp, s, early[0])()
        weight_gradient(grads[3], wide, all_o_ref, low_ref)
        out.start(0)

    @pl.when(step == tiles - 1)
    def _():
        fetch(0, 0).start()

    for slot in range(2):
        @pl.when((step > tiles) & (pair % 2 == slot))
        def _(slot=slot):
            fetch(pair, slot).wait()

            @pl.when(pair + 1 < pairs)
            def _():
                fetch(pair + 1, 1 - slot).start()

    halves = (first_half, second_half)
    steps = lambda reducer, limit, *which: [advance(reducer, s, limit) for s in which]
    half_steps = lambda *which: [advance(r, s, early[1]) for s in which for r in halves]
    middle = range(1, across - 1)
    at(tiles + 1, *steps(mlp, early[0], across - 1), *half_steps(0))
    at(tiles + 2, *steps(out, early[3], 0))
    at(tiles + 3, *half_steps(*middle))
    at(tiles + 4, *steps(mlp, early[0], across), *steps(out, early[3], *middle))
    at(tiles + 5, *steps(mlp, early[0], across + 1), *half_steps(across - 1))
    at(tiles + 6, *steps(mlp, early[0], *range(across + 2, early[0] - 1)), *half_steps(across), *steps(out, early[3], across - 1))

    @pl.when(step > tiles)
    def _():
        column = pl.multiple_of(pair * PAIR, PAIR)
        attend_back_pair(
            q_ref, k_ref, v_ref, o_ref, inv_ref, do_ref[:, pl.ds(column, PAIR)], probs_ref.at[pair % 2], cos_ref, sin_ref,
            dq_ref, dk_ref, dv_ref,
        )

    @pl.when(step == last)
    def _():
        for w, reducer in enumerate(reducers):
            reducer.finish(early[w] - 1)
            stores[w].start()
        wait_all(stores)
        outof.wait()
        wait_all(blocks)


PIECES = 4


def leave_kernel(sizes, gain_ref, other_gain_ref, *refs):
    fsdp, rep, seq = sizes
    reducers, early = (some[1:] for some in early_reducers(sizes))
    whole = late_reducers(sizes)
    count, more = len(reducers), len(whole)
    refs = list(refs)
    pop = lambda n: [refs.pop(0) for _ in range(n)]
    anys = pop(7)
    sums_in = pop(count)
    (home_ref,) = pop(1)
    in_out, out_out, qkv_out, gains_out = pop(4)
    dq_ref, a_ref, dk_ref, dv_ref, w_ref, x_ref, dx1_ref = local = pop(7)
    slots, wide, in_final, out_final, qkv_final = pop(5)
    held, grads = pop(count), pop(more)
    lands = [pop(len(r.scratch(e, len(r.steps)))) for r, e in zip(reducers, early)]
    whole_lands = [pop(len(r.scratch(0, len(r.steps)))) for r in whole]
    (gain_lands,) = pop(1)
    sems = Sems(*refs)
    me, me_seq = lax.axis_index("fsdp"), lax.axis_index("seq")
    own = sems.copy(slots.at[0], home_ref.at[me_seq])
    height = slots.shape[1] // PIECES
    blocks = {
        k: [
            sems.remote(slots.at[k, pl.ds(n * height, height)], home_ref.at[me_seq, pl.ds(n * height, height)], "seq", k)
            for n in range(PIECES)
        ]
        for k in range(1, seq)
    }
    order = sorted(range(1, seq), key=lambda k: (k != 2, k == 1))
    ready = []

    def send_piece(n=1):
        for _ in range(n):
            if ready:
                ready.pop(0).start()

    operands = [sems.copy(src, dst) for src, dst in zip(anys, local)]
    loads = [sems.copy(sums_in[w], held[w]) for w in range(count)]
    stores = [
        sems.copy(src, dst)
        for src, dst in ((in_final, in_out), (out_final, out_out), (qkv_final, qkv_out))
    ]
    finals = [in_final.at[:, pl.ds(0, FF)], in_final.at[:, pl.ds(FF, FF)], out_final]
    for w, reducer in enumerate(reducers):
        reducer.bind(lambda j, w=w: held[w], lands[w], sems, early[w], len(reducer.steps), finals[w])
    for w, reducer in enumerate(whole):
        reducer.bind(
            lambda j, w=w: shard_of(grads[w], whole[w].rows, flip(me, j)), whole_lands[w], sems, 0, len(reducer.steps),
            qkv_final.at[:, pl.ds(w * D, D)],
        )
    hops = [("fsdp", b) for b in bits_of(fsdp)] + [("rep", b) for b in bits_of(rep)] + [("seq", b) for b in bits_of(seq)]
    gain_moves = [sems.remote(gains_out, gain_lands.at[i], axis, bit) for i, (axis, bit) in enumerate(hops)]
    rows = slots.shape[1]

    def advance(some, s):
        for reducer in some:
            if s < len(reducer.steps):
                reducer.finish(s)
                if s + 1 < len(reducer.steps):
                    reducer.start(s + 1)

    def advance_gains(i):
        if i < len(hops):
            gain_moves[i].wait()
            gains_out[...] += gain_lands[i]
            if i + 1 < len(hops):
                gain_moves[i + 1].start()

    def input_slot(k):
        piece = slice(k * rows, (k + 1) * rows)
        da = dot_nt(dq_ref[piece, :], w_ref[:, :D])
        da = da + dot_nt(dk_ref[piece, :], w_ref[:, D : 2 * D])
        da = da + dot_nt(dv_ref[piece, :], w_ref[:, 2 * D :])
        unit, scale = normalize(x_ref[piece, :].astype(f32))
        back, terms = norm_back(unit, scale, gain_ref[0:1, :], da)
        gains_out[0:1, :] += jnp.sum(terms, axis=0, keepdims=True)
        slots[k] = (dx1_ref[piece, :] + back).astype(bf16)
        if k:
            ready.extend(blocks[k])

    def gradient(w, part):
        weight_gradient(grads[w], wide, a_ref, part)
        whole[w].start(0)

    across = len(bits_of(fsdp)) + len(bits_of(rep))
    halves, out, last = reducers[:2], reducers[2:], len(whole[0].steps)
    start_all(operands[:2])
    start_all(loads)
    start_all(operands[2:])
    gains_out[...] = jnp.zeros_like(gains_out)
    gains_out[1:2, :] = other_gain_ref[...]
    meet(all_partners(sizes))
    wait_all(loads)
    for w, (reducer, s) in enumerate(zip(reducers, early)):
        if s < len(reducer.steps):
            reducer.start(s)
        else:
            finals[w][...] = held[w][...]
    wait_all(operands[:2])
    gradient(0, dq_ref)
    wait_all(operands[2:])
    input_slot(order[0])
    send_piece(PIECES // 2)
    advance(whole[:1], 0)
    advance(halves, early[0])
    gradient(1, dk_ref)
    for k in order[1:2]:
        input_slot(k)
    advance(whole[1:2], 0)
    advance(out, early[2])
    send_piece()
    gradient(2, dv_ref)
    for k in order[2:]:
        input_slot(k)
    advance(whole[:1], 1)
    advance(whole[2:], 0)
    send_piece()
    input_slot(0)
    own.start()
    gain_moves[0].start()
    advance(whole[1:2], 1)
    advance(out, early[2] + 1)
    send_piece()
    hop = 0
    for s in range(2, across):
        advance(whole[:1], s)
        advance_gains(hop)
        advance(whole[2:], s - 1)
        advance(whole[1:2], s)
        send_piece()
        hop += 1
    advance(whole[2:], across - 1)
    advance_gains(hop)
    send_piece()
    for s in range(across, last):
        for reducer in whole:
            advance([reducer], s)
            send_piece()
        hop += 1
        advance_gains(hop)
    for i in range(hop + 1, len(hops)):
        advance_gains(i)
    send_piece(len(ready))
    for s in range(early[0] + 1, len(halves[0].steps)):
        advance(halves, s)
    for s in range(early[2] + 2, len(out[0].steps)):
        advance(out, s)
    start_all(stores)
    wait_all(stores)
    own.wait()
    for k in range(1, seq):
        wait_all(blocks[k])


def rows_spec(width):
    return pl.BlockSpec((TILE, width), lambda i: (i, 0))


def whole_spec(*shape):
    return pl.BlockSpec(shape, lambda i: (0,) * len(shape))


def pair_spec(length, offset=0):
    return pl.BlockSpec((length, PAIR), lambda i: (0, i + offset))


def struct(dtype, *shape):
    return jax.ShapeDtypeStruct(shape, dtype)


def call(kernel, grid, in_specs, out_specs, out_shape, flops, scratch=(), collective=None):
    return pl.pallas_call(
        kernel,
        grid=(grid,),
        in_specs=in_specs,
        out_specs=out_specs,
        out_shape=out_shape,
        scratch_shapes=list(scratch),
        compiler_params=pltpu.CompilerParams(
            dimension_semantics=("arbitrary",), vmem_limit_bytes=VMEM_LIMIT,
            collective_id=collective, has_side_effects=collective is not None,
        ),
        cost_estimate=pl.CostEstimate(flops=flops, bytes_accessed=10 * 2**20, transcendentals=0),
    )


MESH = pl.DeviceIdType.MESH
ANY = pl.BlockSpec(memory_space=pl.ANY)


def take(array, index):
    return lax.dynamic_index_in_dim(array, index, 0, keepdims=False)


def flip(index, mask):
    bit = 1
    while bit <= mask:
        if mask & bit:
            index = index + bit - 2 * bit * ((index // bit) % 2)
        bit *= 2
    return index


def flip_by(index, mask, size):
    total = 0
    for bit in bits_of(size):
        ours, theirs = (index // bit) % 2, (mask // bit) % 2
        total = total + bit * (ours + theirs - 2 * ours * theirs)
    return total


def bits_of(size):
    return [1 << i for i in range(size.bit_length() - 1)]


def meet(partners):
    barrier = pltpu.get_barrier_semaphore()
    for axis, mask in partners:
        pl.semaphore_signal(
            barrier, inc=1, device_id={axis: flip(lax.axis_index(axis), mask)}, device_id_type=MESH
        )
    pl.semaphore_wait(barrier, len(partners))


class Sems:
    def __init__(self, send, recv, local):
        self.send, self.recv, self.local = send, recv, local
        self.remote_used = self.local_used = 0

    def remote(self, src, dst, axis, mask):
        i = self.remote_used
        self.remote_used += 1
        return pltpu.make_async_remote_copy(
            src_ref=src, dst_ref=dst, send_sem=self.send.at[i], recv_sem=self.recv.at[i],
            device_id={axis: flip(lax.axis_index(axis), mask)}, device_id_type=MESH,
        )

    def copy(self, src, dst):
        i = self.local_used
        self.local_used += 1
        return pltpu.make_async_copy(src, dst, self.local.at[i])


def sem_shapes(remote, local):
    dma = pltpu.SemaphoreType.DMA
    return [dma((remote,)), dma((remote,)), dma((max(local, 1),))]


def start_all(copies):
    for copy in copies:
        copy.start()


def wait_all(copies):
    for copy in copies:
        copy.wait()


class Gather:
    def __init__(self, sizes, shards, place, sems, order):
        self.sizes, self.shards, self.place, self.sems = sizes, shards, place, sems
        self.pieces = order
        self.me, self.me_rep = lax.axis_index("fsdp"), lax.axis_index("rep")
        self.pending = []

    def part(self, ref, pieces, n):
        width = ref.shape[-1] // (self.sizes[1] * pieces)
        start = (self.me_rep * pieces + n) * width
        return ref.at[:, pl.ds(pl.multiple_of(start, 128), width)]

    def source(self, w, h):
        return self.shards[w] if h == 0 else self.place(w, flip(self.me, h))

    def start(self):
        self.held = [0]
        self.over = self.cross(self.far_bits()[0]) if self.far_bits() else []

    def far_bits(self):
        return list(reversed(bits_of(self.sizes[0])[1:]))

    def cross(self, bit):
        over = []
        for w, pieces, n in self.pieces:
            moved = [
                self.sems.remote(
                    self.part(self.source(w, h), pieces, n),
                    self.part(self.place(w, flip(self.me, h)), pieces, n), "fsdp", bit,
                )
                for h in self.held
            ]
            start_all(moved)
            over.append(moved)
        return over

    def pass_on(self, i, bit):
        w, pieces, n = self.pieces[i]
        for copy in self.over[i]:
            copy.wait_recv()
        self.pending += self.over[i]
        passed = []
        for mask in range(1, self.sizes[1]):
            for h in self.held:
                here = self.part(self.place(w, flip(self.me, h ^ bit)), pieces, n)
                passed.append(self.sems.remote(here, here, "rep", mask))
        start_all(passed)
        self.pending += passed
        return passed

    def events(self, lag=2):
        bits = self.far_bits()
        count = len(self.pieces)
        for bit in bits[:-1]:
            passed = [self.pass_on(i, bit) for i in range(count)]
            self.held = self.held + [h ^ bit for h in self.held]
            for copies in passed:
                for copy in copies:
                    copy.wait_recv()
            self.over = self.cross(bits[bits.index(bit) + 1])
        end = {w: i for i, (w, _, _) in enumerate(self.pieces)}
        passed, near_held = [], self.held + [h ^ bit for bit in bits[-1:] for h in self.held]
        for i in range(count + lag):
            if i < count:
                if bits:
                    passed.append(self.pass_on(i, bits[-1]))
                yield None
            for w, last in end.items():
                if last == i - lag:
                    if bits:
                        for j, (other, _, _) in enumerate(self.pieces):
                            if other == w:
                                for copy in passed[j]:
                                    copy.wait_recv()
                    yield w, self.near(w, near_held)

    def near(self, w, held):
        copies = [self.sems.remote(self.source(w, h), self.place(w, flip(self.me, h)), "fsdp", 1) for h in held]
        start_all(copies)
        return copies

    @staticmethod
    def count(sizes, order, weights):
        held, copies = 1, 0
        for _ in bits_of(sizes[0])[1:]:
            copies += len(order) * held * sizes[1]
            held *= 2
        return copies + weights * held


PASSED = (0, 1, 2, 4, 6, 6, 6)
CROSSED = (4, 5)


class LateGather:
    def __init__(self, sizes, shards, wholes, sems):
        fsdp, rep, _ = sizes
        me, me_rep = lax.axis_index("fsdp"), lax.axis_index("rep")
        place = lambda w, q: shard_of(wholes[w], shards[w].shape[0], q)
        self.own = [sems.copy(shards[w], place(w, me)) for w in range(2)]
        self.far, self.passed, self.near = [], [], [[], []]
        for w in range(2):
            fits = shards[w].shape[-1] % (rep * 3 * 128) == 0
            pieces = 3 if fits else 1
            width = shards[w].shape[-1] // (rep * pieces)
            for n in range(pieces if fsdp > 2 else 0):
                cols = pl.ds(pl.multiple_of((me_rep * pieces + n) * width, 128), width)
                self.far.append(sems.remote(shards[w].at[:, cols], place(w, me).at[:, cols], "fsdp", 2))
                here = place(w, flip(me, 2)).at[:, cols]
                self.passed.append([sems.remote(here, here, "rep", mask) for mask in range(1, rep)])
            for h in range(0, fsdp, 2):
                src = shards[w] if h == 0 else place(w, flip(me, h))
                self.near[w].append(sems.remote(src, place(w, flip(me, h)), "fsdp", 1))
        self.pieces = len(self.far) // 2
        self.count = len(self.far)

    @staticmethod
    def copies(sizes):
        return 2 * (3 * sizes[1] + sizes[0] // 2)

    def pass_on(self, i):
        self.far[i].wait_recv()
        start_all(self.passed[i])

    def cross_core(self, w):
        for copies in self.passed[w * self.pieces : (w + 1) * self.pieces]:
            for copy in copies:
                copy.wait_recv()
        start_all(self.near[w])

    def advance(self, step):
        upto = lambda n: min(n, self.count)
        for i in range(upto(PASSED[step - 1]), upto(PASSED[step])):
            self.pass_on(i)
        for w in range(2):
            if step == CROSSED[w]:
                self.cross_core(w)

    def finish(self, w):
        wait_all(self.own[w : w + 1])
        for i in range(w * self.pieces, (w + 1) * self.pieces):
            self.far[i].wait_send()
            for copy in self.passed[i]:
                copy.wait_send()
        wait_all(self.near[w])


def gather_order(sizes, shards):
    fits = lambda w, n: shards[w].shape[-1] % (sizes[1] * n * 128) == 0
    split = lambda w, n: n if fits(w, n) else 1
    order = []
    for w, n in ((0, 1), (1, 3), (2, 3), (4, 3), (3, 3)):
        if w >= len(shards):
            continue
        n = split(w, n)
        order += [(w, n, i) for i in range(n)]
    return order


def enter_kernel(sizes, count, tokens, *refs):
    fsdp, rep, seq = sizes
    refs = list(refs)
    pop = lambda n: [refs.pop(0) for _ in range(n)]
    shards = pop(count)
    (x_out,) = pop(1)
    fulls = pop(count)
    (bounce_x,) = pop(1)
    bounces = pop(count)
    sems = Sems(*refs)
    me, me_seq = lax.axis_index("fsdp"), lax.axis_index("seq")
    into = [sems.copy(tokens.at[me_seq], bounce_x)] + [sems.copy(shards[w], bounces[w]) for w in range(count)]
    outof = [sems.copy(bounce_x, x_out.at[0])] + [sems.copy(bounces[w], fulls[w].at[me]) for w in range(count)]
    gather = Gather(sizes, shards, lambda w, q: fulls[w].at[q], sems, gather_order(sizes, shards))
    start_all(into)
    meet(all_partners(sizes))
    blocks = [sems.remote(tokens.at[flip(me_seq, k)], x_out.at[k], "seq", k) for k in range(1, seq)]
    start_all(blocks)
    gather.start()
    last = []
    for event in gather.events():
        if event:
            last += event[1]
    wait_all(into)
    start_all(outof)
    for copy in gather.pending:
        copy.wait_send()
    wait_all(last)
    wait_all(blocks)
    wait_all(outof)


def enter(sizes, tokens, shards):
    fsdp = sizes[0]
    count = len(shards)
    hbm = lambda shape: struct(bf16, *shape)
    copies = sizes[2] - 1 + Gather.count(sizes, gather_order(sizes, shards), count)
    return pl.pallas_call(
        functools.partial(enter_kernel, sizes, count),
        in_specs=[ANY] * (1 + count),
        out_specs=[ANY] * (1 + count),
        out_shape=[hbm(tokens.shape)] + [hbm((fsdp,) + s.shape) for s in shards],
        scratch_shapes=[pltpu.VMEM(tokens.shape[1:], bf16)]
        + [pltpu.VMEM(s.shape, bf16) for s in shards]
        + sem_shapes(copies, 2 * (1 + count)),
        compiler_params=pltpu.CompilerParams(collective_id=0, has_side_effects=True),
    )(tokens, *shards)


def turn(row):
    n = row.shape[1]
    diagonal = lax.broadcasted_iota(jnp.int32, (n, n), 0) == lax.broadcasted_iota(jnp.int32, (n, n), 1)
    return jnp.sum(jnp.where(diagonal, row, 0), axis=1, keepdims=True)


def enter_project_kernel(sizes, count, tokens, segments, *refs):
    fsdp, rep, seq = sizes
    refs = list(refs)
    pop = lambda n: [refs.pop(0) for _ in range(n)]
    shards = pop(count)
    x_out, a_out, qkv_out, cos_out, sin_out, marks_out, row_out, gains_out, wq_out = pop(9)
    fulls = [None, None] + pop(count - 2)
    xs, a, qkv, wq, gains = pop(5)
    bounces = pop(count)
    sems = Sems(*refs)
    me, me_seq = lax.axis_index("fsdp"), lax.axis_index("seq")
    shard_rows, rows = shards[1].shape[0], xs.shape[1]
    columns = wq.shape[1]

    def place(w, q):
        if w == 0:
            return gains.at[q]
        if w == 1:
            return wq.at[pl.ds(pl.multiple_of(q * shard_rows, 16), shard_rows)]
        return fulls[w].at[q]

    own = sems.copy(tokens.at[me_seq], xs.at[0])
    into = [sems.copy(shards[w], place(w, me) if w < 2 else bounces[w - 2]) for w in range(count)]
    outof = [sems.copy(bounces[w - 2], place(w, me)) for w in range(2, count)]
    blocks = [sems.remote(tokens.at[flip(me_seq, k)], xs.at[k], "seq", k) for k in range(1, seq)]
    stores = [
        [sems.copy(src.at[k], dst.at[k]) for src, dst in ((xs, x_out), (a, a_out), (qkv, qkv_out))] for k in range(seq)
    ]
    keep = sems.copy(wq, wq_out)
    gather = Gather(sizes, shards, place, sems, gather_order(sizes, shards))
    own.start()
    start_all(into)
    meet(all_partners(sizes))
    gather.start()
    start_all(blocks)

    lane = lax.broadcasted_iota(jnp.int32, (1, PAIR), 1)
    rate = jnp.exp((lane % (HDIM // 2)).astype(f32) * (-2.0 * math.log(THETA) / HDIM))
    sign = jnp.where(lane_halves((1, PAIR)), -1.0, 1.0)
    batch = segments.shape[1]

    def own_segments(block):
        at = pl.multiple_of(block * rows, 128)
        return segments[me_seq // batch, pl.ds(me_seq % batch, 1), pl.ds(at, rows)]

    @pl.loop(0, seq)
    def _(k):
        block = flip_by(me_seq, k, seq)
        piece = pl.ds(pl.multiple_of(k * rows, 128), rows)
        row = own_segments(block)
        column = turn(row)
        earlier = jnp.zeros((rows, 1), jnp.int32)
        for other in range(seq):
            earlier += jnp.sum((own_segments(other) < column).astype(jnp.int32), axis=1, keepdims=True)
        index = block * rows + lax.broadcasted_iota(jnp.int32, (rows, 1), 0)
        angles = (index - earlier).astype(f32) * rate
        cos_out[piece, :] = jnp.cos(angles)
        sin_out[piece, :] = jnp.sin(angles) * sign
        marks_out[piece, :] = column
        row_out[:, piece] = row

    def project(k):
        if k == 0:
            own.wait()
        else:
            blocks[k - 1].wait()
        piece = slice(k * rows, (k + 1) * rows)
        unit, _ = normalize(xs[k].astype(f32))
        low = (unit * gains_out[0:1, :]).astype(bf16)
        a[k] = low
        cosine, sine = cos_out[piece, :], sin_out[piece, :]

        @pl.loop(0, 2 * D // WIDE)
        def _(i):
            at = pl.multiple_of(i * WIDE, WIDE)
            part = dot_nn(low, wq[:, pl.ds(at, WIDE)])
            scale = jnp.where(at < D, QUERY_SCALE, 1.0)
            for half in range(0, WIDE, PAIR):
                value = rotate_pair(part[:, half : half + PAIR], cosine, sine) * scale
                qkv[k, :, pl.ds(at + half, PAIR)] = value.astype(bf16)

        qkv[k, :, 2 * D :] = dot_nn(low, wq[:, 2 * D :]).astype(bf16)
        start_all(stores[k])

    last, queue, since = {}, list(range(seq)), 0
    for event in gather.events():
        if event:
            last[event[0]] = event[1]
            if event[0] == 1:
                for copy in into[:2] + last[0] + last[1]:
                    copy.wait()
                keep.start()
                total = gains[0, :2, :].astype(f32)
                for q in range(1, fsdp):
                    total = total + gains[q, :2, :].astype(f32)
                gains_out[...] = total
                wait_all(into[2:])
                start_all(outof)
                project(queue.pop(0))
        elif 1 in last:
            since += 1
            if since % 2 == 0 and len(queue) > 1:
                project(queue.pop(0))
    for k in queue:
        project(k)
    for copy in gather.pending:
        copy.wait_send()
    for w in range(2, count):
        wait_all(last[w])
    wait_all(outof)
    for group in stores:
        wait_all(group)
    keep.wait()


def enter_project(sizes, tokens, segments, shards):
    fsdp, rep, seq = sizes
    count, rows = len(shards), tokens.shape[1]
    length, columns = seq * rows, shards[1].shape[1]
    vmem = pl.BlockSpec(memory_space=pltpu.VMEM)
    copies = seq - 1 + Gather.count(sizes, gather_order(sizes, shards), count)
    return pl.pallas_call(
        functools.partial(enter_project_kernel, sizes, count),
        in_specs=[ANY, vmem] + [ANY] * count,
        out_specs=[ANY] * 3 + [vmem] * 5 + [ANY] * (count - 1),
        out_shape=[struct(bf16, seq, rows, D), struct(bf16, seq, rows, D), struct(bf16, seq, rows, columns),
                   struct(f32, length, PAIR), struct(f32, length, PAIR), struct(jnp.int32, length, 1),
                   struct(jnp.int32, 1, length), struct(f32, 2, D), struct(bf16, D, columns)]
        + [struct(bf16, fsdp, *s.shape) for s in shards[2:]],
        scratch_shapes=[pltpu.VMEM((seq, rows, D), bf16), pltpu.VMEM((seq, rows, D), bf16),
                        pltpu.VMEM((seq, rows, columns), bf16), pltpu.VMEM((D, columns), bf16),
                        pltpu.VMEM((fsdp,) + shards[0].shape, bf16)]
        + [pltpu.VMEM(s.shape, bf16) for s in shards[2:]] + [pltpu.VMEM((16, 128), bf16)] * 2
        + sem_shapes(copies, 2 + count + count - 2 + 3 * seq),
        compiler_params=pltpu.CompilerParams(
            collective_id=4, has_side_effects=True, vmem_limit_bytes=VMEM_LIMIT
        ),
    )(tokens, segments, *shards)


def add_into(total, term):
    rows = total.shape[0]
    height = 48 if rows % 48 == 0 else rows

    @pl.loop(0, rows // height)
    def _(i):
        at = pl.ds(pl.multiple_of(i * height, 16), height) if height < rows else pl.ds(0, rows)
        total[at, :] = (total[at, :].astype(f32) + term[at, :].astype(f32)).astype(bf16)


class Reducer:
    def __init__(self, parts_shape, sizes, order):
        self.fsdp, self.rows, self.cols = parts_shape
        self.steps = []
        held, rows, cols = list(range(self.fsdp)), self.rows, self.cols
        row_at, col_at = [], []
        for axis, bit in order:
            step = dict(axis=axis, bit=bit, row_at=list(row_at), col_at=list(col_at), rows=rows, cols=cols)
            if axis == "fsdp":
                step["send"] = [j for j in held if j & bit]
                held = [j for j in held if not j & bit]
                step["keep"] = held
                step["shape"] = (len(held), rows, cols)
                step["split"] = None
            else:
                step["keep"] = step["send"] = held
                if (axis, bit) == order[-1]:
                    step["split"] = "none"
                elif (rows // 2) % 16 == 0:
                    rows //= 2
                    row_at = row_at + [(axis, bit, rows)]
                    step["split"] = "rows"
                elif (cols // 2) % 128 == 0:
                    cols //= 2
                    col_at = col_at + [(axis, bit, cols)]
                    step["split"] = "cols"
                else:
                    step["split"] = "none"
                step["shape"] = (len(held), rows, cols)
            self.steps.append(step)
        self.down = len(self.steps)
        for step in reversed(self.steps[: self.down]):
            if step["split"] in ("rows", "cols"):
                self.steps.append(dict(step, up=True))

    @staticmethod
    def offset(terms, align, last=None):
        total = 0
        for i, (axis, bit, extent) in enumerate(terms):
            half = (lax.axis_index(axis) // bit) % 2
            if last == i:
                half = 1 - half
            total = total + half * extent
        return total if isinstance(total, int) else pl.multiple_of(total, align)

    def region(self, step, after, other=False):
        row_at, col_at, rows, cols = step["row_at"], step["col_at"], step["rows"], step["cols"]
        row_last = col_last = None
        if after:
            if step["split"] == "rows":
                rows //= 2
                row_at = row_at + [(step["axis"], step["bit"], rows)]
                row_last = len(row_at) - 1 if other else None
            elif step["split"] == "cols":
                cols //= 2
                col_at = col_at + [(step["axis"], step["bit"], cols)]
                col_last = len(col_at) - 1 if other else None
        return (
            pl.ds(self.offset(row_at, 16, row_last), rows),
            pl.ds(self.offset(col_at, 128, col_last), cols),
        )

    def scratch(self, first, last):
        return [pltpu.VMEM(s["shape"], bf16) for s in self.steps[first:last] if "up" not in s]

    def copies(self, first, last):
        return sum(1 if "up" in s else len(s["send"]) for s in self.steps[first:last])

    def bind(self, parts, lands, sems, first, last, final=None):
        self.parts, self.sems, self.final = parts, sems, final
        self.lands, self.moves = {}, {}
        lands = list(lands)
        for s in range(first, last):
            step = self.steps[s]
            moves = []
            if "up" in step:
                there = final.at[self.region(step, True)]
                moves.append(sems.remote(there, there, step["axis"], step["bit"]))
            else:
                land = self.lands[s] = lands.pop(0)
                for i, j in enumerate(step["send"]):
                    fsdp = step["axis"] == "fsdp"
                    src = self.parts(j).at[self.region(step, not fsdp, not fsdp)]
                    moves.append(sems.remote(src, land.at[i], step["axis"], step["bit"]))
            self.moves[s] = moves

    def start(self, s):
        if s == self.down:
            region = self.region(self.steps[s - 1], True)
            self.final[region] = self.parts(0)[region]
        start_all(self.moves.get(s, []))

    def finish(self, s):
        step = self.steps[s]
        self.finish_step(s, step)
        if s + 1 == len(self.steps) == self.down and self.final is not None:
            self.final[...] = self.parts(0)[...]

    def finish_step(self, s, step):
        for i, move in enumerate(self.moves[s]):
            move.wait()
            if "up" not in step:
                j = step["keep"][i]
                ref = self.parts(j)
                add_into(ref.at[self.region(step, True)], self.lands[s].at[i])


def give_back(slots, home, bounce, sems):
    me = lax.axis_index("seq")
    seq = slots.shape[0]
    return (
        sems.copy(slots.at[0], bounce),
        sems.copy(bounce, home.at[me]),
        [sems.remote(slots.at[k], home.at[me], "seq", k) for k in range(1, seq)],
    )


def body(sizes, tokens, segments, positions, gain_attn, w_qkv, w_out, gain_mlp, w_in, w_mlp_out, cotangent):
    fsdp, rep, seq = sizes
    micro, batch, rows, _ = tokens.shape
    assert micro * batch == seq and rows % TILE == 0
    length = seq * rows
    me_seq, me_fsdp = lax.axis_index("seq"), lax.axis_index("fsdp")

    own_gains = jnp.zeros((16, D), bf16)
    own_gains = lax.dynamic_update_slice(own_gains, jnp.stack([gain_attn, gain_mlp]), (0, me_fsdp * (D // fsdp)))
    shards = [own_gains, w_qkv, w_out, w_mlp_out, w_in]
    tiles, pairs = length // TILE, HEADS // 2
    late = fsdp in (2, 4) and pairs >= 6 and flat(D // fsdp) and flat(FF // fsdp)
    if (D // fsdp) % 16 == 0:
        x, a, qkv, cosine, sine, marks_column, marks_row, gains, wq, *rest = enter_project(
            sizes, tokens.reshape(seq, rows, D), segments, shards[:3] if late else shards
        )
        x, a, qkv = (v.reshape(length, -1) for v in (x, a, qkv))
        wo, *rest = (w.reshape(-1, w.shape[-1]) for w in rest)
        wm, wi = (w_mlp_out, w_in) if late else rest
    else:
        x, gains, wq, wo, wm, wi = enter(sizes, tokens.reshape(seq, rows, D), shards)
        x = x.reshape(length, D)
        gains = jnp.sum(gains[:, :2].astype(f32), axis=0)
        wq, wo, wm, wi = (w.reshape(-1, w.shape[-1]) for w in (wq, wo, wm, wi))

        marks = take(segments.reshape(seq, length), me_seq)
        place = jnp.arange(length, dtype=jnp.int32) - jnp.sum(
            (marks[None, :] < marks[:, None]).astype(jnp.int32), axis=1
        )
        slot_order = [me_seq ^ k for k in range(seq)]
        marks = jnp.concatenate([take(marks.reshape(seq, rows), s) for s in slot_order])
        place = jnp.concatenate([take(place.reshape(seq, rows), s) for s in slot_order])
        half = jnp.arange(0, HDIM, 2).astype(f32) / HDIM
        angles = place.astype(f32)[:, None] * jnp.exp(-half * math.log(THETA))
        cosine, sine = jnp.cos(angles), jnp.sin(angles)
        cosine = jnp.concatenate([cosine] * 4, -1)
        sine = jnp.concatenate([-sine, sine] * 2, -1)

        a, qkv = call(
            first_kernel, tiles,
            [rows_spec(D), whole_spec(2, D), whole_spec(D, 3 * D), rows_spec(PAIR), rows_spec(PAIR)],
            [rows_spec(D), rows_spec(3 * D)],
            [struct(bf16, length, D), struct(bf16, length, 3 * D)],
            2 * length * D * 3 * D,
        )(x, gains, wq, cosine, sine)
        marks_column, marks_row = marks[:, None], marks[None, :]

    vmem = pl.BlockSpec(memory_space=pltpu.VMEM)
    pair_at = lambda offset, lag, n: pl.BlockSpec(
        (length, PAIR), lambda i: (0, jnp.clip(i - lag, 0, n - 1) + offset)
    )
    prob_at = lambda lag: pl.BlockSpec((2, length, length), lambda i: (jnp.clip(i - lag, 0, pairs - 1), 0, 0))
    tile_at = lambda width, lag: pl.BlockSpec((TILE, width), lambda i: (jnp.clip(i - lag, 0, tiles - 1), 0))
    slots = struct(bf16, seq, rows, D)
    o, probs, inv, x1, b, m, slope, act, y, dy, *wholes = call(
        functools.partial(forward_kernel, sizes, pairs, late), pairs + tiles,
        [pair_at(0, 0, pairs), pair_at(pairs, 0, pairs), pair_at(2 * pairs, 0, pairs),
         whole_spec(length, 1), whole_spec(1, length), tile_at(D, pairs), whole_spec(2, D)] + [ANY] * 4,
        [pair_at(0, 0, pairs), prob_at(0), pair_at(0, 0, pairs), tile_at(D, pairs), tile_at(D, pairs)]
        + [tile_at(FF, pairs)] * 3 + [tile_at(D, pairs), ANY] + [ANY] * (2 * late),
        [struct(bf16, length, D), struct(bf16, HEADS, length, length), struct(f32, length, D),
         struct(f32, length, D), struct(bf16, length, D), struct(bf16, length, FF),
         struct(bf16, length, FF), struct(bf16, length, FF), struct(bf16, length, D), slots]
        + [struct(bf16, D, 2 * FF), struct(bf16, FF, D)] * late,
        16 * length * length * D,
        [pltpu.VMEM((length, D), bf16), pltpu.VMEM((D, D), bf16), pltpu.VMEM((D, 2 * FF), bf16), pltpu.VMEM((FF, D), bf16),
         pltpu.VMEM((rows, D), bf16)] + sem_shapes(seq - 1 + LateGather.copies(sizes) * late, 5 + 2 * late), 1,
    )(qkv, qkv, qkv, marks_column, marks_row, x, gains, wo, wi, wm, cotangent.reshape(seq, rows, D))

    if late:
        wi, wm = wholes
    reducers, early = early_reducers(sizes)
    whole = late_reducers(sizes)
    own_shard = lambda r: struct(bf16, r.rows, r.cols)
    full_shard = lambda r: pltpu.VMEM((fsdp * r.rows, r.cols) if flat(r.rows) else (fsdp, r.rows, r.cols), bf16)
    odd = (FF // fsdp) % 16 or (D // fsdp) % 16
    wide = pltpu.VMEM((FF, FF) if odd else (8, 128), f32)
    dx1, dgain_two, dq, dk, dv, block_out, *sums = call(
        functools.partial(backward_kernel, sizes, tiles), tiles + 1 + pairs,
        [tile_at(D, 0), tile_at(FF, 0), tile_at(FF, 0), whole_spec(2, D)]
        + [pair_at(n * pairs, tiles + 1, pairs) for n in range(3)]
        + [pair_at(0, tiles + 1, pairs), pair_at(0, tiles + 1, pairs)] + [ANY] * 11,
        [tile_at(D, 0), whole_spec(1, D)] + [pair_at(0, tiles + 1, pairs)] * 3 + [ANY] * (1 + len(reducers)),
        [struct(f32, length, D), struct(f32, 1, D)] + [struct(bf16, length, D)] * 3 + [slots]
        + [own_shard(r) for r in reducers],
        32 * length * length * D,
        [pltpu.VMEM((D, D), bf16), pltpu.VMEM((D, 2 * FF), bf16), pltpu.VMEM((FF, D), bf16),
         pltpu.VMEM((length, FF), bf16)] + [pltpu.VMEM((length, D), bf16)] * 3
        + [pltpu.VMEM((length, 2 * FF), bf16), pltpu.VMEM((length, D), bf16), pltpu.VMEM((length, D), bf16),
           wide, pltpu.VMEM((rows, D), bf16),
           pltpu.VMEM((2, 2, length, length), bf16)] + [pltpu.VMEM((length, PAIR), f32)] * 2
        + [full_shard(r) for r in reducers] + [pltpu.VMEM((reducers[0].rows, reducers[0].cols), bf16)]
        + [land for r, e in zip(reducers, early) for land in r.scratch(0, e)]
        + sem_shapes(seq - 1 + sum(r.copies(0, e) for r, e in zip(reducers, early)), 13 + len(reducers)), 2,
    )(x1, slope, act, gains, qkv, qkv, qkv, o, inv, probs, cosine, sine,
      wo, wi, wm, m, dy.reshape(length, D), b, o, y.reshape(seq, rows, D))

    hops = sum(len(bits_of(n)) for n in sizes)
    shard = lambda n, width: struct(bf16, n // fsdp, width)
    finals = [shard(D, 2 * FF), shard(D, D), shard(D, 3 * D)]
    operands = [dq, a, dk, dv, wq, x, dx1]
    grad_mlp, *sums = sums
    reducers, early = reducers[1:], early[1:]
    input_grad, grad_in, grad_out, grad_qkv, dgains = pl.pallas_call(
        functools.partial(leave_kernel, sizes),
        in_specs=[vmem] * 2 + [ANY] * (len(operands) + len(reducers)),
        out_specs=[ANY] * 4 + [vmem],
        out_shape=[slots] + finals + [struct(f32, 8, D)],
        scratch_shapes=[pltpu.VMEM(v.shape, v.dtype) for v in operands]
        + [pltpu.VMEM((seq, rows, D), bf16), wide]
        + [pltpu.VMEM(v.shape, v.dtype) for v in finals]
        + [pltpu.VMEM((r.rows, r.cols), bf16) for r in reducers]
        + [full_shard(r) for r in whole]
        + [land for r, e in zip(reducers, early) for land in r.scratch(e, len(r.steps))]
        + [land for r in whole for land in r.scratch(0, len(r.steps))]
        + [pltpu.VMEM((hops, 8, D), f32)]
        + sem_shapes(
            PIECES * (seq - 1) + hops + sum(r.copies(e, len(r.steps)) for r, e in zip(reducers, early))
            + sum(r.copies(0, len(r.steps)) for r in whole),
            1 + len(operands) + len(reducers) + len(finals),
        ),
        compiler_params=pltpu.CompilerParams(
            collective_id=3, has_side_effects=True, vmem_limit_bytes=VMEM_LIMIT
        ),
    )(gains, dgain_two, *operands, *sums)
    dgains = lax.dynamic_slice_in_dim(dgains, me_fsdp * (D // fsdp), D // fsdp, 1)
    return (
        block_out.reshape(tokens.shape),
        input_grad.astype(f32).reshape(tokens.shape),
        dgains[0],
        grad_qkv.astype(f32),
        grad_out.astype(f32),
        dgains[1],
        grad_in.astype(f32),
        grad_mlp.astype(f32),
    )


def solution(mesh):
    sizes = (mesh.shape["fsdp"], mesh.shape["rep"], mesh.shape["seq"])
    wide = P(None, ("rep", "fsdp"), "seq", None)
    placed = (
        wide, P(None, ("rep", "fsdp"), None), P(None, ("rep", "fsdp"), "seq"),
        P("fsdp"), P("fsdp", None), P("fsdp", None), P("fsdp"), P("fsdp", None), P("fsdp", None), wide,
    )
    return jax.shard_map(
        functools.partial(body, sizes),
        mesh=mesh,
        in_specs=placed,
        out_specs=(
            wide, wide, P("fsdp"), P("fsdp", None), P("fsdp", None), P("fsdp"), P("fsdp", None), P("fsdp", None),
        ),
        check_vma=False,
    )
```

```python
import functools
import math

import jax
import jax.numpy as jnp
from jax import lax
from jax.experimental import pallas as pl
from jax.experimental.pallas import tpu as pltpu
from jax.sharding import PartitionSpec as P

D = 768
HEADS = 12
HDIM = 64
FF = 1152
EPS = 1e-05
THETA = 160000.0
MASKED = -1000000000.0
QUERY_SCALE = HDIM**-0.5 / math.log(2.0)
TILE = 256
PAIR = 2 * HDIM
WIDE = 384
HCHUNK = 384
f32 = jnp.float32
bf16 = jnp.bfloat16
VMEM_LIMIT = 62 * 2**20


def dot_nn(left, right):
    return lax.dot_general(left, right, (((1,), (0,)), ((), ())), preferred_element_type=f32)


def dot_nt(left, right):
    return lax.dot_general(left, right, (((1,), (1,)), ((), ())), preferred_element_type=f32)


def dot_tn(left, right):
    return lax.dot_general(left, right, (((0,), (0,)), ((), ())), preferred_element_type=f32)


def normalize(values):
    mean = jnp.mean(values, axis=-1, keepdims=True)
    centered = values - mean
    var = jnp.mean(centered * centered, axis=-1, keepdims=True)
    scale = lax.rsqrt(var + EPS)
    return centered * scale, scale


def norm_back(unit, scale, gain, grad):
    gain_terms = grad * unit
    inner = grad * gain
    first = jnp.mean(inner, axis=-1, keepdims=True)
    second = jnp.mean(inner * unit, axis=-1, keepdims=True)
    return scale * (inner - first - unit * second), gain_terms


def lane_halves(shape):
    lane = lax.broadcasted_iota(jnp.int32, shape, len(shape) - 1)
    return lane % HDIM < HDIM // 2


def rotate_pair(values, cosine, signed_sine):
    swapped = jnp.where(
        lane_halves(values.shape),
        pltpu.roll(values, PAIR - HDIM // 2, 1),
        pltpu.roll(values, HDIM // 2, 1),
    )
    return values * cosine + swapped * signed_sine


def first_kernel(x_ref, gain_ref, w_ref, cos_ref, sin_ref, a_ref, qkv_ref):
    unit, _ = normalize(x_ref[...].astype(f32))
    a = (unit * gain_ref[0:1, :]).astype(bf16)
    a_ref[...] = a
    cosine, sine = cos_ref[...], sin_ref[...]
    for column in range(0, 3 * D, TILE):
        part = dot_nn(a, w_ref[:, column : column + TILE])
        for half in range(0, TILE, PAIR):
            start = column + half
            piece = part[:, half : half + PAIR]
            if start < 2 * D:
                piece = rotate_pair(piece, cosine, sine)
            if start < D:
                piece = piece * QUERY_SCALE
            qkv_ref[:, start : start + PAIR] = piece.astype(bf16)


def head_lanes():
    lane = lax.broadcasted_iota(jnp.int32, (1, PAIR), 1)
    return [lane < HDIM, lane >= HDIM]


def attend_pair(q_ref, k_ref, v_ref, rows_ref, cols_ref, p_ref, inv_ref, write):
    k, v = k_ref[...], v_ref[...]
    length = k.shape[0]
    mine = head_lanes()
    zero, one = jnp.zeros((), bf16), jnp.ones((), bf16)
    summing = [jnp.where(m, v, one) for m in mine]
    items = [(tile, head) for tile in range(0, length, TILE) for head in range(2)]

    def score(item):
        tile, head = item
        return dot_nt(jnp.where(mine[head], q_ref[tile : tile + TILE, :], zero), k)

    ahead = score(items[0])
    kept = None
    for i, (tile, head) in enumerate(items):
        rows = slice(tile, tile + TILE)
        scores = ahead
        if i + 1 < len(items):
            ahead = score(items[i + 1])
        scores = jnp.where(rows_ref[rows, :] == cols_ref[...], scores, MASKED)
        probs = jnp.exp2(scores - jnp.max(scores, axis=-1, keepdims=True)).astype(bf16)
        p_ref[head, rows, :] = probs
        part = dot_nn(probs, summing[head])
        inv = 1.0 / pltpu.roll(part, HDIM, 1)
        if head == 0:
            kept = (part * inv, inv)
        else:
            inv_ref[rows, :] = jnp.where(mine[0], kept[1], inv)
            write(rows, jnp.where(mine[0], kept[0], part * inv).astype(bf16))


def forward_kernel(
    sizes, pairs, late, q_ref, k_ref, v_ref, rows_ref, cols_ref, x_ref, gain_ref, w_out_any, w_in_any, w_mlp_any, cot_ref,
    o_ref, p_ref, inv_ref, x1_ref, b_ref, m_ref, slope_ref, act_ref, y_ref, dy_ref, *refs,
):
    seq = sizes[2]
    refs = list(refs)
    outs = [refs.pop(0) for _ in range(2 * late)]
    joined, w_out_ref, w_in_ref, w_mlp_ref, bounce, *sem_refs = refs
    step, last = pl.program_id(0), pl.num_programs(0) - 1
    sems = Sems(*sem_refs)
    me_seq = lax.axis_index("seq")
    into = sems.copy(cot_ref.at[me_seq], bounce)
    outof = sems.copy(bounce, dy_ref.at[0])
    weights = [sems.copy(w_out_any, w_out_ref)]
    partners = [("seq", k) for k in range(1, seq)]
    if late:
        gather = LateGather(sizes, [w_in_any, w_mlp_any], [w_in_ref, w_mlp_ref], sems)
        weights += gather.own
        keeps = [sems.copy(w_in_ref, outs[0]), sems.copy(w_mlp_ref, outs[1])]
        partners = all_partners(sizes)
    else:
        weights += [sems.copy(w_in_any, w_in_ref), sems.copy(w_mlp_any, w_mlp_ref)]
    blocks = [sems.remote(cot_ref.at[flip(me_seq, k)], dy_ref.at[k], "seq", k) for k in range(1, seq)]

    @pl.when(step == 0)
    def _():
        into.start()
        start_all(weights)
        meet(partners)
        if late:
            start_all(gather.far)
        start_all(blocks)
        into.wait()
        outof.start()

    if late:
        for when in range(1, pairs + 1):
            @pl.when(step == when)
            def _(when=when):
                gather.advance(when)

    @pl.when(step < pairs)
    def _():
        def write(rows, value):
            o_ref[rows, :] = value
            joined[rows, pl.ds(pl.multiple_of(step * PAIR, PAIR), PAIR)] = value

        attend_pair(q_ref, k_ref, v_ref, rows_ref, cols_ref, p_ref, inv_ref, write)

    @pl.when(step == pairs)
    def _():
        if late:
            wait_all(weights[:1])
            gather.finish(0)
            keeps[0].start()
        else:
            wait_all(weights)

    @pl.when(step >= pairs)
    def _():
        start = pl.multiple_of((step - pairs) * TILE, TILE)
        x1 = x_ref[...].astype(f32) + dot_nn(joined[pl.ds(start, TILE), :], w_out_ref[...])
        x1_ref[...] = x1
        unit, _ = normalize(x1)
        b = (unit * gain_ref[1:2, :]).astype(bf16)
        b_ref[...] = b

        def hidden(column):
            return (
                dot_nn(b, w_in_ref[:, column : column + HCHUNK]),
                dot_nn(b, w_in_ref[:, FF + column : FF + column + HCHUNK]),
            )

        ahead = hidden(0)
        for column in range(0, FF, HCHUNK):
            hin, gate = ahead
            if column + HCHUNK < FF:
                ahead = hidden(column + HCHUNK)
            phi = 0.5 + 0.5 * lax.erf(hin * math.sqrt(0.5))
            act = hin * phi
            slope = phi + hin * (jnp.exp(hin * hin * -0.5) * (1.0 / math.sqrt(2.0 * math.pi)))
            m_ref[:, column : column + HCHUNK] = (act * gate).astype(bf16)
            act_ref[:, column : column + HCHUNK] = act.astype(bf16)
            slope_ref[:, column : column + HCHUNK] = (slope * gate).astype(bf16)
        if late:
            @pl.when(step == pairs)
            def _():
                gather.finish(1)
                keeps[1].start()

        y_ref[...] = (x1_ref[...] + dot_nn(m_ref[...], w_mlp_ref[...])).astype(bf16)

    @pl.when(step == last)
    def _():
        if late:
            wait_all(keeps)
        outof.wait()
        wait_all(blocks)


def order_of(sizes, rep_first):
    fsdp, rep, seq = sizes
    core = [("fsdp", 1)]
    rest = [("fsdp", b) for b in bits_of(fsdp)[1:]]
    copies = [("rep", b) for b in bits_of(rep)]
    return core + (copies + rest if rep_first else rest + copies) + [("seq", b) for b in bits_of(seq)]


def all_partners(sizes):
    fsdp, rep, seq = sizes
    return [("seq", k) for k in range(1, seq)] + [("fsdp", b) for b in bits_of(fsdp)] + [("rep", b) for b in bits_of(rep)]


def early_reducers(sizes):
    fsdp, rep, seq = sizes
    shapes = [(fsdp, FF // fsdp, D), (fsdp, D // fsdp, FF), (fsdp, D // fsdp, FF), (fsdp, D // fsdp, D)]
    reducers = [Reducer(shape, sizes, order_of(sizes, w == 2)) for w, shape in enumerate(shapes)]
    across = len(bits_of(fsdp)) + len(bits_of(rep))
    return reducers, [len(reducers[0].steps)] + [across + 2] * 2 + [across + 1]


def late_reducers(sizes):
    fsdp = sizes[0]
    return [Reducer((fsdp, D // fsdp, D), sizes, order_of(sizes, w == 1)) for w in range(3)]


def flat(rows):
    return rows % 16 == 0


def shard_of(ref, rows, q):
    return ref.at[pl.ds(pl.multiple_of(q * rows, 16), rows)] if flat(rows) else ref.at[q]


def weight_gradient(ref, wide, left, right):
    if len(ref.shape) == 2:
        @pl.loop(0, ref.shape[0] // HCHUNK)
        def _(i):
            at = pl.ds(pl.multiple_of(i * HCHUNK, HCHUNK), HCHUNK)
            ref[at, :] = dot_tn(left[:, at], right[...]).astype(bf16)
    else:
        shards, rows, cols = ref.shape
        wide[: shards * rows, :cols] = dot_tn(left[...], right[...])
        for q in range(shards):
            ref[q] = wide[q * rows : (q + 1) * rows, :cols].astype(bf16)


def middle_back_tile(dy, x1_ref, slope_ref, act_ref, gain_ref, w_out_ref, w_in_ref, w_mlp_ref, dh_ref, dgain_ref, dx1_ref):
    ahead = dot_nt(dy, w_mlp_ref[:HCHUNK, :])
    for column in range(0, FF, HCHUNK):
        dm = ahead
        if column + HCHUNK < FF:
            ahead = dot_nt(dy, w_mlp_ref[column + HCHUNK : column + 2 * HCHUNK, :])
        dh_ref[:, column : column + HCHUNK] = (dm * slope_ref[:, column : column + HCHUNK].astype(f32)).astype(bf16)
        dh_ref[:, FF + column : FF + column + HCHUNK] = (
            dm * act_ref[:, column : column + HCHUNK].astype(f32)
        ).astype(bf16)
    db = dot_nt(dh_ref[...], w_in_ref[...])
    unit, scale = normalize(x1_ref[...])
    back, terms = norm_back(unit, scale, gain_ref[1:2, :], db)
    dgain_ref[...] += jnp.sum(terms, axis=0, keepdims=True)
    dx1 = dy.astype(f32) + back
    dx1_ref[...] = dx1
    return dx1.astype(bf16)


def attend_back_pair(q_ref, k_ref, v_ref, o_ref, inv_ref, do, p_ref, cos_ref, sin_ref, dq_ref, dk_ref, dv_ref):
    v = v_ref[...]
    length = v.shape[0]
    mine = head_lanes()
    zero = jnp.zeros((), bf16)
    do = (do.astype(f32) * inv_ref[...]).astype(bf16)
    inner = do.astype(f32) * o_ref[...].astype(f32)
    do_heads = [jnp.where(m, do, zero) for m in mine]
    q_heads = [jnp.where(m, q_ref[...], zero).T for m in mine]
    k_heads = [jnp.where(m, k_ref[...], zero) for m in mine]
    do_turned = [d.T for d in do_heads]
    cosine, sine = cos_ref[...], sin_ref[...]
    dv = dk = None
    for tile in range(0, length, TILE):
        rows = slice(tile, tile + TILE)
        dq = None
        for head in range(2):
            probs = p_ref[head, rows, :]
            delta = jnp.sum(jnp.where(mine[head], inner[rows], 0.0), axis=-1, keepdims=True)
            dp = dot_nt(do_heads[head][rows], v)
            ds = (probs.astype(f32) * (dp - delta)).astype(bf16)
            value_part = dot_nn(do_turned[head][:, rows], probs)
            key_part = dot_nn(q_heads[head][:, rows], ds)
            query_part = dot_nn(ds, k_heads[head])
            dv = value_part if dv is None else dv + value_part
            dk = key_part if dk is None else dk + key_part
            dq = query_part if dq is None else dq + query_part
        dq_ref[rows, :] = rotate_pair(dq * HDIM**-0.5, cosine[rows], -sine[rows]).astype(bf16)
    dk_ref[...] = rotate_pair(dk.T * math.log(2.0), cosine, -sine).astype(bf16)
    dv_ref[...] = dv.T.astype(bf16)


def backward_kernel(
    sizes, tiles, x1_ref, slope_ref, act_ref, gain_ref, q_ref, k_ref, v_ref, o_ref, inv_ref,
    p_any, cos_any, sin_any, w_out_any, w_in_any, w_mlp_any, m_any, dy_any, b_any, o_any, y_ref, *refs,
):
    reducers, early = early_reducers(sizes)
    count = len(reducers)
    refs = list(refs)
    pop = lambda n: [refs.pop(0) for _ in range(n)]
    dx1_ref, dgain_ref, dq_ref, dk_ref, dv_ref, home_ref = pop(6)
    sums_out = pop(count)
    w_out_ref, w_in_ref, w_mlp_ref, m_ref, dy_ref, b_ref, all_o_ref = pop(7)
    dh_ref, low_ref, do_ref, wide, bounce, probs_ref, cos_ref, sin_ref = pop(8)
    grads = pop(count)
    (mlp_final,) = pop(1)
    lands = [pop(len(r.scratch(0, e))) for r, e in zip(reducers, early)]
    sems = Sems(*refs)
    me = lax.axis_index("fsdp")
    step, last = pl.program_id(0), pl.num_programs(0) - 1
    into, outof, blocks = give_back(y_ref, home_ref, bounce, sems)
    loads = [
        sems.copy(src, dst)
        for src, dst in [
            (m_any, m_ref), (dy_any, dy_ref), (w_mlp_any, w_mlp_ref), (w_in_any, w_in_ref), (w_out_any, w_out_ref),
            (b_any, b_ref), (o_any, all_o_ref), (cos_any, cos_ref), (sin_any, sin_ref),
        ]
    ]
    pair, pairs = step - tiles - 1, last - tiles
    slot_sems = [sems.local.at[sems.local_used + i] for i in range(2)]
    sems.local_used += 2

    def fetch(which, slot):
        return pltpu.make_async_copy(p_any.at[pl.ds(which * 2, 2)], probs_ref.at[slot], slot_sems[slot])
    stores = [sems.copy(mlp_final if w == 0 else shard_of(grads[w], reducers[w].rows, me), sums_out[w]) for w in range(count)]
    for w, reducer in enumerate(reducers):
        reducer.bind(lambda j, w=w: shard_of(grads[w], reducers[w].rows, flip(me, j)), lands[w], sems, 0, early[w], mlp_final if w == 0 else None)
    mlp, first_half, second_half, out = reducers

    def at(when, *actions):
        @pl.when(step == when)
        def _():
            for action in actions:
                action()

    def advance(reducer, s, limit):
        def run():
            reducer.finish(s)
            if s + 1 < limit:
                reducer.start(s + 1)
        return run

    @pl.when(step == 0)
    def _():
        start_all(loads)
        into.start()
        meet(all_partners(sizes))
        start_all(blocks)
        dgain_ref[...] = jnp.zeros_like(dgain_ref)
        wait_all(loads[:2])
        weight_gradient(grads[0], wide, m_ref, dy_ref)
        mlp.start(0)
        into.wait()
        outof.start()
        wait_all(loads[2:5])

    at(1, advance(mlp, 0, early[0]))

    @pl.when(step < tiles)
    def _():
        rows = pl.ds(pl.multiple_of(step * TILE, TILE), TILE)
        low = middle_back_tile(
            dy_ref[rows, :], x1_ref, slope_ref, act_ref, gain_ref, w_out_ref, w_in_ref, w_mlp_ref,
            dh_ref.at[rows, :], dgain_ref, dx1_ref,
        )
        low_ref[rows, :] = low
        do_ref[rows, :] = dot_nt(low, w_out_ref[...]).astype(bf16)

    across = len(bits_of(sizes[0])) + len(bits_of(sizes[1]))

    @pl.when(step == tiles)
    def _():
        wait_all(loads[5:])
        weight_gradient(grads[1], wide, b_ref, dh_ref.at[:, :FF])
        first_half.start(0)
        weight_gradient(grads[2], wide, b_ref, dh_ref.at[:, FF:])
        second_half.start(0)
        for s in range(1, across - 1):
            advance(mlp, s, early[0])()
        weight_gradient(grads[3], wide, all_o_ref, low_ref)
        out.start(0)

    @pl.when(step == tiles - 1)
    def _():
        fetch(0, 0).start()

    for slot in range(2):
        @pl.when((step > tiles) & (pair % 2 == slot))
        def _(slot=slot):
            fetch(pair, slot).wait()

            @pl.when(pair + 1 < pairs)
            def _():
                fetch(pair + 1, 1 - slot).start()

    halves = (first_half, second_half)
    steps = lambda reducer, limit, *which: [advance(reducer, s, limit) for s in which]
    half_steps = lambda *which: [advance(r, s, early[1]) for s in which for r in halves]
    middle = range(1, across - 1)
    at(tiles + 1, *steps(mlp, early[0], across - 1), *half_steps(0))
    at(tiles + 2, *steps(out, early[3], 0))
    at(tiles + 3, *half_steps(*middle))
    at(tiles + 4, *steps(mlp, early[0], across), *steps(out, early[3], *middle))
    at(tiles + 5, *steps(mlp, early[0], across + 1), *half_steps(across - 1))
    at(tiles + 6, *steps(mlp, early[0], *range(across + 2, early[0] - 1)), *half_steps(across), *steps(out, early[3], across - 1))

    @pl.when(step > tiles)
    def _():
        column = pl.multiple_of(pair * PAIR, PAIR)
        attend_back_pair(
            q_ref, k_ref, v_ref, o_ref, inv_ref, do_ref[:, pl.ds(column, PAIR)], probs_ref.at[pair % 2], cos_ref, sin_ref,
            dq_ref, dk_ref, dv_ref,
        )

    @pl.when(step == last)
    def _():
        for w, reducer in enumerate(reducers):
            reducer.finish(early[w] - 1)
            stores[w].start()
        wait_all(stores)
        outof.wait()
        wait_all(blocks)


PIECES = 4


def leave_kernel(sizes, gain_ref, other_gain_ref, *refs):
    fsdp, rep, seq = sizes
    reducers, early = (some[1:] for some in early_reducers(sizes))
    whole = late_reducers(sizes)
    count, more = len(reducers), len(whole)
    refs = list(refs)
    pop = lambda n: [refs.pop(0) for _ in range(n)]
    anys = pop(7)
    sums_in = pop(count)
    (home_ref,) = pop(1)
    in_out, out_out, qkv_out, gains_out = pop(4)
    dq_ref, a_ref, dk_ref, dv_ref, w_ref, x_ref, dx1_ref = local = pop(7)
    slots, wide, in_final, out_final, qkv_final = pop(5)
    held, grads = pop(count), pop(more)
    lands = [pop(len(r.scratch(e, len(r.steps)))) for r, e in zip(reducers, early)]
    whole_lands = [pop(len(r.scratch(0, len(r.steps)))) for r in whole]
    (gain_lands,) = pop(1)
    sems = Sems(*refs)
    me, me_seq = lax.axis_index("fsdp"), lax.axis_index("seq")
    own = sems.copy(slots.at[0], home_ref.at[me_seq])
    height = slots.shape[1] // PIECES
    blocks = {
        k: [
            sems.remote(slots.at[k, pl.ds(n * height, height)], home_ref.at[me_seq, pl.ds(n * height, height)], "seq", k)
            for n in range(PIECES)
        ]
        for k in range(1, seq)
    }
    order = sorted(range(1, seq), key=lambda k: (k != 2, k == 1))
    ready = []

    def send_piece(n=1):
        for _ in range(n):
            if ready:
                ready.pop(0).start()

    operands = [sems.copy(src, dst) for src, dst in zip(anys, local)]
    loads = [sems.copy(sums_in[w], held[w]) for w in range(count)]
    stores = [
        sems.copy(src, dst)
        for src, dst in ((in_final, in_out), (out_final, out_out), (qkv_final, qkv_out))
    ]
    finals = [in_final.at[:, pl.ds(0, FF)], in_final.at[:, pl.ds(FF, FF)], out_final]
    for w, reducer in enumerate(reducers):
        reducer.bind(lambda j, w=w: held[w], lands[w], sems, early[w], len(reducer.steps), finals[w])
    for w, reducer in enumerate(whole):
        reducer.bind(
            lambda j, w=w: shard_of(grads[w], whole[w].rows, flip(me, j)), whole_lands[w], sems, 0, len(reducer.steps),
            qkv_final.at[:, pl.ds(w * D, D)],
        )
    hops = [("fsdp", b) for b in bits_of(fsdp)] + [("rep", b) for b in bits_of(rep)] + [("seq", b) for b in bits_of(seq)]
    gain_moves = [sems.remote(gains_out, gain_lands.at[i], axis, bit) for i, (axis, bit) in enumerate(hops)]
    rows = slots.shape[1]

    def advance(some, s):
        for reducer in some:
            if s < len(reducer.steps):
                reducer.finish(s)
                if s + 1 < len(reducer.steps):
                    reducer.start(s + 1)

    def advance_gains(i):
        if i < len(hops):
            gain_moves[i].wait()
            gains_out[...] += gain_lands[i]
            if i + 1 < len(hops):
                gain_moves[i + 1].start()

    def input_slot(k):
        piece = slice(k * rows, (k + 1) * rows)
        da = dot_nt(dq_ref[piece, :], w_ref[:, :D])
        da = da + dot_nt(dk_ref[piece, :], w_ref[:, D : 2 * D])
        da = da + dot_nt(dv_ref[piece, :], w_ref[:, 2 * D :])
        unit, scale = normalize(x_ref[piece, :].astype(f32))
        back, terms = norm_back(unit, scale, gain_ref[0:1, :], da)
        gains_out[0:1, :] += jnp.sum(terms, axis=0, keepdims=True)
        slots[k] = (dx1_ref[piece, :] + back).astype(bf16)
        if k:
            ready.extend(blocks[k])

    def gradient(w, part):
        weight_gradient(grads[w], wide, a_ref, part)
        whole[w].start(0)

    across = len(bits_of(fsdp)) + len(bits_of(rep))
    halves, out, last = reducers[:2], reducers[2:], len(whole[0].steps)
    start_all(operands[:2])
    start_all(loads)
    start_all(operands[2:])
    gains_out[...] = jnp.zeros_like(gains_out)
    gains_out[1:2, :] = other_gain_ref[...]
    meet(all_partners(sizes))
    wait_all(loads)
    for w, (reducer, s) in enumerate(zip(reducers, early)):
        if s < len(reducer.steps):
            reducer.start(s)
        else:
            finals[w][...] = held[w][...]
    wait_all(operands[:2])
    gradient(0, dq_ref)
    wait_all(operands[2:])
    input_slot(order[0])
    send_piece(PIECES // 2)
    advance(whole[:1], 0)
    advance(halves, early[0])
    gradient(1, dk_ref)
    for k in order[1:2]:
        input_slot(k)
    advance(whole[1:2], 0)
    advance(out, early[2])
    send_piece()
    gradient(2, dv_ref)
    for k in order[2:]:
        input_slot(k)
    advance(whole[:1], 1)
    advance(whole[2:], 0)
    send_piece()
    input_slot(0)
    own.start()
    gain_moves[0].start()
    advance(whole[1:2], 1)
    advance(out, early[2] + 1)
    send_piece()
    hop = 0
    for s in range(2, across):
        advance(whole[:1], s)
        advance_gains(hop)
        advance(whole[2:], s - 1)
        advance(whole[1:2], s)
        send_piece()
        hop += 1
    advance(whole[2:], across - 1)
    advance_gains(hop)
    send_piece()
    for s in range(across, last):
        for reducer in whole:
            advance([reducer], s)
            send_piece()
        hop += 1
        advance_gains(hop)
    for i in range(hop + 1, len(hops)):
        advance_gains(i)
    send_piece(len(ready))
    for s in range(early[0] + 1, len(halves[0].steps)):
        advance(halves, s)
    for s in range(early[2] + 2, len(out[0].steps)):
        advance(out, s)
    start_all(stores)
    wait_all(stores)
    own.wait()
    for k in range(1, seq):
        wait_all(blocks[k])


def widen_kernel(count, *refs):
    anys, outs, narrow = refs[:count], refs[count : 2 * count], refs[2 * count : 3 * count]
    wide, sems = refs[3 * count : -1], refs[-1]
    loads = [pltpu.make_async_copy(anys[i], narrow[i], sems.at[i]) for i in range(count)]
    start_all(loads)
    stores = []
    for i in range(count):
        loads[i].wait()
        wide[i][...] = narrow[i][...].astype(wide[i].dtype)
        stores.append(pltpu.make_async_copy(wide[i], outs[i], sems.at[count + i]))
        stores[-1].start()
    wait_all(stores)


def widen(arrays, dtypes):
    count = len(arrays)
    return pl.pallas_call(
        functools.partial(widen_kernel, count),
        in_specs=[ANY] * count,
        out_specs=[ANY] * count,
        out_shape=[struct(t, *v.shape) for v, t in zip(arrays, dtypes)],
        scratch_shapes=[pltpu.VMEM(v.shape, v.dtype) for v in arrays]
        + [pltpu.VMEM(v.shape, t) for v, t in zip(arrays, dtypes)]
        + [pltpu.SemaphoreType.DMA((2 * count,))],
        compiler_params=pltpu.CompilerParams(vmem_limit_bytes=VMEM_LIMIT),
    )(*arrays)


def rows_spec(width):
    return pl.BlockSpec((TILE, width), lambda i: (i, 0))


def whole_spec(*shape):
    return pl.BlockSpec(shape, lambda i: (0,) * len(shape))


def pair_spec(length, offset=0):
    return pl.BlockSpec((length, PAIR), lambda i: (0, i + offset))


def struct(dtype, *shape):
    return jax.ShapeDtypeStruct(shape, dtype)


def call(kernel, grid, in_specs, out_specs, out_shape, flops, scratch=(), collective=None):
    return pl.pallas_call(
        kernel,
        grid=(grid,),
        in_specs=in_specs,
        out_specs=out_specs,
        out_shape=out_shape,
        scratch_shapes=list(scratch),
        compiler_params=pltpu.CompilerParams(
            dimension_semantics=("arbitrary",), vmem_limit_bytes=VMEM_LIMIT,
            collective_id=collective, has_side_effects=collective is not None,
        ),
        cost_estimate=pl.CostEstimate(flops=flops, bytes_accessed=10 * 2**20, transcendentals=0),
    )


MESH = pl.DeviceIdType.MESH
ANY = pl.BlockSpec(memory_space=pl.ANY)


def take(array, index):
    return lax.dynamic_index_in_dim(array, index, 0, keepdims=False)


def flip(index, mask):
    bit = 1
    while bit <= mask:
        if mask & bit:
            index = index + bit - 2 * bit * ((index // bit) % 2)
        bit *= 2
    return index


def flip_by(index, mask, size):
    total = 0
    for bit in bits_of(size):
        ours, theirs = (index // bit) % 2, (mask // bit) % 2
        total = total + bit * (ours + theirs - 2 * ours * theirs)
    return total


def bits_of(size):
    return [1 << i for i in range(size.bit_length() - 1)]


def meet(partners):
    barrier = pltpu.get_barrier_semaphore()
    for axis, mask in partners:
        pl.semaphore_signal(
            barrier, inc=1, device_id={axis: flip(lax.axis_index(axis), mask)}, device_id_type=MESH
        )
    pl.semaphore_wait(barrier, len(partners))


class Sems:
    def __init__(self, send, recv, local):
        self.send, self.recv, self.local = send, recv, local
        self.remote_used = self.local_used = 0

    def remote(self, src, dst, axis, mask):
        i = self.remote_used
        self.remote_used += 1
        return pltpu.make_async_remote_copy(
            src_ref=src, dst_ref=dst, send_sem=self.send.at[i], recv_sem=self.recv.at[i],
            device_id={axis: flip(lax.axis_index(axis), mask)}, device_id_type=MESH,
        )

    def copy(self, src, dst):
        i = self.local_used
        self.local_used += 1
        return pltpu.make_async_copy(src, dst, self.local.at[i])


def sem_shapes(remote, local):
    dma = pltpu.SemaphoreType.DMA
    return [dma((remote,)), dma((remote,)), dma((max(local, 1),))]


def start_all(copies):
    for copy in copies:
        copy.start()


def wait_all(copies):
    for copy in copies:
        copy.wait()


class Gather:
    def __init__(self, sizes, shards, place, sems, order):
        self.sizes, self.shards, self.place, self.sems = sizes, shards, place, sems
        self.pieces = order
        self.me, self.me_rep = lax.axis_index("fsdp"), lax.axis_index("rep")
        self.pending = []

    def part(self, ref, pieces, n):
        width = ref.shape[-1] // (self.sizes[1] * pieces)
        start = (self.me_rep * pieces + n) * width
        return ref.at[:, pl.ds(pl.multiple_of(start, 128), width)]

    def source(self, w, h):
        return self.shards[w] if h == 0 else self.place(w, flip(self.me, h))

    def start(self):
        self.held = [0]
        self.over = self.cross(self.far_bits()[0]) if self.far_bits() else []

    def far_bits(self):
        return list(reversed(bits_of(self.sizes[0])[1:]))

    def cross(self, bit):
        over = []
        for w, pieces, n in self.pieces:
            moved = [
                self.sems.remote(
                    self.part(self.source(w, h), pieces, n),
                    self.part(self.place(w, flip(self.me, h)), pieces, n), "fsdp", bit,
                )
                for h in self.held
            ]
            start_all(moved)
            over.append(moved)
        return over

    def pass_on(self, i, bit):
        w, pieces, n = self.pieces[i]
        for copy in self.over[i]:
            copy.wait_recv()
        self.pending += self.over[i]
        passed = []
        for mask in range(1, self.sizes[1]):
            for h in self.held:
                here = self.part(self.place(w, flip(self.me, h ^ bit)), pieces, n)
                passed.append(self.sems.remote(here, here, "rep", mask))
        start_all(passed)
        self.pending += passed
        return passed

    def events(self, lag=2):
        bits = self.far_bits()
        count = len(self.pieces)
        for bit in bits[:-1]:
            passed = [self.pass_on(i, bit) for i in range(count)]
            self.held = self.held + [h ^ bit for h in self.held]
            for copies in passed:
                for copy in copies:
                    copy.wait_recv()
            self.over = self.cross(bits[bits.index(bit) + 1])
        end = {w: i for i, (w, _, _) in enumerate(self.pieces)}
        passed, near_held = [], self.held + [h ^ bit for bit in bits[-1:] for h in self.held]
        for i in range(count + lag):
            if i < count:
                if bits:
                    passed.append(self.pass_on(i, bits[-1]))
                yield None
            for w, last in end.items():
                if last == i - lag:
                    if bits:
                        for j, (other, _, _) in enumerate(self.pieces):
                            if other == w:
                                for copy in passed[j]:
                                    copy.wait_recv()
                    yield w, self.near(w, near_held)

    def near(self, w, held):
        copies = [self.sems.remote(self.source(w, h), self.place(w, flip(self.me, h)), "fsdp", 1) for h in held]
        start_all(copies)
        return copies

    @staticmethod
    def count(sizes, order, weights):
        held, copies = 1, 0
        for _ in bits_of(sizes[0])[1:]:
            copies += len(order) * held * sizes[1]
            held *= 2
        return copies + weights * held


PASSED = (0, 1, 2, 4, 6, 6, 6)
CROSSED = (4, 5)


class LateGather:
    def __init__(self, sizes, shards, wholes, sems):
        fsdp, rep, _ = sizes
        me, me_rep = lax.axis_index("fsdp"), lax.axis_index("rep")
        place = lambda w, q: shard_of(wholes[w], shards[w].shape[0], q)
        self.own = [sems.copy(shards[w], place(w, me)) for w in range(2)]
        self.far, self.passed, self.near = [], [], [[], []]
        for w in range(2):
            fits = shards[w].shape[-1] % (rep * 3 * 128) == 0
            pieces = 3 if fits else 1
            width = shards[w].shape[-1] // (rep * pieces)
            for n in range(pieces if fsdp > 2 else 0):
                cols = pl.ds(pl.multiple_of((me_rep * pieces + n) * width, 128), width)
                self.far.append(sems.remote(shards[w].at[:, cols], place(w, me).at[:, cols], "fsdp", 2))
                here = place(w, flip(me, 2)).at[:, cols]
                self.passed.append([sems.remote(here, here, "rep", mask) for mask in range(1, rep)])
            for h in range(0, fsdp, 2):
                src = shards[w] if h == 0 else place(w, flip(me, h))
                self.near[w].append(sems.remote(src, place(w, flip(me, h)), "fsdp", 1))
        self.pieces = len(self.far) // 2
        self.count = len(self.far)

    @staticmethod
    def copies(sizes):
        return 2 * (3 * sizes[1] + sizes[0] // 2)

    def pass_on(self, i):
        self.far[i].wait_recv()
        start_all(self.passed[i])

    def cross_core(self, w):
        for copies in self.passed[w * self.pieces : (w + 1) * self.pieces]:
            for copy in copies:
                copy.wait_recv()
        start_all(self.near[w])

    def advance(self, step):
        upto = lambda n: min(n, self.count)
        for i in range(upto(PASSED[step - 1]), upto(PASSED[step])):
            self.pass_on(i)
        for w in range(2):
            if step == CROSSED[w]:
                self.cross_core(w)

    def finish(self, w):
        wait_all(self.own[w : w + 1])
        for i in range(w * self.pieces, (w + 1) * self.pieces):
            self.far[i].wait_send()
            for copy in self.passed[i]:
                copy.wait_send()
        wait_all(self.near[w])


def gather_order(sizes, shards):
    fits = lambda w, n: shards[w].shape[-1] % (sizes[1] * n * 128) == 0
    split = lambda w, n: n if fits(w, n) else 1
    order = []
    for w, n in ((0, 1), (1, 3), (2, 3), (4, 3), (3, 3)):
        if w >= len(shards):
            continue
        n = split(w, n)
        order += [(w, n, i) for i in range(n)]
    return order


def enter_kernel(sizes, count, tokens, *refs):
    fsdp, rep, seq = sizes
    refs = list(refs)
    pop = lambda n: [refs.pop(0) for _ in range(n)]
    shards = pop(count)
    (x_out,) = pop(1)
    fulls = pop(count)
    (bounce_x,) = pop(1)
    bounces = pop(count)
    sems = Sems(*refs)
    me, me_seq = lax.axis_index("fsdp"), lax.axis_index("seq")
    into = [sems.copy(tokens.at[me_seq], bounce_x)] + [sems.copy(shards[w], bounces[w]) for w in range(count)]
    outof = [sems.copy(bounce_x, x_out.at[0])] + [sems.copy(bounces[w], fulls[w].at[me]) for w in range(count)]
    gather = Gather(sizes, shards, lambda w, q: fulls[w].at[q], sems, gather_order(sizes, shards))
    start_all(into)
    meet(all_partners(sizes))
    blocks = [sems.remote(tokens.at[flip(me_seq, k)], x_out.at[k], "seq", k) for k in range(1, seq)]
    start_all(blocks)
    gather.start()
    last = []
    for event in gather.events():
        if event:
            last += event[1]
    wait_all(into)
    start_all(outof)
    for copy in gather.pending:
        copy.wait_send()
    wait_all(last)
    wait_all(blocks)
    wait_all(outof)


def enter(sizes, tokens, shards):
    fsdp = sizes[0]
    count = len(shards)
    hbm = lambda shape: struct(bf16, *shape)
    copies = sizes[2] - 1 + Gather.count(sizes, gather_order(sizes, shards), count)
    return pl.pallas_call(
        functools.partial(enter_kernel, sizes, count),
        in_specs=[ANY] * (1 + count),
        out_specs=[ANY] * (1 + count),
        out_shape=[hbm(tokens.shape)] + [hbm((fsdp,) + s.shape) for s in shards],
        scratch_shapes=[pltpu.VMEM(tokens.shape[1:], bf16)]
        + [pltpu.VMEM(s.shape, bf16) for s in shards]
        + sem_shapes(copies, 2 * (1 + count)),
        compiler_params=pltpu.CompilerParams(collective_id=0, has_side_effects=True),
    )(tokens, *shards)


def turn(row):
    n = row.shape[1]
    diagonal = lax.broadcasted_iota(jnp.int32, (n, n), 0) == lax.broadcasted_iota(jnp.int32, (n, n), 1)
    return jnp.sum(jnp.where(diagonal, row, 0), axis=1, keepdims=True)


def enter_project_kernel(sizes, count, tokens, segments, *refs):
    fsdp, rep, seq = sizes
    refs = list(refs)
    pop = lambda n: [refs.pop(0) for _ in range(n)]
    shards = pop(count)
    x_out, a_out, qkv_out, cos_out, sin_out, marks_out, row_out, gains_out, wq_out = pop(9)
    fulls = [None, None] + pop(count - 2)
    xs, a, qkv, wq, gains = pop(5)
    bounces = pop(count)
    sems = Sems(*refs)
    me, me_seq = lax.axis_index("fsdp"), lax.axis_index("seq")
    shard_rows, rows = shards[1].shape[0], xs.shape[1]
    columns = wq.shape[1]

    def place(w, q):
        if w == 0:
            return gains.at[q]
        if w == 1:
            return wq.at[pl.ds(pl.multiple_of(q * shard_rows, 16), shard_rows)]
        return fulls[w].at[q]

    own = sems.copy(tokens.at[me_seq], xs.at[0])
    into = [sems.copy(shards[w], place(w, me) if w < 2 else bounces[w - 2]) for w in range(count)]
    outof = [sems.copy(bounces[w - 2], place(w, me)) for w in range(2, count)]
    blocks = [sems.remote(tokens.at[flip(me_seq, k)], xs.at[k], "seq", k) for k in range(1, seq)]
    stores = [
        [sems.copy(src.at[k], dst.at[k]) for src, dst in ((xs, x_out), (a, a_out), (qkv, qkv_out))] for k in range(seq)
    ]
    keep = sems.copy(wq, wq_out)
    gather = Gather(sizes, shards, place, sems, gather_order(sizes, shards))
    own.start()
    start_all(into)
    meet(all_partners(sizes))
    gather.start()
    start_all(blocks)

    lane = lax.broadcasted_iota(jnp.int32, (1, PAIR), 1)
    rate = jnp.exp((lane % (HDIM // 2)).astype(f32) * (-2.0 * math.log(THETA) / HDIM))
    sign = jnp.where(lane_halves((1, PAIR)), -1.0, 1.0)
    batch = segments.shape[1]

    def own_segments(block):
        at = pl.multiple_of(block * rows, 128)
        return segments[me_seq // batch, pl.ds(me_seq % batch, 1), pl.ds(at, rows)]

    @pl.loop(0, seq)
    def _(k):
        block = flip_by(me_seq, k, seq)
        piece = pl.ds(pl.multiple_of(k * rows, 128), rows)
        row = own_segments(block)
        column = turn(row)
        earlier = jnp.zeros((rows, 1), jnp.int32)
        for other in range(seq):
            earlier += jnp.sum((own_segments(other) < column).astype(jnp.int32), axis=1, keepdims=True)
        index = block * rows + lax.broadcasted_iota(jnp.int32, (rows, 1), 0)
        angles = (index - earlier).astype(f32) * rate
        cos_out[piece, :] = jnp.cos(angles)
        sin_out[piece, :] = jnp.sin(angles) * sign
        marks_out[piece, :] = column
        row_out[:, piece] = row

    def project(k):
        if k == 0:
            own.wait()
        else:
            blocks[k - 1].wait()
        piece = slice(k * rows, (k + 1) * rows)
        unit, _ = normalize(xs[k].astype(f32))
        low = (unit * gains_out[0:1, :]).astype(bf16)
        a[k] = low
        cosine, sine = cos_out[piece, :], sin_out[piece, :]

        @pl.loop(0, 2 * D // WIDE)
        def _(i):
            at = pl.multiple_of(i * WIDE, WIDE)
            part = dot_nn(low, wq[:, pl.ds(at, WIDE)])
            scale = jnp.where(at < D, QUERY_SCALE, 1.0)
            for half in range(0, WIDE, PAIR):
                value = rotate_pair(part[:, half : half + PAIR], cosine, sine) * scale
                qkv[k, :, pl.ds(at + half, PAIR)] = value.astype(bf16)

        qkv[k, :, 2 * D :] = dot_nn(low, wq[:, 2 * D :]).astype(bf16)
        start_all(stores[k])

    last, queue, since = {}, list(range(seq)), 0
    for event in gather.events():
        if event:
            last[event[0]] = event[1]
            if event[0] == 1:
                for copy in into[:2] + last[0] + last[1]:
                    copy.wait()
                keep.start()
                total = gains[0, :2, :].astype(f32)
                for q in range(1, fsdp):
                    total = total + gains[q, :2, :].astype(f32)
                gains_out[...] = total
                wait_all(into[2:])
                start_all(outof)
                project(queue.pop(0))
        elif 1 in last:
            since += 1
            if since % 2 == 0 and len(queue) > 1:
                project(queue.pop(0))
    for k in queue:
        project(k)
    for copy in gather.pending:
        copy.wait_send()
    for w in range(2, count):
        wait_all(last[w])
    wait_all(outof)
    for group in stores:
        wait_all(group)
    keep.wait()


def enter_project(sizes, tokens, segments, shards):
    fsdp, rep, seq = sizes
    count, rows = len(shards), tokens.shape[1]
    length, columns = seq * rows, shards[1].shape[1]
    vmem = pl.BlockSpec(memory_space=pltpu.VMEM)
    copies = seq - 1 + Gather.count(sizes, gather_order(sizes, shards), count)
    return pl.pallas_call(
        functools.partial(enter_project_kernel, sizes, count),
        in_specs=[ANY, vmem] + [ANY] * count,
        out_specs=[ANY] * 3 + [vmem] * 5 + [ANY] * (count - 1),
        out_shape=[struct(bf16, seq, rows, D), struct(bf16, seq, rows, D), struct(bf16, seq, rows, columns),
                   struct(f32, length, PAIR), struct(f32, length, PAIR), struct(jnp.int32, length, 1),
                   struct(jnp.int32, 1, length), struct(f32, 2, D), struct(bf16, D, columns)]
        + [struct(bf16, fsdp, *s.shape) for s in shards[2:]],
        scratch_shapes=[pltpu.VMEM((seq, rows, D), bf16), pltpu.VMEM((seq, rows, D), bf16),
                        pltpu.VMEM((seq, rows, columns), bf16), pltpu.VMEM((D, columns), bf16),
                        pltpu.VMEM((fsdp,) + shards[0].shape, bf16)]
        + [pltpu.VMEM(s.shape, bf16) for s in shards[2:]] + [pltpu.VMEM((16, 128), bf16)] * 2
        + sem_shapes(copies, 2 + count + count - 2 + 3 * seq),
        compiler_params=pltpu.CompilerParams(
            collective_id=4, has_side_effects=True, vmem_limit_bytes=VMEM_LIMIT
        ),
    )(tokens, segments, *shards)


def add_into(total, term):
    rows = total.shape[0]
    height = 48 if rows % 48 == 0 else rows

    @pl.loop(0, rows // height)
    def _(i):
        at = pl.ds(pl.multiple_of(i * height, 16), height) if height < rows else pl.ds(0, rows)
        total[at, :] = (total[at, :].astype(f32) + term[at, :].astype(f32)).astype(bf16)


class Reducer:
    def __init__(self, parts_shape, sizes, order):
        self.fsdp, self.rows, self.cols = parts_shape
        self.steps = []
        held, rows, cols = list(range(self.fsdp)), self.rows, self.cols
        row_at, col_at = [], []
        for axis, bit in order:
            step = dict(axis=axis, bit=bit, row_at=list(row_at), col_at=list(col_at), rows=rows, cols=cols)
            if axis == "fsdp":
                step["send"] = [j for j in held if j & bit]
                held = [j for j in held if not j & bit]
                step["keep"] = held
                step["shape"] = (len(held), rows, cols)
                step["split"] = None
            else:
                step["keep"] = step["send"] = held
                if (axis, bit) == order[-1]:
                    step["split"] = "none"
                elif (rows // 2) % 16 == 0:
                    rows //= 2
                    row_at = row_at + [(axis, bit, rows)]
                    step["split"] = "rows"
                elif (cols // 2) % 128 == 0:
                    cols //= 2
                    col_at = col_at + [(axis, bit, cols)]
                    step["split"] = "cols"
                else:
                    step["split"] = "none"
                step["shape"] = (len(held), rows, cols)
            self.steps.append(step)
        self.down = len(self.steps)
        for step in reversed(self.steps[: self.down]):
            if step["split"] in ("rows", "cols"):
                self.steps.append(dict(step, up=True))

    @staticmethod
    def offset(terms, align, last=None):
        total = 0
        for i, (axis, bit, extent) in enumerate(terms):
            half = (lax.axis_index(axis) // bit) % 2
            if last == i:
                half = 1 - half
            total = total + half * extent
        return total if isinstance(total, int) else pl.multiple_of(total, align)

    def region(self, step, after, other=False):
        row_at, col_at, rows, cols = step["row_at"], step["col_at"], step["rows"], step["cols"]
        row_last = col_last = None
        if after:
            if step["split"] == "rows":
                rows //= 2
                row_at = row_at + [(step["axis"], step["bit"], rows)]
                row_last = len(row_at) - 1 if other else None
            elif step["split"] == "cols":
                cols //= 2
                col_at = col_at + [(step["axis"], step["bit"], cols)]
                col_last = len(col_at) - 1 if other else None
        return (
            pl.ds(self.offset(row_at, 16, row_last), rows),
            pl.ds(self.offset(col_at, 128, col_last), cols),
        )

    def scratch(self, first, last):
        return [pltpu.VMEM(s["shape"], bf16) for s in self.steps[first:last] if "up" not in s]

    def copies(self, first, last):
        return sum(1 if "up" in s else len(s["send"]) for s in self.steps[first:last])

    def bind(self, parts, lands, sems, first, last, final=None):
        self.parts, self.sems, self.final = parts, sems, final
        self.lands, self.moves = {}, {}
        lands = list(lands)
        for s in range(first, last):
            step = self.steps[s]
            moves = []
            if "up" in step:
                there = final.at[self.region(step, True)]
                moves.append(sems.remote(there, there, step["axis"], step["bit"]))
            else:
                land = self.lands[s] = lands.pop(0)
                for i, j in enumerate(step["send"]):
                    fsdp = step["axis"] == "fsdp"
                    src = self.parts(j).at[self.region(step, not fsdp, not fsdp)]
                    moves.append(sems.remote(src, land.at[i], step["axis"], step["bit"]))
            self.moves[s] = moves

    def start(self, s):
        if s == self.down:
            region = self.region(self.steps[s - 1], True)
            self.final[region] = self.parts(0)[region]
        start_all(self.moves.get(s, []))

    def finish(self, s):
        step = self.steps[s]
        self.finish_step(s, step)
        if s + 1 == len(self.steps) == self.down and self.final is not None:
            self.final[...] = self.parts(0)[...]

    def finish_step(self, s, step):
        for i, move in enumerate(self.moves[s]):
            move.wait()
            if "up" not in step:
                j = step["keep"][i]
                ref = self.parts(j)
                add_into(ref.at[self.region(step, True)], self.lands[s].at[i])


def give_back(slots, home, bounce, sems):
    me = lax.axis_index("seq")
    seq = slots.shape[0]
    return (
        sems.copy(slots.at[0], bounce),
        sems.copy(bounce, home.at[me]),
        [sems.remote(slots.at[k], home.at[me], "seq", k) for k in range(1, seq)],
    )


def body(sizes, tokens, segments, positions, gain_attn, w_qkv, w_out, gain_mlp, w_in, w_mlp_out, cotangent):
    fsdp, rep, seq = sizes
    micro, batch, rows, _ = tokens.shape
    assert micro * batch == seq and rows % TILE == 0
    length = seq * rows
    me_seq, me_fsdp = lax.axis_index("seq"), lax.axis_index("fsdp")

    own_gains = jnp.zeros((16, D), bf16)
    own_gains = lax.dynamic_update_slice(own_gains, jnp.stack([gain_attn, gain_mlp]), (0, me_fsdp * (D // fsdp)))
    shards = [own_gains, w_qkv, w_out, w_mlp_out, w_in]
    tiles, pairs = length // TILE, HEADS // 2
    late = fsdp in (2, 4) and pairs >= 6 and flat(D // fsdp) and flat(FF // fsdp)
    if (D // fsdp) % 16 == 0:
        x, a, qkv, cosine, sine, marks_column, marks_row, gains, wq, *rest = enter_project(
            sizes, tokens.reshape(seq, rows, D), segments, shards[:3] if late else shards
        )
        x, a, qkv = (v.reshape(length, -1) for v in (x, a, qkv))
        wo, *rest = (w.reshape(-1, w.shape[-1]) for w in rest)
        wm, wi = (w_mlp_out, w_in) if late else rest
    else:
        x, gains, wq, wo, wm, wi = enter(sizes, tokens.reshape(seq, rows, D), shards)
        x = x.reshape(length, D)
        gains = jnp.sum(gains[:, :2].astype(f32), axis=0)
        wq, wo, wm, wi = (w.reshape(-1, w.shape[-1]) for w in (wq, wo, wm, wi))

        marks = take(segments.reshape(seq, length), me_seq)
        place = jnp.arange(length, dtype=jnp.int32) - jnp.sum(
            (marks[None, :] < marks[:, None]).astype(jnp.int32), axis=1
        )
        slot_order = [me_seq ^ k for k in range(seq)]
        marks = jnp.concatenate([take(marks.reshape(seq, rows), s) for s in slot_order])
        place = jnp.concatenate([take(place.reshape(seq, rows), s) for s in slot_order])
        half = jnp.arange(0, HDIM, 2).astype(f32) / HDIM
        angles = place.astype(f32)[:, None] * jnp.exp(-half * math.log(THETA))
        cosine, sine = jnp.cos(angles), jnp.sin(angles)
        cosine = jnp.concatenate([cosine] * 4, -1)
        sine = jnp.concatenate([-sine, sine] * 2, -1)

        a, qkv = call(
            first_kernel, tiles,
            [rows_spec(D), whole_spec(2, D), whole_spec(D, 3 * D), rows_spec(PAIR), rows_spec(PAIR)],
            [rows_spec(D), rows_spec(3 * D)],
            [struct(bf16, length, D), struct(bf16, length, 3 * D)],
            2 * length * D * 3 * D,
        )(x, gains, wq, cosine, sine)
        marks_column, marks_row = marks[:, None], marks[None, :]

    vmem = pl.BlockSpec(memory_space=pltpu.VMEM)
    pair_at = lambda offset, lag, n: pl.BlockSpec(
        (length, PAIR), lambda i: (0, jnp.clip(i - lag, 0, n - 1) + offset)
    )
    prob_at = lambda lag: pl.BlockSpec((2, length, length), lambda i: (jnp.clip(i - lag, 0, pairs - 1), 0, 0))
    tile_at = lambda width, lag: pl.BlockSpec((TILE, width), lambda i: (jnp.clip(i - lag, 0, tiles - 1), 0))
    slots = struct(bf16, seq, rows, D)
    o, probs, inv, x1, b, m, slope, act, y, dy, *wholes = call(
        functools.partial(forward_kernel, sizes, pairs, late), pairs + tiles,
        [pair_at(0, 0, pairs), pair_at(pairs, 0, pairs), pair_at(2 * pairs, 0, pairs),
         whole_spec(length, 1), whole_spec(1, length), tile_at(D, pairs), whole_spec(2, D)] + [ANY] * 4,
        [pair_at(0, 0, pairs), prob_at(0), pair_at(0, 0, pairs), tile_at(D, pairs), tile_at(D, pairs)]
        + [tile_at(FF, pairs)] * 3 + [tile_at(D, pairs), ANY] + [ANY] * (2 * late),
        [struct(bf16, length, D), struct(bf16, HEADS, length, length), struct(f32, length, D),
         struct(f32, length, D), struct(bf16, length, D), struct(bf16, length, FF),
         struct(bf16, length, FF), struct(bf16, length, FF), struct(bf16, length, D), slots]
        + [struct(bf16, D, 2 * FF), struct(bf16, FF, D)] * late,
        16 * length * length * D,
        [pltpu.VMEM((length, D), bf16), pltpu.VMEM((D, D), bf16), pltpu.VMEM((D, 2 * FF), bf16), pltpu.VMEM((FF, D), bf16),
         pltpu.VMEM((rows, D), bf16)] + sem_shapes(seq - 1 + LateGather.copies(sizes) * late, 5 + 2 * late), 1,
    )(qkv, qkv, qkv, marks_column, marks_row, x, gains, wo, wi, wm, cotangent.reshape(seq, rows, D))

    if late:
        wi, wm = wholes
    reducers, early = early_reducers(sizes)
    whole = late_reducers(sizes)
    own_shard = lambda r: struct(bf16, r.rows, r.cols)
    full_shard = lambda r: pltpu.VMEM((fsdp * r.rows, r.cols) if flat(r.rows) else (fsdp, r.rows, r.cols), bf16)
    odd = (FF // fsdp) % 16 or (D // fsdp) % 16
    wide = pltpu.VMEM((FF, FF) if odd else (8, 128), f32)
    dx1, dgain_two, dq, dk, dv, block_out, *sums = call(
        functools.partial(backward_kernel, sizes, tiles), tiles + 1 + pairs,
        [tile_at(D, 0), tile_at(FF, 0), tile_at(FF, 0), whole_spec(2, D)]
        + [pair_at(n * pairs, tiles + 1, pairs) for n in range(3)]
        + [pair_at(0, tiles + 1, pairs), pair_at(0, tiles + 1, pairs)] + [ANY] * 11,
        [tile_at(D, 0), whole_spec(1, D)] + [pair_at(0, tiles + 1, pairs)] * 3 + [ANY] * (1 + len(reducers)),
        [struct(f32, length, D), struct(f32, 1, D)] + [struct(bf16, length, D)] * 3 + [slots]
        + [own_shard(r) for r in reducers],
        32 * length * length * D,
        [pltpu.VMEM((D, D), bf16), pltpu.VMEM((D, 2 * FF), bf16), pltpu.VMEM((FF, D), bf16),
         pltpu.VMEM((length, FF), bf16)] + [pltpu.VMEM((length, D), bf16)] * 3
        + [pltpu.VMEM((length, 2 * FF), bf16), pltpu.VMEM((length, D), bf16), pltpu.VMEM((length, D), bf16),
           wide, pltpu.VMEM((rows, D), bf16),
           pltpu.VMEM((2, 2, length, length), bf16)] + [pltpu.VMEM((length, PAIR), f32)] * 2
        + [full_shard(r) for r in reducers] + [pltpu.VMEM((reducers[0].rows, reducers[0].cols), bf16)]
        + [land for r, e in zip(reducers, early) for land in r.scratch(0, e)]
        + sem_shapes(seq - 1 + sum(r.copies(0, e) for r, e in zip(reducers, early)), 13 + len(reducers)), 2,
    )(x1, slope, act, gains, qkv, qkv, qkv, o, inv, probs, cosine, sine,
      wo, wi, wm, m, dy.reshape(length, D), b, o, y.reshape(seq, rows, D))

    hops = sum(len(bits_of(n)) for n in sizes)
    shard = lambda n, width: struct(bf16, n // fsdp, width)
    finals = [shard(D, 2 * FF), shard(D, D), shard(D, 3 * D)]
    operands = [dq, a, dk, dv, wq, x, dx1]
    grad_mlp, *sums = sums
    reducers, early = reducers[1:], early[1:]
    input_grad, grad_in, grad_out, grad_qkv, dgains = pl.pallas_call(
        functools.partial(leave_kernel, sizes),
        in_specs=[vmem] * 2 + [ANY] * (len(operands) + len(reducers)),
        out_specs=[ANY] * 4 + [vmem],
        out_shape=[slots] + finals + [struct(f32, 8, D)],
        scratch_shapes=[pltpu.VMEM(v.shape, v.dtype) for v in operands]
        + [pltpu.VMEM((seq, rows, D), bf16), wide]
        + [pltpu.VMEM(v.shape, v.dtype) for v in finals]
        + [pltpu.VMEM((r.rows, r.cols), bf16) for r in reducers]
        + [full_shard(r) for r in whole]
        + [land for r, e in zip(reducers, early) for land in r.scratch(e, len(r.steps))]
        + [land for r in whole for land in r.scratch(0, len(r.steps))]
        + [pltpu.VMEM((hops, 8, D), f32)]
        + sem_shapes(
            PIECES * (seq - 1) + hops + sum(r.copies(e, len(r.steps)) for r, e in zip(reducers, early))
            + sum(r.copies(0, len(r.steps)) for r in whole),
            1 + len(operands) + len(reducers) + len(finals),
        ),
        compiler_params=pltpu.CompilerParams(
            collective_id=3, has_side_effects=True, vmem_limit_bytes=VMEM_LIMIT
        ),
    )(gains, dgain_two, *operands, *sums)
    dgains = lax.dynamic_slice_in_dim(dgains, me_fsdp * (D // fsdp), D // fsdp, 1)
    input_grad, grad_qkv, grad_in, grad_mlp, grad_out, block_out = widen(
        [input_grad, grad_qkv, grad_in, grad_mlp, grad_out, block_out], [f32] * 5 + [bf16]
    )
    return (
        block_out.reshape(tokens.shape),
        input_grad.reshape(tokens.shape),
        dgains[0],
        grad_qkv,
        grad_out,
        dgains[1],
        grad_in,
        grad_mlp,
    )


def solution(mesh):
    sizes = (mesh.shape["fsdp"], mesh.shape["rep"], mesh.shape["seq"])
    wide = P(None, ("rep", "fsdp"), "seq", None)
    placed = (
        wide, P(None, ("rep", "fsdp"), None), P(None, ("rep", "fsdp"), "seq"),
        P("fsdp"), P("fsdp", None), P("fsdp", None), P("fsdp"), P("fsdp", None), P("fsdp", None), wide,
    )
    return jax.shard_map(
        functools.partial(body, sizes),
        mesh=mesh,
        in_specs=placed,
        out_specs=(
            wide, wide, P("fsdp"), P("fsdp", None), P("fsdp", None), P("fsdp"), P("fsdp", None), P("fsdp", None),
        ),
        check_vma=False,
    )
```

```python
import functools
import math

import jax
import jax.numpy as jnp
from jax import lax
from jax.experimental import pallas as pl
from jax.experimental.pallas import tpu as pltpu
from jax.sharding import PartitionSpec as P

D = 768
HEADS = 12
HDIM = 64
FF = 1152
EPS = 1e-05
THETA = 160000.0
MASKED = -1000000000.0
QUERY_SCALE = HDIM**-0.5 / math.log(2.0)
TILE = 256
PAIR = 2 * HDIM
WIDE = 384
HCHUNK = 384
f32 = jnp.float32
bf16 = jnp.bfloat16
VMEM_LIMIT = 62 * 2**20


def dot_nn(left, right):
    return lax.dot_general(left, right, (((1,), (0,)), ((), ())), preferred_element_type=f32)


def dot_nt(left, right):
    return lax.dot_general(left, right, (((1,), (1,)), ((), ())), preferred_element_type=f32)


def dot_tn(left, right):
    return lax.dot_general(left, right, (((0,), (0,)), ((), ())), preferred_element_type=f32)


def normalize(values):
    mean = jnp.mean(values, axis=-1, keepdims=True)
    centered = values - mean
    var = jnp.mean(centered * centered, axis=-1, keepdims=True)
    scale = lax.rsqrt(var + EPS)
    return centered * scale, scale


def norm_back(unit, scale, gain, grad):
    gain_terms = grad * unit
    inner = grad * gain
    first = jnp.mean(inner, axis=-1, keepdims=True)
    second = jnp.mean(inner * unit, axis=-1, keepdims=True)
    return scale * (inner - first - unit * second), gain_terms


def lane_halves(shape):
    lane = lax.broadcasted_iota(jnp.int32, shape, len(shape) - 1)
    return lane % HDIM < HDIM // 2


def rotate_pair(values, cosine, signed_sine):
    swapped = jnp.where(
        lane_halves(values.shape),
        pltpu.roll(values, PAIR - HDIM // 2, 1),
        pltpu.roll(values, HDIM // 2, 1),
    )
    return values * cosine + swapped * signed_sine


def first_kernel(x_ref, gain_ref, w_ref, cos_ref, sin_ref, a_ref, qkv_ref):
    unit, _ = normalize(x_ref[...].astype(f32))
    a = (unit * gain_ref[0:1, :]).astype(bf16)
    a_ref[...] = a
    cosine, sine = cos_ref[...], sin_ref[...]
    for column in range(0, 3 * D, TILE):
        part = dot_nn(a, w_ref[:, column : column + TILE])
        for half in range(0, TILE, PAIR):
            start = column + half
            piece = part[:, half : half + PAIR]
            if start < 2 * D:
                piece = rotate_pair(piece, cosine, sine)
            if start < D:
                piece = piece * QUERY_SCALE
            qkv_ref[:, start : start + PAIR] = piece.astype(bf16)


def head_lanes():
    lane = lax.broadcasted_iota(jnp.int32, (1, PAIR), 1)
    return [lane < HDIM, lane >= HDIM]


def attend_pair(q_ref, k_ref, v_ref, rows_ref, cols_ref, p_ref, inv_ref, write):
    k, v = k_ref[...], v_ref[...]
    length = k.shape[0]
    mine = head_lanes()
    zero, one = jnp.zeros((), bf16), jnp.ones((), bf16)
    summing = [jnp.where(m, v, one) for m in mine]
    items = [(tile, head) for tile in range(0, length, TILE) for head in range(2)]

    def score(item):
        tile, head = item
        return dot_nt(jnp.where(mine[head], q_ref[tile : tile + TILE, :], zero), k)

    ahead = score(items[0])
    kept = None
    for i, (tile, head) in enumerate(items):
        rows = slice(tile, tile + TILE)
        scores = ahead
        if i + 1 < len(items):
            ahead = score(items[i + 1])
        scores = jnp.where(rows_ref[rows, :] == cols_ref[...], scores, MASKED)
        probs = jnp.exp2(scores - jnp.max(scores, axis=-1, keepdims=True)).astype(bf16)
        p_ref[head, rows, :] = probs
        part = dot_nn(probs, summing[head])
        inv = 1.0 / pltpu.roll(part, HDIM, 1)
        if head == 0:
            kept = (part * inv, inv)
        else:
            inv_ref[rows, :] = jnp.where(mine[0], kept[1], inv)
            write(rows, jnp.where(mine[0], kept[0], part * inv).astype(bf16))


def forward_kernel(
    sizes, pairs, late, q_ref, k_ref, v_ref, rows_ref, cols_ref, x_ref, gain_ref, w_out_any, w_in_any, w_mlp_any, cot_ref,
    o_ref, p_ref, inv_ref, x1_ref, b_ref, m_ref, slope_ref, act_ref, y_ref, dy_ref, *refs,
):
    seq = sizes[2]
    refs = list(refs)
    outs = [refs.pop(0) for _ in range(2 * late)]
    joined, w_out_ref, w_in_ref, w_mlp_ref, bounce, *sem_refs = refs
    step, last = pl.program_id(0), pl.num_programs(0) - 1
    sems = Sems(*sem_refs)
    me_seq = lax.axis_index("seq")
    into = sems.copy(cot_ref.at[me_seq], bounce)
    outof = sems.copy(bounce, dy_ref.at[0])
    weights = [sems.copy(w_out_any, w_out_ref)]
    partners = [("seq", k) for k in range(1, seq)]
    if late:
        gather = LateGather(sizes, [w_in_any, w_mlp_any], [w_in_ref, w_mlp_ref], sems)
        weights += gather.own
        keeps = [sems.copy(w_in_ref, outs[0]), sems.copy(w_mlp_ref, outs[1])]
        partners = all_partners(sizes)
    else:
        weights += [sems.copy(w_in_any, w_in_ref), sems.copy(w_mlp_any, w_mlp_ref)]
    blocks = [sems.remote(cot_ref.at[flip(me_seq, k)], dy_ref.at[k], "seq", k) for k in range(1, seq)]

    @pl.when(step == 0)
    def _():
        into.start()
        start_all(weights)
        meet(partners)
        if late:
            start_all(gather.far)
        start_all(blocks)
        into.wait()
        outof.start()

    if late:
        for when in range(1, pairs + 1):
            @pl.when(step == when)
            def _(when=when):
                gather.advance(when)

    @pl.when(step < pairs)
    def _():
        def write(rows, value):
            o_ref[rows, :] = value
            joined[rows, pl.ds(pl.multiple_of(step * PAIR, PAIR), PAIR)] = value

        attend_pair(q_ref, k_ref, v_ref, rows_ref, cols_ref, p_ref, inv_ref, write)

    @pl.when(step == pairs)
    def _():
        if late:
            wait_all(weights[:1])
            gather.finish(0)
            keeps[0].start()
        else:
            wait_all(weights)

    @pl.when(step >= pairs)
    def _():
        start = pl.multiple_of((step - pairs) * TILE, TILE)
        x1 = x_ref[...].astype(f32) + dot_nn(joined[pl.ds(start, TILE), :], w_out_ref[...])
        x1_ref[...] = x1
        unit, _ = normalize(x1)
        b = (unit * gain_ref[1:2, :]).astype(bf16)
        b_ref[...] = b

        def hidden(column):
            return (
                dot_nn(b, w_in_ref[:, column : column + HCHUNK]),
                dot_nn(b, w_in_ref[:, FF + column : FF + column + HCHUNK]),
            )

        ahead = hidden(0)
        for column in range(0, FF, HCHUNK):
            hin, gate = ahead
            if column + HCHUNK < FF:
                ahead = hidden(column + HCHUNK)
            phi = 0.5 + 0.5 * lax.erf(hin * math.sqrt(0.5))
            act = hin * phi
            slope = phi + hin * (jnp.exp(hin * hin * -0.5) * (1.0 / math.sqrt(2.0 * math.pi)))
            m_ref[:, column : column + HCHUNK] = (act * gate).astype(bf16)
            act_ref[:, column : column + HCHUNK] = act.astype(bf16)
            slope_ref[:, column : column + HCHUNK] = (slope * gate).astype(bf16)
        if late:
            @pl.when(step == pairs)
            def _():
                gather.finish(1)
                keeps[1].start()

        y_ref[...] = (x1_ref[...] + dot_nn(m_ref[...], w_mlp_ref[...])).astype(bf16)

    @pl.when(step == last)
    def _():
        if late:
            wait_all(keeps)
        outof.wait()
        wait_all(blocks)


def order_of(sizes, rep_first):
    fsdp, rep, seq = sizes
    core = [("fsdp", 1)]
    rest = [("fsdp", b) for b in bits_of(fsdp)[1:]]
    copies = [("rep", b) for b in bits_of(rep)]
    return core + (copies + rest if rep_first else rest + copies) + [("seq", b) for b in bits_of(seq)]


def all_partners(sizes):
    fsdp, rep, seq = sizes
    return [("seq", k) for k in range(1, seq)] + [("fsdp", b) for b in bits_of(fsdp)] + [("rep", b) for b in bits_of(rep)]


def early_reducers(sizes):
    fsdp, rep, seq = sizes
    shapes = [(fsdp, FF // fsdp, D), (fsdp, D // fsdp, FF), (fsdp, D // fsdp, FF), (fsdp, D // fsdp, D)]
    reducers = [Reducer(shape, sizes, order_of(sizes, w == 2)) for w, shape in enumerate(shapes)]
    across = len(bits_of(fsdp)) + len(bits_of(rep))
    return reducers, [len(reducers[0].steps)] + [across + 2] * 2 + [across + 1]


def late_reducers(sizes):
    fsdp = sizes[0]
    return [Reducer((fsdp, D // fsdp, D), sizes, order_of(sizes, w == 1)) for w in range(3)]


def flat(rows):
    return rows % 16 == 0


def shard_of(ref, rows, q):
    return ref.at[pl.ds(pl.multiple_of(q * rows, 16), rows)] if flat(rows) else ref.at[q]


def weight_gradient(ref, wide, left, right):
    if len(ref.shape) == 2:
        @pl.loop(0, ref.shape[0] // HCHUNK)
        def _(i):
            at = pl.ds(pl.multiple_of(i * HCHUNK, HCHUNK), HCHUNK)
            ref[at, :] = dot_tn(left[:, at], right[...]).astype(bf16)
    else:
        shards, rows, cols = ref.shape
        wide[: shards * rows, :cols] = dot_tn(left[...], right[...])
        for q in range(shards):
            ref[q] = wide[q * rows : (q + 1) * rows, :cols].astype(bf16)


def middle_back_tile(dy, x1_ref, slope_ref, act_ref, gain_ref, w_out_ref, w_in_ref, w_mlp_ref, dh_ref, dgain_ref, dx1_ref):
    ahead = dot_nt(dy, w_mlp_ref[:HCHUNK, :])
    for column in range(0, FF, HCHUNK):
        dm = ahead
        if column + HCHUNK < FF:
            ahead = dot_nt(dy, w_mlp_ref[column + HCHUNK : column + 2 * HCHUNK, :])
        dh_ref[:, column : column + HCHUNK] = (dm * slope_ref[:, column : column + HCHUNK].astype(f32)).astype(bf16)
        dh_ref[:, FF + column : FF + column + HCHUNK] = (
            dm * act_ref[:, column : column + HCHUNK].astype(f32)
        ).astype(bf16)
    db = dot_nt(dh_ref[...], w_in_ref[...])
    unit, scale = normalize(x1_ref[...])
    back, terms = norm_back(unit, scale, gain_ref[1:2, :], db)
    dgain_ref[...] += jnp.sum(terms, axis=0, keepdims=True)
    dx1 = dy.astype(f32) + back
    dx1_ref[...] = dx1
    return dx1.astype(bf16)


def attend_back_pair(q_ref, k_ref, v_ref, o_ref, inv_ref, do, p_ref, cos_ref, sin_ref, dq_ref, dk_ref, dv_ref):
    v = v_ref[...]
    length = v.shape[0]
    mine = head_lanes()
    zero = jnp.zeros((), bf16)
    do = (do.astype(f32) * inv_ref[...]).astype(bf16)
    inner = do.astype(f32) * o_ref[...].astype(f32)
    do_heads = [jnp.where(m, do, zero) for m in mine]
    q_heads = [jnp.where(m, q_ref[...], zero).T for m in mine]
    k_heads = [jnp.where(m, k_ref[...], zero) for m in mine]
    do_turned = [d.T for d in do_heads]
    cosine, sine = cos_ref[...], sin_ref[...]
    dv = dk = None
    for tile in range(0, length, TILE):
        rows = slice(tile, tile + TILE)
        dq = None
        for head in range(2):
            probs = p_ref[head, rows, :]
            delta = jnp.sum(jnp.where(mine[head], inner[rows], 0.0), axis=-1, keepdims=True)
            dp = dot_nt(do_heads[head][rows], v)
            ds = (probs.astype(f32) * (dp - delta)).astype(bf16)
            value_part = dot_nn(do_turned[head][:, rows], probs)
            key_part = dot_nn(q_heads[head][:, rows], ds)
            query_part = dot_nn(ds, k_heads[head])
            dv = value_part if dv is None else dv + value_part
            dk = key_part if dk is None else dk + key_part
            dq = query_part if dq is None else dq + query_part
        dq_ref[rows, :] = rotate_pair(dq * HDIM**-0.5, cosine[rows], -sine[rows]).astype(bf16)
    dk_ref[...] = rotate_pair(dk.T * math.log(2.0), cosine, -sine).astype(bf16)
    dv_ref[...] = dv.T.astype(bf16)


def backward_kernel(
    sizes, tiles, x1_ref, slope_ref, act_ref, gain_ref, q_ref, k_ref, v_ref, o_ref, inv_ref,
    p_any, cos_any, sin_any, w_out_any, w_in_any, w_mlp_any, m_any, dy_any, b_any, o_any, y_ref, *refs,
):
    reducers, early = early_reducers(sizes)
    count = len(reducers)
    refs = list(refs)
    pop = lambda n: [refs.pop(0) for _ in range(n)]
    dx1_ref, dgain_ref, dq_ref, dk_ref, dv_ref, home_ref = pop(6)
    sums_out = pop(count)
    w_out_ref, w_in_ref, w_mlp_ref, m_ref, dy_ref, b_ref, all_o_ref = pop(7)
    dh_ref, low_ref, do_ref, wide, bounce, probs_ref, cos_ref, sin_ref = pop(8)
    grads = pop(count)
    (mlp_final,) = pop(1)
    lands = [pop(len(r.scratch(0, e))) for r, e in zip(reducers, early)]
    sems = Sems(*refs)
    me = lax.axis_index("fsdp")
    step, last = pl.program_id(0), pl.num_programs(0) - 1
    into, outof, blocks = give_back(y_ref, home_ref, bounce, sems)
    loads = [
        sems.copy(src, dst)
        for src, dst in [
            (m_any, m_ref), (dy_any, dy_ref), (w_mlp_any, w_mlp_ref), (w_in_any, w_in_ref), (w_out_any, w_out_ref),
            (b_any, b_ref), (o_any, all_o_ref), (cos_any, cos_ref), (sin_any, sin_ref),
        ]
    ]
    pair, pairs = step - tiles - 1, last - tiles
    slot_sems = [sems.local.at[sems.local_used + i] for i in range(2)]
    sems.local_used += 2

    def fetch(which, slot):
        return pltpu.make_async_copy(p_any.at[pl.ds(which * 2, 2)], probs_ref.at[slot], slot_sems[slot])
    stores = [sems.copy(mlp_final if w == 0 else shard_of(grads[w], reducers[w].rows, me), sums_out[w]) for w in range(count)]
    for w, reducer in enumerate(reducers):
        reducer.bind(lambda j, w=w: shard_of(grads[w], reducers[w].rows, flip(me, j)), lands[w], sems, 0, early[w], mlp_final if w == 0 else None)
    mlp, first_half, second_half, out = reducers

    def at(when, *actions):
        @pl.when(step == when)
        def _():
            for action in actions:
                action()

    def advance(reducer, s, limit):
        def run():
            reducer.finish(s)
            if s + 1 < limit:
                reducer.start(s + 1)
        return run

    @pl.when(step == 0)
    def _():
        start_all(loads)
        into.start()
        meet(all_partners(sizes))
        start_all(blocks)
        dgain_ref[...] = jnp.zeros_like(dgain_ref)
        wait_all(loads[:2])
        weight_gradient(grads[0], wide, m_ref, dy_ref)
        mlp.start(0)
        into.wait()
        outof.start()
        wait_all(loads[2:5])

    at(1, advance(mlp, 0, early[0]))

    @pl.when(step < tiles)
    def _():
        rows = pl.ds(pl.multiple_of(step * TILE, TILE), TILE)
        low = middle_back_tile(
            dy_ref[rows, :], x1_ref, slope_ref, act_ref, gain_ref, w_out_ref, w_in_ref, w_mlp_ref,
            dh_ref.at[rows, :], dgain_ref, dx1_ref,
        )
        low_ref[rows, :] = low
        do_ref[rows, :] = dot_nt(low, w_out_ref[...]).astype(bf16)

    across = len(bits_of(sizes[0])) + len(bits_of(sizes[1]))

    @pl.when(step == tiles)
    def _():
        wait_all(loads[5:])
        weight_gradient(grads[1], wide, b_ref, dh_ref.at[:, :FF])
        first_half.start(0)
        weight_gradient(grads[2], wide, b_ref, dh_ref.at[:, FF:])
        second_half.start(0)
        for s in range(1, across - 1):
            advance(mlp, s, early[0])()
        weight_gradient(grads[3], wide, all_o_ref, low_ref)
        out.start(0)

    @pl.when(step == tiles - 1)
    def _():
        fetch(0, 0).start()

    for slot in range(2):
        @pl.when((step > tiles) & (pair % 2 == slot))
        def _(slot=slot):
            fetch(pair, slot).wait()

            @pl.when(pair + 1 < pairs)
            def _():
                fetch(pair + 1, 1 - slot).start()

    halves = (first_half, second_half)
    steps = lambda reducer, limit, *which: [advance(reducer, s, limit) for s in which]
    half_steps = lambda *which: [advance(r, s, early[1]) for s in which for r in halves]
    middle = range(1, across - 1)
    at(tiles + 1, *steps(mlp, early[0], across - 1), *half_steps(0))
    at(tiles + 2, *steps(out, early[3], 0))
    at(tiles + 3, *half_steps(*middle))
    at(tiles + 4, *steps(mlp, early[0], across), *steps(out, early[3], *middle))
    at(tiles + 5, *steps(mlp, early[0], across + 1), *half_steps(across - 1))
    at(tiles + 6, *steps(mlp, early[0], *range(across + 2, early[0] - 1)), *half_steps(across), *steps(out, early[3], across - 1))

    @pl.when(step > tiles)
    def _():
        column = pl.multiple_of(pair * PAIR, PAIR)
        attend_back_pair(
            q_ref, k_ref, v_ref, o_ref, inv_ref, do_ref[:, pl.ds(column, PAIR)], probs_ref.at[pair % 2], cos_ref, sin_ref,
            dq_ref, dk_ref, dv_ref,
        )

    @pl.when(step == last)
    def _():
        for w, reducer in enumerate(reducers):
            reducer.finish(early[w] - 1)
            stores[w].start()
        wait_all(stores)
        outof.wait()
        wait_all(blocks)


PIECES = 4


def leave_kernel(sizes, gain_ref, other_gain_ref, *refs):
    fsdp, rep, seq = sizes
    reducers, early = (some[1:] for some in early_reducers(sizes))
    whole = late_reducers(sizes)
    count, more = len(reducers), len(whole)
    refs = list(refs)
    pop = lambda n: [refs.pop(0) for _ in range(n)]
    anys = pop(7)
    sums_in = pop(count)
    (home_ref,) = pop(1)
    in_out, out_out, qkv_out, gains_out = pop(4)
    dq_ref, a_ref, dk_ref, dv_ref, w_ref, x_ref, dx1_ref = local = pop(7)
    slots, wide, in_final, out_final, qkv_final = pop(5)
    held, grads = pop(count), pop(more)
    lands = [pop(len(r.scratch(e, len(r.steps)))) for r, e in zip(reducers, early)]
    whole_lands = [pop(len(r.scratch(0, len(r.steps)))) for r in whole]
    (gain_lands,) = pop(1)
    sems = Sems(*refs)
    me, me_seq = lax.axis_index("fsdp"), lax.axis_index("seq")
    own = sems.copy(slots.at[0], home_ref.at[me_seq])
    height = slots.shape[1] // PIECES
    blocks = {
        k: [
            sems.remote(slots.at[k, pl.ds(n * height, height)], home_ref.at[me_seq, pl.ds(n * height, height)], "seq", k)
            for n in range(PIECES)
        ]
        for k in range(1, seq)
    }
    order = sorted(range(1, seq), key=lambda k: (k != 2, k == 1))
    ready = []

    def send_piece(n=1):
        for _ in range(n):
            if ready:
                ready.pop(0).start()

    operands = [sems.copy(src, dst) for src, dst in zip(anys, local)]
    loads = [sems.copy(sums_in[w], held[w]) for w in range(count)]
    stores = [
        sems.copy(src, dst)
        for src, dst in ((in_final, in_out), (out_final, out_out), (qkv_final, qkv_out))
    ]
    finals = [in_final.at[:, pl.ds(0, FF)], in_final.at[:, pl.ds(FF, FF)], out_final]
    for w, reducer in enumerate(reducers):
        reducer.bind(lambda j, w=w: held[w], lands[w], sems, early[w], len(reducer.steps), finals[w])
    for w, reducer in enumerate(whole):
        reducer.bind(
            lambda j, w=w: shard_of(grads[w], whole[w].rows, flip(me, j)), whole_lands[w], sems, 0, len(reducer.steps),
            qkv_final.at[:, pl.ds(w * D, D)],
        )
    hops = [("fsdp", b) for b in bits_of(fsdp)] + [("rep", b) for b in bits_of(rep)] + [("seq", b) for b in bits_of(seq)]
    gain_moves = [sems.remote(gains_out, gain_lands.at[i], axis, bit) for i, (axis, bit) in enumerate(hops)]
    rows = slots.shape[1]

    def advance(some, s):
        for reducer in some:
            if s < len(reducer.steps):
                reducer.finish(s)
                if s + 1 < len(reducer.steps):
                    reducer.start(s + 1)

    def advance_gains(i):
        if i < len(hops):
            gain_moves[i].wait()
            gains_out[...] += gain_lands[i]
            if i + 1 < len(hops):
                gain_moves[i + 1].start()

    def input_slot(k):
        piece = slice(k * rows, (k + 1) * rows)
        da = dot_nt(dq_ref[piece, :], w_ref[:, :D])
        da = da + dot_nt(dk_ref[piece, :], w_ref[:, D : 2 * D])
        da = da + dot_nt(dv_ref[piece, :], w_ref[:, 2 * D :])
        unit, scale = normalize(x_ref[piece, :].astype(f32))
        back, terms = norm_back(unit, scale, gain_ref[0:1, :], da)
        gains_out[0:1, :] += jnp.sum(terms, axis=0, keepdims=True)
        slots[k] = (dx1_ref[piece, :] + back).astype(bf16)
        if k:
            ready.extend(blocks[k])

    def gradient(w, part):
        weight_gradient(grads[w], wide, a_ref, part)
        whole[w].start(0)

    across = len(bits_of(fsdp)) + len(bits_of(rep))
    halves, out, last = reducers[:2], reducers[2:], len(whole[0].steps)
    start_all(operands[:2])
    start_all(loads)
    start_all(operands[2:])
    gains_out[...] = jnp.zeros_like(gains_out)
    gains_out[1:2, :] = other_gain_ref[...]
    meet(all_partners(sizes))
    wait_all(loads)
    for w, (reducer, s) in enumerate(zip(reducers, early)):
        if s < len(reducer.steps):
            reducer.start(s)
        else:
            finals[w][...] = held[w][...]
    wait_all(operands[:2])
    gradient(0, dq_ref)
    wait_all(operands[2:])
    input_slot(order[0])
    send_piece(PIECES // 2)
    advance(whole[:1], 0)
    advance(halves, early[0])
    gradient(1, dk_ref)
    for k in order[1:2]:
        input_slot(k)
    advance(whole[1:2], 0)
    advance(out, early[2])
    send_piece()
    gradient(2, dv_ref)
    for k in order[2:]:
        input_slot(k)
    advance(whole[:1], 1)
    advance(whole[2:], 0)
    send_piece()
    input_slot(0)
    own.start()
    gain_moves[0].start()
    advance(whole[1:2], 1)
    advance(out, early[2] + 1)
    send_piece()
    hop = 0
    for s in range(2, across):
        advance(whole[:1], s)
        advance_gains(hop)
        advance(whole[2:], s - 1)
        advance(whole[1:2], s)
        send_piece()
        hop += 1
    advance(whole[2:], across - 1)
    advance_gains(hop)
    send_piece()
    for s in range(across, last):
        for reducer in whole:
            advance([reducer], s)
            send_piece()
        hop += 1
        advance_gains(hop)
    for i in range(hop + 1, len(hops)):
        advance_gains(i)
    send_piece(len(ready))
    for s in range(early[0] + 1, len(halves[0].steps)):
        advance(halves, s)
    for s in range(early[2] + 2, len(out[0].steps)):
        advance(out, s)
    start_all(stores)
    wait_all(stores)
    own.wait()
    for k in range(1, seq):
        wait_all(blocks[k])


def widen_kernel(count, *refs):
    anys, outs, narrow = refs[:count], refs[count : 2 * count], refs[2 * count : 3 * count]
    wide, sems = refs[3 * count : -1], refs[-1]
    loads = [pltpu.make_async_copy(anys[i], narrow[i], sems.at[i]) for i in range(count)]
    start_all(loads)
    stores = []
    for i in range(count):
        loads[i].wait()
        wide[i][...] = narrow[i][...].astype(wide[i].dtype)
        stores.append(pltpu.make_async_copy(wide[i], outs[i], sems.at[count + i]))
        stores[-1].start()
    wait_all(stores)


def widen(arrays, dtypes):
    count = len(arrays)
    return pl.pallas_call(
        functools.partial(widen_kernel, count),
        in_specs=[ANY] * count,
        out_specs=[ANY] * count,
        out_shape=[struct(t, *v.shape) for v, t in zip(arrays, dtypes)],
        scratch_shapes=[pltpu.VMEM(v.shape, v.dtype) for v in arrays]
        + [pltpu.VMEM(v.shape, t) for v, t in zip(arrays, dtypes)]
        + [pltpu.SemaphoreType.DMA((2 * count,))],
        compiler_params=pltpu.CompilerParams(vmem_limit_bytes=VMEM_LIMIT),
    )(*arrays)


def rows_spec(width):
    return pl.BlockSpec((TILE, width), lambda i: (i, 0))


def whole_spec(*shape):
    return pl.BlockSpec(shape, lambda i: (0,) * len(shape))


def pair_spec(length, offset=0):
    return pl.BlockSpec((length, PAIR), lambda i: (0, i + offset))


def struct(dtype, *shape):
    return jax.ShapeDtypeStruct(shape, dtype)


def call(kernel, grid, in_specs, out_specs, out_shape, flops, scratch=(), collective=None):
    return pl.pallas_call(
        kernel,
        grid=(grid,),
        in_specs=in_specs,
        out_specs=out_specs,
        out_shape=out_shape,
        scratch_shapes=list(scratch),
        compiler_params=pltpu.CompilerParams(
            dimension_semantics=("arbitrary",), vmem_limit_bytes=VMEM_LIMIT,
            collective_id=collective, has_side_effects=collective is not None,
        ),
        cost_estimate=pl.CostEstimate(flops=flops, bytes_accessed=10 * 2**20, transcendentals=0),
    )


MESH = pl.DeviceIdType.MESH
ANY = pl.BlockSpec(memory_space=pl.ANY)


def take(array, index):
    return lax.dynamic_index_in_dim(array, index, 0, keepdims=False)


def flip(index, mask):
    bit = 1
    while bit <= mask:
        if mask & bit:
            index = index + bit - 2 * bit * ((index // bit) % 2)
        bit *= 2
    return index


def flip_by(index, mask, size):
    total = 0
    for bit in bits_of(size):
        ours, theirs = (index // bit) % 2, (mask // bit) % 2
        total = total + bit * (ours + theirs - 2 * ours * theirs)
    return total


def bits_of(size):
    return [1 << i for i in range(size.bit_length() - 1)]


def meet(partners):
    barrier = pltpu.get_barrier_semaphore()
    for axis, mask in partners:
        pl.semaphore_signal(
            barrier, inc=1, device_id={axis: flip(lax.axis_index(axis), mask)}, device_id_type=MESH
        )
    pl.semaphore_wait(barrier, len(partners))


class Sems:
    def __init__(self, send, recv, local):
        self.send, self.recv, self.local = send, recv, local
        self.remote_used = self.local_used = 0

    def remote(self, src, dst, axis, mask):
        i = self.remote_used
        self.remote_used += 1
        return pltpu.make_async_remote_copy(
            src_ref=src, dst_ref=dst, send_sem=self.send.at[i], recv_sem=self.recv.at[i],
            device_id={axis: flip(lax.axis_index(axis), mask)}, device_id_type=MESH,
        )

    def copy(self, src, dst):
        i = self.local_used
        self.local_used += 1
        return pltpu.make_async_copy(src, dst, self.local.at[i])


def sem_shapes(remote, local):
    dma = pltpu.SemaphoreType.DMA
    return [dma((remote,)), dma((remote,)), dma((max(local, 1),))]


def start_all(copies):
    for copy in copies:
        copy.start()


def wait_all(copies):
    for copy in copies:
        copy.wait()


class Gather:
    def __init__(self, sizes, shards, place, sems, order):
        self.sizes, self.shards, self.place, self.sems = sizes, shards, place, sems
        self.pieces = order
        self.me, self.me_rep = lax.axis_index("fsdp"), lax.axis_index("rep")
        self.pending = []

    def part(self, ref, pieces, n):
        width = ref.shape[-1] // (self.sizes[1] * pieces)
        start = (self.me_rep * pieces + n) * width
        return ref.at[:, pl.ds(pl.multiple_of(start, 128), width)]

    def source(self, w, h):
        return self.shards[w] if h == 0 else self.place(w, flip(self.me, h))

    def start(self):
        self.held = [0]
        self.over = self.cross(self.far_bits()[0]) if self.far_bits() else []

    def far_bits(self):
        return list(reversed(bits_of(self.sizes[0])[1:]))

    def cross(self, bit):
        over = []
        for w, pieces, n in self.pieces:
            moved = [
                self.sems.remote(
                    self.part(self.source(w, h), pieces, n),
                    self.part(self.place(w, flip(self.me, h)), pieces, n), "fsdp", bit,
                )
                for h in self.held
            ]
            start_all(moved)
            over.append(moved)
        return over

    def pass_on(self, i, bit):
        w, pieces, n = self.pieces[i]
        for copy in self.over[i]:
            copy.wait_recv()
        self.pending += self.over[i]
        passed = []
        for mask in range(1, self.sizes[1]):
            for h in self.held:
                here = self.part(self.place(w, flip(self.me, h ^ bit)), pieces, n)
                passed.append(self.sems.remote(here, here, "rep", mask))
        start_all(passed)
        self.pending += passed
        return passed

    def events(self, lag=2):
        bits = self.far_bits()
        count = len(self.pieces)
        for bit in bits[:-1]:
            passed = [self.pass_on(i, bit) for i in range(count)]
            self.held = self.held + [h ^ bit for h in self.held]
            for copies in passed:
                for copy in copies:
                    copy.wait_recv()
            self.over = self.cross(bits[bits.index(bit) + 1])
        end = {w: i for i, (w, _, _) in enumerate(self.pieces)}
        passed, near_held = [], self.held + [h ^ bit for bit in bits[-1:] for h in self.held]
        for i in range(count + lag):
            if i < count:
                if bits:
                    passed.append(self.pass_on(i, bits[-1]))
                yield None
            for w, last in end.items():
                if last == i - lag:
                    if bits:
                        for j, (other, _, _) in enumerate(self.pieces):
                            if other == w:
                                for copy in passed[j]:
                                    copy.wait_recv()
                    yield w, self.near(w, near_held)

    def near(self, w, held):
        copies = [self.sems.remote(self.source(w, h), self.place(w, flip(self.me, h)), "fsdp", 1) for h in held]
        start_all(copies)
        return copies

    @staticmethod
    def count(sizes, order, weights):
        held, copies = 1, 0
        for _ in bits_of(sizes[0])[1:]:
            copies += len(order) * held * sizes[1]
            held *= 2
        return copies + weights * held


PASSED = (0, 1, 2, 4, 6, 6, 6)
CROSSED = (4, 5)


class LateGather:
    def __init__(self, sizes, shards, wholes, sems):
        fsdp, rep, _ = sizes
        me, me_rep = lax.axis_index("fsdp"), lax.axis_index("rep")
        place = lambda w, q: shard_of(wholes[w], shards[w].shape[0], q)
        self.own = [sems.copy(shards[w], place(w, me)) for w in range(2)]
        self.far, self.passed, self.near = [], [], [[], []]
        for w in range(2):
            fits = shards[w].shape[-1] % (rep * 3 * 128) == 0
            pieces = 3 if fits else 1
            width = shards[w].shape[-1] // (rep * pieces)
            for n in range(pieces if fsdp > 2 else 0):
                cols = pl.ds(pl.multiple_of((me_rep * pieces + n) * width, 128), width)
                self.far.append(sems.remote(shards[w].at[:, cols], place(w, me).at[:, cols], "fsdp", 2))
                here = place(w, flip(me, 2)).at[:, cols]
                self.passed.append([sems.remote(here, here, "rep", mask) for mask in range(1, rep)])
            for h in range(0, fsdp, 2):
                src = shards[w] if h == 0 else place(w, flip(me, h))
                self.near[w].append(sems.remote(src, place(w, flip(me, h)), "fsdp", 1))
        self.pieces = len(self.far) // 2
        self.count = len(self.far)

    @staticmethod
    def copies(sizes):
        return 2 * (3 * sizes[1] + sizes[0] // 2)

    def pass_on(self, i):
        self.far[i].wait_recv()
        start_all(self.passed[i])

    def cross_core(self, w):
        for copies in self.passed[w * self.pieces : (w + 1) * self.pieces]:
            for copy in copies:
                copy.wait_recv()
        start_all(self.near[w])

    def advance(self, step):
        upto = lambda n: min(n, self.count)
        for i in range(upto(PASSED[step - 1]), upto(PASSED[step])):
            self.pass_on(i)
        for w in range(2):
            if step == CROSSED[w]:
                self.cross_core(w)

    def finish(self, w):
        wait_all(self.own[w : w + 1])
        for i in range(w * self.pieces, (w + 1) * self.pieces):
            self.far[i].wait_send()
            for copy in self.passed[i]:
                copy.wait_send()
        wait_all(self.near[w])


def gather_order(sizes, shards):
    fits = lambda w, n: shards[w].shape[-1] % (sizes[1] * n * 128) == 0
    split = lambda w, n: n if fits(w, n) else 1
    order = []
    for w, n in ((0, 1), (1, 3), (2, 3), (4, 3), (3, 3)):
        if w >= len(shards):
            continue
        n = split(w, n)
        order += [(w, n, i) for i in range(n)]
    return order


def enter_kernel(sizes, count, tokens, *refs):
    fsdp, rep, seq = sizes
    refs = list(refs)
    pop = lambda n: [refs.pop(0) for _ in range(n)]
    shards = pop(count)
    (x_out,) = pop(1)
    fulls = pop(count)
    (bounce_x,) = pop(1)
    bounces = pop(count)
    sems = Sems(*refs)
    me, me_seq = lax.axis_index("fsdp"), lax.axis_index("seq")
    into = [sems.copy(tokens.at[me_seq], bounce_x)] + [sems.copy(shards[w], bounces[w]) for w in range(count)]
    outof = [sems.copy(bounce_x, x_out.at[0])] + [sems.copy(bounces[w], fulls[w].at[me]) for w in range(count)]
    gather = Gather(sizes, shards, lambda w, q: fulls[w].at[q], sems, gather_order(sizes, shards))
    start_all(into)
    meet(all_partners(sizes))
    blocks = [sems.remote(tokens.at[flip(me_seq, k)], x_out.at[k], "seq", k) for k in range(1, seq)]
    start_all(blocks)
    gather.start()
    last = []
    for event in gather.events():
        if event:
            last += event[1]
    wait_all(into)
    start_all(outof)
    for copy in gather.pending:
        copy.wait_send()
    wait_all(last)
    wait_all(blocks)
    wait_all(outof)


def enter(sizes, tokens, shards):
    fsdp = sizes[0]
    count = len(shards)
    hbm = lambda shape: struct(bf16, *shape)
    copies = sizes[2] - 1 + Gather.count(sizes, gather_order(sizes, shards), count)
    return pl.pallas_call(
        functools.partial(enter_kernel, sizes, count),
        in_specs=[ANY] * (1 + count),
        out_specs=[ANY] * (1 + count),
        out_shape=[hbm(tokens.shape)] + [hbm((fsdp,) + s.shape) for s in shards],
        scratch_shapes=[pltpu.VMEM(tokens.shape[1:], bf16)]
        + [pltpu.VMEM(s.shape, bf16) for s in shards]
        + sem_shapes(copies, 2 * (1 + count)),
        compiler_params=pltpu.CompilerParams(collective_id=0, has_side_effects=True),
    )(tokens, *shards)


def turn(row):
    n = row.shape[1]
    diagonal = lax.broadcasted_iota(jnp.int32, (n, n), 0) == lax.broadcasted_iota(jnp.int32, (n, n), 1)
    return jnp.sum(jnp.where(diagonal, row, 0), axis=1, keepdims=True)


def enter_project_kernel(sizes, count, tokens, segments, *refs):
    fsdp, rep, seq = sizes
    refs = list(refs)
    pop = lambda n: [refs.pop(0) for _ in range(n)]
    shards = pop(count)
    x_out, a_out, qkv_out, cos_out, sin_out, marks_out, row_out, gains_out, wq_out = pop(9)
    fulls = [None, None] + pop(count - 2)
    xs, a, qkv, wq, gains = pop(5)
    bounces = pop(count)
    sems = Sems(*refs)
    me, me_seq = lax.axis_index("fsdp"), lax.axis_index("seq")
    shard_rows, rows = shards[1].shape[0], xs.shape[1]
    columns = wq.shape[1]

    def place(w, q):
        if w == 0:
            return gains.at[q]
        if w == 1:
            return wq.at[pl.ds(pl.multiple_of(q * shard_rows, 16), shard_rows)]
        return fulls[w].at[q]

    own = sems.copy(tokens.at[me_seq], xs.at[0])
    into = [sems.copy(shards[w], place(w, me) if w < 2 else bounces[w - 2]) for w in range(count)]
    outof = [sems.copy(bounces[w - 2], place(w, me)) for w in range(2, count)]
    blocks = [sems.remote(tokens.at[flip(me_seq, k)], xs.at[k], "seq", k) for k in range(1, seq)]
    stores = [
        [sems.copy(src.at[k], dst.at[k]) for src, dst in ((xs, x_out), (a, a_out), (qkv, qkv_out))] for k in range(seq)
    ]
    keep = sems.copy(wq, wq_out)
    gather = Gather(sizes, shards, place, sems, gather_order(sizes, shards))
    own.start()
    start_all(into)
    meet(all_partners(sizes))
    gather.start()
    start_all(blocks)

    lane = lax.broadcasted_iota(jnp.int32, (1, PAIR), 1)
    rate = jnp.exp((lane % (HDIM // 2)).astype(f32) * (-2.0 * math.log(THETA) / HDIM))
    sign = jnp.where(lane_halves((1, PAIR)), -1.0, 1.0)
    batch = segments.shape[1]

    def own_segments(block):
        at = pl.multiple_of(block * rows, 128)
        return segments[me_seq // batch, pl.ds(me_seq % batch, 1), pl.ds(at, rows)]

    @pl.loop(0, seq)
    def _(k):
        block = flip_by(me_seq, k, seq)
        piece = pl.ds(pl.multiple_of(k * rows, 128), rows)
        row = own_segments(block)
        column = turn(row)
        earlier = jnp.zeros((rows, 1), jnp.int32)
        for other in range(seq):
            earlier += jnp.sum((own_segments(other) < column).astype(jnp.int32), axis=1, keepdims=True)
        index = block * rows + lax.broadcasted_iota(jnp.int32, (rows, 1), 0)
        angles = (index - earlier).astype(f32) * rate
        cos_out[piece, :] = jnp.cos(angles)
        sin_out[piece, :] = jnp.sin(angles) * sign
        marks_out[piece, :] = column
        row_out[:, piece] = row

    def project(k):
        if k == 0:
            own.wait()
        else:
            blocks[k - 1].wait()
        piece = slice(k * rows, (k + 1) * rows)
        unit, _ = normalize(xs[k].astype(f32))
        low = (unit * gains_out[0:1, :]).astype(bf16)
        a[k] = low
        cosine, sine = cos_out[piece, :], sin_out[piece, :]

        for at in range(0, 2 * D, WIDE):
            part = dot_nn(low, wq[:, at : at + WIDE])
            for half in range(0, WIDE, PAIR):
                value = rotate_pair(part[:, half : half + PAIR], cosine, sine)
                if at < D:
                    value = value * QUERY_SCALE
                qkv[k, :, at + half : at + half + PAIR] = value.astype(bf16)

        qkv[k, :, 2 * D :] = dot_nn(low, wq[:, 2 * D :]).astype(bf16)
        start_all(stores[k])

    last, queue, since = {}, list(range(seq)), 0
    for event in gather.events():
        if event:
            last[event[0]] = event[1]
            if event[0] == 1:
                for copy in into[:2] + last[0] + last[1]:
                    copy.wait()
                keep.start()
                total = gains[0, :2, :].astype(f32)
                for q in range(1, fsdp):
                    total = total + gains[q, :2, :].astype(f32)
                gains_out[...] = total
                wait_all(into[2:])
                start_all(outof)
                project(queue.pop(0))
        elif 1 in last:
            since += 1
            if since % 2 == 0 and len(queue) > 1:
                project(queue.pop(0))
    for k in queue:
        project(k)
    for copy in gather.pending:
        copy.wait_send()
    for w in range(2, count):
        wait_all(last[w])
    wait_all(outof)
    for group in stores:
        wait_all(group)
    keep.wait()


def enter_project(sizes, tokens, segments, shards):
    fsdp, rep, seq = sizes
    count, rows = len(shards), tokens.shape[1]
    length, columns = seq * rows, shards[1].shape[1]
    vmem = pl.BlockSpec(memory_space=pltpu.VMEM)
    copies = seq - 1 + Gather.count(sizes, gather_order(sizes, shards), count)
    return pl.pallas_call(
        functools.partial(enter_project_kernel, sizes, count),
        in_specs=[ANY, vmem] + [ANY] * count,
        out_specs=[ANY] * 3 + [vmem] * 5 + [ANY] * (count - 1),
        out_shape=[struct(bf16, seq, rows, D), struct(bf16, seq, rows, D), struct(bf16, seq, rows, columns),
                   struct(f32, length, PAIR), struct(f32, length, PAIR), struct(jnp.int32, length, 1),
                   struct(jnp.int32, 1, length), struct(f32, 2, D), struct(bf16, D, columns)]
        + [struct(bf16, fsdp, *s.shape) for s in shards[2:]],
        scratch_shapes=[pltpu.VMEM((seq, rows, D), bf16), pltpu.VMEM((seq, rows, D), bf16),
                        pltpu.VMEM((seq, rows, columns), bf16), pltpu.VMEM((D, columns), bf16),
                        pltpu.VMEM((fsdp,) + shards[0].shape, bf16)]
        + [pltpu.VMEM(s.shape, bf16) for s in shards[2:]] + [pltpu.VMEM((16, 128), bf16)] * 2
        + sem_shapes(copies, 2 + count + count - 2 + 3 * seq),
        compiler_params=pltpu.CompilerParams(
            collective_id=4, has_side_effects=True, vmem_limit_bytes=VMEM_LIMIT
        ),
    )(tokens, segments, *shards)


def add_into(total, term):
    rows = total.shape[0]
    height = 48 if rows % 48 == 0 else rows

    @pl.loop(0, rows // height)
    def _(i):
        at = pl.ds(pl.multiple_of(i * height, 16), height) if height < rows else pl.ds(0, rows)
        total[at, :] = (total[at, :].astype(f32) + term[at, :].astype(f32)).astype(bf16)


class Reducer:
    def __init__(self, parts_shape, sizes, order):
        self.fsdp, self.rows, self.cols = parts_shape
        self.steps = []
        held, rows, cols = list(range(self.fsdp)), self.rows, self.cols
        row_at, col_at = [], []
        for axis, bit in order:
            step = dict(axis=axis, bit=bit, row_at=list(row_at), col_at=list(col_at), rows=rows, cols=cols)
            if axis == "fsdp":
                step["send"] = [j for j in held if j & bit]
                held = [j for j in held if not j & bit]
                step["keep"] = held
                step["shape"] = (len(held), rows, cols)
                step["split"] = None
            else:
                step["keep"] = step["send"] = held
                if (axis, bit) == order[-1]:
                    step["split"] = "none"
                elif (rows // 2) % 16 == 0:
                    rows //= 2
                    row_at = row_at + [(axis, bit, rows)]
                    step["split"] = "rows"
                elif (cols // 2) % 128 == 0:
                    cols //= 2
                    col_at = col_at + [(axis, bit, cols)]
                    step["split"] = "cols"
                else:
                    step["split"] = "none"
                step["shape"] = (len(held), rows, cols)
            self.steps.append(step)
        self.down = len(self.steps)
        for step in reversed(self.steps[: self.down]):
            if step["split"] in ("rows", "cols"):
                self.steps.append(dict(step, up=True))

    @staticmethod
    def offset(terms, align, last=None):
        total = 0
        for i, (axis, bit, extent) in enumerate(terms):
            half = (lax.axis_index(axis) // bit) % 2
            if last == i:
                half = 1 - half
            total = total + half * extent
        return total if isinstance(total, int) else pl.multiple_of(total, align)

    def region(self, step, after, other=False):
        row_at, col_at, rows, cols = step["row_at"], step["col_at"], step["rows"], step["cols"]
        row_last = col_last = None
        if after:
            if step["split"] == "rows":
                rows //= 2
                row_at = row_at + [(step["axis"], step["bit"], rows)]
                row_last = len(row_at) - 1 if other else None
            elif step["split"] == "cols":
                cols //= 2
                col_at = col_at + [(step["axis"], step["bit"], cols)]
                col_last = len(col_at) - 1 if other else None
        return (
            pl.ds(self.offset(row_at, 16, row_last), rows),
            pl.ds(self.offset(col_at, 128, col_last), cols),
        )

    def scratch(self, first, last):
        return [pltpu.VMEM(s["shape"], bf16) for s in self.steps[first:last] if "up" not in s]

    def copies(self, first, last):
        return sum(1 if "up" in s else len(s["send"]) for s in self.steps[first:last])

    def bind(self, parts, lands, sems, first, last, final=None):
        self.parts, self.sems, self.final = parts, sems, final
        self.lands, self.moves = {}, {}
        lands = list(lands)
        for s in range(first, last):
            step = self.steps[s]
            moves = []
            if "up" in step:
                there = final.at[self.region(step, True)]
                moves.append(sems.remote(there, there, step["axis"], step["bit"]))
            else:
                land = self.lands[s] = lands.pop(0)
                for i, j in enumerate(step["send"]):
                    fsdp = step["axis"] == "fsdp"
                    src = self.parts(j).at[self.region(step, not fsdp, not fsdp)]
                    moves.append(sems.remote(src, land.at[i], step["axis"], step["bit"]))
            self.moves[s] = moves

    def start(self, s):
        if s == self.down:
            region = self.region(self.steps[s - 1], True)
            self.final[region] = self.parts(0)[region]
        start_all(self.moves.get(s, []))

    def finish(self, s):
        step = self.steps[s]
        self.finish_step(s, step)
        if s + 1 == len(self.steps) == self.down and self.final is not None:
            self.final[...] = self.parts(0)[...]

    def finish_step(self, s, step):
        for i, move in enumerate(self.moves[s]):
            move.wait()
            if "up" not in step:
                j = step["keep"][i]
                ref = self.parts(j)
                add_into(ref.at[self.region(step, True)], self.lands[s].at[i])


def give_back(slots, home, bounce, sems):
    me = lax.axis_index("seq")
    seq = slots.shape[0]
    return (
        sems.copy(slots.at[0], bounce),
        sems.copy(bounce, home.at[me]),
        [sems.remote(slots.at[k], home.at[me], "seq", k) for k in range(1, seq)],
    )


def body(sizes, tokens, segments, positions, gain_attn, w_qkv, w_out, gain_mlp, w_in, w_mlp_out, cotangent):
    fsdp, rep, seq = sizes
    micro, batch, rows, _ = tokens.shape
    assert micro * batch == seq and rows % TILE == 0
    length = seq * rows
    me_seq, me_fsdp = lax.axis_index("seq"), lax.axis_index("fsdp")

    own_gains = jnp.zeros((16, D), bf16)
    own_gains = lax.dynamic_update_slice(own_gains, jnp.stack([gain_attn, gain_mlp]), (0, me_fsdp * (D // fsdp)))
    shards = [own_gains, w_qkv, w_out, w_mlp_out, w_in]
    tiles, pairs = length // TILE, HEADS // 2
    late = fsdp in (2, 4) and pairs >= 6 and flat(D // fsdp) and flat(FF // fsdp)
    if (D // fsdp) % 16 == 0:
        x, a, qkv, cosine, sine, marks_column, marks_row, gains, wq, *rest = enter_project(
            sizes, tokens.reshape(seq, rows, D), segments, shards[:3] if late else shards
        )
        x, a, qkv = (v.reshape(length, -1) for v in (x, a, qkv))
        wo, *rest = (w.reshape(-1, w.shape[-1]) for w in rest)
        wm, wi = (w_mlp_out, w_in) if late else rest
    else:
        x, gains, wq, wo, wm, wi = enter(sizes, tokens.reshape(seq, rows, D), shards)
        x = x.reshape(length, D)
        gains = jnp.sum(gains[:, :2].astype(f32), axis=0)
        wq, wo, wm, wi = (w.reshape(-1, w.shape[-1]) for w in (wq, wo, wm, wi))

        marks = take(segments.reshape(seq, length), me_seq)
        place = jnp.arange(length, dtype=jnp.int32) - jnp.sum(
            (marks[None, :] < marks[:, None]).astype(jnp.int32), axis=1
        )
        slot_order = [me_seq ^ k for k in range(seq)]
        marks = jnp.concatenate([take(marks.reshape(seq, rows), s) for s in slot_order])
        place = jnp.concatenate([take(place.reshape(seq, rows), s) for s in slot_order])
        half = jnp.arange(0, HDIM, 2).astype(f32) / HDIM
        angles = place.astype(f32)[:, None] * jnp.exp(-half * math.log(THETA))
        cosine, sine = jnp.cos(angles), jnp.sin(angles)
        cosine = jnp.concatenate([cosine] * 4, -1)
        sine = jnp.concatenate([-sine, sine] * 2, -1)

        a, qkv = call(
            first_kernel, tiles,
            [rows_spec(D), whole_spec(2, D), whole_spec(D, 3 * D), rows_spec(PAIR), rows_spec(PAIR)],
            [rows_spec(D), rows_spec(3 * D)],
            [struct(bf16, length, D), struct(bf16, length, 3 * D)],
            2 * length * D * 3 * D,
        )(x, gains, wq, cosine, sine)
        marks_column, marks_row = marks[:, None], marks[None, :]

    vmem = pl.BlockSpec(memory_space=pltpu.VMEM)
    pair_at = lambda offset, lag, n: pl.BlockSpec(
        (length, PAIR), lambda i: (0, jnp.clip(i - lag, 0, n - 1) + offset)
    )
    prob_at = lambda lag: pl.BlockSpec((2, length, length), lambda i: (jnp.clip(i - lag, 0, pairs - 1), 0, 0))
    tile_at = lambda width, lag: pl.BlockSpec((TILE, width), lambda i: (jnp.clip(i - lag, 0, tiles - 1), 0))
    slots = struct(bf16, seq, rows, D)
    o, probs, inv, x1, b, m, slope, act, y, dy, *wholes = call(
        functools.partial(forward_kernel, sizes, pairs, late), pairs + tiles,
        [pair_at(0, 0, pairs), pair_at(pairs, 0, pairs), pair_at(2 * pairs, 0, pairs),
         whole_spec(length, 1), whole_spec(1, length), tile_at(D, pairs), whole_spec(2, D)] + [ANY] * 4,
        [pair_at(0, 0, pairs), prob_at(0), pair_at(0, 0, pairs), tile_at(D, pairs), tile_at(D, pairs)]
        + [tile_at(FF, pairs)] * 3 + [tile_at(D, pairs), ANY] + [ANY] * (2 * late),
        [struct(bf16, length, D), struct(bf16, HEADS, length, length), struct(f32, length, D),
         struct(f32, length, D), struct(bf16, length, D), struct(bf16, length, FF),
         struct(bf16, length, FF), struct(bf16, length, FF), struct(bf16, length, D), slots]
        + [struct(bf16, D, 2 * FF), struct(bf16, FF, D)] * late,
        16 * length * length * D,
        [pltpu.VMEM((length, D), bf16), pltpu.VMEM((D, D), bf16), pltpu.VMEM((D, 2 * FF), bf16), pltpu.VMEM((FF, D), bf16),
         pltpu.VMEM((rows, D), bf16)] + sem_shapes(seq - 1 + LateGather.copies(sizes) * late, 5 + 2 * late), 1,
    )(qkv, qkv, qkv, marks_column, marks_row, x, gains, wo, wi, wm, cotangent.reshape(seq, rows, D))

    if late:
        wi, wm = wholes
    reducers, early = early_reducers(sizes)
    whole = late_reducers(sizes)
    own_shard = lambda r: struct(bf16, r.rows, r.cols)
    full_shard = lambda r: pltpu.VMEM((fsdp * r.rows, r.cols) if flat(r.rows) else (fsdp, r.rows, r.cols), bf16)
    odd = (FF // fsdp) % 16 or (D // fsdp) % 16
    wide = pltpu.VMEM((FF, FF) if odd else (8, 128), f32)
    dx1, dgain_two, dq, dk, dv, block_out, *sums = call(
        functools.partial(backward_kernel, sizes, tiles), tiles + 1 + pairs,
        [tile_at(D, 0), tile_at(FF, 0), tile_at(FF, 0), whole_spec(2, D)]
        + [pair_at(n * pairs, tiles + 1, pairs) for n in range(3)]
        + [pair_at(0, tiles + 1, pairs), pair_at(0, tiles + 1, pairs)] + [ANY] * 11,
        [tile_at(D, 0), whole_spec(1, D)] + [pair_at(0, tiles + 1, pairs)] * 3 + [ANY] * (1 + len(reducers)),
        [struct(f32, length, D), struct(f32, 1, D)] + [struct(bf16, length, D)] * 3 + [slots]
        + [own_shard(r) for r in reducers],
        32 * length * length * D,
        [pltpu.VMEM((D, D), bf16), pltpu.VMEM((D, 2 * FF), bf16), pltpu.VMEM((FF, D), bf16),
         pltpu.VMEM((length, FF), bf16)] + [pltpu.VMEM((length, D), bf16)] * 3
        + [pltpu.VMEM((length, 2 * FF), bf16), pltpu.VMEM((length, D), bf16), pltpu.VMEM((length, D), bf16),
           wide, pltpu.VMEM((rows, D), bf16),
           pltpu.VMEM((2, 2, length, length), bf16)] + [pltpu.VMEM((length, PAIR), f32)] * 2
        + [full_shard(r) for r in reducers] + [pltpu.VMEM((reducers[0].rows, reducers[0].cols), bf16)]
        + [land for r, e in zip(reducers, early) for land in r.scratch(0, e)]
        + sem_shapes(seq - 1 + sum(r.copies(0, e) for r, e in zip(reducers, early)), 13 + len(reducers)), 2,
    )(x1, slope, act, gains, qkv, qkv, qkv, o, inv, probs, cosine, sine,
      wo, wi, wm, m, dy.reshape(length, D), b, o, y.reshape(seq, rows, D))

    hops = sum(len(bits_of(n)) for n in sizes)
    shard = lambda n, width: struct(bf16, n // fsdp, width)
    finals = [shard(D, 2 * FF), shard(D, D), shard(D, 3 * D)]
    operands = [dq, a, dk, dv, wq, x, dx1]
    grad_mlp, *sums = sums
    reducers, early = reducers[1:], early[1:]
    input_grad, grad_in, grad_out, grad_qkv, dgains = pl.pallas_call(
        functools.partial(leave_kernel, sizes),
        in_specs=[vmem] * 2 + [ANY] * (len(operands) + len(reducers)),
        out_specs=[ANY] * 4 + [vmem],
        out_shape=[slots] + finals + [struct(f32, 8, D)],
        scratch_shapes=[pltpu.VMEM(v.shape, v.dtype) for v in operands]
        + [pltpu.VMEM((seq, rows, D), bf16), wide]
        + [pltpu.VMEM(v.shape, v.dtype) for v in finals]
        + [pltpu.VMEM((r.rows, r.cols), bf16) for r in reducers]
        + [full_shard(r) for r in whole]
        + [land for r, e in zip(reducers, early) for land in r.scratch(e, len(r.steps))]
        + [land for r in whole for land in r.scratch(0, len(r.steps))]
        + [pltpu.VMEM((hops, 8, D), f32)]
        + sem_shapes(
            PIECES * (seq - 1) + hops + sum(r.copies(e, len(r.steps)) for r, e in zip(reducers, early))
            + sum(r.copies(0, len(r.steps)) for r in whole),
            1 + len(operands) + len(reducers) + len(finals),
        ),
        compiler_params=pltpu.CompilerParams(
            collective_id=3, has_side_effects=True, vmem_limit_bytes=VMEM_LIMIT
        ),
    )(gains, dgain_two, *operands, *sums)
    dgains = lax.dynamic_slice_in_dim(dgains, me_fsdp * (D // fsdp), D // fsdp, 1)
    input_grad, grad_qkv, grad_in, grad_mlp, grad_out, block_out = widen(
        [input_grad, grad_qkv, grad_in, grad_mlp, grad_out, block_out], [f32] * 5 + [bf16]
    )
    return (
        block_out.reshape(tokens.shape),
        input_grad.reshape(tokens.shape),
        dgains[0],
        grad_qkv,
        grad_out,
        dgains[1],
        grad_in,
        grad_mlp,
    )


def solution(mesh):
    sizes = (mesh.shape["fsdp"], mesh.shape["rep"], mesh.shape["seq"])
    wide = P(None, ("rep", "fsdp"), "seq", None)
    placed = (
        wide, P(None, ("rep", "fsdp"), None), P(None, ("rep", "fsdp"), "seq"),
        P("fsdp"), P("fsdp", None), P("fsdp", None), P("fsdp"), P("fsdp", None), P("fsdp", None), wide,
    )
    return jax.shard_map(
        functools.partial(body, sizes),
        mesh=mesh,
        in_specs=placed,
        out_specs=(
            wide, wide, P("fsdp"), P("fsdp", None), P("fsdp", None), P("fsdp"), P("fsdp", None), P("fsdp", None),
        ),
        check_vma=False,
    )
```
